32 devices in a mesh: patch: 8 (over z, y), var: 4 (over x, core).
Axes of the slice: x: 2, y: 2, z: 4, core: 2. Of those that a mesh axis runs over, the one named last changes fastest.
Arguments:
- input_field: bfloat16 [4, 1024, 48, 16], P(None, 'patch', 'var'), may hold values from -6 to 6
- counts: int32 [4], replicated, may hold values from 256 to 1024, as said below
- var_ids: int32 [4, 48], replicated, may hold values from 0 to 47, each once within a row
- patch_weight: bfloat16 [48, 16, 1024], replicated, may hold values from -1.5 to 1.5
- var_embed: bfloat16 [48, 1024], replicated, may hold values from -6 to 6
- agg_query: bfloat16 [1024], replicated, may hold values from -6 to 6
- query_proj: bfloat16 [1024, 1024], replicated, may hold values from -0.1875 to 0.1875
- key_proj: bfloat16 [1024, 1024], replicated, may hold values from -0.1875 to 0.1875
- value_proj: bfloat16 [1024, 1024], replicated, may hold values from -0.1875 to 0.1875
- agg_out: bfloat16 [1024, 1024], replicated, may hold values from -0.375 to 0.375
- norm_one: bfloat16 [1024], replicated, may hold values from 0.099609375 to 1.8984375
- trunk_qkv: bfloat16 [1024, 3072], replicated, may hold values from -0.1875 to 0.1875
- trunk_out: bfloat16 [1024, 1024], replicated, may hold values from -1.5 to 1.5
- norm_two: bfloat16 [1024], replicated, may hold values from 0.099609375 to 1.8984375
- mlp_in: bfloat16 [1024, 4096], replicated, may hold values from -0.1875 to 0.1875
- mlp_out: bfloat16 [4096, 1024], replicated, may hold values from -0.09375 to 0.09375
- cotangent: bfloat16 [4, 1024, 1024], P('var', 'patch'), may hold values from -6 to 6
Outputs:
- block_out: bfloat16 [4, 1024, 1024], P('var', 'patch')
- field_grad: bfloat16 [4, 1024, 48, 16], P(None, 'patch', 'var')
- patch_weight_grad: float32 [48, 16, 1024], P(None, None, 'patch')
- var_embed_grad: float32 [48, 1024], P(None, 'patch')
- agg_query_grad: float32 [1024], P('patch')
- query_proj_grad: float32 [1024, 1024], P('patch')
- key_proj_grad: float32 [1024, 1024], P('patch')
- value_proj_grad: float32 [1024, 1024], P('patch')
- agg_out_grad: float32 [1024, 1024], P('patch')
- norm_one_grad: float32 [1024], P('patch')
- trunk_qkv_grad: float32 [1024, 3072], P('patch')
- trunk_out_grad: float32 [1024, 1024], P('patch')
- norm_two_grad: float32 [1024], P('patch')
- mlp_in_grad: float32 [1024, 4096], P('patch')
- mlp_out_grad: float32 [4096, 1024], P('patch')
The draws below stay inside these ranges and needn't reach their ends.
Inputs may be any that keep to these rules, and one draw needn't show every extreme that they name: Each sample fills its first counts slots; every count is 256 or 1024; some sample has 1024 and some other sample has 256. `var_ids`: each row is a permutation of the 48 variables.
All inputs are finite; a program needn't handle non-finite values.
Results may differ from the reference program's by a relative error of at most 0.04.
Values may be sent and summed in bfloat16 or wider, within the bound.
No kernel may reach another device: no remote copies, remote signals or barrier semaphores. Data moves between devices by JAX's collectives and lax.ppermute only.
A program may use at most 384 MiB of HBM per device.

```python
import math
import jax
import jax.numpy as jnp
from jax import lax

D = 1024
HEADS = 16
HEAD_DIM = 64
FF = 4096
VARS = 48
PIX = 16
LENGTH = 1024
ROWS = 4


def draw_counts(key, part):
    first_key, second_key = jax.random.split(jax.random.fold_in(key, 17))
    longer = jax.random.randint(first_key, (ROWS,), 0, 2)
    order = jax.random.permutation(second_key, ROWS)
    slots = jnp.arange(ROWS)
    longer = jnp.where(slots == order[0], 1, longer)
    longer = jnp.where(slots == order[1], 0, longer)
    return (LENGTH // 4 + longer * (LENGTH - LENGTH // 4)).astype(jnp.int32)


def block_levels(key, shape, cuts, smallest, largest):
    level = 1.0
    for dim, blocks in cuts:
        draws = jax.random.uniform(jax.random.fold_in(jax.random.fold_in(key, 6), dim), (blocks,), jnp.float32, smallest / len(cuts), largest / len(cuts))
        level = level * jnp.repeat(jnp.exp(draws), shape[dim] // blocks).reshape((-1,) + (1,) * (len(shape) - 1 - dim))
    return level


def gaussian(key, extent, scale, most, cuts=(), dtype=jnp.bfloat16):
    loudness = block_levels(key, extent, cuts, -0.22, 0.18) if cuts else 1.0
    values = jax.random.normal(key, extent, jnp.float32) * scale * loudness
    return jnp.minimum(jnp.maximum(values, -most), most).astype(dtype)


def setup_inputs(seed: int = 0) -> dict:
    streams_of = jax.random.split(jax.random.key(seed), 18)
    input_field = gaussian(streams_of[0], (ROWS, LENGTH, VARS, PIX), 1.0, 6.0, ((1, 8), (2, 4)))
    counts = draw_counts(jax.random.fold_in(streams_of[17], 71), 0)
    var_ids = jax.vmap(lambda own: jax.random.permutation(own, VARS))(jax.random.split(streams_of[2], ROWS)).reshape((ROWS, VARS)).astype(jnp.int32)
    patch_weight = gaussian(streams_of[3], (VARS, PIX, D), PIX ** -0.5, 1.5)
    var_embed = gaussian(streams_of[4], (VARS, D), 1.0, 6.0)
    agg_query = gaussian(streams_of[5], (D,), 1.0, 6.0)
    query_proj = gaussian(streams_of[6], (D, D), D ** -0.5, 0.1875)
    key_proj = gaussian(streams_of[7], (D, D), D ** -0.5, 0.1875)
    value_proj = gaussian(streams_of[8], (D, D), D ** -0.5, 0.1875)
    agg_out = gaussian(streams_of[9], (D, D), (D // 4) ** -0.5, 0.375)
    norm_one = jnp.clip(1.0 + 0.18 * jax.random.normal(streams_of[10], (D,), jnp.float32), 0.099609375, 1.8984375).astype(jnp.bfloat16)
    trunk_qkv = gaussian(streams_of[11], (D, 3 * D), D ** -0.5, 0.1875)
    trunk_out = gaussian(streams_of[12], (D, D), (D // 64) ** -0.5, 1.5)
    norm_two = jnp.clip(1.0 + 0.18 * jax.random.normal(streams_of[13], (D,), jnp.float32), 0.099609375, 1.8984375).astype(jnp.bfloat16)
    mlp_in = gaussian(streams_of[14], (D, FF), D ** -0.5, 0.1875)
    mlp_out = gaussian(streams_of[15], (FF, D), FF ** -0.5, 0.09375)
    cotangent = gaussian(streams_of[16], (ROWS, LENGTH, D), 1.0, 6.0, ((0, 4), (1, 8)))
    return {"input_field": input_field, "counts": counts, "var_ids": var_ids, "patch_weight": patch_weight, "var_embed": var_embed, "agg_query": agg_query, "query_proj": query_proj, "key_proj": key_proj, "value_proj": value_proj, "agg_out": agg_out, "norm_one": norm_one, "trunk_qkv": trunk_qkv, "trunk_out": trunk_out, "norm_two": norm_two, "mlp_in": mlp_in, "mlp_out": mlp_out, "cotangent": cotangent}


@jax.custom_vjp
def low(v):
    return lax.optimization_barrier(v.astype(jnp.bfloat16)).astype(jnp.float32)

@jax.custom_vjp
def low_back(v):
    return v

def low_keep(v):
    return (low(v), None)

def low_pass(kept, grad):
    return (grad,)

def back_keep(v):
    return (v, None)

def back_low(kept, grad):
    return (low(grad),)
low.defvjp(low_keep, low_pass)
low_back.defvjp(back_keep, back_low)
HIGHEST = lax.Precision.HIGHEST
EPSILON = 1e-05
MASKED = -1e+30

def round_both(values):
    return low(low_back(values))

def layer_norm(values, gain_vec):
    average = lax.optimization_barrier(jnp.mean(values, axis=-1, keepdims=True))
    center = values - average
    spread = lax.optimization_barrier(jnp.mean(center * center, axis=-1, keepdims=True))
    return center * lax.rsqrt(spread + EPSILON) * gain_vec

def gelu_exact(values):
    return jax.nn.gelu(values, approximate=False)

def front_block(block_field, row_weight, row_embed, agg_q, key_proj, value_proj, agg_out):
    positions = block_field.shape[0]
    scaling = 1.0 / math.sqrt(HEAD_DIM)
    embedded = jnp.einsum('pjx,jxd->pjd', block_field, row_weight, precision=HIGHEST) + row_embed[None]
    embedded = round_both(embedded)
    flat_rows = embedded.reshape(-1, D)
    key_rows = round_both(jnp.dot(flat_rows, key_proj, precision=HIGHEST)).reshape(positions, VARS, HEADS, HEAD_DIM)
    value_rows = round_both(jnp.dot(flat_rows, value_proj, precision=HIGHEST)).reshape(positions, VARS, HEADS, HEAD_DIM)
    scores = lax.optimization_barrier(jnp.sum(key_rows * agg_q.reshape(HEADS, HEAD_DIM), axis=-1)) * scaling
    row_max = lax.optimization_barrier(jnp.max(scores, axis=1, keepdims=True))
    exponent = jnp.exp(scores - row_max)
    shares = exponent / lax.optimization_barrier(jnp.sum(exponent, axis=1, keepdims=True))
    mixed_rows = lax.optimization_barrier(jnp.sum(shares[..., None] * value_rows, axis=1)).reshape(positions, D)
    mixed_rows = round_both(mixed_rows)
    return low_back(jnp.dot(mixed_rows, agg_out, precision=HIGHEST))

def attend_block(query_block, key_all, value_all, key_valid):
    scaling = 1.0 / math.sqrt(HEAD_DIM)
    scores = jnp.einsum('qhd,khd->hqk', query_block, key_all, precision=HIGHEST) * scaling
    scores = low_back(scores)
    masked = jnp.where(key_valid[None, None, :], scores, MASKED)
    row_max = lax.optimization_barrier(jnp.max(masked, axis=-1, keepdims=True))
    exponent = jnp.exp(masked - row_max)
    shares = exponent / lax.optimization_barrier(jnp.sum(exponent, axis=-1, keepdims=True))
    shares = low(shares)
    return jnp.einsum('hqk,khd->qhd', shares, value_all, precision=HIGHEST)

def one_row(row_field, row_count, row_ids, weights):
    patch_weight, var_embed, agg_query, query_proj, key_proj, value_proj, agg_out, norm_one, trunk_qkv, trunk_out, norm_two, mlp_in, mlp_out = weights
    row_weight = patch_weight[row_ids]
    row_embed = var_embed[row_ids]
    agg_q = jnp.dot(agg_query, query_proj, precision=HIGHEST)
    span = min(512, LENGTH)
    field_blocks = row_field.reshape(LENGTH // span, span, VARS, PIX)

    def front_piece(piece):
        return front_block(piece, row_weight, row_embed, agg_q, key_proj, value_proj, agg_out)
    front_out = lax.map(jax.checkpoint(front_piece), field_blocks).reshape(LENGTH, D)
    positions = jnp.arange(LENGTH)
    valid_rows = (positions < row_count).astype(jnp.float32)
    front_out = front_out * valid_rows[:, None]
    normed_one = low(layer_norm(front_out, norm_one))
    triple = jnp.dot(normed_one, trunk_qkv, precision=HIGHEST)
    queries = round_both(triple[:, :D]).reshape(LENGTH // span, span, HEADS, HEAD_DIM)
    key_all = round_both(triple[:, D:2 * D]).reshape(LENGTH, HEADS, HEAD_DIM)
    value_all = round_both(triple[:, 2 * D:]).reshape(LENGTH, HEADS, HEAD_DIM)
    key_valid = positions < row_count

    def attend_piece(piece):
        return attend_block(piece, key_all, value_all, key_valid)
    attended = lax.map(jax.checkpoint(attend_piece), queries).reshape(LENGTH, D)
    attended = round_both(attended)
    after_attn = front_out + low_back(jnp.dot(attended, trunk_out, precision=HIGHEST))
    normed_two = low(layer_norm(after_attn, norm_two))
    inner_rows = low_back(jnp.dot(normed_two, mlp_in, precision=HIGHEST))
    active = low(gelu_exact(inner_rows))
    result = after_attn + low_back(jnp.dot(active, mlp_out, precision=HIGHEST))
    return result * valid_rows[:, None]

def reference(input_field, counts, var_ids, patch_weight, var_embed, agg_query, query_proj, key_proj, value_proj, agg_out, norm_one, trunk_qkv, trunk_out, norm_two, mlp_in, mlp_out, cotangent):
    floats = (input_field, patch_weight, var_embed, agg_query, query_proj, key_proj, value_proj, agg_out, norm_one, trunk_qkv, trunk_out, norm_two, mlp_in, mlp_out)
    floats = tuple((array.astype(jnp.float32) for array in floats))

    def forward(field_all, *weights):

        def row_fn(inputs):
            return one_row(inputs[0], inputs[1], inputs[2], weights)
        return lax.map(jax.checkpoint(row_fn), (field_all, counts.astype(jnp.int32), var_ids.astype(jnp.int32)))
    output, pullback = jax.vjp(forward, *floats)
    grads = pullback(cotangent.astype(jnp.float32))
    return (output.astype(jnp.bfloat16), grads[0].astype(jnp.bfloat16), grads[1], grads[2], grads[3], grads[4], grads[5], grads[6], grads[7], grads[8], grads[9], grads[10], grads[11], grads[12], grads[13])
```

```python
import functools
import math

import jax
import jax.numpy as jnp
from jax import lax
from jax.experimental import pallas as pl
from jax.experimental.pallas import tpu as pltpu
from jax.sharding import PartitionSpec as P

HEADS = 16
VARS = 48
EPSILON = 1e-05
MASKED = -1e30
HIGHEST = lax.Precision.HIGHEST
BF16 = jnp.bfloat16
F32 = jnp.float32
NN = (((1,), (0,)), ((), ()))
NT = (((1,), (1,)), ((), ()))
TN = (((0,), (0,)), ((), ()))


def mm(a, b, dims=NN, precision=None):
    return lax.dot_general(a, b, dims, precision=precision, preferred_element_type=F32)


def layer_norm(values, gain_vec):
    average = jnp.mean(values, axis=-1, keepdims=True)
    center = values - average
    spread = jnp.mean(center * center, axis=-1, keepdims=True)
    return center * lax.rsqrt(spread + EPSILON) * gain_vec


def gelu_exact(values):
    return jax.nn.gelu(values, approximate=False)


def split_high_low(values):
    high = values.astype(BF16)
    return high, (values - high.astype(F32)).astype(BF16)


def front_forward_kernel(
    pixels, ids_ref, field_ref, spread_ref, bias_ref, vwt_ref, vet_ref, x_ref, p_ref, mixed_ref, mt_ref
):
    seg = field_ref.shape[1]
    head_dim = mixed_ref.shape[1] // HEADS
    for slot in range(VARS):
        start = pl.multiple_of(ids_ref[0, slot] * pixels, pixels)
        x_ref[pl.ds(start, pixels), :] = field_ref[slot * pixels : (slot + 1) * pixels, :]
    scores = mm(spread_ref[...], x_ref[...]) + bias_ref[...]
    scores = scores.reshape(HEADS, VARS, seg)
    top = jnp.max(scores, axis=1, keepdims=True)
    exponent = jnp.exp(scores - top)
    total = jnp.sum(exponent, axis=1, keepdims=True)
    p_ref[...] = (exponent * (1.0 / total)).reshape(HEADS * VARS, seg)

    def head(h, carry):
        shares = p_ref[pl.ds(pl.multiple_of(h * VARS, VARS), VARS), :]
        pix = x_ref[...].astype(F32).reshape(VARS, pixels, seg)
        scaled = (pix * shares[:, None, :]).astype(BF16).reshape(VARS * pixels, seg)
        rows = pl.ds(pl.multiple_of(h * head_dim, head_dim), head_dim)
        mt_ref[rows, :] = mm(vwt_ref[rows, :], scaled) + mm(vet_ref[rows, :], shares.astype(BF16))
        return carry

    lax.fori_loop(0, HEADS, head, 0)
    mixed_ref[...] = mt_ref[...].T.astype(BF16)


def front_forward(own_ids, own_field, spread, bias, vwt, vet):
    rows, seg = own_field.shape
    width = vwt.shape[0]
    vmem = pl.BlockSpec(memory_space=pltpu.VMEM)
    return pl.pallas_call(
        functools.partial(front_forward_kernel, rows // VARS),
        out_shape=(
            jax.ShapeDtypeStruct((rows, seg), BF16),
            jax.ShapeDtypeStruct((HEADS * VARS, seg), F32),
            jax.ShapeDtypeStruct((seg, width), BF16),
        ),
        in_specs=[pl.BlockSpec(memory_space=pltpu.SMEM)] + [vmem] * 5,
        out_specs=(vmem,) * 3,
        scratch_shapes=[pltpu.VMEM((width, seg), F32)],
        name="front_forward",
    )(own_ids, own_field, spread, bias, vwt, vet)


def front_backward_kernel(
    pixels,
    ids_ref,
    x_ref,
    p_ref,
    mg_ref,
    vw_ref,
    ve_ref,
    spread_ref,
    field_ref,
    m_ref,
    me_ref,
    s_ref,
    se_ref,
    fs_ref,
    dx_ref,
):
    rows, seg = x_ref.shape
    width = mg_ref.shape[1]
    head_dim = width // HEADS
    pair_dim = 2 * head_dim
    lane = lax.broadcasted_iota(jnp.int32, (seg, pair_dim), 1)
    dx_ref[...] = jnp.zeros_like(dx_ref)

    def pair(q, carry):
        cols = pl.ds(pl.multiple_of(q * pair_dim, pair_dim), pair_dim)
        grad = mg_ref[:, cols]
        none = jnp.zeros_like(grad)
        both = jnp.concatenate(
            [jnp.where(lane < head_dim, grad, none), jnp.where(lane >= head_dim, grad, none)], axis=0
        )
        inner = mm(vw_ref[:, cols], both, NT)
        inner_e = mm(ve_ref[:, cols], both, NT)
        pix = x_ref[...].astype(F32).reshape(VARS, pixels, seg)
        scaled, weights = [], []
        for k in range(2):
            hrows = pl.ds(pl.multiple_of((2 * q + k) * VARS, VARS), VARS)
            shares = p_ref[hrows, :]
            part = inner[:, k * seg : (k + 1) * seg].reshape(VARS, pixels, seg)
            share_grad = jnp.sum(pix * part, axis=1) + inner_e[:, k * seg : (k + 1) * seg]
            delta = jnp.sum(shares * share_grad, axis=0, keepdims=True)
            fs_ref[hrows, :] = shares * (share_grad - delta)
            wide = shares[:, None, :]
            dx_ref[...] += (part * wide).reshape(rows, seg)
            scaled.append((pix * wide).astype(BF16).reshape(rows, seg))
            weights.append(shares.astype(BF16))
        m_ref[:, cols] = mm(jnp.concatenate(scaled, axis=1), both).astype(BF16)
        me_ref[:, cols] = mm(jnp.concatenate(weights, axis=1), both).astype(BF16)
        return carry

    lax.fori_loop(0, HEADS // 2, pair, 0)
    score_grad = fs_ref[...]
    low = score_grad.astype(BF16)
    dx = dx_ref[...] + mm(spread_ref[...], low, TN)
    dx_ref[...] = dx
    for slot in range(VARS):
        start = pl.multiple_of(ids_ref[0, slot] * pixels, pixels)
        field_ref[slot * pixels : (slot + 1) * pixels, :] = dx_ref[pl.ds(start, pixels), :].astype(BF16)
    se_ref[...] = jnp.sum(score_grad, axis=1, keepdims=True)
    var_row = lax.broadcasted_iota(jnp.int32, (VARS, rows), 0)
    var_col = lax.broadcasted_iota(jnp.int32, (VARS, rows), 1) // pixels
    keep = var_row == var_col
    for h in range(HEADS):
        outer = mm(low[h * VARS : (h + 1) * VARS, :], x_ref[...], NT)
        s_ref[h : h + 1, :] = jnp.sum(jnp.where(keep, outer, 0.0), axis=0, keepdims=True)


def front_backward(own_ids, x_own, shares, mixed_grad, vw, ve, spread):
    rows, seg = x_own.shape
    width = mixed_grad.shape[1]
    vmem = pl.BlockSpec(memory_space=pltpu.VMEM)
    return pl.pallas_call(
        functools.partial(front_backward_kernel, rows // VARS),
        out_shape=(
            jax.ShapeDtypeStruct((rows, seg), BF16),
            jax.ShapeDtypeStruct((rows, width), BF16),
            jax.ShapeDtypeStruct((VARS, width), BF16),
            jax.ShapeDtypeStruct((HEADS, rows), F32),
            jax.ShapeDtypeStruct((HEADS * VARS, 1), F32),
        ),
        in_specs=[pl.BlockSpec(memory_space=pltpu.SMEM)] + [vmem] * 6,
        out_specs=(vmem,) * 5,
        scratch_shapes=[pltpu.VMEM((HEADS * VARS, seg), F32), pltpu.VMEM((rows, seg), F32)],
        name="front_backward",
    )(own_ids, x_own, shares, mixed_grad, vw, ve, spread)


def load_parts(ref, part, seg, out_ref):
    for source in range(ref.shape[0]):
        out_ref[source * seg : (source + 1) * seg, :] = ref[source, part * seg : (part + 1) * seg, :]


def attend_forward_kernel(head_dim, block, count_ref, qkv_ref, out_ref, lse_ref, q_ref, k_ref, vt_ref):
    full, width = q_ref.shape
    seg = full // qkv_ref.shape[0]
    scaling = 1.0 / math.sqrt(head_dim)
    load_parts(qkv_ref, 2, seg, q_ref)
    vt_ref[...] = q_ref[...].T
    load_parts(qkv_ref, 0, seg, q_ref)
    load_parts(qkv_ref, 1, seg, k_ref)
    count = count_ref[0, 0]
    lane = lax.broadcasted_iota(jnp.int32, (block, width), 1) // head_dim
    row = lax.broadcasted_iota(jnp.int32, (width, block), 0) // head_dim
    valid = lax.broadcasted_iota(jnp.int32, (full, block), 0) < count

    def step(i, carry):
        part = pl.ds(pl.multiple_of(i * block, block), block)
        query = q_ref[part, :]
        total = jnp.zeros((width, block), F32)
        for h in range(width // head_dim):
            own = jnp.where(lane == h, query, jnp.zeros_like(query))
            scores = jnp.where(valid, mm(k_ref[...], own, NT) * scaling, MASKED)
            top = jnp.max(scores, axis=0, keepdims=True)
            exponent = jnp.exp(scores - top)
            denominator = jnp.sum(exponent, axis=0, keepdims=True)
            shares = (exponent * (1.0 / denominator)).astype(BF16)
            lse_ref[h : h + 1, part] = top + jnp.log(denominator)
            total = jnp.where(row == h, mm(vt_ref[...], shares), total)
        out_ref[part, :] = total.T.astype(BF16)
        return carry

    lax.fori_loop(0, full // block, step, 0)


def attend_forward(count, qkv, head_dim):
    parts, triple_rows, width = qkv.shape
    full = parts * triple_rows // 3
    vmem = pl.BlockSpec(memory_space=pltpu.VMEM)
    block = min(256, full)
    return pl.pallas_call(
        functools.partial(attend_forward_kernel, head_dim, block),
        out_shape=(
            jax.ShapeDtypeStruct((full, width), BF16),
            jax.ShapeDtypeStruct((width // head_dim, full), F32),
        ),
        in_specs=[pl.BlockSpec(memory_space=pltpu.SMEM), vmem],
        out_specs=(vmem, vmem),
        scratch_shapes=[
            pltpu.VMEM((full, width), BF16),
            pltpu.VMEM((full, width), BF16),
            pltpu.VMEM((width, full), BF16),
        ],
        name="attend_forward",
    )(count, qkv)


def attend_backward_kernel(
    head_dim, block, count_ref, qkv_ref, grad_ref, lse_ref, out_ref, q_ref, k_ref, v_ref, kt_ref, dk_ref, dv_ref
):
    full, width = q_ref.shape
    seg = full // qkv_ref.shape[0]
    scaling = 1.0 / math.sqrt(head_dim)
    load_parts(qkv_ref, 0, seg, q_ref)
    load_parts(qkv_ref, 1, seg, k_ref)
    load_parts(qkv_ref, 2, seg, v_ref)
    kt_ref[...] = k_ref[...].T
    dk_ref[...] = jnp.zeros_like(dk_ref)
    dv_ref[...] = jnp.zeros_like(dv_ref)
    count = count_ref[0, 0]
    lane = lax.broadcasted_iota(jnp.int32, (block, width), 1) // head_dim
    row = lax.broadcasted_iota(jnp.int32, (width, block), 0) // head_dim
    valid = lax.broadcasted_iota(jnp.int32, (full, block), 0) < count

    def step(i, carry):
        part = pl.ds(pl.multiple_of(i * block, block), block)
        query = q_ref[part, :]
        grad = grad_ref[part, :]
        total = jnp.zeros((width, block), F32)
        for h in range(width // head_dim):
            own = jnp.where(lane == h, query, jnp.zeros_like(query))
            own_grad = jnp.where(lane == h, grad, jnp.zeros_like(grad))
            scores = jnp.where(valid, mm(k_ref[...], own, NT) * scaling, MASKED)
            shares = jnp.exp(scores - lse_ref[h : h + 1, part])
            share_grad = mm(v_ref[...], own_grad, NT)
            dot = jnp.sum(shares * share_grad, axis=0, keepdims=True)
            score_grad = (shares * (share_grad - dot)).astype(BF16)
            dv_ref[...] += mm(shares.astype(BF16), own_grad)
            dk_ref[...] += mm(score_grad, own)
            total = jnp.where(row == h, mm(kt_ref[...], score_grad), total)
        turned = (total * scaling).T.astype(BF16)
        for piece in range(block // seg):
            out_ref[i * (block // seg) + piece, 0:seg, :] = turned[piece * seg : (piece + 1) * seg, :]
        return carry

    lax.fori_loop(0, full // block, step, 0)
    for source in range(full // seg):
        rows = slice(source * seg, (source + 1) * seg)
        out_ref[source, seg : 2 * seg, :] = (dk_ref[rows, :] * scaling).astype(BF16)
        out_ref[source, 2 * seg : 3 * seg, :] = dv_ref[rows, :].astype(BF16)


def attend_backward(count, qkv, grad, lse, head_dim):
    parts, triple_rows, width = qkv.shape
    full = parts * triple_rows // 3
    vmem = pl.BlockSpec(memory_space=pltpu.VMEM)
    block = min(256, full)
    return pl.pallas_call(
        functools.partial(attend_backward_kernel, head_dim, block),
        out_shape=jax.ShapeDtypeStruct(qkv.shape, BF16),
        in_specs=[pl.BlockSpec(memory_space=pltpu.SMEM), vmem, vmem, vmem],
        out_specs=vmem,
        scratch_shapes=[pltpu.VMEM((full, width), BF16)] * 3
        + [pltpu.VMEM((width, full), BF16)]
        + [pltpu.VMEM((full, width), F32)] * 2,
        name="attend_backward",
    )(count, qkv, grad, lse)


def gathered_attention(triple, count, head_dim):
    seg, triple_width = triple.shape
    width = triple_width // 3
    scaling = 1.0 / math.sqrt(head_dim)
    full = seg * lax.axis_size("patch")
    query = triple[:, :width].reshape(seg, HEADS, head_dim)
    key = lax.all_gather(triple[:, width : 2 * width], "patch", axis=0, tiled=True)
    value = lax.all_gather(triple[:, 2 * width :], "patch", axis=0, tiled=True)
    key = key.reshape(full, HEADS, head_dim)
    value = value.reshape(full, HEADS, head_dim)
    valid = (jnp.arange(full, dtype=jnp.int32) < count)[None, None, :]

    def score():
        raw = jnp.einsum("qhd,khd->hqk", query, key, preferred_element_type=F32) * scaling
        return jnp.where(valid, raw, MASKED)

    masked = score()
    top = jnp.max(masked, axis=-1, keepdims=True)
    exponent = jnp.exp(masked - top)
    denominator = jnp.sum(exponent, axis=-1, keepdims=True)
    shares_low = (exponent / denominator).astype(BF16)
    lse = top + jnp.log(denominator)
    attended = jnp.einsum("hqk,khd->qhd", shares_low, value, preferred_element_type=F32)

    def backward(grad):
        grad = grad.reshape(seg, HEADS, head_dim)
        shares = jnp.exp(score() - lse)
        share_grad = jnp.einsum("qhd,khd->hqk", grad, value, preferred_element_type=F32)
        dot = jnp.sum(shares * share_grad, axis=-1, keepdims=True)
        score_grad = (shares * (share_grad - dot)).astype(BF16)
        q_grad = jnp.einsum("hqk,khd->qhd", score_grad, key, preferred_element_type=F32) * scaling
        v_all = jnp.einsum("hqk,qhd->khd", shares.astype(BF16), grad, preferred_element_type=F32)
        k_all = jnp.einsum("hqk,qhd->khd", score_grad, query, preferred_element_type=F32) * scaling
        k_grad, v_grad = (
            lax.psum_scatter(
                part.reshape(full, width).astype(BF16), "patch", scatter_dimension=0, tiled=True
            )
            for part in (k_all, v_all)
        )
        return jnp.concatenate([q_grad.reshape(seg, width).astype(BF16), k_grad, v_grad], axis=1)

    return attended.reshape(seg, width).astype(BF16), backward


def exchanged_attention(triple, count, head_dim):
    seg, triple_width = triple.shape
    width = triple_width // 3
    parts = lax.axis_size("patch")
    own = width // parts
    count = count.reshape(1, 1)
    send = triple.reshape(seg, 3, parts, own).transpose(2, 1, 0, 3).reshape(parts, 3 * seg, own)
    qkv = lax.all_to_all(send, "patch", split_axis=0, concat_axis=0, tiled=True)
    out, lse = attend_forward(count, qkv, head_dim)
    back = lax.all_to_all(out.reshape(parts, seg, own), "patch", split_axis=0, concat_axis=0, tiled=True)
    attended = back.transpose(1, 0, 2).reshape(seg, width)

    def backward(grad):
        grads = grad.reshape(seg, parts, own).transpose(1, 0, 2)
        grads = lax.all_to_all(grads, "patch", split_axis=0, concat_axis=0, tiled=True)
        result = attend_backward(count, qkv, grads.reshape(parts * seg, own), lse, head_dim)
        result = lax.all_to_all(result, "patch", split_axis=0, concat_axis=0, tiled=True)
        result = result.reshape(parts, 3, seg, own).transpose(2, 1, 0, 3)
        return result.reshape(seg, 3 * width)

    return attended, backward


def send(values, axis, pairs):
    return lax.ppermute(values, axis, pairs)


def swap(values, axis, bit):
    return lax.ppermute(values, axis, [(i, i ^ bit) for i in range(lax.axis_size(axis))])


def tokens_of_group(values, plan):
    if plan:
        across = swap(values, "var", 2)
        return jnp.concatenate([values, across, swap(values, "var", 1), swap(across, "var", 1)], axis=0)
    return lax.all_gather(values, "var", axis=0, tiled=True)


def slices_of_group(piece_of, plan):
    me = lax.axis_index("var")
    if plan:
        return jnp.concatenate(
            [piece_of(me)] + [swap(piece_of(me ^ bit), "var", bit) for bit in (2, 1, 3)], axis=0
        )
    stacked = jnp.stack([piece_of(v) for v in range(lax.axis_size("var"))])
    moved = lax.all_to_all(stacked, "var", split_axis=0, concat_axis=0, tiled=True)
    return moved.reshape(-1, moved.shape[-1])


def scatter_over_patch(partial, plan):
    parts = lax.axis_size("patch")
    rows, cols = partial.shape[0] // parts, partial.shape[1]
    if not plan:
        return lax.psum_scatter(partial.astype(BF16), "patch", scatter_dimension=0, tiled=True)
    ys, zs = plan
    index = lax.axis_index("patch")
    z, y = index // ys, index % ys
    blocks = partial.reshape(zs, ys, rows, cols)
    away = lax.dynamic_index_in_dim(blocks, 1 - y, 1, keepdims=False).astype(BF16)
    near = lax.dynamic_index_in_dim(blocks, y, 1, keepdims=False)
    held = near + swap(away, "patch", 1).astype(F32)

    def block_of(t):
        return lax.dynamic_index_in_dim(held, jnp.clip(t, 0, zs - 1), 0, keepdims=False)

    up = down = None
    for s in range(1, zs):
        up_out, down_out = block_of(zs + z - s), block_of(z + s - zs)
        if up is not None:
            up_out, down_out = up_out + up.astype(F32), down_out + down.astype(F32)
        up_pairs = [(a * ys + b, (a + 1) * ys + b) for a in range(s) for b in range(ys)]
        down_pairs = [(a * ys + b, (a - 1) * ys + b) for a in range(zs - s, zs) for b in range(ys)]
        up = send(up_out.astype(BF16), "patch", up_pairs)
        down = send(down_out.astype(BF16), "patch", down_pairs)
    return (block_of(z) + up.astype(F32) + down.astype(F32)).astype(BF16)


def gather_over_var(own, plan):
    if not plan:
        return lax.all_gather(own, "var", axis=0)
    me = lax.axis_index("var")
    across = swap(own, "var", 2)
    stacked = jnp.stack([own, swap(own, "var", 1), across, swap(across, "var", 1)])
    return jnp.stack(
        [lax.dynamic_index_in_dim(stacked, me ^ v, 0, keepdims=False) for v in range(lax.axis_size("var"))]
    )


def sum_over_all(values, plan):
    if not plan:
        return lax.psum(values, ("patch", "var"))
    me = lax.axis_index("var")
    half = values.shape[1] // 2
    core, x = me % 2, me // 2

    def part(array, which, size):
        return lax.dynamic_slice_in_dim(array, which * size, size, 1)

    kept = part(values, core, half).astype(F32) + swap(part(values, 1 - core, half), "var", 1).astype(F32)
    quarter = half // 2
    kept = part(kept, x, quarter) + swap(part(kept, 1 - x, quarter).astype(BF16), "var", 2).astype(F32)
    kept = kept.astype(BF16)
    for bit in (1, 2, 4):
        kept = (kept.astype(F32) + swap(kept, "patch", bit).astype(F32)).astype(BF16)
    pieces = gather_over_var(kept, plan)
    return jnp.concatenate([pieces[(v % 2) * 2 + v // 2] for v in range(4)], axis=1)


def small_sum_over_all(values, plan):
    if not plan:
        return lax.psum(values, ("patch", "var"))
    for axis, bit in (("var", 1), ("var", 2), ("patch", 1), ("patch", 2), ("patch", 4)):
        values = values + swap(values, axis, bit)
    return values


def local(
    input_field,
    counts,
    var_ids,
    patch_weight,
    var_embed,
    agg_query,
    query_proj,
    key_proj,
    value_proj,
    agg_out,
    norm_one,
    trunk_qkv,
    trunk_out,
    norm_two,
    mlp_in,
    mlp_out,
    cotangent,
):
    patches, group = lax.axis_size("patch"), lax.axis_size("var")
    plan = (2, 4) if (patches, group) == (8, 4) else None
    var_index = lax.axis_index("var")
    patch_index = lax.axis_index("patch")
    all_rows, seg, var_local, pixels = input_field.shape
    width = agg_out.shape[0]
    head_dim = width // HEADS
    hidden = mlp_in.shape[1]
    scaling = 1.0 / math.sqrt(head_dim)

    turned = input_field.transpose(0, 2, 3, 1).reshape(all_rows, var_local * pixels, seg)
    own_field = lax.all_to_all(turned, "var", split_axis=0, concat_axis=1, tiled=True)
    own_field = own_field.reshape(VARS * pixels, seg)
    own_ids = lax.dynamic_slice_in_dim(var_ids, var_index, 1, 0)
    own_count = lax.dynamic_slice_in_dim(counts, var_index, 1, 0)
    positions = patch_index * seg + jnp.arange(seg, dtype=jnp.int32)
    valid_rows = (positions < own_count).astype(F32)[:, None]
    out_grad = cotangent.reshape(seg, width).astype(F32) * valid_rows
    out_grad_low = out_grad.astype(BF16)
    out_grad_group = tokens_of_group(out_grad_low, plan)

    weight_rows = patch_weight.reshape(VARS * pixels, width)
    agg_q = mm(agg_query[None], query_proj)[0]
    in_head = jnp.arange(width, dtype=jnp.int32)[:, None] // head_dim == jnp.arange(HEADS)[None, :]
    head_query = jnp.where(in_head, agg_q[:, None] * scaling, 0.0)
    key_query = mm(key_proj, jnp.concatenate(split_high_low(head_query), axis=1))
    key_query = key_query[:, :HEADS] + key_query[:, HEADS:]
    key_query_parts = jnp.concatenate(split_high_low(key_query), axis=1)
    score_weight = mm(key_query_parts, weight_rows, (((0,), (1,)), ((), ())))
    score_weight = score_weight[:HEADS] + score_weight[HEADS:]
    score_embed = mm(key_query_parts, var_embed, (((0,), (1,)), ((), ())))
    score_embed = (score_embed[:HEADS] + score_embed[HEADS:]).reshape(HEADS * VARS, 1)
    same_var = (jnp.arange(VARS)[:, None] == jnp.arange(VARS * pixels)[None, :] // pixels)[None]
    spread = jnp.where(same_var, score_weight[:, None, :], 0.0).astype(BF16)
    spread = spread.reshape(HEADS * VARS, VARS * pixels)
    vw = mm(weight_rows, value_proj).astype(BF16)
    ve = mm(var_embed, value_proj).astype(BF16)
    vwt = mm(value_proj, weight_rows, (((0,), (1,)), ((), ()))).astype(BF16)
    vet = mm(value_proj, var_embed, (((0,), (1,)), ((), ()))).astype(BF16)

    x_own, shares, mixed_low = front_forward(own_ids, own_field, spread, score_embed, vwt, vet)

    mixed_group = tokens_of_group(mixed_low, plan)
    front_out = mm(mixed_low, agg_out) * valid_rows
    normed_one, norm_one_pull = jax.vjp(layer_norm, front_out, norm_one.astype(F32))
    normed_one_low = normed_one.astype(BF16)
    triple = mm(normed_one_low, trunk_qkv).astype(BF16)
    normed_one_group = tokens_of_group(normed_one_low, plan)
    attention = exchanged_attention if HEADS % patches == 0 else gathered_attention
    attended, attention_pull = attention(triple, own_count, head_dim)
    attended_group = tokens_of_group(attended, plan)
    after_attn = front_out + mm(attended, trunk_out)
    normed_two, norm_two_pull = jax.vjp(layer_norm, after_attn, norm_two.astype(F32))
    normed_two_low = normed_two.astype(BF16)
    normed_two_group = tokens_of_group(normed_two_low, plan)
    inner = mm(normed_two_low, mlp_in)
    active, gelu_pull = jax.vjp(gelu_exact, inner)
    active_low = active.astype(BF16)
    result = after_attn + mm(active_low, mlp_out)
    block_out = (result * valid_rows).astype(BF16)[None]

    def column_slice(values):
        size = values.shape[1] // group
        return lambda v: lax.dynamic_slice_in_dim(values, v * size, size, 1)

    def hidden_slice(values):
        size = hidden // (patches * group)

        def piece(v):
            return jnp.concatenate(
                [lax.dynamic_slice_in_dim(values, (p * group + v) * size, size, 1) for p in range(patches)], axis=1
            )

        return piece

    active_group = slices_of_group(hidden_slice(active_low), plan)
    inner_grad = gelu_pull(mm(out_grad_low, mlp_out, NT))[0].astype(BF16)
    inner_grad_group = slices_of_group(column_slice(inner_grad), plan)
    normed_two_grad = mm(inner_grad, mlp_in, NT)
    after_ln_grad, norm_two_grad = norm_two_pull(normed_two_grad)
    after_grad = out_grad + after_ln_grad
    branch_low = after_grad.astype(BF16)
    branch_group = slices_of_group(column_slice(branch_low), plan)
    attended_grad = mm(branch_low, trunk_out, NT).astype(BF16)
    mlp_out_own = scatter_over_patch(mm(active_group, out_grad_group, TN), plan)
    mlp_in_own = scatter_over_patch(mm(normed_two_group, inner_grad_group, TN), plan)
    triple_grad = attention_pull(attended_grad)
    triple_grad_group = slices_of_group(column_slice(triple_grad), plan)
    normed_one_grad = mm(triple_grad, trunk_qkv, NT)
    front_ln_grad, norm_one_grad = norm_one_pull(normed_one_grad)
    agg_grad = ((after_grad + front_ln_grad) * valid_rows).astype(BF16)
    agg_grad_group = slices_of_group(column_slice(agg_grad), plan)
    mixed_grad = mm(agg_grad, agg_out, NT).astype(BF16)

    field_grad, m_part, me_part, s_part, se_part = front_backward(
        own_ids, x_own, shares, mixed_grad, vw, ve, spread
    )
    field_grad = lax.all_to_all(
        field_grad.reshape(1, VARS * pixels, seg), "var", split_axis=1, concat_axis=0, tiled=True
    )
    field_grad = field_grad.reshape(all_rows, var_local, pixels, seg).transpose(0, 3, 1, 2)

    square = jnp.concatenate(
        [
            mm(attended_group, branch_group, TN),
            mm(mixed_group, agg_grad_group, TN),
            mm(normed_one_group, triple_grad_group, TN),
        ],
        axis=1,
    )
    square_own = scatter_over_patch(square, plan)

    small = jnp.concatenate(
        [
            s_part,
            jnp.pad(se_part.reshape(HEADS, VARS), ((0, 0), (0, 2 * width - VARS * pixels - VARS))),
        ],
        axis=1,
    )
    norms = jnp.concatenate([norm_one_grad, norm_two_grad])[None]
    small = small_sum_over_all(jnp.concatenate([small, norms], axis=0), plan)
    s_all = small[:HEADS, : VARS * pixels]
    se_all = small[:HEADS, VARS * pixels : VARS * pixels + VARS]
    norm_sums = small[HEADS]
    m_all = sum_over_all(jnp.concatenate([m_part, me_part], axis=0), plan)
    m_sum, me_sum = m_all[: VARS * pixels], m_all[VARS * pixels :]

    own_width = width // patches
    start = patch_index * own_width

    def own_cols(values):
        return lax.dynamic_slice_in_dim(values, start, own_width, 1)

    def own_rows(values):
        return lax.dynamic_slice_in_dim(values, start, own_width, 0)

    value_proj_grad = mm(own_cols(weight_rows), m_sum, TN) + mm(own_cols(var_embed), me_sum, TN)
    value_rows = own_rows(value_proj)
    key_query_rows = own_rows(key_query)
    patch_grad = mm(m_sum, value_rows, NT) + mm(
        s_all, key_query_rows, (((0,), (1,)), ((), ())), precision=HIGHEST
    )
    patch_grad = patch_grad.reshape(VARS, pixels, own_width)
    embed_grad = mm(me_sum, value_rows, NT) + mm(
        se_all, key_query_rows, (((0,), (1,)), ((), ())), precision=HIGHEST
    )
    s_parts = jnp.concatenate(split_high_low(s_all), axis=0)
    se_parts = jnp.concatenate(split_high_low(se_all), axis=0)
    key_sum = mm(s_parts, weight_rows) + mm(se_parts, var_embed)
    key_sum = (key_sum[:HEADS] + key_sum[HEADS:]) * scaling
    head_rows = jnp.where(in_head.T, agg_q[None, :], 0.0)
    key_proj_grad = mm(own_cols(key_sum), head_rows, TN, precision=HIGHEST)
    crossed = mm(jnp.concatenate(split_high_low(key_sum), axis=0), key_proj)
    crossed = crossed[:HEADS] + crossed[HEADS:]
    aggq_grad = jnp.sum(jnp.where(in_head.T, crossed, 0.0), axis=0)
    own_query = lax.dynamic_slice_in_dim(agg_query, start, own_width, 0).astype(F32)
    query_proj_grad = own_query[:, None] * aggq_grad[None, :]
    agg_query_grad = jnp.sum(own_rows(query_proj).astype(F32) * aggq_grad[None, :], axis=1)

    def joined(values):
        pieces = gather_over_var(values, plan)
        return jnp.concatenate([pieces[v] for v in range(group)], axis=1).astype(F32)

    mlp_out_grad = gather_over_var(mlp_out_own, plan).reshape(hidden // patches, width).astype(F32)
    mlp_in_grad = joined(mlp_in_own)
    part = width // group
    trunk_out_grad = joined(square_own[:, :part])
    agg_out_grad = joined(square_own[:, part : 2 * part])
    trunk_qkv_grad = joined(square_own[:, 2 * part :])
    norm_one_grad = lax.dynamic_slice_in_dim(norm_sums, start, own_width, 0)
    norm_two_grad = lax.dynamic_slice_in_dim(norm_sums, width + start, own_width, 0)
    return (
        block_out,
        field_grad,
        patch_grad,
        embed_grad,
        agg_query_grad,
        query_proj_grad,
        key_proj_grad,
        value_proj_grad,
        agg_out_grad,
        norm_one_grad,
        trunk_qkv_grad,
        trunk_out_grad,
        norm_two_grad,
        mlp_in_grad,
        mlp_out_grad,
    )


def solution(mesh):
    whole = P()
    placed = (P(None, "patch", "var", None),) + (whole,) * 15 + (P("var", "patch", None),)
    rows = P("patch", None)
    return jax.shard_map(
        local,
        mesh=mesh,
        in_specs=placed,
        out_specs=(
            P("var", "patch", None),
            P(None, "patch", "var", None),
            P(None, None, "patch"),
            P(None, "patch"),
            P("patch"),
            rows,
            rows,
            rows,
            rows,
            P("patch"),
            rows,
            rows,
            P("patch"),
            rows,
            rows,
        ),
        check_vma=False,
    )
```

```python
import functools
import math

import jax
import jax.numpy as jnp
from jax import lax
from jax.experimental import pallas as pl
from jax.experimental.pallas import tpu as pltpu
from jax.sharding import PartitionSpec as P

HEADS = 16
VARS = 48
EPSILON = 1e-05
MASKED = -1e30
HIGHEST = lax.Precision.HIGHEST
BF16 = jnp.bfloat16
F32 = jnp.float32
NN = (((1,), (0,)), ((), ()))
NT = (((1,), (1,)), ((), ()))
TN = (((0,), (0,)), ((), ()))


def cost(flops):
    return pl.CostEstimate(flops=flops, bytes_accessed=1 << 20, transcendentals=0)


def mm(a, b, dims=NN, precision=None):
    return lax.dot_general(a, b, dims, precision=precision, preferred_element_type=F32)


def layer_norm(values, gain_vec):
    average = jnp.mean(values, axis=-1, keepdims=True)
    center = values - average
    spread = jnp.mean(center * center, axis=-1, keepdims=True)
    return center * lax.rsqrt(spread + EPSILON) * gain_vec


def gelu_exact(values):
    return jax.nn.gelu(values, approximate=False)


def split_high_low(values):
    high = values.astype(BF16)
    return high, (values - high.astype(F32)).astype(BF16)


def front_forward_kernel(
    pixels, ids_ref, field_ref, spread_ref, bias_ref, vwt_ref, vet_ref, x_ref, p_ref, mixed_ref, mt_ref
):
    seg = field_ref.shape[1]
    head_dim = mixed_ref.shape[1] // HEADS
    for slot in range(VARS):
        start = pl.multiple_of(ids_ref[0, slot] * pixels, pixels)
        x_ref[pl.ds(start, pixels), :] = field_ref[slot * pixels : (slot + 1) * pixels, :]
    scores = mm(spread_ref[...], x_ref[...]) + bias_ref[...]
    scores = scores.reshape(HEADS, VARS, seg)
    top = jnp.max(scores, axis=1, keepdims=True)
    exponent = jnp.exp(scores - top)
    total = jnp.sum(exponent, axis=1, keepdims=True)
    p_ref[...] = (exponent * (1.0 / total)).reshape(HEADS * VARS, seg)

    def head(h, carry):
        shares = p_ref[pl.ds(pl.multiple_of(h * VARS, VARS), VARS), :]
        pix = x_ref[...].astype(F32).reshape(VARS, pixels, seg)
        scaled = (pix * shares[:, None, :]).astype(BF16).reshape(VARS * pixels, seg)
        rows = pl.ds(pl.multiple_of(h * head_dim, head_dim), head_dim)
        mt_ref[rows, :] = mm(vwt_ref[rows, :], scaled) + mm(vet_ref[rows, :], shares.astype(BF16))
        return carry

    lax.fori_loop(0, HEADS, head, 0)
    mixed_ref[...] = mt_ref[...].T.astype(BF16)


def front_forward(own_ids, own_field, spread, bias, vwt, vet):
    rows, seg = own_field.shape
    width = vwt.shape[0]
    vmem = pl.BlockSpec(memory_space=pltpu.VMEM)
    return pl.pallas_call(
        functools.partial(front_forward_kernel, rows // VARS),
        out_shape=(
            jax.ShapeDtypeStruct((rows, seg), BF16),
            jax.ShapeDtypeStruct((HEADS * VARS, seg), F32),
            jax.ShapeDtypeStruct((seg, width), BF16),
        ),
        in_specs=[pl.BlockSpec(memory_space=pltpu.SMEM)] + [vmem] * 5,
        out_specs=(vmem,) * 3,
        scratch_shapes=[pltpu.VMEM((width, seg), F32)],
        cost_estimate=cost(6 * 10**9),
        name="front_forward",
    )(own_ids, own_field, spread, bias, vwt, vet)


def front_backward_kernel(
    pixels,
    fast,
    place_ref,
    ids_ref,
    x_ref,
    p_ref,
    mg_ref,
    vw_ref,
    ve_ref,
    spread_ref,
    norms_ref,
    field_ref,
    *rest,
):
    rows, seg = x_ref.shape
    m_refs, (fs_ref, dx_ref, s_ref) = rest[:-3], rest[-3:]
    size = m_refs[0].shape[-1]

    def quarter_of(quarter, store):
        if not fast:
            store(m_refs[0].at[quarter])
            return
        mine = quarter // 2 == place_ref[CORE]
        pl.when(mine)(lambda: store(m_refs[0].at[quarter % 2]))
        pl.when(jnp.logical_not(mine))(lambda: store(m_refs[1].at[quarter % 2]))
    width = mg_ref.shape[1]
    head_dim = width // HEADS
    pair_dim = 2 * head_dim
    lane = lax.broadcasted_iota(jnp.int32, (seg, pair_dim), 1)
    dx_ref[...] = jnp.zeros_like(dx_ref)
    pairs = size // pair_dim

    def pair(q, carry):
        cols = pl.ds(pl.multiple_of(q * pair_dim, pair_dim), pair_dim)
        grad = mg_ref[:, cols]
        none = jnp.zeros_like(grad)
        both = jnp.concatenate(
            [jnp.where(lane < head_dim, grad, none), jnp.where(lane >= head_dim, grad, none)], axis=0
        )
        inner = mm(vw_ref[:, cols], both, NT)
        inner_e = mm(ve_ref[:, cols], both, NT)
        pix = x_ref[...].astype(F32).reshape(VARS, pixels, seg)
        scaled, weights = [], []
        for k in range(2):
            hrows = pl.ds(pl.multiple_of((2 * q + k) * VARS, VARS), VARS)
            shares = p_ref[hrows, :]
            part = inner[:, k * seg : (k + 1) * seg].reshape(VARS, pixels, seg)
            share_grad = jnp.sum(pix * part, axis=1) + inner_e[:, k * seg : (k + 1) * seg]
            delta = jnp.sum(shares * share_grad, axis=0, keepdims=True)
            fs_ref[hrows, :] = shares * (share_grad - delta)
            wide = shares[:, None, :]
            dx_ref[...] += (part * wide).reshape(rows, seg)
            scaled.append((pix * wide).astype(BF16).reshape(rows, seg))
            weights.append(shares.astype(BF16))
        quarter, within = q // pairs, pl.ds(pl.multiple_of(q % pairs * pair_dim, pair_dim), pair_dim)
        m_part = mm(jnp.concatenate(scaled, axis=1), both).astype(BF16)
        me_part = mm(jnp.concatenate(weights, axis=1), both).astype(BF16)

        def store(ref):
            ref[0:rows, within] = m_part
            ref[rows : rows + VARS, within] = me_part

        quarter_of(quarter, store)
        return carry

    lax.fori_loop(0, HEADS // 2, pair, 0)
    score_grad = fs_ref[...]
    low = score_grad.astype(BF16)
    dx = dx_ref[...] + mm(spread_ref[...], low, TN)
    dx_ref[...] = dx
    for slot in range(VARS):
        start = pl.multiple_of(ids_ref[0, slot] * pixels, pixels)
        field_ref[slot * pixels : (slot + 1) * pixels, :] = dx_ref[pl.ds(start, pixels), :].astype(BF16)
    ones = jnp.ones((8, seg), F32)
    s_ref[...] = jnp.zeros_like(s_ref)
    var_row = lax.broadcasted_iota(jnp.int32, (VARS, rows), 0)
    var_col = lax.broadcasted_iota(jnp.int32, (VARS, rows), 1) // pixels
    keep = var_row == var_col
    for h in range(HEADS):
        outer = mm(low[h * VARS : (h + 1) * VARS, :], x_ref[...], NT)
        s_ref[h : h + 1, 0:rows] = jnp.sum(jnp.where(keep, outer, 0.0), axis=0, keepdims=True)
        sums = mm(ones, score_grad[h * VARS : (h + 1) * VARS, :], NT, precision=HIGHEST)
        s_ref[h : h + 1, rows : rows + VARS] = sums[0:1, :]
    s_ref[:, width - norms_ref.shape[1] :] = norms_ref[...]
    for quarter in range(4):
        part = s_ref[:, quarter * size : (quarter + 1) * size].astype(BF16)

        def store_sums(ref, part=part):
            ref[rows + VARS :, :] = part

        quarter_of(quarter, store_sums)


def front_backward(fast, place, own_ids, x_own, shares, mixed_grad, vw, ve, spread, norms):
    rows, seg = x_own.shape
    width = mixed_grad.shape[1]
    vmem = pl.BlockSpec(memory_space=pltpu.VMEM)
    smem = pl.BlockSpec(memory_space=pltpu.SMEM)
    tall = rows + VARS + HEADS
    if fast:
        sums = (jax.ShapeDtypeStruct((2, tall, width // 4), BF16),) * 2
    else:
        sums = (jax.ShapeDtypeStruct((4, tall, width // 4), BF16),)
    return pl.pallas_call(
        functools.partial(front_backward_kernel, rows // VARS, fast),
        out_shape=(jax.ShapeDtypeStruct((rows, seg), BF16), *sums),
        in_specs=[smem, smem] + [vmem] * 7,
        out_specs=(vmem,) * (1 + len(sums)),
        scratch_shapes=[
            pltpu.VMEM((HEADS * VARS, seg), F32),
            pltpu.VMEM((rows, seg), F32),
            pltpu.VMEM((HEADS, width), F32),
        ],
        cost_estimate=cost(80 * 10**9),
        name="front_backward",
    )(place, own_ids, x_own, shares, mixed_grad, vw, ve, spread, norms)


def load_parts(ref, part, seg, out_ref):
    for source in range(ref.shape[0]):
        out_ref[source * seg : (source + 1) * seg, :] = ref[source, part * seg : (part + 1) * seg, :]


def attend_forward_kernel(head_dim, block, count_ref, qkv_ref, out_ref, lse_ref, q_ref, k_ref, vt_ref):
    full, width = q_ref.shape
    seg = full // qkv_ref.shape[0]
    scaling = 1.0 / math.sqrt(head_dim)
    load_parts(qkv_ref, 2, seg, q_ref)
    vt_ref[...] = q_ref[...].T
    load_parts(qkv_ref, 0, seg, q_ref)
    load_parts(qkv_ref, 1, seg, k_ref)
    count = count_ref[0, 0]
    lane = lax.broadcasted_iota(jnp.int32, (block, width), 1) // head_dim
    row = lax.broadcasted_iota(jnp.int32, (width, block), 0) // head_dim
    valid = lax.broadcasted_iota(jnp.int32, (full, block), 0) < count

    def step(i, carry):
        part = pl.ds(pl.multiple_of(i * block, block), block)
        query = q_ref[part, :]
        total = jnp.zeros((width, block), F32)
        for h in range(width // head_dim):
            own = jnp.where(lane == h, query, jnp.zeros_like(query))
            scores = jnp.where(valid, mm(k_ref[...], own, NT) * scaling, MASKED)
            top = jnp.max(scores, axis=0, keepdims=True)
            exponent = jnp.exp(scores - top)
            denominator = jnp.sum(exponent, axis=0, keepdims=True)
            shares = (exponent * (1.0 / denominator)).astype(BF16)
            lse_ref[h : h + 1, part] = top + jnp.log(denominator)
            total = jnp.where(row == h, mm(vt_ref[...], shares), total)
        out_ref[part, :] = total.T.astype(BF16)
        return carry

    lax.fori_loop(0, full // block, step, 0)


def attend_forward(count, qkv, head_dim):
    parts, triple_rows, width = qkv.shape
    full = parts * triple_rows // 3
    vmem = pl.BlockSpec(memory_space=pltpu.VMEM)
    block = min(256, full)
    return pl.pallas_call(
        functools.partial(attend_forward_kernel, head_dim, block),
        out_shape=(
            jax.ShapeDtypeStruct((full, width), BF16),
            jax.ShapeDtypeStruct((width // head_dim, full), F32),
        ),
        in_specs=[pl.BlockSpec(memory_space=pltpu.SMEM), vmem],
        out_specs=(vmem, vmem),
        scratch_shapes=[
            pltpu.VMEM((full, width), BF16),
            pltpu.VMEM((full, width), BF16),
            pltpu.VMEM((width, full), BF16),
        ],
        cost_estimate=cost(10 * 10**9),
        name="attend_forward",
    )(count, qkv)


def attend_backward_kernel(
    head_dim, block, count_ref, qkv_ref, grad_ref, lse_ref, out_ref, q_ref, k_ref, v_ref, kt_ref, dk_ref, dv_ref
):
    full, width = q_ref.shape
    seg = full // qkv_ref.shape[0]
    scaling = 1.0 / math.sqrt(head_dim)
    load_parts(qkv_ref, 0, seg, q_ref)
    load_parts(qkv_ref, 1, seg, k_ref)
    load_parts(qkv_ref, 2, seg, v_ref)
    kt_ref[...] = k_ref[...].T
    dk_ref[...] = jnp.zeros_like(dk_ref)
    dv_ref[...] = jnp.zeros_like(dv_ref)
    count = count_ref[0, 0]
    lane = lax.broadcasted_iota(jnp.int32, (block, width), 1) // head_dim
    row = lax.broadcasted_iota(jnp.int32, (width, block), 0) // head_dim
    valid = lax.broadcasted_iota(jnp.int32, (full, block), 0) < count

    def step(i, carry):
        part = pl.ds(pl.multiple_of(i * block, block), block)
        query = q_ref[part, :]
        grad = grad_ref[part, :]
        total = jnp.zeros((width, block), F32)
        for h in range(width // head_dim):
            own = jnp.where(lane == h, query, jnp.zeros_like(query))
            own_grad = jnp.where(lane == h, grad, jnp.zeros_like(grad))
            scores = jnp.where(valid, mm(k_ref[...], own, NT) * scaling, MASKED)
            shares = jnp.exp(scores - lse_ref[h : h + 1, part])
            share_grad = mm(v_ref[...], own_grad, NT)
            dot = jnp.sum(shares * share_grad, axis=0, keepdims=True)
            score_grad = (shares * (share_grad - dot)).astype(BF16)
            dv_ref[...] += mm(shares.astype(BF16), own_grad)
            dk_ref[...] += mm(score_grad, own)
            total = jnp.where(row == h, mm(kt_ref[...], score_grad), total)
        turned = (total * scaling).T.astype(BF16)
        for piece in range(block // seg):
            out_ref[i * (block // seg) + piece, 0:seg, :] = turned[piece * seg : (piece + 1) * seg, :]
        return carry

    lax.fori_loop(0, full // block, step, 0)
    for source in range(full // seg):
        rows = slice(source * seg, (source + 1) * seg)
        out_ref[source, seg : 2 * seg, :] = (dk_ref[rows, :] * scaling).astype(BF16)
        out_ref[source, 2 * seg : 3 * seg, :] = dv_ref[rows, :].astype(BF16)


def attend_backward(count, qkv, grad, lse, head_dim):
    parts, triple_rows, width = qkv.shape
    full = parts * triple_rows // 3
    vmem = pl.BlockSpec(memory_space=pltpu.VMEM)
    block = min(256, full)
    return pl.pallas_call(
        functools.partial(attend_backward_kernel, head_dim, block),
        out_shape=jax.ShapeDtypeStruct(qkv.shape, BF16),
        in_specs=[pl.BlockSpec(memory_space=pltpu.SMEM), vmem, vmem, vmem],
        out_specs=vmem,
        scratch_shapes=[pltpu.VMEM((full, width), BF16)] * 3
        + [pltpu.VMEM((width, full), BF16)]
        + [pltpu.VMEM((full, width), F32)] * 2,
        cost_estimate=cost(50 * 10**9),
        name="attend_backward",
    )(count, qkv, grad, lse)


def gathered_attention(triple, count, head_dim):
    seg, triple_width = triple.shape
    width = triple_width // 3
    scaling = 1.0 / math.sqrt(head_dim)
    full = seg * lax.axis_size("patch")
    query = triple[:, :width].reshape(seg, HEADS, head_dim)
    key = lax.all_gather(triple[:, width : 2 * width], "patch", axis=0, tiled=True)
    value = lax.all_gather(triple[:, 2 * width :], "patch", axis=0, tiled=True)
    key = key.reshape(full, HEADS, head_dim)
    value = value.reshape(full, HEADS, head_dim)
    valid = (jnp.arange(full, dtype=jnp.int32) < count)[None, None, :]

    def score():
        raw = jnp.einsum("qhd,khd->hqk", query, key, preferred_element_type=F32) * scaling
        return jnp.where(valid, raw, MASKED)

    masked = score()
    top = jnp.max(masked, axis=-1, keepdims=True)
    exponent = jnp.exp(masked - top)
    denominator = jnp.sum(exponent, axis=-1, keepdims=True)
    shares_low = (exponent / denominator).astype(BF16)
    lse = top + jnp.log(denominator)
    attended = jnp.einsum("hqk,khd->qhd", shares_low, value, preferred_element_type=F32)

    def backward(grad):
        grad = grad.reshape(seg, HEADS, head_dim)
        shares = jnp.exp(score() - lse)
        share_grad = jnp.einsum("qhd,khd->hqk", grad, value, preferred_element_type=F32)
        dot = jnp.sum(shares * share_grad, axis=-1, keepdims=True)
        score_grad = (shares * (share_grad - dot)).astype(BF16)
        q_grad = jnp.einsum("hqk,khd->qhd", score_grad, key, preferred_element_type=F32) * scaling
        v_all = jnp.einsum("hqk,qhd->khd", shares.astype(BF16), grad, preferred_element_type=F32)
        k_all = jnp.einsum("hqk,qhd->khd", score_grad, query, preferred_element_type=F32) * scaling
        k_grad, v_grad = (
            lax.psum_scatter(
                part.reshape(full, width).astype(BF16), "patch", scatter_dimension=0, tiled=True
            )
            for part in (k_all, v_all)
        )
        return jnp.concatenate([q_grad.reshape(seg, width).astype(BF16), k_grad, v_grad], axis=1)

    return attended.reshape(seg, width).astype(BF16), backward


def to_heads(values):
    return lax.all_to_all(values, "patch", split_axis=0, concat_axis=0, tiled=True)


def queries_to_heads(triple):
    seg, triple_width = triple.shape
    parts = lax.axis_size("patch")
    own = triple_width // (3 * parts)
    moved = triple.reshape(seg, 3, parts, own).transpose(2, 1, 0, 3).reshape(parts, 3 * seg, own)
    return to_heads(moved)


def weight_grad_kernel(jobs, place_ref, *refs):
    arrays, (near_ref, away_ref) = refs[:-2], refs[-2:]
    y = place_ref[Y]
    rows = near_ref.shape[1]
    start = 0
    for left, left_start, right, right_start, cols in jobs:
        values = [arrays[4 * right + s][:, pl.ds(right_start, cols)] for s in range(4)]
        values = jnp.concatenate(values, axis=0)
        for target, side in ((away_ref, 1 - y), (near_ref, y)):
            for z in range(near_ref.shape[0]):
                block = pl.ds(pl.multiple_of(left_start + (2 * z + side) * rows, rows), rows)
                factor = jnp.concatenate([arrays[4 * left + s][:, block] for s in range(4)], axis=0)
                target[z, :, start : start + cols] = mm(factor, values, TN).astype(BF16)
        start += cols


def weight_grads(place, jobs, groups, rows, zs):
    arrays = [array for group in groups for array in group]
    total = sum(job[-1] for job in jobs)
    vmem = pl.BlockSpec(memory_space=pltpu.VMEM)
    shape = jax.ShapeDtypeStruct((zs, rows, total), BF16)
    return pl.pallas_call(
        functools.partial(weight_grad_kernel, jobs),
        out_shape=(shape, shape),
        in_specs=[pl.BlockSpec(memory_space=pltpu.SMEM)] + [vmem] * len(arrays),
        out_specs=(vmem, vmem),
        cost_estimate=cost(40 * 10**9),
        name="weight_grads",
    )(place, *arrays)


def swap(values, axis, bit):
    return lax.ppermute(values, axis, [(i, i ^ bit) for i in range(lax.axis_size(axis))])


def together(*values):
    return lax.optimization_barrier(values)


def small_call(kernel, place, arrays, shapes, scratch=(), effort=20, name="small"):
    vmem = pl.BlockSpec(memory_space=pltpu.VMEM)
    return pl.pallas_call(
        kernel,
        out_shape=tuple(jax.ShapeDtypeStruct(dims, dtype) for dims, dtype in shapes),
        in_specs=[pl.BlockSpec(memory_space=pltpu.SMEM)] + [vmem] * len(arrays),
        out_specs=(vmem,) * len(shapes),
        scratch_shapes=list(scratch),
        cost_estimate=cost(effort * 10**9),
        name=name,
    )(place, *arrays)


ME, CORE, X, Y, Z = range(5)


def tokens_of_group(values):
    across = swap(values, "var", 2)
    return values, swap(values, "var", 1), across, swap(across, "var", 1)


def slices_of_group(pieces):
    return (pieces[0],) + tuple(swap(pieces[bit], "var", bit) for bit in (1, 2, 3))


def z_pieces(place, near, got):
    _, rows, cols = near.shape

    def kernel(place_ref, near_ref, got_ref, *outs):
        for bit in range(4):
            block = place_ref[Z] ^ bit
            outs[bit][...] = (near_ref[block].astype(F32) + got_ref[block].astype(F32)).astype(BF16)

    return small_call(kernel, place, (near, got), [((rows, cols), BF16)] * 4, name="z_pieces")


def z_exchange(pieces):
    return (pieces[0],) + tuple(swap(pieces[bit], "patch", 2 * bit) for bit in (1, 2, 3))


def z_sum(place, arrays):

    def kernel(place_ref, first, second, third, fourth, out):
        total = first[...].astype(F32) + second[...].astype(F32) + third[...].astype(F32) + fourth[...].astype(F32)
        out[...] = total.astype(BF16)

    return small_call(kernel, place, arrays, [(arrays[0].shape, BF16)], name="z_sum")[0]


def gather_over_var(own):
    across = swap(own, "var", 2)
    return own, swap(own, "var", 1), across, swap(across, "var", 1)


def join_columns(place, pieces, widths):
    rows = pieces[0].shape[0]

    def kernel(place_ref, *refs):
        start = 0
        for out, size in zip(refs[4:], widths):
            for s in range(4):
                cols = pl.ds(pl.multiple_of((place_ref[ME] ^ s) * size, size), size)
                out[:, cols] = refs[s][:, start : start + size].astype(F32)
            start += size

    return small_call(kernel, place, pieces, [((rows, 4 * size), F32) for size in widths], name="join_columns")


def join_rows(place, pieces):
    def kernel(place_ref, *refs):
        for s in range(4):
            refs[4][place_ref[ME] ^ s] = refs[s][...].astype(F32)

    return small_call(kernel, place, pieces, [((4, *pieces[0].shape), F32)], name="join_rows")[0]


def sum_over_all(place, stay, away, hooks):
    _, rows, cols = stay.shape
    half = rows // 2
    size = half // 4
    hooks = iter(hooks)

    def core_kernel(place_ref, stay_ref, got_ref, stay_out, away_out):
        for out, which in ((away_out, 1 - place_ref[X]), (stay_out, place_ref[X])):
            out[...] = (stay_ref[which].astype(F32) + got_ref[which].astype(F32)).astype(BF16)

    got = next(hooks)(swap(away, "var", 1))
    stay, away = small_call(core_kernel, place, (stay, got), [((rows, cols), BF16)] * 2, name="core_sum")

    def x_kernel(place_ref, stay_ref, got_ref, stay_out, away_out):
        for out, which in ((away_out, 1 - place_ref[Y]), (stay_out, place_ref[Y])):
            out[...] = (stay_ref[which].astype(F32) + got_ref[which].astype(F32)).astype(BF16)

    got = next(hooks)(swap(away, "var", 2))
    halves = (2, half, cols)
    stay, away = small_call(
        x_kernel, place, (stay.reshape(halves), got.reshape(halves)), [((half, cols), BF16)] * 2, name="x_sum"
    )
    got = next(hooks)(swap(away, "patch", 1))
    pieces = z_exchange(z_pieces(place, stay.reshape(4, size, cols), got.reshape(4, size, cols)))
    kept = z_sum(place, next(hooks)(pieces))

    def z_kernel(place_ref, *refs):
        for s in range(4):
            refs[4][place_ref[Z] ^ s] = refs[s][...]

    arrays = (kept,) + tuple(swap(kept, "patch", 2 * bit) for bit in (1, 2, 3))
    own = small_call(z_kernel, place, next(hooks)(arrays), [((4, size, cols), BF16)], name="z_join")[0]

    def y_kernel(place_ref, own_ref, other_ref, out):
        out[place_ref[Y]] = own_ref[...]
        out[1 - place_ref[Y]] = other_ref[...]

    own = own.reshape(half, cols)
    arrays = (own, next(hooks)(swap(own, "patch", 1)))
    full = small_call(y_kernel, place, arrays, [(halves, BF16)], name="y_join")[0].reshape(rows, cols)

    def var_kernel(place_ref, *refs):
        for s in range(4):
            v = place_ref[ME] ^ s
            refs[4][:, pl.ds(pl.multiple_of((v % 2 * 2 + v // 2) * cols, cols), cols)] = refs[s][...]

    return small_call(var_kernel, place, gather_over_var(full), [((rows, 4 * cols), BF16)], name="var_join")[0]


def middle_kernel(
    place_ref,
    att_ref,
    front_ref,
    valid_ref,
    og_ref,
    tout_ref,
    gain_ref,
    win_ref,
    wout_ref,
    block_ref,
    late_ref,
    *refs,
):
    actives, middles = refs[0:4], refs[4:8]
    grad_ref, after_ref, gain_grad_ref, residual_ref, unit_ref, rate_ref, acc_ref, back_ref, wide_ref, branch_ref = refs[8:]
    step = pl.program_id(0)
    seg, width = front_ref.shape
    parts = att_ref.shape[0]
    own = width // parts
    me = place_ref[0]
    slot = actives[0].shape[1] // pl.num_programs(0)

    @pl.when(step == 0)
    def _():
        for p in range(parts):
            late_ref[:, p * own : (p + 1) * own] = att_ref[p]
        after = front_ref[...] + mm(late_ref[:, 0:width], tout_ref[...])
        residual_ref[...] = after
        center = after - jnp.mean(after, axis=1, keepdims=True)
        rate = lax.rsqrt(jnp.mean(center * center, axis=1, keepdims=True) + EPSILON)
        unit = center * rate
        unit_ref[...] = unit
        rate_ref[...] = rate
        late_ref[:, width : 2 * width] = (unit * gain_ref[...]).astype(BF16)
        acc_ref[...] = jnp.zeros_like(acc_ref)
        back_ref[...] = jnp.zeros_like(back_ref)

    inner = mm(late_ref[:, width : 2 * width], win_ref[...])
    cumulative = 0.5 * (1.0 + lax.erf(inner * math.sqrt(0.5)))
    active = (inner * cumulative).astype(BF16)
    acc_ref[...] += mm(active, wout_ref[...])
    slope = cumulative + inner * (jnp.exp(-0.5 * inner * inner) * (1.0 / math.sqrt(2.0 * math.pi)))
    inner_grad = (mm(og_ref[...], wout_ref[...], NT) * slope).astype(BF16)
    back_ref[...] += mm(inner_grad, win_ref[...], NT)
    wide_ref[...] = active
    cols = pl.ds(pl.multiple_of(step * slot, slot), slot)
    for s in range(4):
        actives[s][:, cols] = wide_ref[:, pl.ds(pl.multiple_of((me ^ s) * slot, slot), slot)]
    block = inner_grad.shape[1]
    owner = step * block // width
    place = pl.ds(pl.multiple_of(step * block - owner * width, block), block)
    for s in range(4):

        @pl.when((me ^ s) == owner)
        def _(s=s):
            middles[s][:, place] = inner_grad

    @pl.when(step == pl.num_programs(0) - 1)
    def _():
        valid = valid_ref[...]
        block_ref[...] = ((residual_ref[...] + acc_ref[...]) * valid).astype(BF16)
        unit = unit_ref[...]
        back = back_ref[...]
        gain_grad_ref[...] = jnp.sum(back * unit, axis=0, keepdims=True)
        scaled = back * gain_ref[...]
        inside = jnp.mean(scaled * unit, axis=1, keepdims=True)
        total = rate_ref[...] * (scaled - jnp.mean(scaled, axis=1, keepdims=True) - unit * inside)
        total = og_ref[...].astype(F32) + total
        after_ref[...] = total
        branch_ref[...] = total.astype(BF16)
        quarter = width // 4
        for s in range(4):
            start = pl.multiple_of((me ^ s) * quarter, quarter)
            middles[s][:, width : width + quarter] = branch_ref[:, pl.ds(start, quarter)]
        turned = mm(branch_ref[...], tout_ref[...], NT).astype(BF16)
        for p in range(parts):
            grad_ref[p] = turned[:, p * own : (p + 1) * own]


def middle(place, attended, front_out, valid, out_grad, trunk_out, gain, mlp_in, mlp_out):
    seg, width = front_out.shape
    hidden = mlp_in.shape[1]
    parts = attended.shape[0]
    block = hidden // parts
    shape = jax.ShapeDtypeStruct

    def still(*dims):
        return pl.BlockSpec(dims, lambda i: (0,) * len(dims))

    piece, wider = shape((seg, hidden // 4), BF16), shape((seg, width + width // 4), BF16)
    return pl.pallas_call(
        middle_kernel,
        grid=(parts,),
        out_shape=(
            shape((seg, width), BF16),
            shape((seg, 2 * width), BF16),
            *((piece,) * 4),
            *((wider,) * 4),
            shape(attended.shape, BF16),
            shape((seg, width), F32),
            shape((1, width), F32),
        ),
        in_specs=[
            pl.BlockSpec(memory_space=pltpu.SMEM),
            still(*attended.shape),
            still(seg, width),
            still(seg, 1),
            still(seg, width),
            still(width, width),
            still(1, width),
            pl.BlockSpec((width, block), lambda i: (0, i)),
            pl.BlockSpec((block, width), lambda i: (i, 0)),
        ],
        out_specs=(
            still(seg, width),
            still(seg, 2 * width),
            *((still(*piece.shape),) * 4),
            *((still(*wider.shape),) * 4),
            still(*attended.shape),
            still(seg, width),
            still(1, width),
        ),
        scratch_shapes=[
            pltpu.VMEM((seg, width), F32),
            pltpu.VMEM((seg, width), F32),
            pltpu.VMEM((seg, 1), F32),
            pltpu.VMEM((seg, width), F32),
            pltpu.VMEM((seg, width), F32),
            pltpu.VMEM((seg, block), BF16),
            pltpu.VMEM((seg, width), BF16),
        ],
        compiler_params=pltpu.CompilerParams(dimension_semantics=("arbitrary",)),
        cost_estimate=cost(15 * 10**9),
        name="trunk_middle",
    )(place, attended, front_out, valid, out_grad, trunk_out, gain, mlp_in, mlp_out)


def local(
    input_field,
    counts,
    var_ids,
    patch_weight,
    var_embed,
    agg_query,
    query_proj,
    key_proj,
    value_proj,
    agg_out,
    norm_one,
    trunk_qkv,
    trunk_out,
    norm_two,
    mlp_in,
    mlp_out,
    cotangent,
):
    patches, group = lax.axis_size("patch"), lax.axis_size("var")
    fast = (patches, group) == (8, 4)
    me, spot = lax.axis_index("var"), lax.axis_index("patch")
    place = jnp.stack([me, me % 2, me // 2, spot % 2, spot // 2]).astype(jnp.int32)
    var_index = lax.axis_index("var")
    patch_index = lax.axis_index("patch")
    all_rows, seg, var_local, pixels = input_field.shape
    width = agg_out.shape[0]
    head_dim = width // HEADS
    hidden = mlp_in.shape[1]
    scaling = 1.0 / math.sqrt(head_dim)

    turned = input_field.transpose(0, 2, 3, 1).reshape(all_rows, var_local * pixels, seg)
    own_field = lax.all_to_all(turned, "var", split_axis=0, concat_axis=1, tiled=True)
    own_field = own_field.reshape(VARS * pixels, seg)
    own_ids = lax.dynamic_slice_in_dim(var_ids, var_index, 1, 0)
    own_count = lax.dynamic_slice_in_dim(counts, var_index, 1, 0)
    positions = patch_index * seg + jnp.arange(seg, dtype=jnp.int32)
    valid_rows = (positions < own_count).astype(F32)[:, None]
    out_grad = cotangent.reshape(seg, width).astype(F32) * valid_rows
    out_grad_low = out_grad.astype(BF16)

    weight_rows = patch_weight.reshape(VARS * pixels, width)
    agg_q = mm(agg_query[None], query_proj)[0]
    in_head = jnp.arange(width, dtype=jnp.int32)[:, None] // head_dim == jnp.arange(HEADS)[None, :]
    head_query = jnp.where(in_head, agg_q[:, None] * scaling, 0.0)
    key_query = mm(key_proj, jnp.concatenate(split_high_low(head_query), axis=1))
    key_query = key_query[:, :HEADS] + key_query[:, HEADS:]
    key_query_parts = jnp.concatenate(split_high_low(key_query), axis=1)
    score_weight = mm(key_query_parts, weight_rows, (((0,), (1,)), ((), ())))
    score_weight = score_weight[:HEADS] + score_weight[HEADS:]
    score_embed = mm(key_query_parts, var_embed, (((0,), (1,)), ((), ())))
    score_embed = (score_embed[:HEADS] + score_embed[HEADS:]).reshape(HEADS * VARS, 1)
    same_var = (jnp.arange(VARS)[:, None] == jnp.arange(VARS * pixels)[None, :] // pixels)[None]
    spread = jnp.where(same_var, score_weight[:, None, :], 0.0).astype(BF16)
    spread = spread.reshape(HEADS * VARS, VARS * pixels)
    vw = mm(weight_rows, value_proj).astype(BF16)
    ve = mm(var_embed, value_proj).astype(BF16)
    vwt = mm(value_proj, weight_rows, (((0,), (1,)), ((), ()))).astype(BF16)
    vet = mm(value_proj, var_embed, (((0,), (1,)), ((), ()))).astype(BF16)

    x_own, shares, mixed_low = front_forward(own_ids, own_field, spread, score_embed, vwt, vet)

    front_out = mm(mixed_low, agg_out) * valid_rows
    normed_one, norm_one_pull = jax.vjp(layer_norm, front_out, norm_one.astype(F32))
    normed_one_low = normed_one.astype(BF16)
    triple = mm(normed_one_low, trunk_qkv).astype(BF16)
    part = width // group
    own_width = width // patches
    quarter = hidden // group
    zs = patches // 2
    if fast:
        early = tokens_of_group(jnp.concatenate([out_grad_low, mixed_low, normed_one_low], axis=1))
        qkv, vw, ve = together(queries_to_heads(triple), vw, ve)
        count = own_count.reshape(1, 1)
        heads, lse = attend_forward(count, qkv, head_dim)
        results = middle(
            place,
            to_heads(heads.reshape(patches, seg, own_width)),
            front_out,
            valid_rows,
            out_grad_low,
            trunk_out,
            norm_two.astype(F32)[None],
            mlp_in,
            mlp_out,
        )
        block_out, late, grads, after_grad, norm_two_grad = results[0], results[1], results[10], results[11], results[12][0]
        block_out = block_out[None]
        late = tokens_of_group(late)
        active_group, middle_group = slices_of_group(results[2:6]), results[6:10]
        grads = to_heads(grads)
        first = weight_grads(place, ((0, 0, 1, 0, width),), (active_group, early), own_width, zs)
        grads, *rest = together(grads, *first, *late, *middle_group)
        near, away, late, middle_group = rest[0], rest[1], tuple(rest[2:6]), slices_of_group(rest[6:10])
        result = attend_backward(count, qkv, grads.reshape(patches * seg, own_width), lse, head_dim)
        result = to_heads(result)
        got, *rest = together(swap(away, "patch", 1), *late, *middle_group)
        jobs = ((0, width, 1, 0, quarter), (0, 0, 1, quarter, part))
        second = weight_grads(place, jobs, (rest[:4], rest[4:]), own_width, zs)
        result, *rest = together(result, *second, *z_pieces(place, near, got))
        second, first = rest[:2], rest[2:]
        triple_grad = result.reshape(patches, 3, seg, own_width).transpose(2, 1, 0, 3).reshape(seg, 3 * width)
    else:
        attended, attention_pull = gathered_attention(triple, own_count, head_dim)
        after_attn = front_out + mm(attended, trunk_out)
        normed_two, norm_two_pull = jax.vjp(layer_norm, after_attn, norm_two.astype(F32))
        normed_two_low = normed_two.astype(BF16)
        inner = mm(normed_two_low, mlp_in)
        active, gelu_pull = jax.vjp(gelu_exact, inner)
        active_low = active.astype(BF16)
        result = after_attn + mm(active_low, mlp_out)
        block_out = (result * valid_rows).astype(BF16)[None]
        inner_grad = gelu_pull(mm(out_grad_low, mlp_out, NT))[0].astype(BF16)
        normed_two_grad = mm(inner_grad, mlp_in, NT)
        after_ln_grad, norm_two_grad = norm_two_pull(normed_two_grad)
        after_grad = out_grad + after_ln_grad
        branch_low = after_grad.astype(BF16)
        triple_grad = attention_pull(mm(branch_low, trunk_out, NT).astype(BF16))
    normed_one_grad = mm(triple_grad, trunk_qkv, NT)
    front_ln_grad, norm_one_grad = norm_one_pull(normed_one_grad)
    agg_grad = ((after_grad + front_ln_grad) * valid_rows).astype(BF16)
    mixed_grad = mm(agg_grad, agg_out, NT).astype(BF16)
    if fast:

        def last_kernel(place_ref, triple_ref, agg_ref, *outs):
            for s in range(4):
                v = place_ref[ME] ^ s
                outs[s][:, 0 : 3 * part] = triple_ref[:, pl.ds(pl.multiple_of(v * 3 * part, part), 3 * part)]
                outs[s][:, 3 * part :] = agg_ref[:, pl.ds(pl.multiple_of(v * part, part), part)]

        pieces = small_call(last_kernel, place, (triple_grad, agg_grad), [((seg, width), BF16)] * 4, name="last_pieces")
        mixed_grad, *pieces = together(mixed_grad, *pieces)
        last_group = slices_of_group(pieces)

    norms = jnp.concatenate([norm_one_grad.reshape(HEADS, -1), norm_two_grad.reshape(HEADS, -1)], axis=1)
    field_low, *m_parts = front_backward(fast, place, own_ids, x_own, shares, mixed_grad, vw, ve, spread, norms)

    if fast:
        near, away = second
        got = swap(away, "patch", 1)
        field_low, *rest = together(field_low, *m_parts, *z_exchange(first), got)
        m_parts, first, got = rest[:2], z_sum(place, rest[2:6]), rest[6]
        second = z_pieces(place, near, got)
        held = {}

        def core_done(values):
            across = swap(first, "var", 2)
            values, held["across"], *held["last"] = together(values, across, *last_group)
            return values

        def x_done(values):
            across = held["across"]
            parts = (first, swap(first, "var", 1), across, swap(across, "var", 1))
            jobs = ((0, 2 * width, 1, 0, 3 * part), (0, width, 1, 3 * part, part))
            sums = weight_grads(place, jobs, (early, held["last"]), own_width, zs)
            values, *rest = together(values, *sums, *parts, *z_exchange(second))
            held["third"], held["first"], held["second"] = rest[:2], rest[2:6], z_sum(place, rest[6:])
            return values

        def y_done(values):
            near, away = held["third"]
            across = swap(held["second"], "var", 2)
            values, got, held["across"] = together(values, swap(away, "patch", 1), across)
            held["third"] = z_pieces(place, near, got)
            return values

        def z_done(values):
            own, across = held["second"], held["across"]
            parts = (own, swap(own, "var", 1), across, swap(across, "var", 1))
            rest = together(*values, *parts)
            held["second"] = rest[4:]
            return rest[:4]

        def b_done(values):
            rest = together(*values, *z_exchange(held["third"]))
            held["third"] = z_sum(place, rest[4:])
            return rest[:4]

        def y_back(values):
            values, held["across"] = together(values, swap(held["third"], "var", 2))
            return values

        m_all = sum_over_all(place, *m_parts, (core_done, x_done, y_done, z_done, b_done, y_back))
        mlp_out_grad = join_rows(place, held["first"]).reshape(hidden // patches, width)
        mlp_in_grad, trunk_out_grad = join_columns(place, held["second"], (quarter, part))
        own, across = held["third"], held["across"]
        third = (own, swap(own, "var", 1), across, swap(across, "var", 1))
        trunk_qkv_grad, agg_out_grad = join_columns(place, third, (3 * part, part))
    else:

        def slices(values):
            values = values.reshape(seg, group, values.shape[1] // group).transpose(1, 0, 2)
            return lax.all_to_all(values, "var", split_axis=0, concat_axis=0, tiled=True)

        def everyone(values):
            return lax.all_gather(values, "var", axis=0, tiled=True)

        def total(left, right):
            value = mm(left.reshape(-1, left.shape[-1]), right.reshape(-1, right.shape[-1]), TN).astype(BF16)
            value = lax.psum_scatter(value, "patch", scatter_dimension=0, tiled=True)
            return lax.all_gather(value, "var", axis=0)

        def joined(value):
            return value.transpose(1, 0, 2).reshape(value.shape[1], -1).astype(F32)

        size = hidden // (patches * group)
        active_rows = active_low.reshape(seg, patches, group, size).transpose(0, 2, 1, 3).reshape(seg, hidden)
        mlp_out_grad = total(slices(active_rows), everyone(out_grad_low)).reshape(hidden // patches, width).astype(F32)
        mlp_in_grad = joined(total(everyone(normed_two_low), slices(inner_grad)))
        trunk_out_grad = joined(total(everyone(attended), slices(branch_low)))
        trunk_qkv_grad = joined(total(everyone(normed_one_low), slices(triple_grad)))
        agg_out_grad = joined(total(everyone(mixed_low), slices(agg_grad)))
        m_all = lax.psum(m_parts[0], ("patch", "var")).transpose(1, 0, 2).reshape(-1, width)
    field_grad = lax.all_to_all(
        field_low.reshape(1, VARS * pixels, seg), "var", split_axis=1, concat_axis=0, tiled=True
    )
    field_grad = field_grad.reshape(all_rows, var_local, pixels, seg).transpose(0, 3, 1, 2)
    s_rows = m_all[VARS * pixels + VARS :].astype(F32)
    s_all = s_rows[:, : VARS * pixels]
    se_all = s_rows[:, VARS * pixels : VARS * pixels + VARS]
    norm_sums = s_rows[:, width - 2 * head_dim :]
    m_sum, me_sum = m_all[: VARS * pixels], m_all[VARS * pixels : VARS * pixels + VARS]

    start = patch_index * own_width

    def own_cols(values):
        return lax.dynamic_slice_in_dim(values, start, own_width, 1)

    def own_rows(values):
        return lax.dynamic_slice_in_dim(values, start, own_width, 0)

    value_proj_grad = mm(own_cols(weight_rows), m_sum, TN) + mm(own_cols(var_embed), me_sum, TN)
    value_rows = own_rows(value_proj)
    key_query_rows = own_rows(key_query)
    patch_grad = mm(m_sum, value_rows, NT) + mm(
        s_all, key_query_rows, (((0,), (1,)), ((), ())), precision=HIGHEST
    )
    patch_grad = patch_grad.reshape(VARS, pixels, own_width)
    embed_grad = mm(me_sum, value_rows, NT) + mm(
        se_all, key_query_rows, (((0,), (1,)), ((), ())), precision=HIGHEST
    )
    s_parts = jnp.concatenate(split_high_low(s_all), axis=0)
    se_parts = jnp.concatenate(split_high_low(se_all), axis=0)
    key_sum = mm(s_parts, weight_rows) + mm(se_parts, var_embed)
    key_sum = (key_sum[:HEADS] + key_sum[HEADS:]) * scaling
    head_rows = jnp.where(in_head.T, agg_q[None, :], 0.0)
    key_proj_grad = mm(own_cols(key_sum), head_rows, TN, precision=HIGHEST)
    crossed = mm(jnp.concatenate(split_high_low(key_sum), axis=0), key_proj)
    crossed = crossed[:HEADS] + crossed[HEADS:]
    aggq_grad = jnp.sum(jnp.where(in_head.T, crossed, 0.0), axis=0)
    own_query = lax.dynamic_slice_in_dim(agg_query, start, own_width, 0).astype(F32)
    query_proj_grad = own_query[:, None] * aggq_grad[None, :]
    agg_query_grad = jnp.sum(own_rows(query_proj).astype(F32) * aggq_grad[None, :], axis=1)

    norm_one_grad = lax.dynamic_slice_in_dim(norm_sums[:, :head_dim].reshape(width), start, own_width, 0)
    norm_two_grad = lax.dynamic_slice_in_dim(norm_sums[:, head_dim:].reshape(width), start, own_width, 0)
    return (
        block_out,
        field_grad,
        patch_grad,
        embed_grad,
        agg_query_grad,
        query_proj_grad,
        key_proj_grad,
        value_proj_grad,
        agg_out_grad,
        norm_one_grad,
        trunk_qkv_grad,
        trunk_out_grad,
        norm_two_grad,
        mlp_in_grad,
        mlp_out_grad,
    )


def solution(mesh):
    whole = P()
    placed = (P(None, "patch", "var", None),) + (whole,) * 15 + (P("var", "patch", None),)
    rows = P("patch", None)
    return jax.shard_map(
        local,
        mesh=mesh,
        in_specs=placed,
        out_specs=(
            P("var", "patch", None),
            P(None, "patch", "var", None),
            P(None, None, "patch"),
            P(None, "patch"),
            P("patch"),
            rows,
            rows,
            rows,
            rows,
            P("patch"),
            rows,
            rows,
            P("patch"),
            rows,
            rows,
        ),
        check_vma=False,
    )
```

```python
import functools
import math

import jax
import jax.numpy as jnp
from jax import lax
from jax.experimental import pallas as pl
from jax.experimental.pallas import tpu as pltpu
from jax.sharding import PartitionSpec as P

HEADS = 16
VARS = 48
EPSILON = 1e-05
MASKED = -1e30
HIGHEST = lax.Precision.HIGHEST
BF16 = jnp.bfloat16
F32 = jnp.float32
NN = (((1,), (0,)), ((), ()))
NT = (((1,), (1,)), ((), ()))
TN = (((0,), (0,)), ((), ()))


def cost(flops):
    return pl.CostEstimate(flops=flops, bytes_accessed=1 << 20, transcendentals=0)


def mm(a, b, dims=NN, precision=None):
    return lax.dot_general(a, b, dims, precision=precision, preferred_element_type=F32)


def layer_norm(values, gain_vec):
    average = jnp.mean(values, axis=-1, keepdims=True)
    center = values - average
    spread = jnp.mean(center * center, axis=-1, keepdims=True)
    return center * lax.rsqrt(spread + EPSILON) * gain_vec


def gelu_exact(values):
    return jax.nn.gelu(values, approximate=False)


def split_high_low(values):
    high = values.astype(BF16)
    return high, (values - high.astype(F32)).astype(BF16)


def front_forward_kernel(
    pixels, ids_ref, field_ref, spread_ref, bias_ref, vwt_ref, vet_ref, x_ref, p_ref, mixed_ref, mt_ref
):
    seg = field_ref.shape[1]
    head_dim = mixed_ref.shape[1] // HEADS
    for slot in range(VARS):
        start = pl.multiple_of(ids_ref[0, slot] * pixels, pixels)
        x_ref[pl.ds(start, pixels), :] = field_ref[slot * pixels : (slot + 1) * pixels, :]
    scores = mm(spread_ref[...], x_ref[...]) + bias_ref[...]
    scores = scores.reshape(HEADS, VARS, seg)
    top = jnp.max(scores, axis=1, keepdims=True)
    exponent = jnp.exp(scores - top)
    total = jnp.sum(exponent, axis=1, keepdims=True)
    p_ref[...] = (exponent * (1.0 / total)).reshape(HEADS * VARS, seg)

    def head(h, carry):
        shares = p_ref[pl.ds(pl.multiple_of(h * VARS, VARS), VARS), :]
        pix = x_ref[...].astype(F32).reshape(VARS, pixels, seg)
        scaled = (pix * shares[:, None, :]).astype(BF16).reshape(VARS * pixels, seg)
        rows = pl.ds(pl.multiple_of(h * head_dim, head_dim), head_dim)
        mt_ref[rows, :] = mm(vwt_ref[rows, :], scaled) + mm(vet_ref[rows, :], shares.astype(BF16))
        return carry

    lax.fori_loop(0, HEADS, head, 0)
    mixed_ref[...] = mt_ref[...].T.astype(BF16)


def front_forward(own_ids, own_field, spread, bias, vwt, vet):
    rows, seg = own_field.shape
    width = vwt.shape[0]
    vmem = pl.BlockSpec(memory_space=pltpu.VMEM)
    return pl.pallas_call(
        functools.partial(front_forward_kernel, rows // VARS),
        out_shape=(
            jax.ShapeDtypeStruct((rows, seg), BF16),
            jax.ShapeDtypeStruct((HEADS * VARS, seg), F32),
            jax.ShapeDtypeStruct((seg, width), BF16),
        ),
        in_specs=[pl.BlockSpec(memory_space=pltpu.SMEM)] + [vmem] * 5,
        out_specs=(vmem,) * 3,
        scratch_shapes=[pltpu.VMEM((width, seg), F32)],
        cost_estimate=cost(6 * 10**9),
        name="front_forward",
    )(own_ids, own_field, spread, bias, vwt, vet)


def front_backward_kernel(
    pixels,
    fast,
    place_ref,
    ids_ref,
    x_ref,
    p_ref,
    mg_ref,
    vw_ref,
    ve_ref,
    spread_ref,
    norm_one_ref,
    norm_two_ref,
    field_ref,
    *rest,
):
    rows, seg = x_ref.shape
    m_refs, (fs_ref, dx_ref, s_ref) = rest[:-3], rest[-3:]
    size = m_refs[0].shape[-1]

    def quarter_of(quarter, store):
        if not fast:
            store(m_refs[0].at[quarter])
            return
        mine = quarter // 2 == place_ref[CORE]
        pl.when(mine)(lambda: store(m_refs[0].at[quarter % 2]))
        pl.when(jnp.logical_not(mine))(lambda: store(m_refs[1].at[quarter % 2]))
    width = mg_ref.shape[1]
    head_dim = width // HEADS
    pair_dim = 2 * head_dim
    lane = lax.broadcasted_iota(jnp.int32, (seg, pair_dim), 1)
    dx_ref[...] = jnp.zeros_like(dx_ref)
    pairs = size // pair_dim

    def pair(q, carry):
        cols = pl.ds(pl.multiple_of(q * pair_dim, pair_dim), pair_dim)
        grad = mg_ref[:, cols]
        none = jnp.zeros_like(grad)
        both = jnp.concatenate(
            [jnp.where(lane < head_dim, grad, none), jnp.where(lane >= head_dim, grad, none)], axis=0
        )
        inner = mm(vw_ref[:, cols], both, NT)
        inner_e = mm(ve_ref[:, cols], both, NT)
        pix = x_ref[...].astype(F32).reshape(VARS, pixels, seg)
        scaled, weights = [], []
        for k in range(2):
            hrows = pl.ds(pl.multiple_of((2 * q + k) * VARS, VARS), VARS)
            shares = p_ref[hrows, :]
            part = inner[:, k * seg : (k + 1) * seg].reshape(VARS, pixels, seg)
            share_grad = jnp.sum(pix * part, axis=1) + inner_e[:, k * seg : (k + 1) * seg]
            delta = jnp.sum(shares * share_grad, axis=0, keepdims=True)
            fs_ref[hrows, :] = shares * (share_grad - delta)
            wide = shares[:, None, :]
            dx_ref[...] += (part * wide).reshape(rows, seg)
            scaled.append((pix * wide).astype(BF16).reshape(rows, seg))
            weights.append(shares.astype(BF16))
        quarter, within = q // pairs, pl.ds(pl.multiple_of(q % pairs * pair_dim, pair_dim), pair_dim)
        m_part = mm(jnp.concatenate(scaled, axis=1), both).astype(BF16)
        me_part = mm(jnp.concatenate(weights, axis=1), both).astype(BF16)

        def store(ref):
            ref[0:rows, within] = m_part
            ref[rows : rows + VARS, within] = me_part

        quarter_of(quarter, store)
        return carry

    lax.fori_loop(0, HEADS // 2, pair, 0)
    score_grad = fs_ref[...]
    low = score_grad.astype(BF16)
    dx = dx_ref[...] + mm(spread_ref[...], low, TN)
    dx_ref[...] = dx
    for slot in range(VARS):
        start = pl.multiple_of(ids_ref[0, slot] * pixels, pixels)
        field_ref[slot * pixels : (slot + 1) * pixels, :] = dx_ref[pl.ds(start, pixels), :].astype(BF16)
    ones = jnp.ones((8, seg), F32)
    s_ref[...] = jnp.zeros_like(s_ref)
    var_row = lax.broadcasted_iota(jnp.int32, (VARS, rows), 0)
    var_col = lax.broadcasted_iota(jnp.int32, (VARS, rows), 1) // pixels
    keep = var_row == var_col
    for h in range(HEADS):
        outer = mm(low[h * VARS : (h + 1) * VARS, :], x_ref[...], NT)
        s_ref[h : h + 1, 0:rows] = jnp.sum(jnp.where(keep, outer, 0.0), axis=0, keepdims=True)
        sums = mm(ones, score_grad[h * VARS : (h + 1) * VARS, :], NT, precision=HIGHEST)
        s_ref[h : h + 1, rows : rows + VARS] = sums[0:1, :]
    for h in range(HEADS):
        for ref, first in ((norm_one_ref, width - pair_dim), (norm_two_ref, width - head_dim)):
            s_ref[h : h + 1, first : first + head_dim] = ref[:, h * head_dim : (h + 1) * head_dim]
    for quarter in range(4):
        part = s_ref[:, quarter * size : (quarter + 1) * size].astype(BF16)

        def store_sums(ref, part=part):
            ref[rows + VARS :, :] = part

        quarter_of(quarter, store_sums)


def front_backward(fast, place, own_ids, x_own, shares, mixed_grad, vw, ve, spread, norm_one, norm_two):
    rows, seg = x_own.shape
    width = mixed_grad.shape[1]
    vmem = pl.BlockSpec(memory_space=pltpu.VMEM)
    smem = pl.BlockSpec(memory_space=pltpu.SMEM)
    tall = rows + VARS + HEADS
    if fast:
        sums = (jax.ShapeDtypeStruct((2, tall, width // 4), BF16),) * 2
    else:
        sums = (jax.ShapeDtypeStruct((4, tall, width // 4), BF16),)
    return pl.pallas_call(
        functools.partial(front_backward_kernel, rows // VARS, fast),
        out_shape=(jax.ShapeDtypeStruct((rows, seg), BF16), *sums),
        in_specs=[smem, smem] + [vmem] * 8,
        out_specs=(vmem,) * (1 + len(sums)),
        scratch_shapes=[
            pltpu.VMEM((HEADS * VARS, seg), F32),
            pltpu.VMEM((rows, seg), F32),
            pltpu.VMEM((HEADS, width), F32),
        ],
        cost_estimate=cost(10**8),
        name="front_backward",
    )(place, own_ids, x_own, shares, mixed_grad, vw, ve, spread, norm_one, norm_two)


def load_parts(ref, part, seg, out_ref):
    for source in range(ref.shape[0]):
        out_ref[source * seg : (source + 1) * seg, :] = ref[source, part * seg : (part + 1) * seg, :]


def attend_forward_kernel(head_dim, block, count_ref, qkv_ref, out_ref, lse_ref, q_ref, k_ref, vt_ref):
    full, width = q_ref.shape
    seg = full // qkv_ref.shape[0]
    scaling = 1.0 / math.sqrt(head_dim)
    load_parts(qkv_ref, 2, seg, q_ref)
    vt_ref[...] = q_ref[...].T
    load_parts(qkv_ref, 0, seg, q_ref)
    load_parts(qkv_ref, 1, seg, k_ref)
    count = count_ref[0, 0]
    lane = lax.broadcasted_iota(jnp.int32, (block, width), 1) // head_dim
    row = lax.broadcasted_iota(jnp.int32, (width, block), 0) // head_dim
    valid = lax.broadcasted_iota(jnp.int32, (full, block), 0) < count

    def step(i, carry):
        part = pl.ds(pl.multiple_of(i * block, block), block)
        query = q_ref[part, :]
        total = jnp.zeros((width, block), F32)
        for h in range(width // head_dim):
            own = jnp.where(lane == h, query, jnp.zeros_like(query))
            scores = jnp.where(valid, mm(k_ref[...], own, NT) * scaling, MASKED)
            top = jnp.max(scores, axis=0, keepdims=True)
            exponent = jnp.exp(scores - top)
            denominator = jnp.sum(exponent, axis=0, keepdims=True)
            shares = (exponent * (1.0 / denominator)).astype(BF16)
            lse_ref[h : h + 1, part] = top + jnp.log(denominator)
            total = jnp.where(row == h, mm(vt_ref[...], shares), total)
        out_ref[part, :] = total.T.astype(BF16)
        return carry

    lax.fori_loop(0, full // block, step, 0)


def attend_forward(count, qkv, head_dim):
    parts, triple_rows, width = qkv.shape
    full = parts * triple_rows // 3
    vmem = pl.BlockSpec(memory_space=pltpu.VMEM)
    block = min(256, full)
    return pl.pallas_call(
        functools.partial(attend_forward_kernel, head_dim, block),
        out_shape=(
            jax.ShapeDtypeStruct((full, width), BF16),
            jax.ShapeDtypeStruct((width // head_dim, full), F32),
        ),
        in_specs=[pl.BlockSpec(memory_space=pltpu.SMEM), vmem],
        out_specs=(vmem, vmem),
        scratch_shapes=[
            pltpu.VMEM((full, width), BF16),
            pltpu.VMEM((full, width), BF16),
            pltpu.VMEM((width, full), BF16),
        ],
        cost_estimate=cost(10 * 10**9),
        name="attend_forward",
    )(count, qkv)


def attend_backward_kernel(
    head_dim, block, count_ref, qkv_ref, grad_ref, lse_ref, out_ref, q_ref, k_ref, v_ref, kt_ref, dk_ref, dv_ref
):
    full, width = q_ref.shape
    seg = full // qkv_ref.shape[0]
    scaling = 1.0 / math.sqrt(head_dim)
    load_parts(qkv_ref, 0, seg, q_ref)
    load_parts(qkv_ref, 1, seg, k_ref)
    load_parts(qkv_ref, 2, seg, v_ref)
    kt_ref[...] = k_ref[...].T
    dk_ref[...] = jnp.zeros_like(dk_ref)
    dv_ref[...] = jnp.zeros_like(dv_ref)
    count = count_ref[0, 0]
    lane = lax.broadcasted_iota(jnp.int32, (block, width), 1) // head_dim
    row = lax.broadcasted_iota(jnp.int32, (width, block), 0) // head_dim
    valid = lax.broadcasted_iota(jnp.int32, (full, block), 0) < count

    def step(i, carry):
        part = pl.ds(pl.multiple_of(i * block, block), block)
        query = q_ref[part, :]
        grad = grad_ref[part, :]
        total = jnp.zeros((width, block), F32)
        for h in range(width // head_dim):
            own = jnp.where(lane == h, query, jnp.zeros_like(query))
            own_grad = jnp.where(lane == h, grad, jnp.zeros_like(grad))
            scores = jnp.where(valid, mm(k_ref[...], own, NT) * scaling, MASKED)
            shares = jnp.exp(scores - lse_ref[h : h + 1, part])
            share_grad = mm(v_ref[...], own_grad, NT)
            dot = jnp.sum(shares * share_grad, axis=0, keepdims=True)
            score_grad = (shares * (share_grad - dot)).astype(BF16)
            dv_ref[...] += mm(shares.astype(BF16), own_grad)
            dk_ref[...] += mm(score_grad, own)
            total = jnp.where(row == h, mm(kt_ref[...], score_grad), total)
        turned = (total * scaling).T.astype(BF16)
        for piece in range(block // seg):
            out_ref[i * (block // seg) + piece, 0:seg, :] = turned[piece * seg : (piece + 1) * seg, :]
        return carry

    lax.fori_loop(0, full // block, step, 0)
    for source in range(full // seg):
        rows = slice(source * seg, (source + 1) * seg)
        out_ref[source, seg : 2 * seg, :] = (dk_ref[rows, :] * scaling).astype(BF16)
        out_ref[source, 2 * seg : 3 * seg, :] = dv_ref[rows, :].astype(BF16)


def attend_backward(count, qkv, grad, lse, head_dim):
    parts, triple_rows, width = qkv.shape
    full = parts * triple_rows // 3
    vmem = pl.BlockSpec(memory_space=pltpu.VMEM)
    block = min(256, full)
    return pl.pallas_call(
        functools.partial(attend_backward_kernel, head_dim, block),
        out_shape=jax.ShapeDtypeStruct(qkv.shape, BF16),
        in_specs=[pl.BlockSpec(memory_space=pltpu.SMEM), vmem, vmem, vmem],
        out_specs=vmem,
        scratch_shapes=[pltpu.VMEM((full, width), BF16)] * 3
        + [pltpu.VMEM((width, full), BF16)]
        + [pltpu.VMEM((full, width), F32)] * 2,
        cost_estimate=cost(50 * 10**9),
        name="attend_backward",
    )(count, qkv, grad, lse)


def gathered_attention(triple, count, head_dim):
    seg, triple_width = triple.shape
    width = triple_width // 3
    scaling = 1.0 / math.sqrt(head_dim)
    full = seg * lax.axis_size("patch")
    query = triple[:, :width].reshape(seg, HEADS, head_dim)
    key = lax.all_gather(triple[:, width : 2 * width], "patch", axis=0, tiled=True)
    value = lax.all_gather(triple[:, 2 * width :], "patch", axis=0, tiled=True)
    key = key.reshape(full, HEADS, head_dim)
    value = value.reshape(full, HEADS, head_dim)
    valid = (jnp.arange(full, dtype=jnp.int32) < count)[None, None, :]

    def score():
        raw = jnp.einsum("qhd,khd->hqk", query, key, preferred_element_type=F32) * scaling
        return jnp.where(valid, raw, MASKED)

    masked = score()
    top = jnp.max(masked, axis=-1, keepdims=True)
    exponent = jnp.exp(masked - top)
    denominator = jnp.sum(exponent, axis=-1, keepdims=True)
    shares_low = (exponent / denominator).astype(BF16)
    lse = top + jnp.log(denominator)
    attended = jnp.einsum("hqk,khd->qhd", shares_low, value, preferred_element_type=F32)

    def backward(grad):
        grad = grad.reshape(seg, HEADS, head_dim)
        shares = jnp.exp(score() - lse)
        share_grad = jnp.einsum("qhd,khd->hqk", grad, value, preferred_element_type=F32)
        dot = jnp.sum(shares * share_grad, axis=-1, keepdims=True)
        score_grad = (shares * (share_grad - dot)).astype(BF16)
        q_grad = jnp.einsum("hqk,khd->qhd", score_grad, key, preferred_element_type=F32) * scaling
        v_all = jnp.einsum("hqk,qhd->khd", shares.astype(BF16), grad, preferred_element_type=F32)
        k_all = jnp.einsum("hqk,qhd->khd", score_grad, query, preferred_element_type=F32) * scaling
        k_grad, v_grad = (
            lax.psum_scatter(
                part.reshape(full, width).astype(BF16), "patch", scatter_dimension=0, tiled=True
            )
            for part in (k_all, v_all)
        )
        return jnp.concatenate([q_grad.reshape(seg, width).astype(BF16), k_grad, v_grad], axis=1)

    return attended.reshape(seg, width).astype(BF16), backward


def to_heads(values):
    return lax.all_to_all(values, "patch", split_axis=0, concat_axis=0, tiled=True)


def queries_to_heads(triple):
    seg, triple_width = triple.shape
    parts = lax.axis_size("patch")
    own = triple_width // (3 * parts)
    moved = triple.reshape(seg, 3, parts, own).transpose(2, 1, 0, 3).reshape(parts, 3 * seg, own)
    return to_heads(moved)


def weight_grad_kernel(jobs, near, away, place_ref, *refs):
    split = len(refs) - len(near) - len(away)
    arrays, outs = refs[:split], refs[split:]
    rows = outs[0].shape[1]
    sides = (1 - place_ref[Y],) * len(away) + (place_ref[Y],) * len(near)
    start = 0
    for left, left_start, right, right_start, cols in jobs:
        values = [arrays[4 * right + s][:, pl.ds(right_start, cols)] for s in range(4)]
        values = jnp.concatenate(values, axis=0)
        for out, side, blocks in zip(outs, sides, away + near):
            for slot, k in enumerate(blocks):
                source = 2 * (place_ref[Z] ^ k) + side
                group = arrays[4 * left : 4 * left + 4]
                if len(group[0].shape) == 3:
                    factor = [ref[source] for ref in group]
                else:
                    block = pl.ds(pl.multiple_of(left_start + source * rows, rows), rows)
                    factor = [ref[:, block] for ref in group]
                factor = jnp.concatenate(factor, axis=0)
                out[slot, :, start : start + cols] = mm(factor, values, TN).astype(BF16)
        start += cols


def weight_grads(place, jobs, groups, rows, near, away):
    arrays = [array for group in groups for array in group]
    total = sum(job[-1] for job in jobs)
    shapes = [((len(blocks), rows, total), BF16) for blocks in away + near]
    kernel = functools.partial(weight_grad_kernel, jobs, near, away)
    outs = small_call(kernel, place, arrays, shapes, effort=40, name="weight_grads")
    return outs[len(away) :], outs[: len(away)]


def swap(values, axis, bit):
    return lax.ppermute(values, axis, [(i, i ^ bit) for i in range(lax.axis_size(axis))])


def together(*values):
    return lax.optimization_barrier(values)


def after(value, *others):
    return lax.optimization_barrier((value, *others))[0]


def small_call(kernel, place, arrays, shapes, scratch=(), effort=20, name="small"):
    vmem = pl.BlockSpec(memory_space=pltpu.VMEM)
    return pl.pallas_call(
        kernel,
        out_shape=tuple(jax.ShapeDtypeStruct(dims, dtype) for dims, dtype in shapes),
        in_specs=[pl.BlockSpec(memory_space=pltpu.SMEM)] + [vmem] * len(arrays),
        out_specs=(vmem,) * len(shapes),
        scratch_shapes=list(scratch),
        cost_estimate=cost(effort * 10**9),
        name=name,
    )(place, *arrays)


ME, CORE, X, Y, Z = range(5)


def tokens_of_group(values):
    across = swap(values, "var", 2)
    return values, swap(values, "var", 1), across, swap(across, "var", 1)


def copies_of_group(values):
    return (values,) + tuple(swap(values, "var", bit) for bit in (1, 2, 3))


def slices_of_group(pieces):
    return (pieces[0],) + tuple(swap(pieces[bit], "var", bit) for bit in (1, 2, 3))


def z_pieces(place, near, got):
    _, rows, cols = near.shape

    def kernel(place_ref, near_ref, got_ref, *outs):
        for bit in range(4):
            block = place_ref[Z] ^ bit
            outs[bit][...] = (near_ref[block].astype(F32) + got_ref[block].astype(F32)).astype(BF16)

    return small_call(kernel, place, (near, got), [((rows, cols), BF16)] * 4, name="z_pieces")


def z_exchange(pieces):
    return (pieces[0],) + tuple(swap(pieces[bit], "patch", 2 * bit) for bit in (1, 2, 3))


def z_sum(place, arrays):

    def kernel(place_ref, first, second, third, fourth, out):
        total = first[...].astype(F32) + second[...].astype(F32) + third[...].astype(F32) + fourth[...].astype(F32)
        out[...] = total.astype(BF16)

    return small_call(kernel, place, arrays, [(arrays[0].shape, BF16)], name="z_sum")[0]


def pair_sum(place, near, gots):
    def kernel(place_ref, near_ref, *refs):
        for k in range(2):
            got = refs[0][k] if len(refs) == 2 else refs[k][0]
            refs[-1][k] = (near_ref[k].astype(F32) + got.astype(F32)).astype(BF16)

    return small_call(kernel, place, (near, *gots), [(near.shape, BF16)], name="pair_sum")[0]


def z_first_sum(place, near, gots, far):
    def kernel(place_ref, near_ref, *refs):
        gots, (far_ref, stay, away) = refs[:-3], refs[-3:]
        for out, k in ((away, 1), (stay, 0)):
            got = gots[0][k] if len(gots) == 1 else gots[k][0]
            out[...] = (near_ref[k].astype(F32) + got.astype(F32) + far_ref[k].astype(F32)).astype(BF16)

    return small_call(kernel, place, (near, *gots, far), [(near.shape[1:], BF16)] * 2, name="z_first_sum")


def z_last_sum(place, near, got):
    def kernel(place_ref, near_ref, got_ref, out):
        out[...] = (near_ref[...].astype(F32) + got_ref[...].astype(F32)).astype(BF16)

    return small_call(kernel, place, (near, got), [(near.shape, BF16)], name="z_last_sum")[0]


def gather_over_var(own):
    across = swap(own, "var", 2)
    return own, swap(own, "var", 1), across, swap(across, "var", 1)


def join(place, pieces, widths, stacked):
    rows = pieces[0].shape[0]

    def kernel(place_ref, *refs):
        start = 0
        for k, (out, size) in enumerate(zip(refs[4:], widths)):
            for s in range(4):
                v = place_ref[ME] ^ s
                values = refs[s][:, start : start + size].astype(F32)
                if k < stacked:
                    out[v] = values
                else:
                    out[:, pl.ds(pl.multiple_of(v * size, size), size)] = values
            start += size

    shapes = [((4, rows, size) if k < stacked else (rows, 4 * size), F32) for k, size in enumerate(widths)]
    return small_call(kernel, place, pieces, shapes, name="join")


def sum_over_all(place, stay, away, hooks):
    _, rows, cols = stay.shape
    half = rows // 2
    size = half // 4
    hooks = iter(hooks)

    def core_kernel(place_ref, stay_ref, got_ref, stay_out, away_out):
        for out, which in ((away_out, 1 - place_ref[X]), (stay_out, place_ref[X])):
            out[...] = (stay_ref[which].astype(F32) + got_ref[which].astype(F32)).astype(BF16)

    got = next(hooks)(swap(away, "var", 1))
    stay, away = small_call(core_kernel, place, (stay, got), [((rows, cols), BF16)] * 2, name="core_sum")

    def x_kernel(place_ref, stay_ref, got_ref, stay_out, away_out):
        for out, which in ((away_out, 1 - place_ref[Y]), (stay_out, place_ref[Y])):
            out[...] = (stay_ref[which].astype(F32) + got_ref[which].astype(F32)).astype(BF16)

    got = next(hooks)(swap(away, "var", 2))
    halves = (2, half, cols)
    stay, away = small_call(
        x_kernel, place, (stay.reshape(halves), got.reshape(halves)), [((half, cols), BF16)] * 2, name="x_sum"
    )
    got = next(hooks)(swap(away, "patch", 1))
    pieces = z_exchange(z_pieces(place, stay.reshape(4, size, cols), got.reshape(4, size, cols)))
    kept = z_sum(place, next(hooks)(pieces))

    def z_kernel(place_ref, *refs):
        for s in range(4):
            refs[4][place_ref[Z] ^ s] = refs[s][...]

    arrays = (kept,) + tuple(swap(kept, "patch", 2 * bit) for bit in (1, 2, 3))
    own = small_call(z_kernel, place, next(hooks)(arrays), [((4, size, cols), BF16)], name="z_join")[0]

    def y_kernel(place_ref, own_ref, other_ref, out):
        out[place_ref[Y]] = own_ref[...]
        out[1 - place_ref[Y]] = other_ref[...]

    own = own.reshape(half, cols)
    arrays = (own, next(hooks)(swap(own, "patch", 1)))
    full = small_call(y_kernel, place, arrays, [(halves, BF16)], name="y_join")[0].reshape(rows, cols)

    return gather_over_var(full)


def middle_kernel(
    place_ref,
    att_ref,
    front_ref,
    valid_ref,
    og_ref,
    tout_ref,
    gain_ref,
    win_ref,
    wout_ref,
    block_ref,
    late_ref,
    *refs,
):
    actives, middles = refs[0:4], refs[4:8]
    grad_ref, after_ref, gain_grad_ref, residual_ref, unit_ref, rate_ref, acc_ref, back_ref, wide_ref, branch_ref = refs[8:]
    step = pl.program_id(0)
    seg, width = front_ref.shape
    parts = att_ref.shape[0]
    own = width // parts
    me = place_ref[0]
    slot = actives[0].shape[1] // pl.num_programs(0)

    @pl.when(step == 0)
    def _():
        for p in range(parts):
            branch_ref[:, p * own : (p + 1) * own] = att_ref[p]
        after = front_ref[...] + mm(branch_ref[...], tout_ref[...])
        residual_ref[...] = after
        center = after - jnp.mean(after, axis=1, keepdims=True)
        rate = lax.rsqrt(jnp.mean(center * center, axis=1, keepdims=True) + EPSILON)
        unit = center * rate
        unit_ref[...] = unit
        rate_ref[...] = rate
        late_ref[...] = (unit * gain_ref[...]).astype(BF16)
        acc_ref[...] = jnp.zeros_like(acc_ref)
        back_ref[...] = jnp.zeros_like(back_ref)

    inner = mm(late_ref[...], win_ref[...])
    cumulative = 0.5 * (1.0 + lax.erf(inner * math.sqrt(0.5)))
    active = (inner * cumulative).astype(BF16)
    acc_ref[...] += mm(active, wout_ref[...])
    slope = cumulative + inner * (jnp.exp(-0.5 * inner * inner) * (1.0 / math.sqrt(2.0 * math.pi)))
    inner_grad = (mm(og_ref[...], wout_ref[...], NT) * slope).astype(BF16)
    back_ref[...] += mm(inner_grad, win_ref[...], NT)
    wide_ref[...] = active
    cols = pl.ds(pl.multiple_of(step * slot, slot), slot)
    for s in range(4):
        actives[s][:, cols] = wide_ref[:, pl.ds(pl.multiple_of((me ^ s) * slot, slot), slot)]
    block = inner_grad.shape[1]
    owner = step * block // width
    place = pl.ds(pl.multiple_of(step * block - owner * width, block), block)
    for s in range(4):

        @pl.when((me ^ s) == owner)
        def _(s=s):
            middles[s][:, place] = inner_grad

    @pl.when(step == pl.num_programs(0) - 1)
    def _():
        valid = valid_ref[...]
        block_ref[...] = ((residual_ref[...] + acc_ref[...]) * valid).astype(BF16)
        unit = unit_ref[...]
        back = back_ref[...]
        gain_grad_ref[...] = jnp.sum(back * unit, axis=0, keepdims=True)
        scaled = back * gain_ref[...]
        inside = jnp.mean(scaled * unit, axis=1, keepdims=True)
        total = rate_ref[...] * (scaled - jnp.mean(scaled, axis=1, keepdims=True) - unit * inside)
        total = og_ref[...].astype(F32) + total
        after_ref[...] = total
        branch_ref[...] = total.astype(BF16)
        quarter = width // 4
        for s in range(4):
            start = pl.multiple_of((me ^ s) * quarter, quarter)
            middles[s][:, width : width + quarter] = branch_ref[:, pl.ds(start, quarter)]
        turned = mm(branch_ref[...], tout_ref[...], NT).astype(BF16)
        for p in range(parts):
            grad_ref[p] = turned[:, p * own : (p + 1) * own]


def middle(place, attended, front_out, valid, out_grad, trunk_out, gain, mlp_in, mlp_out):
    seg, width = front_out.shape
    hidden = mlp_in.shape[1]
    parts = attended.shape[0]
    block = hidden // parts
    shape = jax.ShapeDtypeStruct

    def still(*dims):
        return pl.BlockSpec(dims, lambda i: (0,) * len(dims))

    piece, wider = shape((seg, hidden // 4), BF16), shape((seg, width + width // 4), BF16)
    return pl.pallas_call(
        middle_kernel,
        grid=(parts,),
        out_shape=(
            shape((seg, width), BF16),
            shape((seg, width), BF16),
            *((piece,) * 4),
            *((wider,) * 4),
            shape(attended.shape, BF16),
            shape((seg, width), F32),
            shape((1, width), F32),
        ),
        in_specs=[
            pl.BlockSpec(memory_space=pltpu.SMEM),
            still(*attended.shape),
            still(seg, width),
            still(seg, 1),
            still(seg, width),
            still(width, width),
            still(1, width),
            pl.BlockSpec((width, block), lambda i: (0, i)),
            pl.BlockSpec((block, width), lambda i: (i, 0)),
        ],
        out_specs=(
            still(seg, width),
            still(seg, width),
            *((still(*piece.shape),) * 4),
            *((still(*wider.shape),) * 4),
            still(*attended.shape),
            still(seg, width),
            still(1, width),
        ),
        scratch_shapes=[
            pltpu.VMEM((seg, width), F32),
            pltpu.VMEM((seg, width), F32),
            pltpu.VMEM((seg, 1), F32),
            pltpu.VMEM((seg, width), F32),
            pltpu.VMEM((seg, width), F32),
            pltpu.VMEM((seg, block), BF16),
            pltpu.VMEM((seg, width), BF16),
        ],
        compiler_params=pltpu.CompilerParams(dimension_semantics=("arbitrary",)),
        cost_estimate=cost(60 * 10**9),
        name="trunk_middle",
    )(place, attended, front_out, valid, out_grad, trunk_out, gain, mlp_in, mlp_out)


def trunk_back_kernel(
    place_ref, grads_ref, front_ref, gain_ref, after_ref, valid_ref, aout_ref, wqkv_ref, mixed_ref, gain_grad_ref, *rest
):
    pieces, triple_ref, back_ref, wide_ref = rest[:4], rest[4], rest[5], rest[6]
    step = pl.program_id(0)
    parts = grads_ref.shape[0]
    seg, width = front_ref.shape
    own = width // parts
    me = place_ref[ME]

    @pl.when(step == 0)
    def _():
        for c in range(3):
            for p in range(parts):
                triple_ref[c, :, p * own : (p + 1) * own] = grads_ref[p, c * seg : (c + 1) * seg, :]
        back_ref[...] = jnp.zeros_like(back_ref)

    back_ref[...] += mm(triple_ref[step], wqkv_ref[...], NT)

    @pl.when(step == pl.num_programs(0) - 1)
    def _():
        front = front_ref[...]
        center = front - jnp.mean(front, axis=1, keepdims=True)
        rate = lax.rsqrt(jnp.mean(center * center, axis=1, keepdims=True) + EPSILON)
        unit = center * rate
        back = back_ref[...]
        gain_grad_ref[...] = jnp.sum(back * unit, axis=0, keepdims=True)
        scaled = back * gain_ref[...]
        inside = jnp.mean(scaled * unit, axis=1, keepdims=True)
        total = rate * (scaled - jnp.mean(scaled, axis=1, keepdims=True) - unit * inside)
        total = ((after_ref[...] + total) * valid_ref[...]).astype(BF16)
        mixed_ref[...] = mm(total, aout_ref[...], NT).astype(BF16)
        wide_ref[...] = total
        part = width // 4
        for s in range(4):
            v = me ^ s
            pieces[s][:, 3 * part :] = wide_ref[:, pl.ds(pl.multiple_of(v * part, part), part)]
            for k in range(3):
                block = 3 * v + k
                cols = pl.ds(pl.multiple_of(block % 4 * part, part), part)
                pieces[s][:, k * part : (k + 1) * part] = triple_ref[block // 4, :, cols]


def trunk_back(place, grads, front_out, gain, after_grad, valid, agg_out, trunk_qkv):
    seg, width = front_out.shape
    shape = jax.ShapeDtypeStruct

    def still(*dims):
        return pl.BlockSpec(dims, lambda i: (0,) * len(dims))

    piece = shape((seg, width), BF16)
    return pl.pallas_call(
        trunk_back_kernel,
        grid=(3,),
        out_shape=(piece, shape((1, width), F32), *((piece,) * 4)),
        in_specs=[
            pl.BlockSpec(memory_space=pltpu.SMEM),
            still(*grads.shape),
            still(seg, width),
            still(1, width),
            still(seg, width),
            still(seg, 1),
            still(width, width),
            pl.BlockSpec((width, width), lambda i: (0, i)),
        ],
        out_specs=(still(seg, width), still(1, width), *((still(seg, width),) * 4)),
        scratch_shapes=[
            pltpu.VMEM((3, seg, width), BF16),
            pltpu.VMEM((seg, width), F32),
            pltpu.VMEM((seg, width), BF16),
        ],
        compiler_params=pltpu.CompilerParams(dimension_semantics=("arbitrary",)),
        cost_estimate=cost(80 * 10**9),
        name="trunk_back",
    )(place, grads, front_out, gain, after_grad, valid, agg_out, trunk_qkv)


def front_last_kernel(
    pixels,
    place_ref,
    m0,
    m1,
    m2,
    m3,
    weight_ref,
    embed_ref,
    weight_own_ref,
    embed_own_ref,
    value_rows_ref,
    key_query_ref,
    key_ref,
    aggq_ref,
    query_rows_ref,
    query_own_ref,
    value_out,
    patch_out,
    embed_out,
    key_out,
    query_out,
    agg_query_out,
    norm_one_out,
    norm_two_out,
    m_ref,
    sum_ref,
):
    rows, width = weight_ref.shape
    own = weight_own_ref.shape[1]
    size = m0.shape[1]
    head_dim = width // HEADS
    scaling = 1.0 / math.sqrt(head_dim)
    for s, ref in enumerate((m0, m1, m2, m3)):
        v = place_ref[ME] ^ s
        m_ref[:, pl.ds(pl.multiple_of((v % 2 * 2 + v // 2) * size, size), size)] = ref[...]
    m_sum, me_sum = m_ref[0:rows, :], m_ref[rows : rows + VARS, :]
    value_out[...] = mm(weight_own_ref[...], m_sum, TN) + mm(embed_own_ref[...], me_sum, TN)
    s_all = m_ref[rows + VARS : rows + VARS + HEADS, :]
    twice = jnp.concatenate([s_all, s_all], axis=0)
    patch_out[...] = mm(m_sum, value_rows_ref[...], NT) + mm(twice[:, 0:rows], key_query_ref[...], TN)
    embed_out[...] = mm(me_sum, value_rows_ref[...], NT) + mm(
        twice[:, rows : rows + VARS], key_query_ref[...], TN
    )
    key_sum = (mm(s_all[:, 0:rows], weight_ref[...]) + mm(s_all[:, rows : rows + VARS], embed_ref[...])) * scaling
    sum_ref[...] = key_sum
    lane = lax.broadcasted_iota(jnp.int32, (HEADS, width), 1) // head_dim
    mine = lane == lax.broadcasted_iota(jnp.int32, (HEADS, width), 0)
    start = pl.multiple_of((place_ref[Z] * 2 + place_ref[Y]) * own, own)
    head_rows = jnp.where(mine, aggq_ref[...], 0.0)
    key_out[...] = mm(sum_ref[:, pl.ds(start, own)], head_rows, TN, precision=HIGHEST)
    crossed = mm(jnp.concatenate(split_high_low(key_sum), axis=0), key_ref[...])
    crossed = crossed[0:HEADS, :] + crossed[HEADS:, :]
    aggq_grad = jnp.sum(jnp.where(mine, crossed, 0.0), axis=0, keepdims=True)
    query_out[...] = query_own_ref[...] * aggq_grad
    high, low = split_high_low(aggq_grad)
    agg_query_out[...] = mm(high, query_rows_ref[...], NT) + mm(low, query_rows_ref[...], NT)
    row = lax.broadcasted_iota(jnp.int32, (HEADS, own), 0)
    tail = s_all[:, width - own :].astype(F32)
    for k in range(own // head_dim):
        line = jnp.sum(jnp.where(row == start // head_dim + k, tail, 0.0), axis=0, keepdims=True)
        norm_one_out[:, k * head_dim : (k + 1) * head_dim] = line[:, 0:head_dim]
        norm_two_out[:, k * head_dim : (k + 1) * head_dim] = line[:, head_dim:own]


def front_last(place, pieces, arrays):
    weight_rows, own_weight, value_rows = arrays[0], arrays[2], arrays[4]
    rows, width = weight_rows.shape
    own = own_weight.shape[1]
    tall = pieces[0].shape[0]
    shapes = [((own, width), F32), ((rows, own), F32), ((VARS, own), F32)] + [((own, width), F32)] * 2
    shapes += [((1, own), F32)] * 3
    return small_call(
        functools.partial(front_last_kernel, rows // VARS),
        place,
        (*pieces, *arrays),
        shapes,
        scratch=[pltpu.VMEM((tall, width), BF16), pltpu.VMEM((HEADS, width), F32)],
        name="front_last",
    )


def local(
    input_field,
    counts,
    var_ids,
    patch_weight,
    var_embed,
    agg_query,
    query_proj,
    key_proj,
    value_proj,
    agg_out,
    norm_one,
    trunk_qkv,
    trunk_out,
    norm_two,
    mlp_in,
    mlp_out,
    cotangent,
):
    patches, group = lax.axis_size("patch"), lax.axis_size("var")
    fast = (patches, group) == (8, 4)
    me, spot = lax.axis_index("var"), lax.axis_index("patch")
    place = jnp.stack([me, me % 2, me // 2, spot % 2, spot // 2]).astype(jnp.int32)
    var_index = lax.axis_index("var")
    patch_index = lax.axis_index("patch")
    all_rows, seg, var_local, pixels = input_field.shape
    width = agg_out.shape[0]
    head_dim = width // HEADS
    hidden = mlp_in.shape[1]
    scaling = 1.0 / math.sqrt(head_dim)

    turned = input_field.transpose(0, 2, 3, 1).reshape(all_rows, var_local * pixels, seg)
    own_field = lax.all_to_all(turned, "var", split_axis=0, concat_axis=1, tiled=True)
    own_field = own_field.reshape(VARS * pixels, seg)
    own_ids = lax.dynamic_slice_in_dim(var_ids, var_index, 1, 0)
    own_count = lax.dynamic_slice_in_dim(counts, var_index, 1, 0)
    positions = patch_index * seg + jnp.arange(seg, dtype=jnp.int32)
    valid_rows = (positions < own_count).astype(F32)[:, None]
    out_grad = cotangent.reshape(seg, width).astype(F32) * valid_rows
    out_grad_low = out_grad.astype(BF16)

    weight_rows = patch_weight.reshape(VARS * pixels, width)
    agg_q = mm(agg_query[None], query_proj)[0]
    in_head = jnp.arange(width, dtype=jnp.int32)[:, None] // head_dim == jnp.arange(HEADS)[None, :]
    head_query = jnp.where(in_head, agg_q[:, None] * scaling, 0.0)
    key_query = mm(key_proj, jnp.concatenate(split_high_low(head_query), axis=1))
    key_query = key_query[:, :HEADS] + key_query[:, HEADS:]
    key_query_parts = jnp.concatenate(split_high_low(key_query), axis=1)
    score_weight = mm(key_query_parts, weight_rows, (((0,), (1,)), ((), ())))
    score_weight = score_weight[:HEADS] + score_weight[HEADS:]
    score_embed = mm(key_query_parts, var_embed, (((0,), (1,)), ((), ())))
    score_embed = (score_embed[:HEADS] + score_embed[HEADS:]).reshape(HEADS * VARS, 1)
    same_var = (jnp.arange(VARS)[:, None] == jnp.arange(VARS * pixels)[None, :] // pixels)[None]
    spread = jnp.where(same_var, score_weight[:, None, :], 0.0).astype(BF16)
    spread = spread.reshape(HEADS * VARS, VARS * pixels)
    vw = mm(weight_rows, value_proj).astype(BF16)
    ve = mm(var_embed, value_proj).astype(BF16)
    vwt = mm(value_proj, weight_rows, (((0,), (1,)), ((), ()))).astype(BF16)
    vet = mm(value_proj, var_embed, (((0,), (1,)), ((), ()))).astype(BF16)

    own_width = width // patches
    start = patch_index * own_width

    def own_cols(values):
        return lax.dynamic_slice_in_dim(values, start, own_width, 1)

    def own_rows(values):
        return lax.dynamic_slice_in_dim(values, start, own_width, 0)

    value_rows = own_rows(value_proj)
    key_query_rows = own_rows(key_query)
    own_query = lax.dynamic_slice_in_dim(agg_query, start, own_width, 0).astype(F32)[:, None]
    if fast:
        arrays = (
            weight_rows,
            var_embed,
            own_cols(weight_rows),
            own_cols(var_embed),
            value_rows,
            jnp.concatenate(split_high_low(key_query_rows), axis=1).T,
            key_proj,
            agg_q[None],
            own_rows(query_proj),
            own_query,
        )

    x_own, shares, mixed_low = front_forward(own_ids, own_field, spread, score_embed, vwt, vet)

    front_out = mm(mixed_low, agg_out) * valid_rows
    normed_one, norm_one_pull = jax.vjp(layer_norm, front_out, norm_one.astype(F32))
    normed_one_low = normed_one.astype(BF16)
    triple = mm(normed_one_low, trunk_qkv).astype(BF16)
    part = width // group
    quarter = hidden // group
    zs = patches // 2
    if fast:
        early = tokens_of_group(jnp.concatenate([out_grad_low, mixed_low, normed_one_low], axis=1))
        qkv, vw, ve, *arrays = together(queries_to_heads(triple), vw, ve, *arrays)
        count = own_count.reshape(1, 1)
        heads, lse = attend_forward(count, qkv, head_dim)
        attended = to_heads(heads.reshape(patches, seg, own_width))
        results = middle(
            place,
            attended,
            front_out,
            valid_rows,
            out_grad_low,
            trunk_out,
            norm_two.astype(F32)[None],
            mlp_in,
            mlp_out,
        )
        attended_group = copies_of_group(attended)
        results = together(*results, *attended_group, *early)
        attended_group, early = results[13:17], results[17:]
        block_out, normed_two_low, grads, after_grad, norm_two_grad = (results[k] for k in (0, 1, 10, 11, 12))
        block_out = block_out[None]
        grads = to_heads(grads)
        active_group, middle_group = slices_of_group(results[2:6]), results[6:10]
        across = swap(normed_two_low, "var", 2)
        result = attend_backward(count, qkv, grads.reshape(patches * seg, own_width), lse, head_dim)
        result, across, *rest = together(result, across, *active_group, *middle_group)
        active_group, middle_group = rest[:4], slices_of_group(rest[4:])
        normed_group = (normed_two_low, swap(normed_two_low, "var", 1), across, swap(across, "var", 1))
        result = to_heads(result)
        pairs = ((1, 3), (0, 2))
        jobs = ((0, 0, 1, 0, width), (2, 0, 4, 0, quarter), (3, 0, 4, quarter, part))
        groups = (active_group, early, normed_group, attended_group, middle_group)
        near, away = weight_grads(place, jobs, groups, own_width, pairs, pairs)
        result = after(result, *near)
        mlp = {"near": near, "away": away}
        mixed_grad, norm_one_grad, *pieces = trunk_back(
            place, result, front_out, norm_one.astype(F32)[None], after_grad, valid_rows, agg_out, trunk_qkv
        )
        mixed_grad, *pieces = together(mixed_grad, *pieces)
        last_group = slices_of_group(pieces)
    else:
        attended, attention_pull = gathered_attention(triple, own_count, head_dim)
        after_attn = front_out + mm(attended, trunk_out)
        normed_two, norm_two_pull = jax.vjp(layer_norm, after_attn, norm_two.astype(F32))
        normed_two_low = normed_two.astype(BF16)
        inner = mm(normed_two_low, mlp_in)
        active, gelu_pull = jax.vjp(gelu_exact, inner)
        active_low = active.astype(BF16)
        result = after_attn + mm(active_low, mlp_out)
        block_out = (result * valid_rows).astype(BF16)[None]
        inner_grad = gelu_pull(mm(out_grad_low, mlp_out, NT))[0].astype(BF16)
        normed_two_grad = mm(inner_grad, mlp_in, NT)
        after_ln_grad, norm_two_grad = norm_two_pull(normed_two_grad)
        after_grad = out_grad + after_ln_grad
        branch_low = after_grad.astype(BF16)
        triple_grad = attention_pull(mm(branch_low, trunk_out, NT).astype(BF16))
        normed_one_grad = mm(triple_grad, trunk_qkv, NT)
        front_ln_grad, norm_one_grad = norm_one_pull(normed_one_grad)
        agg_grad = ((after_grad + front_ln_grad) * valid_rows).astype(BF16)
        mixed_grad = mm(agg_grad, agg_out, NT).astype(BF16)
        norm_one_grad, norm_two_grad = norm_one_grad[None], norm_two_grad[None]

    field_low, *m_parts = front_backward(
        fast, place, own_ids, x_own, shares, mixed_grad, vw, ve, spread, norm_one_grad, norm_two_grad
    )

    field_low = field_low.reshape(group, var_local * pixels, seg)
    field_grad = lax.all_to_all(field_low, "var", split_axis=0, concat_axis=0, tiled=True)

    if fast:
        got = swap(mlp["away"][0], "patch", 1)
        m_stay, m_away, got = together(*m_parts, got)
        m_parts = (m_stay, m_away)
        mlp["far"] = pair_sum(place, mlp["near"][0], (got,))
        last = {}

        def core_done(values):
            return after(values, mlp["far"], *last_group)

        def x_done(values):
            jobs = ((0, 2 * width, 1, 0, 3 * part), (0, width, 1, 3 * part, part))
            last["near"], last["away"] = weight_grads(place, jobs, (early, last_group), own_width, pairs, pairs)
            values, mlp["got"], *_ = together(values, swap(mlp["away"][1], "patch", 1), *last["near"])
            return values

        def y_done(values):
            got, far = swap(last["away"][0], "patch", 1), swap(mlp["far"], "patch", 2)
            values, got, far, _ = together(values, got, far, field_grad)
            mlp["pair"] = z_first_sum(place, mlp["near"][1], (mlp["got"],), far)
            last["far"] = pair_sum(place, last["near"][0], (got,))
            return values

        def z_done(values):
            got = swap(last["away"][1], "patch", 1)
            rest = together(*values, got, last["far"], *mlp["pair"])
            last["got"] = rest[4]
            return rest[:4]

        def b_done(values):
            near, away = mlp["pair"]
            *values, got, far = together(*values, swap(away, "patch", 4), swap(last["far"], "patch", 2))
            mlp["own"] = z_last_sum(place, near, got)
            last["pair"] = z_first_sum(place, last["near"][1], (last["got"],), far)
            return values

        def y_back(values):
            near, away = last["pair"]
            values, got, mlp["across"] = together(values, swap(away, "patch", 4), swap(mlp["own"], "var", 2))
            last["own"] = z_last_sum(place, near, got)
            return values

        m_pieces = sum_over_all(place, *m_parts, (core_done, x_done, y_done, z_done, b_done, y_back))
        own, across = mlp["own"], mlp["across"]
        parts = (own, swap(own, "var", 1), across, swap(across, "var", 1))
        mlp_out_grad, mlp_in_grad, trunk_out_grad = join(place, parts, (width, quarter, part), 1)
        mlp_out_grad = mlp_out_grad.reshape(hidden // patches, width)
        trunk_qkv_grad, agg_out_grad = join(place, gather_over_var(last["own"]), (3 * part, part), 0)
    else:

        def slices(values):
            values = values.reshape(seg, group, values.shape[1] // group).transpose(1, 0, 2)
            return lax.all_to_all(values, "var", split_axis=0, concat_axis=0, tiled=True)

        def everyone(values):
            return lax.all_gather(values, "var", axis=0, tiled=True)

        def total(left, right):
            value = mm(left.reshape(-1, left.shape[-1]), right.reshape(-1, right.shape[-1]), TN).astype(BF16)
            value = lax.psum_scatter(value, "patch", scatter_dimension=0, tiled=True)
            return lax.all_gather(value, "var", axis=0)

        def joined(value):
            return value.transpose(1, 0, 2).reshape(value.shape[1], -1).astype(F32)

        size = hidden // (patches * group)
        active_rows = active_low.reshape(seg, patches, group, size).transpose(0, 2, 1, 3).reshape(seg, hidden)
        mlp_out_grad = total(slices(active_rows), everyone(out_grad_low)).reshape(hidden // patches, width).astype(F32)
        mlp_in_grad = joined(total(everyone(normed_two_low), slices(inner_grad)))
        trunk_out_grad = joined(total(everyone(attended), slices(branch_low)))
        trunk_qkv_grad = joined(total(everyone(normed_one_low), slices(triple_grad)))
        agg_out_grad = joined(total(everyone(mixed_low), slices(agg_grad)))
        m_all = lax.psum(m_parts[0], ("patch", "var")).transpose(1, 0, 2).reshape(-1, width)
    if fast:
        value_proj_grad, patch_grad, embed_grad, key_proj_grad, query_proj_grad, *lines = front_last(
            place, m_pieces, arrays
        )
        agg_query_grad, norm_one_grad, norm_two_grad = (line[0] for line in lines)
    else:
        m_sum, me_sum = m_all[: VARS * pixels], m_all[VARS * pixels : VARS * pixels + VARS]
        s_rows = m_all[VARS * pixels + VARS :].astype(F32)
        s_all = s_rows[:, : VARS * pixels]
        se_all = s_rows[:, VARS * pixels : VARS * pixels + VARS]
        norm_sums = s_rows[:, width - 2 * head_dim :]
        value_proj_grad = mm(own_cols(weight_rows), m_sum, TN) + mm(own_cols(var_embed), me_sum, TN)
        patch_grad = mm(m_sum, value_rows, NT) + mm(
            s_all, key_query_rows, (((0,), (1,)), ((), ())), precision=HIGHEST
        )
        embed_grad = mm(me_sum, value_rows, NT) + mm(
            se_all, key_query_rows, (((0,), (1,)), ((), ())), precision=HIGHEST
        )
        key_sum = (mm(s_all.astype(BF16), weight_rows) + mm(se_all.astype(BF16), var_embed)) * scaling
        head_rows = jnp.where(in_head.T, agg_q[None, :], 0.0)
        key_proj_grad = mm(own_cols(key_sum), head_rows, TN, precision=HIGHEST)
        crossed = mm(jnp.concatenate(split_high_low(key_sum), axis=0), key_proj)
        crossed = crossed[:HEADS] + crossed[HEADS:]
        aggq_grad = jnp.sum(jnp.where(in_head.T, crossed, 0.0), axis=0)
        query_proj_grad = own_query * aggq_grad[None, :]
        agg_query_grad = jnp.sum(own_rows(query_proj).astype(F32) * aggq_grad[None, :], axis=1)
        norm_one_grad = lax.dynamic_slice_in_dim(norm_sums[:, :head_dim].reshape(width), start, own_width, 0)
        norm_two_grad = lax.dynamic_slice_in_dim(norm_sums[:, head_dim:].reshape(width), start, own_width, 0)
    patch_grad = patch_grad.reshape(VARS, pixels, own_width)
    field_grad = field_grad.reshape(all_rows, var_local, pixels, seg).transpose(0, 3, 1, 2)
    return (
        block_out,
        field_grad,
        patch_grad,
        embed_grad,
        agg_query_grad,
        query_proj_grad,
        key_proj_grad,
        value_proj_grad,
        agg_out_grad,
        norm_one_grad,
        trunk_qkv_grad,
        trunk_out_grad,
        norm_two_grad,
        mlp_in_grad,
        mlp_out_grad,
    )


def solution(mesh):
    whole = P()
    placed = (P(None, "patch", "var", None),) + (whole,) * 15 + (P("var", "patch", None),)
    rows = P("patch", None)
    return jax.shard_map(
        local,
        mesh=mesh,
        in_specs=placed,
        out_specs=(
            P("var", "patch", None),
            P(None, "patch", "var", None),
            P(None, None, "patch"),
            P(None, "patch"),
            P("patch"),
            rows,
            rows,
            rows,
            rows,
            P("patch"),
            rows,
            rows,
            P("patch"),
            rows,
            rows,
        ),
        check_vma=False,
    )
```

```python
import functools
import math

import jax
import jax.numpy as jnp
from jax import lax
from jax.experimental import pallas as pl
from jax.experimental.pallas import tpu as pltpu
from jax.sharding import PartitionSpec as P

HEADS = 16
VARS = 48
EPSILON = 1e-05
MASKED = -1e30
HIGHEST = lax.Precision.HIGHEST
BF16 = jnp.bfloat16
F32 = jnp.float32
NN = (((1,), (0,)), ((), ()))
NT = (((1,), (1,)), ((), ()))
TN = (((0,), (0,)), ((), ()))


def cost(flops):
    return pl.CostEstimate(flops=flops, bytes_accessed=1 << 20, transcendentals=0)


def mm(a, b, dims=NN, precision=None):
    return lax.dot_general(a, b, dims, precision=precision, preferred_element_type=F32)


def layer_norm(values, gain_vec):
    average = jnp.mean(values, axis=-1, keepdims=True)
    center = values - average
    spread = jnp.mean(center * center, axis=-1, keepdims=True)
    return center * lax.rsqrt(spread + EPSILON) * gain_vec


def gelu_exact(values):
    return jax.nn.gelu(values, approximate=False)


def split_high_low(values):
    high = values.astype(BF16)
    return high, (values - high.astype(F32)).astype(BF16)


def front_forward_kernel(
    pixels, ids_ref, field_ref, spread_ref, bias_ref, vwt_ref, vet_ref, x_ref, p_ref, mixed_ref, mt_ref
):
    seg = field_ref.shape[1]
    head_dim = mixed_ref.shape[1] // HEADS
    for slot in range(VARS):
        start = pl.multiple_of(ids_ref[0, slot] * pixels, pixels)
        x_ref[pl.ds(start, pixels), :] = field_ref[slot * pixels : (slot + 1) * pixels, :]
    scores = mm(spread_ref[...], x_ref[...]) + bias_ref[...]
    scores = scores.reshape(HEADS, VARS, seg)
    top = jnp.max(scores, axis=1, keepdims=True)
    exponent = jnp.exp(scores - top)
    total = jnp.sum(exponent, axis=1, keepdims=True)
    p_ref[...] = (exponent * (1.0 / total)).reshape(HEADS * VARS, seg)

    def head(h, carry):
        shares = p_ref[pl.ds(pl.multiple_of(h * VARS, VARS), VARS), :]
        pix = x_ref[...].astype(F32).reshape(VARS, pixels, seg)
        scaled = (pix * shares[:, None, :]).astype(BF16).reshape(VARS * pixels, seg)
        rows = pl.ds(pl.multiple_of(h * head_dim, head_dim), head_dim)
        mt_ref[rows, :] = mm(vwt_ref[rows, :], scaled) + mm(vet_ref[rows, :], shares.astype(BF16))
        return carry

    lax.fori_loop(0, HEADS, head, 0)
    mixed_ref[...] = mt_ref[...].T.astype(BF16)


def front_forward(own_ids, own_field, spread, bias, vwt, vet):
    rows, seg = own_field.shape
    width = vwt.shape[0]
    vmem = pl.BlockSpec(memory_space=pltpu.VMEM)
    return pl.pallas_call(
        functools.partial(front_forward_kernel, rows // VARS),
        out_shape=(
            jax.ShapeDtypeStruct((rows, seg), BF16),
            jax.ShapeDtypeStruct((HEADS * VARS, seg), F32),
            jax.ShapeDtypeStruct((seg, width), BF16),
        ),
        in_specs=[pl.BlockSpec(memory_space=pltpu.SMEM)] + [vmem] * 5,
        out_specs=(vmem,) * 3,
        scratch_shapes=[pltpu.VMEM((width, seg), F32)],
        cost_estimate=cost(60000000000),
        name="front_forward",
    )(own_ids, own_field, spread, bias, vwt, vet)


def front_backward_kernel(
    pixels,
    fast,
    place_ref,
    ids_ref,
    x_ref,
    p_ref,
    mg_ref,
    vw_ref,
    ve_ref,
    spread_ref,
    norm_one_ref,
    norm_two_ref,
    field_ref,
    *rest,
):
    rows, seg = x_ref.shape
    m_refs, (fs_ref, dx_ref, s_ref) = rest[:-3], rest[-3:]
    size = m_refs[0].shape[-1]

    def quarter_of(quarter, store):
        if not fast:
            store(m_refs[0].at[quarter])
            return
        mine = quarter // 2 == place_ref[CORE]
        pl.when(mine)(lambda: store(m_refs[0].at[quarter % 2]))
        pl.when(jnp.logical_not(mine))(lambda: store(m_refs[1].at[quarter % 2]))
    width = mg_ref.shape[1]
    head_dim = width // HEADS
    pair_dim = 2 * head_dim
    lane = lax.broadcasted_iota(jnp.int32, (seg, pair_dim), 1)
    dx_ref[...] = jnp.zeros_like(dx_ref)
    pairs = size // pair_dim

    def pair(q, carry):
        cols = pl.ds(pl.multiple_of(q * pair_dim, pair_dim), pair_dim)
        grad = mg_ref[:, cols]
        none = jnp.zeros_like(grad)
        both = jnp.concatenate(
            [jnp.where(lane < head_dim, grad, none), jnp.where(lane >= head_dim, grad, none)], axis=0
        )
        inner = mm(vw_ref[:, cols], both, NT)
        inner_e = mm(ve_ref[:, cols], both, NT)
        pix = x_ref[...].astype(F32).reshape(VARS, pixels, seg)
        scaled, weights = [], []
        for k in range(2):
            hrows = pl.ds(pl.multiple_of((2 * q + k) * VARS, VARS), VARS)
            shares = p_ref[hrows, :]
            part = inner[:, k * seg : (k + 1) * seg].reshape(VARS, pixels, seg)
            share_grad = jnp.sum(pix * part, axis=1) + inner_e[:, k * seg : (k + 1) * seg]
            delta = jnp.sum(shares * share_grad, axis=0, keepdims=True)
            fs_ref[hrows, :] = shares * (share_grad - delta)
            wide = shares[:, None, :]
            dx_ref[...] += (part * wide).reshape(rows, seg)
            scaled.append((pix * wide).astype(BF16).reshape(rows, seg))
            weights.append(shares.astype(BF16))
        quarter, within = q // pairs, pl.ds(pl.multiple_of(q % pairs * pair_dim, pair_dim), pair_dim)
        m_part = mm(jnp.concatenate(scaled, axis=1), both).astype(BF16)
        me_part = mm(jnp.concatenate(weights, axis=1), both).astype(BF16)

        def store(ref):
            ref[0:rows, within] = m_part
            ref[rows : rows + VARS, within] = me_part

        quarter_of(quarter, store)
        return carry

    lax.fori_loop(0, HEADS // 2, pair, 0)
    score_grad = fs_ref[...]
    low = score_grad.astype(BF16)
    dx = dx_ref[...] + mm(spread_ref[...], low, TN)
    dx_ref[...] = dx
    for slot in range(VARS):
        start = pl.multiple_of(ids_ref[0, slot] * pixels, pixels)
        field_ref[slot * pixels : (slot + 1) * pixels, :] = dx_ref[pl.ds(start, pixels), :].astype(BF16)
    ones = jnp.ones((8, seg), F32)
    s_ref[...] = jnp.zeros_like(s_ref)
    var_row = lax.broadcasted_iota(jnp.int32, (VARS, rows), 0)
    var_col = lax.broadcasted_iota(jnp.int32, (VARS, rows), 1) // pixels
    keep = var_row == var_col
    for h in range(HEADS):
        outer = mm(low[h * VARS : (h + 1) * VARS, :], x_ref[...], NT)
        s_ref[h : h + 1, 0:rows] = jnp.sum(jnp.where(keep, outer, 0.0), axis=0, keepdims=True)
        sums = mm(ones, score_grad[h * VARS : (h + 1) * VARS, :], NT, precision=HIGHEST)
        s_ref[h : h + 1, rows : rows + VARS] = sums[0:1, :]
    for h in range(HEADS):
        for ref, first in ((norm_one_ref, width - pair_dim), (norm_two_ref, width - head_dim)):
            s_ref[h : h + 1, first : first + head_dim] = ref[:, h * head_dim : (h + 1) * head_dim]
    for quarter in range(4):
        part = s_ref[:, quarter * size : (quarter + 1) * size].astype(BF16)

        def store_sums(ref, part=part):
            ref[rows + VARS :, :] = part

        quarter_of(quarter, store_sums)


def front_backward(fast, place, own_ids, x_own, shares, mixed_grad, vw, ve, spread, norm_one, norm_two):
    rows, seg = x_own.shape
    width = mixed_grad.shape[1]
    vmem = pl.BlockSpec(memory_space=pltpu.VMEM)
    smem = pl.BlockSpec(memory_space=pltpu.SMEM)
    tall = rows + VARS + HEADS
    if fast:
        sums = (jax.ShapeDtypeStruct((2, tall, width // 4), BF16),) * 2
    else:
        sums = (jax.ShapeDtypeStruct((4, tall, width // 4), BF16),)
    return pl.pallas_call(
        functools.partial(front_backward_kernel, rows // VARS, fast),
        out_shape=(jax.ShapeDtypeStruct((rows, seg), BF16), *sums),
        in_specs=[smem, smem] + [vmem] * 8,
        out_specs=(vmem,) * (1 + len(sums)),
        scratch_shapes=[
            pltpu.VMEM((HEADS * VARS, seg), F32),
            pltpu.VMEM((rows, seg), F32),
            pltpu.VMEM((HEADS, width), F32),
        ],
        cost_estimate=cost(100000000),
        name="front_backward",
    )(place, own_ids, x_own, shares, mixed_grad, vw, ve, spread, norm_one, norm_two)


def load_parts(ref, part, seg, out_ref):
    for source in range(ref.shape[0]):
        out_ref[source * seg : (source + 1) * seg, :] = ref[source, part * seg : (part + 1) * seg, :]


def attend_forward_kernel(head_dim, block, count_ref, qkv_ref, out_ref, lse_ref, q_ref, k_ref, vt_ref):
    full, width = q_ref.shape
    seg = full // qkv_ref.shape[0]
    scaling = jnp.asarray(1.0 / math.sqrt(head_dim), BF16)
    load_parts(qkv_ref, 2, seg, q_ref)
    vt_ref[...] = q_ref[...].T
    load_parts(qkv_ref, 0, seg, q_ref)
    load_parts(qkv_ref, 1, seg, k_ref)
    count = count_ref[0, 0]
    lane = lax.broadcasted_iota(jnp.int32, (block, width), 1) // head_dim
    row = lax.broadcasted_iota(jnp.int32, (width, block), 0) // head_dim
    valid = lax.broadcasted_iota(jnp.int32, (full, block), 0) < count

    def step(i, carry):
        part = pl.ds(pl.multiple_of(i * block, block), block)
        query = q_ref[part, :]
        total = jnp.zeros((width, block), F32)
        for h in range(width // head_dim):
            own = jnp.where(lane == h, query, jnp.zeros_like(query)) * scaling
            scores = jnp.where(valid, mm(k_ref[...], own, NT), MASKED)
            top = jnp.max(scores, axis=0, keepdims=True)
            exponent = jnp.exp(scores - top)
            denominator = jnp.sum(exponent, axis=0, keepdims=True)
            lse_ref[h : h + 1, part] = top + jnp.log(denominator)
            mixed = mm(vt_ref[...], exponent.astype(BF16)) * (1.0 / denominator)
            total = jnp.where(row == h, mixed, total)
        out_ref[part, :] = total.T.astype(BF16)
        return carry

    lax.fori_loop(0, full // block, step, 0)


def attend_forward(count, qkv, head_dim):
    parts, triple_rows, width = qkv.shape
    full = parts * triple_rows // 3
    vmem = pl.BlockSpec(memory_space=pltpu.VMEM)
    block = min(256, full)
    return pl.pallas_call(
        functools.partial(attend_forward_kernel, head_dim, block),
        out_shape=(
            jax.ShapeDtypeStruct((full, width), BF16),
            jax.ShapeDtypeStruct((width // head_dim, full), F32),
        ),
        in_specs=[pl.BlockSpec(memory_space=pltpu.SMEM), vmem],
        out_specs=(vmem, vmem),
        scratch_shapes=[
            pltpu.VMEM((full, width), BF16),
            pltpu.VMEM((full, width), BF16),
            pltpu.VMEM((width, full), BF16),
        ],
        cost_estimate=cost(60000000000),
        name="attend_forward",
    )(count, qkv)


def attend_backward_kernel(
    head_dim, block, count_ref, qkv_ref, grad_ref, lse_ref, out_ref, q_ref, k_ref, v_ref, kt_ref, dk_ref, dv_ref
):
    full, width = q_ref.shape
    seg = full // qkv_ref.shape[0]
    scaling = 1.0 / math.sqrt(head_dim)
    load_parts(qkv_ref, 0, seg, q_ref)
    load_parts(qkv_ref, 1, seg, k_ref)
    load_parts(qkv_ref, 2, seg, v_ref)
    kt_ref[...] = k_ref[...].T
    dk_ref[...] = jnp.zeros_like(dk_ref)
    dv_ref[...] = jnp.zeros_like(dv_ref)
    count = count_ref[0, 0]
    lane = lax.broadcasted_iota(jnp.int32, (block, width), 1) // head_dim
    row = lax.broadcasted_iota(jnp.int32, (width, block), 0) // head_dim
    valid = lax.broadcasted_iota(jnp.int32, (full, block), 0) < count

    def step(i, carry):
        part = pl.ds(pl.multiple_of(i * block, block), block)
        query = q_ref[part, :]
        grad = grad_ref[part, :]
        total = jnp.zeros((width, block), F32)
        for h in range(width // head_dim):
            own = jnp.where(lane == h, query, jnp.zeros_like(query)) * jnp.asarray(scaling, BF16)
            own_grad = jnp.where(lane == h, grad, jnp.zeros_like(grad))
            scores = jnp.where(valid, mm(k_ref[...], own, NT), MASKED)
            shares = jnp.exp(scores - lse_ref[h : h + 1, part])
            share_grad = mm(v_ref[...], own_grad, NT)
            dot = jnp.sum(shares * share_grad, axis=0, keepdims=True)
            score_grad = (shares * (share_grad - dot)).astype(BF16)
            dv_ref[...] += mm(shares.astype(BF16), own_grad)
            dk_ref[...] += mm(score_grad, own)
            total = jnp.where(row == h, mm(kt_ref[...], score_grad), total)
        turned = (total * scaling).T.astype(BF16)
        for piece in range(block // seg):
            out_ref[i * (block // seg) + piece, 0:seg, :] = turned[piece * seg : (piece + 1) * seg, :]
        return carry

    lax.fori_loop(0, full // block, step, 0)
    for source in range(full // seg):
        rows = slice(source * seg, (source + 1) * seg)
        out_ref[source, seg : 2 * seg, :] = dk_ref[rows, :].astype(BF16)
        out_ref[source, 2 * seg : 3 * seg, :] = dv_ref[rows, :].astype(BF16)


def attend_backward(count, qkv, grad, lse, head_dim):
    parts, triple_rows, width = qkv.shape
    full = parts * triple_rows // 3
    vmem = pl.BlockSpec(memory_space=pltpu.VMEM)
    block = min(256, full)
    return pl.pallas_call(
        functools.partial(attend_backward_kernel, head_dim, block),
        out_shape=jax.ShapeDtypeStruct(qkv.shape, BF16),
        in_specs=[pl.BlockSpec(memory_space=pltpu.SMEM), vmem, vmem, vmem],
        out_specs=vmem,
        scratch_shapes=[pltpu.VMEM((full, width), BF16)] * 3
        + [pltpu.VMEM((width, full), BF16)]
        + [pltpu.VMEM((full, width), F32)] * 2,
        cost_estimate=cost(100000000000),
        name="attend_backward",
    )(count, qkv, grad, lse)


def gathered_attention(triple, count, head_dim):
    seg, triple_width = triple.shape
    width = triple_width // 3
    scaling = 1.0 / math.sqrt(head_dim)
    full = seg * lax.axis_size("patch")
    query = triple[:, :width].reshape(seg, HEADS, head_dim)
    key = lax.all_gather(triple[:, width : 2 * width], "patch", axis=0, tiled=True)
    value = lax.all_gather(triple[:, 2 * width :], "patch", axis=0, tiled=True)
    key = key.reshape(full, HEADS, head_dim)
    value = value.reshape(full, HEADS, head_dim)
    valid = (jnp.arange(full, dtype=jnp.int32) < count)[None, None, :]

    def score():
        raw = jnp.einsum("qhd,khd->hqk", query, key, preferred_element_type=F32) * scaling
        return jnp.where(valid, raw, MASKED)

    masked = score()
    top = jnp.max(masked, axis=-1, keepdims=True)
    exponent = jnp.exp(masked - top)
    denominator = jnp.sum(exponent, axis=-1, keepdims=True)
    shares_low = (exponent / denominator).astype(BF16)
    lse = top + jnp.log(denominator)
    attended = jnp.einsum("hqk,khd->qhd", shares_low, value, preferred_element_type=F32)

    def backward(grad):
        grad = grad.reshape(seg, HEADS, head_dim)
        shares = jnp.exp(score() - lse)
        share_grad = jnp.einsum("qhd,khd->hqk", grad, value, preferred_element_type=F32)
        dot = jnp.sum(shares * share_grad, axis=-1, keepdims=True)
        score_grad = (shares * (share_grad - dot)).astype(BF16)
        q_grad = jnp.einsum("hqk,khd->qhd", score_grad, key, preferred_element_type=F32) * scaling
        v_all = jnp.einsum("hqk,qhd->khd", shares.astype(BF16), grad, preferred_element_type=F32)
        k_all = jnp.einsum("hqk,qhd->khd", score_grad, query, preferred_element_type=F32) * scaling
        k_grad, v_grad = (
            lax.psum_scatter(
                part.reshape(full, width).astype(BF16), "patch", scatter_dimension=0, tiled=True
            )
            for part in (k_all, v_all)
        )
        return jnp.concatenate([q_grad.reshape(seg, width).astype(BF16), k_grad, v_grad], axis=1)

    return attended.reshape(seg, width).astype(BF16), backward


def to_heads(values):
    return lax.all_to_all(values, "patch", split_axis=0, concat_axis=0, tiled=True)


def queries_to_heads(triple):
    seg, triple_width = triple.shape
    parts = lax.axis_size("patch")
    own = triple_width // (3 * parts)
    moved = triple.reshape(seg, 3, parts, own).transpose(2, 1, 0, 3).reshape(parts, 3 * seg, own)
    return to_heads(moved)


def weight_grad_kernel(jobs, near, away, place_ref, *refs):
    split = len(refs) - len(near) - len(away)
    arrays, outs = refs[:split], refs[split:]
    rows = outs[0].shape[1]
    sides = (1 - place_ref[Y],) * len(away) + (place_ref[Y],) * len(near)
    start = 0
    for left, left_start, right, right_start, cols in jobs:
        values = [arrays[4 * right + s][:, pl.ds(right_start, cols)] for s in range(4)]
        values = jnp.concatenate(values, axis=0)
        for out, side, blocks in zip(outs, sides, away + near):
            for slot, k in enumerate(blocks):
                source = 2 * (place_ref[Z] ^ k) + side
                group = arrays[4 * left : 4 * left + 4]
                if len(group[0].shape) == 3:
                    factor = [ref[source] for ref in group]
                else:
                    block = pl.ds(pl.multiple_of(left_start + source * rows, rows), rows)
                    factor = [ref[:, block] for ref in group]
                factor = jnp.concatenate(factor, axis=0)
                out[slot, :, start : start + cols] = mm(factor, values, TN).astype(BF16)
        start += cols


def weight_grads(place, jobs, groups, rows, near, away):
    arrays = [array for group in groups for array in group]
    total = sum(job[-1] for job in jobs)
    shapes = [((len(blocks), rows, total), BF16) for blocks in away + near]
    kernel = functools.partial(weight_grad_kernel, jobs, near, away)
    outs = small_call(kernel, place, arrays, shapes, effort=2000, name="weight_grads")
    return outs[len(away) :], outs[: len(away)]


def swap(values, axis, bit):
    return lax.ppermute(values, axis, [(i, i ^ bit) for i in range(lax.axis_size(axis))])


def together(*values):
    return lax.optimization_barrier(values)


def after(value, *others):
    return lax.optimization_barrier((value, *others))[0]


def small_call(kernel, place, arrays, shapes, scratch=(), effort=200, name="small"):
    vmem = pl.BlockSpec(memory_space=pltpu.VMEM)
    return pl.pallas_call(
        kernel,
        out_shape=tuple(jax.ShapeDtypeStruct(dims, dtype) for dims, dtype in shapes),
        in_specs=[pl.BlockSpec(memory_space=pltpu.SMEM)] + [vmem] * len(arrays),
        out_specs=(vmem,) * len(shapes),
        scratch_shapes=list(scratch),
        cost_estimate=cost(int(effort * 10**9)),
        name=name,
    )(place, *arrays)


ME, CORE, X, Y, Z = range(5)


def tokens_of_group(values):
    across = swap(values, "var", 2)
    return values, swap(values, "var", 1), across, swap(across, "var", 1)


def copies_of_group(values):
    return (values,) + tuple(swap(values, "var", bit) for bit in (1, 2, 3))


def slices_of_group(pieces):
    return (pieces[0],) + tuple(swap(pieces[bit], "var", bit) for bit in (1, 2, 3))


def z_pieces(place, near, got):
    _, rows, cols = near.shape

    def kernel(place_ref, near_ref, got_ref, *outs):
        for bit in range(4):
            block = place_ref[Z] ^ bit
            outs[bit][...] = (near_ref[block].astype(F32) + got_ref[block].astype(F32)).astype(BF16)

    return small_call(kernel, place, (near, got), [((rows, cols), BF16)] * 4, name="z_pieces")


def z_exchange(pieces):
    return (pieces[0],) + tuple(swap(pieces[bit], "patch", 2 * bit) for bit in (1, 2, 3))


def z_sum(place, arrays):

    def kernel(place_ref, first, second, third, fourth, out):
        total = first[...].astype(F32) + second[...].astype(F32) + third[...].astype(F32) + fourth[...].astype(F32)
        out[...] = total.astype(BF16)

    return small_call(kernel, place, arrays, [(arrays[0].shape, BF16)], name="z_sum")[0]


def pair_sum(place, near, got):
    def kernel(place_ref, near_ref, got_ref, out):
        for k in range(2):
            out[k] = (near_ref[k].astype(F32) + got_ref[k].astype(F32)).astype(BF16)

    return small_call(kernel, place, (near, got), [(near.shape, BF16)], name="pair_sum")[0]


def z_first_sum(place, near, got, far):
    first = got.shape[0] - 2

    def kernel(place_ref, near_ref, got_ref, far_ref, stay, away):
        for out, k in ((away, 1), (stay, 0)):
            total = near_ref[k].astype(F32) + got_ref[first + k].astype(F32) + far_ref[k].astype(F32)
            out[...] = total.astype(BF16)

    return small_call(kernel, place, (near, got, far), [(near.shape[1:], BF16)] * 2, name="z_first_sum")


def z_last_sum(place, near, got):
    def kernel(place_ref, near_ref, got_ref, out):
        out[...] = (near_ref[...].astype(F32) + got_ref[...].astype(F32)).astype(BF16)

    return small_call(kernel, place, (near, got), [(near.shape, BF16)], name="z_last_sum")[0]


def gather_over_var(own):
    across = swap(own, "var", 2)
    return own, swap(own, "var", 1), across, swap(across, "var", 1)


def join(place, pieces, widths, stacked):
    rows = pieces[0].shape[0]

    def kernel(place_ref, *refs):
        start = 0
        for k, (out, size) in enumerate(zip(refs[4:], widths)):
            for s in range(4):
                v = place_ref[ME] ^ s
                values = refs[s][:, start : start + size].astype(F32)
                if k < stacked:
                    out[v] = values
                else:
                    out[:, pl.ds(pl.multiple_of(v * size, size), size)] = values
            start += size

    shapes = [((4, rows, size) if k < stacked else (rows, 4 * size), F32) for k, size in enumerate(widths)]
    return small_call(kernel, place, pieces, shapes, name="join")


def sum_over_all(place, stay, away, hooks):
    _, rows, cols = stay.shape
    half = rows // 2
    size = half // 4
    hooks = iter(hooks)

    def core_kernel(place_ref, stay_ref, got_ref, stay_out, away_out):
        for out, which in ((away_out, 1 - place_ref[X]), (stay_out, place_ref[X])):
            out[...] = (stay_ref[which].astype(F32) + got_ref[which].astype(F32)).astype(BF16)

    got = next(hooks)(swap(away, "var", 1))
    stay, away = small_call(core_kernel, place, (stay, got), [((rows, cols), BF16)] * 2, name="core_sum")

    def x_kernel(place_ref, stay_ref, got_ref, stay_out, away_out):
        for out, which in ((away_out, 1 - place_ref[Y]), (stay_out, place_ref[Y])):
            out[...] = (stay_ref[which].astype(F32) + got_ref[which].astype(F32)).astype(BF16)

    got = next(hooks)(swap(away, "var", 2))
    halves = (2, half, cols)
    stay, away = small_call(
        x_kernel, place, (stay.reshape(halves), got.reshape(halves)), [((half, cols), BF16)] * 2, name="x_sum"
    )
    got = next(hooks)(swap(away, "patch", 1))
    pieces = z_exchange(z_pieces(place, stay.reshape(4, size, cols), got.reshape(4, size, cols)))
    kept = z_sum(place, next(hooks)(pieces))

    def z_kernel(place_ref, *refs):
        for s in range(4):
            refs[4][place_ref[Z] ^ s] = refs[s][...]

    arrays = (kept,) + tuple(swap(kept, "patch", 2 * bit) for bit in (1, 2, 3))
    own = small_call(z_kernel, place, next(hooks)(arrays), [((4, size, cols), BF16)], name="z_join")[0]

    def y_kernel(place_ref, own_ref, other_ref, out):
        out[place_ref[Y]] = own_ref[...]
        out[1 - place_ref[Y]] = other_ref[...]

    own = own.reshape(half, cols)
    arrays = (own, next(hooks)(swap(own, "patch", 1)))
    full = small_call(y_kernel, place, arrays, [(halves, BF16)], name="y_join")[0].reshape(rows, cols)

    across = next(hooks)(swap(full, "var", 2))
    return full, swap(full, "var", 1), across, swap(across, "var", 1)


def middle_kernel(
    place_ref,
    att_ref,
    front_ref,
    valid_ref,
    og_ref,
    tout_ref,
    gain_ref,
    win_ref,
    wout_ref,
    block_ref,
    late_ref,
    *refs,
):
    slices = refs[0:4]
    grad_ref, after_ref, gain_grad_ref, residual_ref, unit_ref, rate_ref, acc_ref, back_ref, wide_ref, branch_ref = refs[4:]
    step = pl.program_id(0)
    seg, width = front_ref.shape
    parts = att_ref.shape[0]
    own = width // parts
    me = place_ref[0]
    block = win_ref.shape[1]
    slot = block // 4
    quarter = width // 4
    hidden = slot * pl.num_programs(0)

    @pl.when(step == 0)
    def _():
        for p in range(parts):
            branch_ref[:, p * own : (p + 1) * own] = att_ref[p]
        after = front_ref[...] + mm(branch_ref[...], tout_ref[...])
        residual_ref[...] = after
        center = after - jnp.mean(after, axis=1, keepdims=True)
        rate = lax.rsqrt(jnp.mean(center * center, axis=1, keepdims=True) + EPSILON)
        unit = center * rate
        unit_ref[...] = unit
        rate_ref[...] = rate
        late_ref[...] = (unit * gain_ref[...]).astype(BF16)
        acc_ref[...] = jnp.zeros_like(acc_ref)
        back_ref[...] = jnp.zeros_like(back_ref)

    inner = mm(late_ref[...], win_ref[...])
    cumulative = 0.5 * (1.0 + lax.erf(inner * math.sqrt(0.5)))
    active = (inner * cumulative).astype(BF16)
    acc_ref[...] += mm(active, wout_ref[...])
    slope = cumulative + inner * (jnp.exp(-0.5 * inner * inner) * (1.0 / math.sqrt(2.0 * math.pi)))
    inner_grad = (mm(og_ref[...], wout_ref[...], NT) * slope).astype(BF16)
    back_ref[...] += mm(inner_grad, win_ref[...], NT)
    wide_ref[...] = active
    cols = pl.ds(pl.multiple_of(step * slot, slot), slot)
    for s in range(4):
        slices[s][:, cols] = wide_ref[:, pl.ds(pl.multiple_of((me ^ s) * slot, slot), slot)]
    owner = step * block // hidden
    place = pl.ds(pl.multiple_of(hidden + step * block - owner * hidden, block), block)
    for s in range(4):

        @pl.when((me ^ s) == owner)
        def _(s=s):
            slices[s][:, place] = inner_grad

    @pl.when(step == pl.num_programs(0) - 1)
    def _():
        valid = valid_ref[...]
        block_ref[...] = ((residual_ref[...] + acc_ref[...]) * valid).astype(BF16)
        unit = unit_ref[...]
        back = back_ref[...]
        gain_grad_ref[...] = jnp.sum(back * unit, axis=0, keepdims=True)
        scaled = back * gain_ref[...]
        inside = jnp.mean(scaled * unit, axis=1, keepdims=True)
        total = rate_ref[...] * (scaled - jnp.mean(scaled, axis=1, keepdims=True) - unit * inside)
        total = og_ref[...].astype(F32) + total
        after_ref[...] = total
        branch_ref[...] = total.astype(BF16)
        for s in range(4):
            start = pl.multiple_of((me ^ s) * quarter, quarter)
            slices[s][:, 2 * hidden :] = branch_ref[:, pl.ds(start, quarter)]
        turned = mm(branch_ref[...], tout_ref[...], NT).astype(BF16)
        for p in range(parts):
            grad_ref[p] = turned[:, p * own : (p + 1) * own]


def middle(place, attended, front_out, valid, out_grad, trunk_out, gain, mlp_in, mlp_out):
    seg, width = front_out.shape
    hidden = mlp_in.shape[1]
    parts = attended.shape[0]
    block = hidden // parts
    shape = jax.ShapeDtypeStruct

    def still(*dims):
        return pl.BlockSpec(dims, lambda i: (0,) * len(dims))

    piece = shape((seg, hidden // 2 + width // 4), BF16)
    return pl.pallas_call(
        middle_kernel,
        grid=(parts,),
        out_shape=(
            shape((seg, width), BF16),
            shape((seg, width), BF16),
            *((piece,) * 4),
            shape(attended.shape, BF16),
            shape((seg, width), F32),
            shape((1, width), F32),
        ),
        in_specs=[
            pl.BlockSpec(memory_space=pltpu.SMEM),
            still(*attended.shape),
            still(seg, width),
            still(seg, 1),
            still(seg, width),
            still(width, width),
            still(1, width),
            pl.BlockSpec((width, block), lambda i: (0, i)),
            pl.BlockSpec((block, width), lambda i: (i, 0)),
        ],
        out_specs=(
            still(seg, width),
            still(seg, width),
            *((still(*piece.shape),) * 4),
            still(*attended.shape),
            still(seg, width),
            still(1, width),
        ),
        scratch_shapes=[
            pltpu.VMEM((seg, width), F32),
            pltpu.VMEM((seg, width), F32),
            pltpu.VMEM((seg, 1), F32),
            pltpu.VMEM((seg, width), F32),
            pltpu.VMEM((seg, width), F32),
            pltpu.VMEM((seg, block), BF16),
            pltpu.VMEM((seg, width), BF16),
        ],
        compiler_params=pltpu.CompilerParams(dimension_semantics=("arbitrary",)),
        cost_estimate=cost(100000000000),
        name="trunk_middle",
    )(place, attended, front_out, valid, out_grad, trunk_out, gain, mlp_in, mlp_out)


def trunk_back_kernel(
    place_ref, grads_ref, front_ref, gain_ref, after_ref, valid_ref, aout_ref, wqkv_ref, mixed_ref, gain_grad_ref, *rest
):
    pieces, triple_ref, back_ref, wide_ref = rest[:4], rest[4], rest[5], rest[6]
    step = pl.program_id(0)
    parts = grads_ref.shape[0]
    seg, width = front_ref.shape
    own = width // parts
    me = place_ref[ME]

    @pl.when(step == 0)
    def _():
        for c in range(3):
            for p in range(parts):
                triple_ref[c, :, p * own : (p + 1) * own] = grads_ref[p, c * seg : (c + 1) * seg, :]
        back_ref[...] = jnp.zeros_like(back_ref)

    back_ref[...] += mm(triple_ref[step], wqkv_ref[...], NT)

    @pl.when(step == pl.num_programs(0) - 1)
    def _():
        front = front_ref[...]
        center = front - jnp.mean(front, axis=1, keepdims=True)
        rate = lax.rsqrt(jnp.mean(center * center, axis=1, keepdims=True) + EPSILON)
        unit = center * rate
        back = back_ref[...]
        gain_grad_ref[...] = jnp.sum(back * unit, axis=0, keepdims=True)
        scaled = back * gain_ref[...]
        inside = jnp.mean(scaled * unit, axis=1, keepdims=True)
        total = rate * (scaled - jnp.mean(scaled, axis=1, keepdims=True) - unit * inside)
        total = ((after_ref[...] + total) * valid_ref[...]).astype(BF16)
        mixed_ref[...] = mm(total, aout_ref[...], NT).astype(BF16)
        wide_ref[...] = total
        part = width // 4
        for s in range(4):
            v = me ^ s
            pieces[s][:, 3 * part :] = wide_ref[:, pl.ds(pl.multiple_of(v * part, part), part)]
            for k in range(3):
                block = 3 * v + k
                cols = pl.ds(pl.multiple_of(block % 4 * part, part), part)
                pieces[s][:, k * part : (k + 1) * part] = triple_ref[block // 4, :, cols]


def trunk_back(place, grads, front_out, gain, after_grad, valid, agg_out, trunk_qkv):
    seg, width = front_out.shape
    shape = jax.ShapeDtypeStruct

    def still(*dims):
        return pl.BlockSpec(dims, lambda i: (0,) * len(dims))

    piece = shape((seg, width), BF16)
    return pl.pallas_call(
        trunk_back_kernel,
        grid=(3,),
        out_shape=(piece, shape((1, width), F32), *((piece,) * 4)),
        in_specs=[
            pl.BlockSpec(memory_space=pltpu.SMEM),
            still(*grads.shape),
            still(seg, width),
            still(1, width),
            still(seg, width),
            still(seg, 1),
            still(width, width),
            pl.BlockSpec((width, width), lambda i: (0, i)),
        ],
        out_specs=(still(seg, width), still(1, width), *((still(seg, width),) * 4)),
        scratch_shapes=[
            pltpu.VMEM((3, seg, width), BF16),
            pltpu.VMEM((seg, width), F32),
            pltpu.VMEM((seg, width), BF16),
        ],
        compiler_params=pltpu.CompilerParams(dimension_semantics=("arbitrary",)),
        cost_estimate=cost(100000000000),
        name="trunk_back",
    )(place, grads, front_out, gain, after_grad, valid, agg_out, trunk_qkv)


def front_last_kernel(
    pixels,
    place_ref,
    m0,
    m1,
    m2,
    m3,
    weight_ref,
    embed_ref,
    weight_own_ref,
    embed_own_ref,
    value_rows_ref,
    key_query_ref,
    key_ref,
    aggq_ref,
    query_rows_ref,
    query_own_ref,
    value_out,
    patch_out,
    embed_out,
    key_out,
    query_out,
    agg_query_out,
    norm_one_out,
    norm_two_out,
    m_ref,
    sum_ref,
):
    rows, width = weight_ref.shape
    own = weight_own_ref.shape[1]
    size = m0.shape[1]
    head_dim = width // HEADS
    scaling = 1.0 / math.sqrt(head_dim)
    for s, ref in enumerate((m0, m1, m2, m3)):
        v = place_ref[ME] ^ s
        m_ref[:, pl.ds(pl.multiple_of((v % 2 * 2 + v // 2) * size, size), size)] = ref[...]
    m_sum, me_sum = m_ref[0:rows, :], m_ref[rows : rows + VARS, :]
    value_out[...] = mm(weight_own_ref[...], m_sum, TN) + mm(embed_own_ref[...], me_sum, TN)
    s_all = m_ref[rows + VARS : rows + VARS + HEADS, :]
    twice = jnp.concatenate([s_all, s_all], axis=0)
    patch_out[...] = mm(m_sum, value_rows_ref[...], NT) + mm(twice[:, 0:rows], key_query_ref[...], TN)
    embed_out[...] = mm(me_sum, value_rows_ref[...], NT) + mm(
        twice[:, rows : rows + VARS], key_query_ref[...], TN
    )
    key_sum = (mm(s_all[:, 0:rows], weight_ref[...]) + mm(s_all[:, rows : rows + VARS], embed_ref[...])) * scaling
    sum_ref[...] = key_sum
    lane = lax.broadcasted_iota(jnp.int32, (HEADS, width), 1) // head_dim
    mine = lane == lax.broadcasted_iota(jnp.int32, (HEADS, width), 0)
    start = pl.multiple_of((place_ref[Z] * 2 + place_ref[Y]) * own, own)
    head_rows = jnp.where(mine, aggq_ref[...], 0.0)
    key_out[...] = mm(sum_ref[:, pl.ds(start, own)], head_rows, TN, precision=HIGHEST)
    crossed = mm(jnp.concatenate(split_high_low(key_sum), axis=0), key_ref[...])
    crossed = crossed[0:HEADS, :] + crossed[HEADS:, :]
    aggq_grad = jnp.sum(jnp.where(mine, crossed, 0.0), axis=0, keepdims=True)
    query_out[...] = query_own_ref[...] * aggq_grad
    high, low = split_high_low(aggq_grad)
    agg_query_out[...] = mm(high, query_rows_ref[...], NT) + mm(low, query_rows_ref[...], NT)
    row = lax.broadcasted_iota(jnp.int32, (HEADS, own), 0)
    tail = s_all[:, width - own :].astype(F32)
    for k in range(own // head_dim):
        line = jnp.sum(jnp.where(row == start // head_dim + k, tail, 0.0), axis=0, keepdims=True)
        norm_one_out[:, k * head_dim : (k + 1) * head_dim] = line[:, 0:head_dim]
        norm_two_out[:, k * head_dim : (k + 1) * head_dim] = line[:, head_dim:own]


def front_last(place, pieces, arrays):
    weight_rows, own_weight, value_rows = arrays[0], arrays[2], arrays[4]
    rows, width = weight_rows.shape
    own = own_weight.shape[1]
    tall = pieces[0].shape[0]
    shapes = [((own, width), F32), ((rows, own), F32), ((VARS, own), F32)] + [((own, width), F32)] * 2
    shapes += [((1, own), F32)] * 3
    return small_call(
        functools.partial(front_last_kernel, rows // VARS),
        place,
        (*pieces, *arrays),
        shapes,
        scratch=[pltpu.VMEM((tall, width), BF16), pltpu.VMEM((HEADS, width), F32)],
        name="front_last",
    )


def local(
    input_field,
    counts,
    var_ids,
    patch_weight,
    var_embed,
    agg_query,
    query_proj,
    key_proj,
    value_proj,
    agg_out,
    norm_one,
    trunk_qkv,
    trunk_out,
    norm_two,
    mlp_in,
    mlp_out,
    cotangent,
):
    patches, group = lax.axis_size("patch"), lax.axis_size("var")
    fast = (patches, group) == (8, 4)
    me, spot = lax.axis_index("var"), lax.axis_index("patch")
    place = jnp.stack([me, me % 2, me // 2, spot % 2, spot // 2]).astype(jnp.int32)
    var_index = lax.axis_index("var")
    patch_index = lax.axis_index("patch")
    all_rows, seg, var_local, pixels = input_field.shape
    width = agg_out.shape[0]
    head_dim = width // HEADS
    hidden = mlp_in.shape[1]
    scaling = 1.0 / math.sqrt(head_dim)

    turned = input_field.transpose(0, 2, 3, 1).reshape(all_rows, var_local * pixels, seg)
    own_field = lax.all_to_all(turned, "var", split_axis=0, concat_axis=1, tiled=True)
    own_field = own_field.reshape(VARS * pixels, seg)
    own_ids = lax.dynamic_slice_in_dim(var_ids, var_index, 1, 0)
    own_count = lax.dynamic_slice_in_dim(counts, var_index, 1, 0)
    positions = patch_index * seg + jnp.arange(seg, dtype=jnp.int32)
    valid_rows = (positions < own_count).astype(F32)[:, None]
    out_grad = cotangent.reshape(seg, width).astype(F32) * valid_rows
    out_grad_low = out_grad.astype(BF16)

    weight_rows = patch_weight.reshape(VARS * pixels, width)
    agg_q = mm(agg_query[None], query_proj)[0]
    in_head = jnp.arange(width, dtype=jnp.int32)[:, None] // head_dim == jnp.arange(HEADS)[None, :]
    head_query = jnp.where(in_head, agg_q[:, None] * scaling, 0.0)
    key_query = mm(key_proj, jnp.concatenate(split_high_low(head_query), axis=1))
    key_query = key_query[:, :HEADS] + key_query[:, HEADS:]
    key_query_parts = jnp.concatenate(split_high_low(key_query), axis=1)
    score_weight = mm(key_query_parts, weight_rows, (((0,), (1,)), ((), ())))
    score_weight = score_weight[:HEADS] + score_weight[HEADS:]
    score_embed = mm(key_query_parts, var_embed, (((0,), (1,)), ((), ())))
    score_embed = (score_embed[:HEADS] + score_embed[HEADS:]).reshape(HEADS * VARS, 1)
    same_var = (jnp.arange(VARS)[:, None] == jnp.arange(VARS * pixels)[None, :] // pixels)[None]
    spread = jnp.where(same_var, score_weight[:, None, :], 0.0).astype(BF16)
    spread = spread.reshape(HEADS * VARS, VARS * pixels)
    vwt = mm(value_proj, weight_rows, (((0,), (1,)), ((), ()))).astype(BF16)
    vet = mm(value_proj, var_embed, (((0,), (1,)), ((), ()))).astype(BF16)

    own_width = width // patches
    start = patch_index * own_width

    def own_cols(values):
        return lax.dynamic_slice_in_dim(values, start, own_width, 1)

    def own_rows(values):
        return lax.dynamic_slice_in_dim(values, start, own_width, 0)

    def own_query(values):
        return lax.dynamic_slice_in_dim(values, start, own_width, 0).astype(F32)[:, None]

    def last_operands(ready):
        weights, embeds, values, queries, line, key_queries, _ = together(
            weight_rows, var_embed, value_proj, query_proj, agg_query, key_query, ready
        )
        return (
            weights,
            embeds,
            own_cols(weights),
            own_cols(embeds),
            own_rows(values),
            jnp.concatenate(split_high_low(own_rows(key_queries)), axis=1).T,
            key_proj,
            agg_q[None],
            own_rows(queries),
            own_query(line),
        )

    x_own, shares, mixed_low = front_forward(own_ids, own_field, spread, score_embed, vwt, vet)

    front_out = mm(mixed_low, agg_out) * valid_rows
    normed_one, norm_one_pull = jax.vjp(layer_norm, front_out, norm_one.astype(F32))
    normed_one_low = normed_one.astype(BF16)
    triple = mm(normed_one_low, trunk_qkv).astype(BF16)
    part = width // group
    quarter = hidden // group
    zs = patches // 2
    ready = after(value_proj, triple)
    vw = mm(weight_rows, ready).astype(BF16)
    ve = mm(var_embed, ready).astype(BF16)
    if fast:
        early = tokens_of_group(jnp.concatenate([out_grad_low, mixed_low, normed_one_low], axis=1))
        qkv, vw, ve, *arrays = together(queries_to_heads(triple), vw, ve, *last_operands(triple))
        count = own_count.reshape(1, 1)
        heads, lse = attend_forward(count, qkv, head_dim)
        attended = to_heads(heads.reshape(patches, seg, own_width))
        results = middle(
            place,
            attended,
            front_out,
            valid_rows,
            out_grad_low,
            trunk_out,
            norm_two.astype(F32)[None],
            mlp_in,
            mlp_out,
        )
        attended_group = copies_of_group(attended)
        results = together(*results, *attended_group, *early)
        attended_group, early = results[9:13], results[13:]
        block_out, normed_two_low, grads, after_grad, norm_two_grad = (results[k] for k in (0, 1, 6, 7, 8))
        block_out = block_out[None]
        grads = to_heads(grads)
        mlp_group = slices_of_group(results[2:6])
        across = swap(normed_two_low, "var", 2)
        result = attend_backward(count, qkv, grads.reshape(patches * seg, own_width), lse, head_dim)
        result, across = together(result, across)
        normed_group = (normed_two_low, swap(normed_two_low, "var", 1), across, swap(across, "var", 1))
        result = to_heads(result)
        pairs = ((1, 3), (0, 2))
        jobs = ((0, 0, 1, 0, width), (2, 0, 0, quarter, quarter), (3, 0, 0, 2 * quarter, part))
        groups = (mlp_group, early, normed_group, attended_group)
        _, away = weight_grads(place, jobs, groups, own_width, (), pairs[:1])
        held = together(away[0], *groups[0])
        near, more = weight_grads(place, jobs, (held[1:], *groups[1:]), own_width, pairs, pairs[1:])
        away = (*away, *more)
        result = after(result, *near)
        mlp = {"near": near, "away": away}
        mixed_grad, norm_one_grad, *pieces = trunk_back(
            place, result, front_out, norm_one.astype(F32)[None], after_grad, valid_rows, agg_out, trunk_qkv
        )
        mixed_grad, *pieces = together(mixed_grad, *pieces)
        last_group = slices_of_group(pieces)
    else:
        attended, attention_pull = gathered_attention(triple, own_count, head_dim)
        after_attn = front_out + mm(attended, trunk_out)
        normed_two, norm_two_pull = jax.vjp(layer_norm, after_attn, norm_two.astype(F32))
        normed_two_low = normed_two.astype(BF16)
        inner = mm(normed_two_low, mlp_in)
        active, gelu_pull = jax.vjp(gelu_exact, inner)
        active_low = active.astype(BF16)
        result = after_attn + mm(active_low, mlp_out)
        block_out = (result * valid_rows).astype(BF16)[None]
        inner_grad = gelu_pull(mm(out_grad_low, mlp_out, NT))[0].astype(BF16)
        normed_two_grad = mm(inner_grad, mlp_in, NT)
        after_ln_grad, norm_two_grad = norm_two_pull(normed_two_grad)
        after_grad = out_grad + after_ln_grad
        branch_low = after_grad.astype(BF16)
        triple_grad = attention_pull(mm(branch_low, trunk_out, NT).astype(BF16))
        normed_one_grad = mm(triple_grad, trunk_qkv, NT)
        front_ln_grad, norm_one_grad = norm_one_pull(normed_one_grad)
        agg_grad = ((after_grad + front_ln_grad) * valid_rows).astype(BF16)
        mixed_grad = mm(agg_grad, agg_out, NT).astype(BF16)
        norm_one_grad, norm_two_grad = norm_one_grad[None], norm_two_grad[None]

    field_low, *m_parts = front_backward(
        fast, place, own_ids, x_own, shares, mixed_grad, vw, ve, spread, norm_one_grad, norm_two_grad
    )

    field_low = field_low.reshape(group, var_local * pixels, seg)
    field_grad = lax.all_to_all(field_low, "var", split_axis=0, concat_axis=0, tiled=True)

    if fast:
        got = swap(mlp["away"][0], "patch", 1)
        m_stay, m_away, got = together(*m_parts, got)
        m_parts = (m_stay, m_away)
        mlp["first"] = got
        mlp["far"] = pair_sum(place, mlp["near"][0], got)
        last = {}

        def core_done(values):
            return values

        def x_done(values):
            jobs = ((0, 2 * width, 1, 0, 3 * part), (0, width, 1, 3 * part, part))
            groups = (early, last_group)
            last["near"], last["away"] = weight_grads(place, jobs, groups, own_width, pairs, ((1, 3, 0, 2),))
            return after(values, mlp["far"], field_grad, *last["near"])

        def y_done(values):
            got = swap(after(mlp["away"][1], mlp["first"]), "patch", 1)
            values, got, far = together(values, got, swap(mlp["far"], "patch", 2))
            mlp["pair"] = z_first_sum(place, mlp["near"][1], got, far)
            return after(values, mlp["pair"][0])

        def z_done(values):
            *values, last["got"] = together(*values, swap(last["away"][0], "patch", 1))
            last["far"] = pair_sum(place, last["near"][0], last["got"])
            return [after(values[0], last["far"]), *values[1:]]

        def b_done(values):
            near, away = mlp["pair"]
            *values, got = together(*values, swap(away, "patch", 4))
            mlp["own"] = z_last_sum(place, near, got)
            return values

        def y_back(values):
            return values

        def var_done(values):
            far, across = swap(last["far"], "patch", 2), swap(mlp["own"], "var", 2)
            near, away = z_first_sum(place, last["near"][1], last["got"], far)
            values, got, across = together(values, swap(away, "patch", 4), across)
            mlp["parts"] = (mlp["own"], swap(mlp["own"], "var", 1), across, swap(across, "var", 1))
            last["own"] = z_last_sum(place, near, got)
            return values

        m_pieces = sum_over_all(place, *m_parts, (core_done, x_done, y_done, z_done, b_done, y_back, var_done))
        mlp_out_grad, mlp_in_grad, trunk_out_grad = join(place, mlp["parts"], (width, quarter, part), 1)
        mlp_out_grad = mlp_out_grad.reshape(hidden // patches, width)
        trunk_qkv_grad, agg_out_grad = join(place, gather_over_var(last["own"]), (3 * part, part), 0)
    else:

        def slices(values):
            values = values.reshape(seg, group, values.shape[1] // group).transpose(1, 0, 2)
            return lax.all_to_all(values, "var", split_axis=0, concat_axis=0, tiled=True)

        def everyone(values):
            return lax.all_gather(values, "var", axis=0, tiled=True)

        def total(left, right):
            value = mm(left.reshape(-1, left.shape[-1]), right.reshape(-1, right.shape[-1]), TN).astype(BF16)
            value = lax.psum_scatter(value, "patch", scatter_dimension=0, tiled=True)
            return lax.all_gather(value, "var", axis=0)

        def joined(value):
            return value.transpose(1, 0, 2).reshape(value.shape[1], -1).astype(F32)

        size = hidden // (patches * group)
        active_rows = active_low.reshape(seg, patches, group, size).transpose(0, 2, 1, 3).reshape(seg, hidden)
        mlp_out_grad = total(slices(active_rows), everyone(out_grad_low)).reshape(hidden // patches, width).astype(F32)
        mlp_in_grad = joined(total(everyone(normed_two_low), slices(inner_grad)))
        trunk_out_grad = joined(total(everyone(attended), slices(branch_low)))
        trunk_qkv_grad = joined(total(everyone(normed_one_low), slices(triple_grad)))
        agg_out_grad = joined(total(everyone(mixed_low), slices(agg_grad)))
        m_all = lax.psum(m_parts[0], ("patch", "var")).transpose(1, 0, 2).reshape(-1, width)
    if fast:
        value_proj_grad, patch_grad, embed_grad, key_proj_grad, query_proj_grad, *lines = front_last(
            place, m_pieces, arrays
        )
        agg_query_grad, norm_one_grad, norm_two_grad = (line[0] for line in lines)
    else:
        value_rows, key_query_rows = own_rows(value_proj), own_rows(key_query)
        m_sum, me_sum = m_all[: VARS * pixels], m_all[VARS * pixels : VARS * pixels + VARS]
        s_rows = m_all[VARS * pixels + VARS :].astype(F32)
        s_all = s_rows[:, : VARS * pixels]
        se_all = s_rows[:, VARS * pixels : VARS * pixels + VARS]
        norm_sums = s_rows[:, width - 2 * head_dim :]
        value_proj_grad = mm(own_cols(weight_rows), m_sum, TN) + mm(own_cols(var_embed), me_sum, TN)
        patch_grad = mm(m_sum, value_rows, NT) + mm(
            s_all, key_query_rows, (((0,), (1,)), ((), ())), precision=HIGHEST
        )
        embed_grad = mm(me_sum, value_rows, NT) + mm(
            se_all, key_query_rows, (((0,), (1,)), ((), ())), precision=HIGHEST
        )
        key_sum = (mm(s_all.astype(BF16), weight_rows) + mm(se_all.astype(BF16), var_embed)) * scaling
        head_rows = jnp.where(in_head.T, agg_q[None, :], 0.0)
        key_proj_grad = mm(own_cols(key_sum), head_rows, TN, precision=HIGHEST)
        crossed = mm(jnp.concatenate(split_high_low(key_sum), axis=0), key_proj)
        crossed = crossed[:HEADS] + crossed[HEADS:]
        aggq_grad = jnp.sum(jnp.where(in_head.T, crossed, 0.0), axis=0)
        query_proj_grad = own_query(agg_query) * aggq_grad[None, :]
        agg_query_grad = jnp.sum(own_rows(query_proj).astype(F32) * aggq_grad[None, :], axis=1)
        norm_one_grad = lax.dynamic_slice_in_dim(norm_sums[:, :head_dim].reshape(width), start, own_width, 0)
        norm_two_grad = lax.dynamic_slice_in_dim(norm_sums[:, head_dim:].reshape(width), start, own_width, 0)
    patch_grad = patch_grad.reshape(VARS, pixels, own_width)
    field_grad = field_grad.reshape(all_rows, var_local, pixels, seg).transpose(0, 3, 1, 2)
    return (
        block_out,
        field_grad,
        patch_grad,
        embed_grad,
        agg_query_grad,
        query_proj_grad,
        key_proj_grad,
        value_proj_grad,
        agg_out_grad,
        norm_one_grad,
        trunk_qkv_grad,
        trunk_out_grad,
        norm_two_grad,
        mlp_in_grad,
        mlp_out_grad,
    )


def solution(mesh):
    whole = P()
    placed = (P(None, "patch", "var", None),) + (whole,) * 15 + (P("var", "patch", None),)
    rows = P("patch", None)
    return jax.shard_map(
        local,
        mesh=mesh,
        in_specs=placed,
        out_specs=(
            P("var", "patch", None),
            P(None, "patch", "var", None),
            P(None, None, "patch"),
            P(None, "patch"),
            P("patch"),
            rows,
            rows,
            rows,
            rows,
            P("patch"),
            rows,
            rows,
            P("patch"),
            rows,
            rows,
        ),
        check_vma=False,
    )
```

```python
import functools
import math

import jax
import jax.numpy as jnp
from jax import lax
from jax.experimental import pallas as pl
from jax.experimental.pallas import tpu as pltpu
from jax.sharding import PartitionSpec as P

HEADS = 16
VARS = 48
EPSILON = 1e-05
MASKED = -1e30
HIGHEST = lax.Precision.HIGHEST
BF16 = jnp.bfloat16
F32 = jnp.float32
NN = (((1,), (0,)), ((), ()))
NT = (((1,), (1,)), ((), ()))
TN = (((0,), (0,)), ((), ()))


def cost(flops):
    return pl.CostEstimate(flops=flops, bytes_accessed=1 << 20, transcendentals=0)


def mm(a, b, dims=NN, precision=None):
    return lax.dot_general(a, b, dims, precision=precision, preferred_element_type=F32)


def layer_norm(values, gain_vec):
    average = jnp.mean(values, axis=-1, keepdims=True)
    center = values - average
    spread = jnp.mean(center * center, axis=-1, keepdims=True)
    return center * lax.rsqrt(spread + EPSILON) * gain_vec


def gelu_exact(values):
    return jax.nn.gelu(values, approximate=False)


def split_high_low(values):
    high = values.astype(BF16)
    return high, (values - high.astype(F32)).astype(BF16)


def front_forward_kernel(
    pixels, ids_ref, field_ref, spread_ref, bias_ref, vwt_ref, vet_ref, x_ref, p_ref, mixed_ref, mt_ref
):
    seg = field_ref.shape[1]
    head_dim = mixed_ref.shape[1] // HEADS
    for slot in range(VARS):
        start = pl.multiple_of(ids_ref[0, slot] * pixels, pixels)
        x_ref[pl.ds(start, pixels), :] = field_ref[slot * pixels : (slot + 1) * pixels, :]
    scores = mm(spread_ref[...], x_ref[...]) + bias_ref[...]
    scores = scores.reshape(HEADS, VARS, seg)
    top = jnp.max(scores, axis=1, keepdims=True)
    exponent = jnp.exp(scores - top)
    total = jnp.sum(exponent, axis=1, keepdims=True)
    p_ref[...] = (exponent * (1.0 / total)).reshape(HEADS * VARS, seg)

    def head(h, carry):
        shares = p_ref[pl.ds(pl.multiple_of(h * VARS, VARS), VARS), :]
        pix = x_ref[...].astype(F32).reshape(VARS, pixels, seg)
        scaled = (pix * shares[:, None, :]).astype(BF16).reshape(VARS * pixels, seg)
        rows = pl.ds(pl.multiple_of(h * head_dim, head_dim), head_dim)
        mt_ref[rows, :] = mm(vwt_ref[rows, :], scaled) + mm(vet_ref[rows, :], shares.astype(BF16))
        return carry

    lax.fori_loop(0, HEADS, head, 0)
    mixed_ref[...] = mt_ref[...].T.astype(BF16)


def front_forward(own_ids, own_field, spread, bias, vwt, vet):
    rows, seg = own_field.shape
    width = vwt.shape[0]
    vmem = pl.BlockSpec(memory_space=pltpu.VMEM)
    return pl.pallas_call(
        functools.partial(front_forward_kernel, rows // VARS),
        out_shape=(
            jax.ShapeDtypeStruct((rows, seg), BF16),
            jax.ShapeDtypeStruct((HEADS * VARS, seg), F32),
            jax.ShapeDtypeStruct((seg, width), BF16),
        ),
        in_specs=[pl.BlockSpec(memory_space=pltpu.SMEM)] + [vmem] * 5,
        out_specs=(vmem,) * 3,
        scratch_shapes=[pltpu.VMEM((width, seg), F32)],
        cost_estimate=cost(60000000000),
        name="front_forward",
    )(own_ids, own_field, spread, bias, vwt, vet)


def front_backward_kernel(
    pixels,
    fast,
    place_ref,
    ids_ref,
    x_ref,
    p_ref,
    mg_ref,
    vw_ref,
    ve_ref,
    spread_ref,
    norm_one_ref,
    norm_two_ref,
    field_ref,
    *rest,
):
    rows, seg = x_ref.shape
    m_refs, (fs_ref, dx_ref, s_ref) = rest[:-3], rest[-3:]
    size = m_refs[0].shape[-1]

    def quarter_of(quarter, store):
        if not fast:
            store(m_refs[0].at[quarter])
            return
        mine = quarter // 2 == place_ref[CORE]
        pl.when(mine)(lambda: store(m_refs[0].at[quarter % 2]))
        pl.when(jnp.logical_not(mine))(lambda: store(m_refs[1].at[quarter % 2]))
    width = mg_ref.shape[1]
    head_dim = width // HEADS
    pair_dim = 2 * head_dim
    lane = lax.broadcasted_iota(jnp.int32, (seg, pair_dim), 1)
    dx_ref[...] = jnp.zeros_like(dx_ref)
    pairs = size // pair_dim

    def pair(q, carry):
        cols = pl.ds(pl.multiple_of(q * pair_dim, pair_dim), pair_dim)
        grad = mg_ref[:, cols]
        none = jnp.zeros_like(grad)
        both = jnp.concatenate(
            [jnp.where(lane < head_dim, grad, none), jnp.where(lane >= head_dim, grad, none)], axis=0
        )
        inner = mm(vw_ref[:, cols], both, NT)
        inner_e = mm(ve_ref[:, cols], both, NT)
        pix = x_ref[...].astype(F32).reshape(VARS, pixels, seg)
        scaled, weights = [], []
        for k in range(2):
            hrows = pl.ds(pl.multiple_of((2 * q + k) * VARS, VARS), VARS)
            shares = p_ref[hrows, :]
            part = inner[:, k * seg : (k + 1) * seg].reshape(VARS, pixels, seg)
            share_grad = jnp.sum(pix * part, axis=1) + inner_e[:, k * seg : (k + 1) * seg]
            delta = jnp.sum(shares * share_grad, axis=0, keepdims=True)
            fs_ref[hrows, :] = shares * (share_grad - delta)
            wide = shares[:, None, :]
            dx_ref[...] += (part * wide).reshape(rows, seg)
            scaled.append((pix * wide).astype(BF16).reshape(rows, seg))
            weights.append(shares.astype(BF16))
        quarter, within = q // pairs, pl.ds(pl.multiple_of(q % pairs * pair_dim, pair_dim), pair_dim)
        m_part = mm(jnp.concatenate(scaled, axis=1), both).astype(BF16)
        me_part = mm(jnp.concatenate(weights, axis=1), both).astype(BF16)

        def store(ref):
            ref[0:rows, within] = m_part
            ref[rows : rows + VARS, within] = me_part

        quarter_of(quarter, store)
        return carry

    lax.fori_loop(0, HEADS // 2, pair, 0)
    score_grad = fs_ref[...]
    low = score_grad.astype(BF16)
    dx = dx_ref[...] + mm(spread_ref[...], low, TN)
    dx_ref[...] = dx
    for slot in range(VARS):
        start = pl.multiple_of(ids_ref[0, slot] * pixels, pixels)
        field_ref[slot * pixels : (slot + 1) * pixels, :] = dx_ref[pl.ds(start, pixels), :].astype(BF16)
    ones = jnp.ones((8, seg), F32)
    s_ref[...] = jnp.zeros_like(s_ref)
    var_row = lax.broadcasted_iota(jnp.int32, (VARS, rows), 0)
    var_col = lax.broadcasted_iota(jnp.int32, (VARS, rows), 1) // pixels
    keep = var_row == var_col
    for h in range(HEADS):
        outer = mm(low[h * VARS : (h + 1) * VARS, :], x_ref[...], NT)
        s_ref[h : h + 1, 0:rows] = jnp.sum(jnp.where(keep, outer, 0.0), axis=0, keepdims=True)
        sums = mm(ones, score_grad[h * VARS : (h + 1) * VARS, :], NT, precision=HIGHEST)
        s_ref[h : h + 1, rows : rows + VARS] = sums[0:1, :]
    for h in range(HEADS):
        for ref, first in ((norm_one_ref, width - pair_dim), (norm_two_ref, width - head_dim)):
            s_ref[h : h + 1, first : first + head_dim] = ref[:, h * head_dim : (h + 1) * head_dim]
    for quarter in range(4):
        part = s_ref[:, quarter * size : (quarter + 1) * size].astype(BF16)

        def store_sums(ref, part=part):
            ref[rows + VARS :, :] = part

        quarter_of(quarter, store_sums)


def front_backward(fast, place, own_ids, x_own, shares, mixed_grad, vw, ve, spread, norm_one, norm_two):
    rows, seg = x_own.shape
    width = mixed_grad.shape[1]
    vmem = pl.BlockSpec(memory_space=pltpu.VMEM)
    smem = pl.BlockSpec(memory_space=pltpu.SMEM)
    tall = rows + VARS + HEADS
    if fast:
        sums = (jax.ShapeDtypeStruct((2, tall, width // 4), BF16),) * 2
    else:
        sums = (jax.ShapeDtypeStruct((4, tall, width // 4), BF16),)
    return pl.pallas_call(
        functools.partial(front_backward_kernel, rows // VARS, fast),
        out_shape=(jax.ShapeDtypeStruct((rows, seg), BF16), *sums),
        in_specs=[smem, smem] + [vmem] * 8,
        out_specs=(vmem,) * (1 + len(sums)),
        scratch_shapes=[
            pltpu.VMEM((HEADS * VARS, seg), F32),
            pltpu.VMEM((rows, seg), F32),
            pltpu.VMEM((HEADS, width), F32),
        ],
        cost_estimate=cost(100000000),
        name="front_backward",
    )(place, own_ids, x_own, shares, mixed_grad, vw, ve, spread, norm_one, norm_two)


def load_parts(ref, part, seg, out_ref):
    for source in range(ref.shape[0]):
        out_ref[source * seg : (source + 1) * seg, :] = ref[source, part * seg : (part + 1) * seg, :]


def attend_forward_kernel(head_dim, block, count_ref, qkv_ref, out_ref, lse_ref, q_ref, k_ref, vt_ref):
    full, width = q_ref.shape
    seg = full // qkv_ref.shape[0]
    scaling = jnp.asarray(1.0 / math.sqrt(head_dim), BF16)
    load_parts(qkv_ref, 2, seg, q_ref)
    vt_ref[...] = q_ref[...].T
    load_parts(qkv_ref, 0, seg, q_ref)
    load_parts(qkv_ref, 1, seg, k_ref)
    count = count_ref[0, 0]
    lane = lax.broadcasted_iota(jnp.int32, (block, width), 1) // head_dim
    row = lax.broadcasted_iota(jnp.int32, (width, block), 0) // head_dim
    valid = lax.broadcasted_iota(jnp.int32, (full, block), 0) < count

    def step(i, carry):
        part = pl.ds(pl.multiple_of(i * block, block), block)
        query = q_ref[part, :]
        total = jnp.zeros((width, block), F32)
        for h in range(width // head_dim):
            own = jnp.where(lane == h, query, jnp.zeros_like(query)) * scaling
            scores = jnp.where(valid, mm(k_ref[...], own, NT), MASKED)
            top = jnp.max(scores, axis=0, keepdims=True)
            exponent = jnp.exp(scores - top)
            denominator = jnp.sum(exponent, axis=0, keepdims=True)
            lse_ref[h : h + 1, part] = top + jnp.log(denominator)
            mixed = mm(vt_ref[...], exponent.astype(BF16)) * (1.0 / denominator)
            total = jnp.where(row == h, mixed, total)
        out_ref[part, :] = total.T.astype(BF16)
        return carry

    lax.fori_loop(0, full // block, step, 0)


def attend_forward(count, qkv, head_dim):
    parts, triple_rows, width = qkv.shape
    full = parts * triple_rows // 3
    vmem = pl.BlockSpec(memory_space=pltpu.VMEM)
    block = min(256, full)
    return pl.pallas_call(
        functools.partial(attend_forward_kernel, head_dim, block),
        out_shape=(
            jax.ShapeDtypeStruct((full, width), BF16),
            jax.ShapeDtypeStruct((width // head_dim, full), F32),
        ),
        in_specs=[pl.BlockSpec(memory_space=pltpu.SMEM), vmem],
        out_specs=(vmem, vmem),
        scratch_shapes=[
            pltpu.VMEM((full, width), BF16),
            pltpu.VMEM((full, width), BF16),
            pltpu.VMEM((width, full), BF16),
        ],
        cost_estimate=cost(60000000000),
        name="attend_forward",
    )(count, qkv)


def attend_backward_kernel(
    head_dim, block, count_ref, qkv_ref, grad_ref, lse_ref, out_ref, q_ref, k_ref, v_ref, kt_ref, dk_ref, dv_ref
):
    full, width = q_ref.shape
    seg = full // qkv_ref.shape[0]
    scaling = 1.0 / math.sqrt(head_dim)
    load_parts(qkv_ref, 0, seg, q_ref)
    load_parts(qkv_ref, 1, seg, k_ref)
    load_parts(qkv_ref, 2, seg, v_ref)
    kt_ref[...] = k_ref[...].T
    dk_ref[...] = jnp.zeros_like(dk_ref)
    dv_ref[...] = jnp.zeros_like(dv_ref)
    count = count_ref[0, 0]
    lane = lax.broadcasted_iota(jnp.int32, (block, width), 1) // head_dim
    row = lax.broadcasted_iota(jnp.int32, (width, block), 0) // head_dim
    valid = lax.broadcasted_iota(jnp.int32, (full, block), 0) < count

    def step(i, carry):
        part = pl.ds(pl.multiple_of(i * block, block), block)
        query = q_ref[part, :]
        grad = grad_ref[part, :]
        total = jnp.zeros((width, block), F32)
        for h in range(width // head_dim):
            own = jnp.where(lane == h, query, jnp.zeros_like(query)) * jnp.asarray(scaling, BF16)
            own_grad = jnp.where(lane == h, grad, jnp.zeros_like(grad))
            scores = jnp.where(valid, mm(k_ref[...], own, NT), MASKED)
            shares = jnp.exp(scores - lse_ref[h : h + 1, part])
            share_grad = mm(v_ref[...], own_grad, NT)
            dot = jnp.sum(shares * share_grad, axis=0, keepdims=True)
            score_grad = (shares * (share_grad - dot)).astype(BF16)
            dv_ref[...] += mm(shares.astype(BF16), own_grad)
            dk_ref[...] += mm(score_grad, own)
            total = jnp.where(row == h, mm(kt_ref[...], score_grad), total)
        turned = (total * scaling).T.astype(BF16)
        for piece in range(block // seg):
            out_ref[i * (block // seg) + piece, 0:seg, :] = turned[piece * seg : (piece + 1) * seg, :]
        return carry

    lax.fori_loop(0, full // block, step, 0)
    for source in range(full // seg):
        rows = slice(source * seg, (source + 1) * seg)
        out_ref[source, seg : 2 * seg, :] = dk_ref[rows, :].astype(BF16)
        out_ref[source, 2 * seg : 3 * seg, :] = dv_ref[rows, :].astype(BF16)


def attend_backward(count, qkv, grad, lse, head_dim):
    parts, triple_rows, width = qkv.shape
    full = parts * triple_rows // 3
    vmem = pl.BlockSpec(memory_space=pltpu.VMEM)
    block = min(256, full)
    return pl.pallas_call(
        functools.partial(attend_backward_kernel, head_dim, block),
        out_shape=jax.ShapeDtypeStruct(qkv.shape, BF16),
        in_specs=[pl.BlockSpec(memory_space=pltpu.SMEM), vmem, vmem, vmem],
        out_specs=vmem,
        scratch_shapes=[pltpu.VMEM((full, width), BF16)] * 3
        + [pltpu.VMEM((width, full), BF16)]
        + [pltpu.VMEM((full, width), F32)] * 2,
        cost_estimate=cost(100000000000),
        name="attend_backward",
    )(count, qkv, grad, lse)


def gathered_attention(triple, count, head_dim):
    seg, triple_width = triple.shape
    width = triple_width // 3
    scaling = 1.0 / math.sqrt(head_dim)
    full = seg * lax.axis_size("patch")
    query = triple[:, :width].reshape(seg, HEADS, head_dim)
    key = lax.all_gather(triple[:, width : 2 * width], "patch", axis=0, tiled=True)
    value = lax.all_gather(triple[:, 2 * width :], "patch", axis=0, tiled=True)
    key = key.reshape(full, HEADS, head_dim)
    value = value.reshape(full, HEADS, head_dim)
    valid = (jnp.arange(full, dtype=jnp.int32) < count)[None, None, :]

    def score():
        raw = jnp.einsum("qhd,khd->hqk", query, key, preferred_element_type=F32) * scaling
        return jnp.where(valid, raw, MASKED)

    masked = score()
    top = jnp.max(masked, axis=-1, keepdims=True)
    exponent = jnp.exp(masked - top)
    denominator = jnp.sum(exponent, axis=-1, keepdims=True)
    shares_low = (exponent / denominator).astype(BF16)
    lse = top + jnp.log(denominator)
    attended = jnp.einsum("hqk,khd->qhd", shares_low, value, preferred_element_type=F32)

    def backward(grad):
        grad = grad.reshape(seg, HEADS, head_dim)
        shares = jnp.exp(score() - lse)
        share_grad = jnp.einsum("qhd,khd->hqk", grad, value, preferred_element_type=F32)
        dot = jnp.sum(shares * share_grad, axis=-1, keepdims=True)
        score_grad = (shares * (share_grad - dot)).astype(BF16)
        q_grad = jnp.einsum("hqk,khd->qhd", score_grad, key, preferred_element_type=F32) * scaling
        v_all = jnp.einsum("hqk,qhd->khd", shares.astype(BF16), grad, preferred_element_type=F32)
        k_all = jnp.einsum("hqk,qhd->khd", score_grad, query, preferred_element_type=F32) * scaling
        k_grad, v_grad = (
            lax.psum_scatter(
                part.reshape(full, width).astype(BF16), "patch", scatter_dimension=0, tiled=True
            )
            for part in (k_all, v_all)
        )
        return jnp.concatenate([q_grad.reshape(seg, width).astype(BF16), k_grad, v_grad], axis=1)

    return attended.reshape(seg, width).astype(BF16), backward


def to_heads(values):
    return lax.all_to_all(values, "patch", split_axis=0, concat_axis=0, tiled=True)


def queries_to_heads(triple):
    seg, triple_width = triple.shape
    parts = lax.axis_size("patch")
    own = triple_width // (3 * parts)
    moved = triple.reshape(seg, 3, parts, own).transpose(2, 1, 0, 3).reshape(parts, 3 * seg, own)
    return to_heads(moved)


def weight_grad_kernel(jobs, index, near, away, place_ref, *refs):
    split = len(refs) - len(near) - len(away)
    arrays, outs = refs[:split], refs[split:]
    rows = outs[0].shape[1]

    def member(group, s):
        first, stacked = index[group]
        return arrays[first].at[place_ref[ME] ^ s] if stacked else arrays[first + s]

    sides = (1 - place_ref[Y],) * len(away) + (place_ref[Y],) * len(near)
    start = 0
    for left, left_start, right, right_start, cols in jobs:
        values = [member(right, s)[:, pl.ds(right_start, cols)] for s in range(4)]
        values = jnp.concatenate(values, axis=0)
        for out, side, blocks in zip(outs, sides, away + near):
            for slot, k in enumerate(blocks):
                source = 2 * (place_ref[Z] ^ k) + side
                group = [member(left, s) for s in range(4)]
                if len(group[0].shape) == 3:
                    factor = [ref[source] for ref in group]
                else:
                    block = pl.ds(pl.multiple_of(left_start + source * rows, rows), rows)
                    factor = [ref[:, block] for ref in group]
                factor = jnp.concatenate(factor, axis=0)
                out[slot, :, start : start + cols] = mm(factor, values, TN).astype(BF16)
        start += cols


def weight_grads(place, jobs, groups, rows, near, away):
    arrays, index = [], []
    for group in groups:
        stacked = not isinstance(group, (list, tuple))
        index.append((len(arrays), stacked))
        arrays += [group] if stacked else list(group)
    total = sum(job[-1] for job in jobs)
    shapes = [((len(blocks), rows, total), BF16) for blocks in away + near]
    kernel = functools.partial(weight_grad_kernel, jobs, index, near, away)
    outs = small_call(kernel, place, arrays, shapes, effort=2000, name="weight_grads")
    return outs[len(away) :], outs[: len(away)]


def swap(values, axis, bit):
    return lax.ppermute(values, axis, [(i, i ^ bit) for i in range(lax.axis_size(axis))])


def together(*values):
    return lax.optimization_barrier(values)


def after(value, *others):
    return lax.optimization_barrier((value, *others))[0]


def small_call(kernel, place, arrays, shapes, scratch=(), effort=200, name="small"):
    vmem = pl.BlockSpec(memory_space=pltpu.VMEM)
    return pl.pallas_call(
        kernel,
        out_shape=tuple(jax.ShapeDtypeStruct(dims, dtype) for dims, dtype in shapes),
        in_specs=[pl.BlockSpec(memory_space=pltpu.SMEM)] + [vmem] * len(arrays),
        out_specs=(vmem,) * len(shapes),
        scratch_shapes=list(scratch),
        cost_estimate=cost(int(effort * 10**9)),
        name=name,
    )(place, *arrays)


ME, CORE, X, Y, Z = range(5)


def tokens_of_group(values):
    across = swap(values, "var", 2)
    return values, swap(values, "var", 1), across, swap(across, "var", 1)


def copies_of_group(values):
    return (values,) + tuple(swap(values, "var", bit) for bit in (1, 2, 3))


def slices_of_group(pieces):
    return (pieces[0],) + tuple(swap(pieces[bit], "var", bit) for bit in (1, 2, 3))


def z_pieces(place, near, got):
    _, rows, cols = near.shape

    def kernel(place_ref, near_ref, got_ref, *outs):
        for bit in range(4):
            block = place_ref[Z] ^ bit
            outs[bit][...] = (near_ref[block].astype(F32) + got_ref[block].astype(F32)).astype(BF16)

    return small_call(kernel, place, (near, got), [((rows, cols), BF16)] * 4, name="z_pieces")


def z_exchange(pieces):
    return (pieces[0],) + tuple(swap(pieces[bit], "patch", 2 * bit) for bit in (1, 2, 3))


def z_sum(place, arrays):

    def kernel(place_ref, first, second, third, fourth, out):
        total = first[...].astype(F32) + second[...].astype(F32) + third[...].astype(F32) + fourth[...].astype(F32)
        out[...] = total.astype(BF16)

    return small_call(kernel, place, arrays, [(arrays[0].shape, BF16)], name="z_sum")[0]


def pair_sum(place, near, got):
    def kernel(place_ref, near_ref, got_ref, out):
        for k in range(2):
            out[k] = (near_ref[k].astype(F32) + got_ref[k].astype(F32)).astype(BF16)

    return small_call(kernel, place, (near, got), [(near.shape, BF16)], name="pair_sum")[0]


def z_first_sum(place, near, got, far):
    first = got.shape[0] - 2

    def kernel(place_ref, near_ref, got_ref, far_ref, stay, away):
        for out, k in ((away, 1), (stay, 0)):
            total = near_ref[k].astype(F32) + got_ref[first + k].astype(F32) + far_ref[k].astype(F32)
            out[...] = total.astype(BF16)

    return small_call(kernel, place, (near, got, far), [(near.shape[1:], BF16)] * 2, name="z_first_sum")


def z_last_sum(place, near, got):
    def kernel(place_ref, near_ref, got_ref, out):
        out[...] = (near_ref[...].astype(F32) + got_ref[...].astype(F32)).astype(BF16)

    return small_call(kernel, place, (near, got), [(near.shape, BF16)], name="z_last_sum")[0]


def gather_over_var(own):
    across = swap(own, "var", 2)
    return own, swap(own, "var", 1), across, swap(across, "var", 1)


def join(place, pieces, widths, stacked):
    rows = pieces[0].shape[0]

    def kernel(place_ref, *refs):
        start = 0
        for k, (out, size) in enumerate(zip(refs[4:], widths)):
            for s in range(4):
                v = place_ref[ME] ^ s
                values = refs[s][:, start : start + size].astype(F32)
                if k < stacked:
                    out[v] = values
                else:
                    out[:, pl.ds(pl.multiple_of(v * size, size), size)] = values
            start += size

    shapes = [((4, rows, size) if k < stacked else (rows, 4 * size), F32) for k, size in enumerate(widths)]
    return small_call(kernel, place, pieces, shapes, name="join")


def sum_over_all(place, stay, away, hooks, marks):
    _, rows, cols = stay.shape
    half = rows // 2
    size = half // 4
    hooks = iter(hooks)

    def core_kernel(place_ref, stay_ref, got_ref, stay_out, away_out):
        for out, which in ((away_out, 1 - place_ref[X]), (stay_out, place_ref[X])):
            out[...] = (stay_ref[which].astype(F32) + got_ref[which].astype(F32)).astype(BF16)

    got = next(hooks)(swap(away, "var", 1))
    stay, away = small_call(core_kernel, place, (stay, got), [((rows, cols), BF16)] * 2, name="core_sum")
    marks.append(stay)

    def x_kernel(place_ref, stay_ref, got_ref, stay_out, away_out):
        for out, which in ((away_out, 1 - place_ref[Y]), (stay_out, place_ref[Y])):
            out[...] = (stay_ref[which].astype(F32) + got_ref[which].astype(F32)).astype(BF16)

    got = next(hooks)(swap(away, "var", 2))
    halves = (2, half, cols)
    stay, away = small_call(
        x_kernel, place, (stay.reshape(halves), got.reshape(halves)), [((half, cols), BF16)] * 2, name="x_sum"
    )
    marks.append(stay)
    got = next(hooks)(swap(away, "patch", 1))
    pieces = z_exchange(z_pieces(place, stay.reshape(4, size, cols), got.reshape(4, size, cols)))
    kept = z_sum(place, next(hooks)(pieces))

    def z_kernel(place_ref, *refs):
        for s in range(4):
            refs[4][place_ref[Z] ^ s] = refs[s][...]

    arrays = (kept,) + tuple(swap(kept, "patch", 2 * bit) for bit in (1, 2, 3))
    own = small_call(z_kernel, place, next(hooks)(arrays), [((4, size, cols), BF16)], name="z_join")[0]

    def y_kernel(place_ref, own_ref, other_ref, out):
        out[place_ref[Y]] = own_ref[...]
        out[1 - place_ref[Y]] = other_ref[...]

    own = own.reshape(half, cols)
    arrays = (own, next(hooks)(swap(own, "patch", 1)))
    full = small_call(y_kernel, place, arrays, [(halves, BF16)], name="y_join")[0].reshape(rows, cols)

    across = next(hooks)(swap(full, "var", 2))
    return full, swap(full, "var", 1), across, swap(across, "var", 1)


def middle_kernel(
    place_ref,
    att_ref,
    front_ref,
    valid_ref,
    og_ref,
    tout_ref,
    gain_ref,
    win_ref,
    wout_ref,
    block_ref,
    late_ref,
    *refs,
):
    actives, middles = refs[0:4], refs[4:8]
    grad_ref, after_ref, gain_grad_ref, residual_ref, unit_ref, rate_ref, acc_ref, back_ref, wide_ref, branch_ref = refs[8:]
    step = pl.program_id(0)
    seg, width = front_ref.shape
    parts = att_ref.shape[0]
    own = width // parts
    me = place_ref[0]
    block = win_ref.shape[1]
    slot = block // 4
    quarter = width // 4
    hidden = slot * pl.num_programs(0)

    @pl.when(step == 0)
    def _():
        for p in range(parts):
            branch_ref[:, p * own : (p + 1) * own] = att_ref[p]
        after = front_ref[...] + mm(branch_ref[...], tout_ref[...])
        residual_ref[...] = after
        center = after - jnp.mean(after, axis=1, keepdims=True)
        rate = lax.rsqrt(jnp.mean(center * center, axis=1, keepdims=True) + EPSILON)
        unit = center * rate
        unit_ref[...] = unit
        rate_ref[...] = rate
        late_ref[...] = (unit * gain_ref[...]).astype(BF16)
        acc_ref[...] = jnp.zeros_like(acc_ref)
        back_ref[...] = jnp.zeros_like(back_ref)

    inner = mm(late_ref[...], win_ref[...])
    cumulative = 0.5 * (1.0 + lax.erf(inner * math.sqrt(0.5)))
    active = (inner * cumulative).astype(BF16)
    acc_ref[...] += mm(active, wout_ref[...])
    slope = cumulative + inner * (jnp.exp(-0.5 * inner * inner) * (1.0 / math.sqrt(2.0 * math.pi)))
    inner_grad = (mm(og_ref[...], wout_ref[...], NT) * slope).astype(BF16)
    back_ref[...] += mm(inner_grad, win_ref[...], NT)
    wide_ref[...] = active
    cols = pl.ds(pl.multiple_of(step * slot, slot), slot)
    for s in range(4):
        actives[s][:, cols] = wide_ref[:, pl.ds(pl.multiple_of((me ^ s) * slot, slot), slot)]
    owner = step * block // hidden
    place = pl.ds(pl.multiple_of(step * block - owner * hidden, block), block)
    for s in range(4):

        @pl.when((me ^ s) == owner)
        def _(s=s):
            middles[s][:, place] = inner_grad

    @pl.when(step == pl.num_programs(0) - 1)
    def _():
        valid = valid_ref[...]
        block_ref[...] = ((residual_ref[...] + acc_ref[...]) * valid).astype(BF16)
        unit = unit_ref[...]
        back = back_ref[...]
        gain_grad_ref[...] = jnp.sum(back * unit, axis=0, keepdims=True)
        scaled = back * gain_ref[...]
        inside = jnp.mean(scaled * unit, axis=1, keepdims=True)
        total = rate_ref[...] * (scaled - jnp.mean(scaled, axis=1, keepdims=True) - unit * inside)
        total = og_ref[...].astype(F32) + total
        after_ref[...] = total
        branch_ref[...] = total.astype(BF16)
        for s in range(4):
            start = pl.multiple_of((me ^ s) * quarter, quarter)
            middles[s][:, hidden:] = branch_ref[:, pl.ds(start, quarter)]
        turned = mm(branch_ref[...], tout_ref[...], NT).astype(BF16)
        for p in range(parts):
            grad_ref[p] = turned[:, p * own : (p + 1) * own]


def middle(place, attended, front_out, valid, out_grad, trunk_out, gain, mlp_in, mlp_out):
    seg, width = front_out.shape
    hidden = mlp_in.shape[1]
    parts = attended.shape[0]
    block = hidden // parts
    shape = jax.ShapeDtypeStruct

    def still(*dims):
        return pl.BlockSpec(dims, lambda i: (0,) * len(dims))

    piece, wider = shape((seg, hidden // 4), BF16), shape((seg, hidden // 4 + width // 4), BF16)
    return pl.pallas_call(
        middle_kernel,
        grid=(parts,),
        out_shape=(
            shape((seg, width), BF16),
            shape((seg, width), BF16),
            *((piece,) * 4),
            *((wider,) * 4),
            shape(attended.shape, BF16),
            shape((seg, width), F32),
            shape((1, width), F32),
        ),
        in_specs=[
            pl.BlockSpec(memory_space=pltpu.SMEM),
            still(*attended.shape),
            still(seg, width),
            still(seg, 1),
            still(seg, width),
            still(width, width),
            still(1, width),
            pl.BlockSpec((width, block), lambda i: (0, i)),
            pl.BlockSpec((block, width), lambda i: (i, 0)),
        ],
        out_specs=(
            still(seg, width),
            still(seg, width),
            *((still(*piece.shape),) * 4),
            *((still(*wider.shape),) * 4),
            still(*attended.shape),
            still(seg, width),
            still(1, width),
        ),
        scratch_shapes=[
            pltpu.VMEM((seg, width), F32),
            pltpu.VMEM((seg, width), F32),
            pltpu.VMEM((seg, 1), F32),
            pltpu.VMEM((seg, width), F32),
            pltpu.VMEM((seg, width), F32),
            pltpu.VMEM((seg, block), BF16),
            pltpu.VMEM((seg, width), BF16),
        ],
        compiler_params=pltpu.CompilerParams(dimension_semantics=("arbitrary",)),
        cost_estimate=cost(100000000000),
        name="trunk_middle",
    )(place, attended, front_out, valid, out_grad, trunk_out, gain, mlp_in, mlp_out)


def trunk_back_kernel(
    place_ref, grads_ref, front_ref, gain_ref, after_ref, valid_ref, aout_ref, wqkv_ref, mixed_ref, gain_grad_ref, *rest
):
    stack_ref, triple_ref, back_ref = rest
    step = pl.program_id(0)
    parts = grads_ref.shape[0]
    seg, width = front_ref.shape
    own = width // parts
    me = place_ref[ME]

    @pl.when(step == 0)
    def _():
        for c in range(3):
            for p in range(parts):
                triple_ref[c, :, p * own : (p + 1) * own] = grads_ref[p, c * seg : (c + 1) * seg, :]
        back_ref[...] = jnp.zeros_like(back_ref)

    back_ref[...] += mm(triple_ref[step], wqkv_ref[...], NT)

    @pl.when(step == pl.num_programs(0) - 1)
    def _():
        front = front_ref[...]
        center = front - jnp.mean(front, axis=1, keepdims=True)
        rate = lax.rsqrt(jnp.mean(center * center, axis=1, keepdims=True) + EPSILON)
        unit = center * rate
        back = back_ref[...]
        gain_grad_ref[...] = jnp.sum(back * unit, axis=0, keepdims=True)
        scaled = back * gain_ref[...]
        inside = jnp.mean(scaled * unit, axis=1, keepdims=True)
        total = rate * (scaled - jnp.mean(scaled, axis=1, keepdims=True) - unit * inside)
        total = ((after_ref[...] + total) * valid_ref[...]).astype(BF16)
        mixed_ref[...] = mm(total, aout_ref[...], NT).astype(BF16)
        part = width // 4
        for v in range(4):
            stack_ref[v, :, 3 * part :] = total[:, v * part : (v + 1) * part]
            for k in range(3):
                block = 3 * v + k
                source = triple_ref[block // 4, :, block % 4 * part : (block % 4 + 1) * part]
                stack_ref[v, :, k * part : (k + 1) * part] = source


def trunk_back(place, grads, front_out, gain, after_grad, valid, agg_out, trunk_qkv):
    seg, width = front_out.shape
    shape = jax.ShapeDtypeStruct

    def still(*dims):
        return pl.BlockSpec(dims, lambda i: (0,) * len(dims))

    piece = shape((seg, width), BF16)
    return pl.pallas_call(
        trunk_back_kernel,
        grid=(3,),
        out_shape=(piece, shape((1, width), F32), shape((4, seg, width), BF16)),
        in_specs=[
            pl.BlockSpec(memory_space=pltpu.SMEM),
            still(*grads.shape),
            still(seg, width),
            still(1, width),
            still(seg, width),
            still(seg, 1),
            still(width, width),
            pl.BlockSpec((width, width), lambda i: (0, i)),
        ],
        out_specs=(still(seg, width), still(1, width), still(4, seg, width)),
        scratch_shapes=[
            pltpu.VMEM((3, seg, width), BF16),
            pltpu.VMEM((seg, width), F32),
        ],
        compiler_params=pltpu.CompilerParams(dimension_semantics=("arbitrary",)),
        cost_estimate=cost(100000000000),
        name="trunk_back",
    )(place, grads, front_out, gain, after_grad, valid, agg_out, trunk_qkv)


def front_last_kernel(
    pixels,
    place_ref,
    m0,
    m1,
    m2,
    m3,
    weight_ref,
    embed_ref,
    weight_own_ref,
    embed_own_ref,
    value_rows_ref,
    key_query_ref,
    key_ref,
    aggq_ref,
    query_rows_ref,
    query_own_ref,
    value_out,
    patch_out,
    embed_out,
    key_out,
    query_out,
    agg_query_out,
    norm_one_out,
    norm_two_out,
    m_ref,
    sum_ref,
):
    rows, width = weight_ref.shape
    own = weight_own_ref.shape[1]
    size = m0.shape[1]
    head_dim = width // HEADS
    scaling = 1.0 / math.sqrt(head_dim)
    for s, ref in enumerate((m0, m1, m2, m3)):
        v = place_ref[ME] ^ s
        m_ref[:, pl.ds(pl.multiple_of((v % 2 * 2 + v // 2) * size, size), size)] = ref[...]
    m_sum, me_sum = m_ref[0:rows, :], m_ref[rows : rows + VARS, :]
    value_out[...] = mm(weight_own_ref[...], m_sum, TN) + mm(embed_own_ref[...], me_sum, TN)
    s_all = m_ref[rows + VARS : rows + VARS + HEADS, :]
    twice = jnp.concatenate([s_all, s_all], axis=0)
    patch_out[...] = mm(m_sum, value_rows_ref[...], NT) + mm(twice[:, 0:rows], key_query_ref[...], TN)
    embed_out[...] = mm(me_sum, value_rows_ref[...], NT) + mm(
        twice[:, rows : rows + VARS], key_query_ref[...], TN
    )
    key_sum = (mm(s_all[:, 0:rows], weight_ref[...]) + mm(s_all[:, rows : rows + VARS], embed_ref[...])) * scaling
    sum_ref[...] = key_sum
    lane = lax.broadcasted_iota(jnp.int32, (HEADS, width), 1) // head_dim
    mine = lane == lax.broadcasted_iota(jnp.int32, (HEADS, width), 0)
    start = pl.multiple_of((place_ref[Z] * 2 + place_ref[Y]) * own, own)
    head_rows = jnp.where(mine, aggq_ref[...], 0.0)
    key_out[...] = mm(sum_ref[:, pl.ds(start, own)], head_rows, TN, precision=HIGHEST)
    crossed = mm(jnp.concatenate(split_high_low(key_sum), axis=0), key_ref[...])
    crossed = crossed[0:HEADS, :] + crossed[HEADS:, :]
    aggq_grad = jnp.sum(jnp.where(mine, crossed, 0.0), axis=0, keepdims=True)
    query_out[...] = query_own_ref[...] * aggq_grad
    high, low = split_high_low(aggq_grad)
    agg_query_out[...] = mm(high, query_rows_ref[...], NT) + mm(low, query_rows_ref[...], NT)
    row = lax.broadcasted_iota(jnp.int32, (HEADS, own), 0)
    tail = s_all[:, width - own :].astype(F32)
    for k in range(own // head_dim):
        line = jnp.sum(jnp.where(row == start // head_dim + k, tail, 0.0), axis=0, keepdims=True)
        norm_one_out[:, k * head_dim : (k + 1) * head_dim] = line[:, 0:head_dim]
        norm_two_out[:, k * head_dim : (k + 1) * head_dim] = line[:, head_dim:own]


def front_last(place, pieces, arrays):
    weight_rows, own_weight, value_rows = arrays[0], arrays[2], arrays[4]
    rows, width = weight_rows.shape
    own = own_weight.shape[1]
    tall = pieces[0].shape[0]
    shapes = [((own, width), F32), ((rows, own), F32), ((VARS, own), F32)] + [((own, width), F32)] * 2
    shapes += [((1, own), F32)] * 3
    return small_call(
        functools.partial(front_last_kernel, rows // VARS),
        place,
        (*pieces, *arrays),
        shapes,
        scratch=[pltpu.VMEM((tall, width), BF16), pltpu.VMEM((HEADS, width), F32)],
        name="front_last",
    )


def local(
    input_field,
    counts,
    var_ids,
    patch_weight,
    var_embed,
    agg_query,
    query_proj,
    key_proj,
    value_proj,
    agg_out,
    norm_one,
    trunk_qkv,
    trunk_out,
    norm_two,
    mlp_in,
    mlp_out,
    cotangent,
):
    patches, group = lax.axis_size("patch"), lax.axis_size("var")
    fast = (patches, group) == (8, 4)
    me, spot = lax.axis_index("var"), lax.axis_index("patch")
    place = jnp.stack([me, me % 2, me // 2, spot % 2, spot // 2]).astype(jnp.int32)
    var_index = lax.axis_index("var")
    patch_index = lax.axis_index("patch")
    all_rows, seg, var_local, pixels = input_field.shape
    width = agg_out.shape[0]
    head_dim = width // HEADS
    hidden = mlp_in.shape[1]
    scaling = 1.0 / math.sqrt(head_dim)

    turned = input_field.transpose(0, 2, 3, 1).reshape(all_rows, var_local * pixels, seg)
    own_field = lax.all_to_all(turned, "var", split_axis=0, concat_axis=1, tiled=True)
    own_field = own_field.reshape(VARS * pixels, seg)
    own_ids = lax.dynamic_slice_in_dim(var_ids, var_index, 1, 0)
    own_count = lax.dynamic_slice_in_dim(counts, var_index, 1, 0)
    positions = patch_index * seg + jnp.arange(seg, dtype=jnp.int32)
    valid_rows = (positions < own_count).astype(F32)[:, None]
    out_grad = cotangent.reshape(seg, width).astype(F32) * valid_rows
    out_grad_low = out_grad.astype(BF16)

    weight_rows = patch_weight.reshape(VARS * pixels, width)
    agg_q = mm(agg_query[None], query_proj)[0]
    in_head = jnp.arange(width, dtype=jnp.int32)[:, None] // head_dim == jnp.arange(HEADS)[None, :]
    head_query = jnp.where(in_head, agg_q[:, None] * scaling, 0.0)
    key_query = mm(key_proj, jnp.concatenate(split_high_low(head_query), axis=1))
    key_query = key_query[:, :HEADS] + key_query[:, HEADS:]
    key_query_parts = jnp.concatenate(split_high_low(key_query), axis=1)
    score_weight = mm(key_query_parts, weight_rows, (((0,), (1,)), ((), ())))
    score_weight = score_weight[:HEADS] + score_weight[HEADS:]
    score_embed = mm(key_query_parts, var_embed, (((0,), (1,)), ((), ())))
    score_embed = (score_embed[:HEADS] + score_embed[HEADS:]).reshape(HEADS * VARS, 1)
    same_var = (jnp.arange(VARS)[:, None] == jnp.arange(VARS * pixels)[None, :] // pixels)[None]
    spread = jnp.where(same_var, score_weight[:, None, :], 0.0).astype(BF16)
    spread = spread.reshape(HEADS * VARS, VARS * pixels)
    vwt = mm(value_proj, weight_rows, (((0,), (1,)), ((), ()))).astype(BF16)
    vet = mm(value_proj, var_embed, (((0,), (1,)), ((), ()))).astype(BF16)

    own_width = width // patches
    start = patch_index * own_width

    def own_cols(values):
        return lax.dynamic_slice_in_dim(values, start, own_width, 1)

    def own_rows(values):
        return lax.dynamic_slice_in_dim(values, start, own_width, 0)

    def own_query(values):
        return lax.dynamic_slice_in_dim(values, start, own_width, 0).astype(F32)[:, None]

    def last_operands(ready):
        weights, embeds, values, queries, line, key_queries, _ = together(
            weight_rows, var_embed, value_proj, query_proj, agg_query, key_query, ready
        )
        return (
            weights,
            embeds,
            own_cols(weights),
            own_cols(embeds),
            own_rows(values),
            jnp.concatenate(split_high_low(own_rows(key_queries)), axis=1).T,
            key_proj,
            agg_q[None],
            own_rows(queries),
            own_query(line),
        )

    x_own, shares, mixed_low = front_forward(own_ids, own_field, spread, score_embed, vwt, vet)

    front_out = mm(mixed_low, agg_out) * valid_rows
    normed_one, norm_one_pull = jax.vjp(layer_norm, front_out, norm_one.astype(F32))
    normed_one_low = normed_one.astype(BF16)
    triple = mm(normed_one_low, trunk_qkv).astype(BF16)
    part = width // group
    quarter = hidden // group
    zs = patches // 2
    ready = after(value_proj, triple)
    vw = mm(weight_rows, ready).astype(BF16)
    ve = mm(var_embed, ready).astype(BF16)
    if fast:
        early = tokens_of_group(jnp.concatenate([out_grad_low, mixed_low, normed_one_low], axis=1))
        qkv, vw, ve, *arrays = together(queries_to_heads(triple), vw, ve, *last_operands(triple))
        count = own_count.reshape(1, 1)
        heads, lse = attend_forward(count, qkv, head_dim)
        attended = to_heads(heads.reshape(patches, seg, own_width))
        results = middle(
            place,
            attended,
            front_out,
            valid_rows,
            out_grad_low,
            trunk_out,
            norm_two.astype(F32)[None],
            mlp_in,
            mlp_out,
        )
        attended_group = copies_of_group(attended)
        results = together(*results, *attended_group, *early)
        attended_group, early = results[13:17], results[17:]
        block_out, normed_two_low, grads, after_grad, norm_two_grad = (results[k] for k in (0, 1, 10, 11, 12))
        block_out = block_out[None]
        grads = to_heads(grads)
        active_group = slices_of_group(results[2:6])
        across = swap(normed_two_low, "var", 2)
        result = attend_backward(count, qkv, grads.reshape(patches * seg, own_width), lse, head_dim)
        result, across, *rest = together(result, across, *active_group, *results[6:10])
        active_group, middle_group = rest[:4], slices_of_group(rest[4:])
        normed_group = (normed_two_low, swap(normed_two_low, "var", 1), across, swap(across, "var", 1))
        result = to_heads(result)
        pairs, whole_order = ((1, 3), (0, 2)), ((1, 3, 0, 2),)
        jobs = ((0, 0, 1, 0, width),)
        near_one, away_one = weight_grads(place, jobs, (active_group, early), own_width, pairs, whole_order)
        jobs = ((0, 0, 2, 0, quarter), (1, 0, 2, quarter, part))
        groups = (together(normed_group[0], *near_one)[:1] + normed_group[1:], attended_group, middle_group)
        near_two, away_two = weight_grads(place, jobs, groups, own_width, pairs, pairs)
        result = after(result, *near_two)
        one = {"near": near_one, "got": swap(away_one[0], "patch", 1)}
        two = {"near": near_two, "away": away_two}
        mixed_grad, norm_one_grad, stack = trunk_back(
            place, result, front_out, norm_one.astype(F32)[None], after_grad, valid_rows, agg_out, trunk_qkv
        )
        one["far"] = pair_sum(place, after(one["near"][0], mixed_grad), one["got"])
        mixed_grad = after(mixed_grad, one["far"])
        last_group = lax.all_to_all(stack, "var", split_axis=0, concat_axis=0, tiled=True)
    else:
        attended, attention_pull = gathered_attention(triple, own_count, head_dim)
        after_attn = front_out + mm(attended, trunk_out)
        normed_two, norm_two_pull = jax.vjp(layer_norm, after_attn, norm_two.astype(F32))
        normed_two_low = normed_two.astype(BF16)
        inner = mm(normed_two_low, mlp_in)
        active, gelu_pull = jax.vjp(gelu_exact, inner)
        active_low = active.astype(BF16)
        result = after_attn + mm(active_low, mlp_out)
        block_out = (result * valid_rows).astype(BF16)[None]
        inner_grad = gelu_pull(mm(out_grad_low, mlp_out, NT))[0].astype(BF16)
        normed_two_grad = mm(inner_grad, mlp_in, NT)
        after_ln_grad, norm_two_grad = norm_two_pull(normed_two_grad)
        after_grad = out_grad + after_ln_grad
        branch_low = after_grad.astype(BF16)
        triple_grad = attention_pull(mm(branch_low, trunk_out, NT).astype(BF16))
        normed_one_grad = mm(triple_grad, trunk_qkv, NT)
        front_ln_grad, norm_one_grad = norm_one_pull(normed_one_grad)
        agg_grad = ((after_grad + front_ln_grad) * valid_rows).astype(BF16)
        mixed_grad = mm(agg_grad, agg_out, NT).astype(BF16)
        norm_one_grad, norm_two_grad = norm_one_grad[None], norm_two_grad[None]

    field_low, *m_parts = front_backward(
        fast, place, own_ids, x_own, shares, mixed_grad, vw, ve, spread, norm_one_grad, norm_two_grad
    )

    field_low = field_low.reshape(group, var_local * pixels, seg)
    field_grad = None if fast else lax.all_to_all(field_low, "var", split_axis=0, concat_axis=0, tiled=True)

    if fast:
        m_stay, m_away, two["first"], last_group = together(*m_parts, swap(two["away"][0], "patch", 1), last_group)
        m_parts = (m_stay, m_away)
        two["far"] = pair_sum(place, two["near"][0], two["first"])
        last, marks = {}, []

        def core_done(values):
            return values

        def x_done(values):
            far = swap(one["far"], "patch", 2)
            far, near, _ = together(far, one["near"][1], *marks)
            one["pair"] = z_first_sum(place, near, one["got"], far)
            return after(values, one["pair"][0])

        def y_done(values):
            jobs = ((0, 2 * width, 1, 0, 3 * part), (0, width, 1, 3 * part, part))
            groups = (early, after(last_group, marks[-1]))
            last["near"], last["away"] = weight_grads(place, jobs, groups, own_width, pairs, whole_order)
            got = swap(after(two["away"][1], two["first"]), "patch", 1)
            values, got, far, *_ = together(values, got, swap(two["far"], "patch", 2), *last["near"])
            two["pair"] = z_first_sum(place, two["near"][1], got, far)
            return values

        def z_done(values):
            near, away = one["pair"]
            *values, got, _ = together(*values, swap(away, "patch", 4), two["pair"][0])
            one["own"] = z_last_sum(place, near, got)
            return values

        def b_done(values):
            near, away = two["pair"]
            *values, last["got"], got = together(*values, swap(last["away"][0], "patch", 1), swap(away, "patch", 4))
            late = after(field_low, last["got"])
            last["field"] = lax.all_to_all(late, "var", split_axis=0, concat_axis=0, tiled=True)
            last["far"] = pair_sum(place, last["near"][0], last["got"])
            two["own"] = z_last_sum(place, near, got)
            return [after(values[0], last["far"]), *values[1:]]

        def y_back(values):
            values, one["across"], last["field"] = together(values, swap(one["own"], "var", 2), last["field"])
            return values

        def var_done(values):
            far, across = swap(last["far"], "patch", 2), swap(two["own"], "var", 2)
            near, away = z_first_sum(place, last["near"][1], last["got"], far)
            two["parts"] = (two["own"], swap(two["own"], "var", 1), across, swap(across, "var", 1))
            last["own"] = z_last_sum(place, near, swap(away, "patch", 4))
            own, across = one["own"], one["across"]
            values, inner, corner, _ = together(values, swap(own, "var", 1), swap(across, "var", 1), near)
            one["parts"] = (own, inner, across, corner)
            return values

        m_pieces = sum_over_all(place, *m_parts, (core_done, x_done, y_done, z_done, b_done, y_back, var_done), marks)
        field_grad = last["field"]
        (mlp_out_grad,) = join(place, one["parts"], (width,), 1)
        mlp_in_grad, trunk_out_grad = join(place, two["parts"], (quarter, part), 0)
        mlp_out_grad = mlp_out_grad.reshape(hidden // patches, width)
        trunk_qkv_grad, agg_out_grad = join(place, gather_over_var(last["own"]), (3 * part, part), 0)
    else:

        def slices(values):
            values = values.reshape(seg, group, values.shape[1] // group).transpose(1, 0, 2)
            return lax.all_to_all(values, "var", split_axis=0, concat_axis=0, tiled=True)

        def everyone(values):
            return lax.all_gather(values, "var", axis=0, tiled=True)

        def total(left, right):
            value = mm(left.reshape(-1, left.shape[-1]), right.reshape(-1, right.shape[-1]), TN).astype(BF16)
            value = lax.psum_scatter(value, "patch", scatter_dimension=0, tiled=True)
            return lax.all_gather(value, "var", axis=0)

        def joined(value):
            return value.transpose(1, 0, 2).reshape(value.shape[1], -1).astype(F32)

        size = hidden // (patches * group)
        active_rows = active_low.reshape(seg, patches, group, size).transpose(0, 2, 1, 3).reshape(seg, hidden)
        mlp_out_grad = total(slices(active_rows), everyone(out_grad_low)).reshape(hidden // patches, width).astype(F32)
        mlp_in_grad = joined(total(everyone(normed_two_low), slices(inner_grad)))
        trunk_out_grad = joined(total(everyone(attended), slices(branch_low)))
        trunk_qkv_grad = joined(total(everyone(normed_one_low), slices(triple_grad)))
        agg_out_grad = joined(total(everyone(mixed_low), slices(agg_grad)))
        m_all = lax.psum(m_parts[0], ("patch", "var")).transpose(1, 0, 2).reshape(-1, width)
    if fast:
        value_proj_grad, patch_grad, embed_grad, key_proj_grad, query_proj_grad, *lines = front_last(
            place, m_pieces, arrays
        )
        agg_query_grad, norm_one_grad, norm_two_grad = (line[0] for line in lines)
    else:
        value_rows, key_query_rows = own_rows(value_proj), own_rows(key_query)
        m_sum, me_sum = m_all[: VARS * pixels], m_all[VARS * pixels : VARS * pixels + VARS]
        s_rows = m_all[VARS * pixels + VARS :].astype(F32)
        s_all = s_rows[:, : VARS * pixels]
        se_all = s_rows[:, VARS * pixels : VARS * pixels + VARS]
        norm_sums = s_rows[:, width - 2 * head_dim :]
        value_proj_grad = mm(own_cols(weight_rows), m_sum, TN) + mm(own_cols(var_embed), me_sum, TN)
        patch_grad = mm(m_sum, value_rows, NT) + mm(
            s_all, key_query_rows, (((0,), (1,)), ((), ())), precision=HIGHEST
        )
        embed_grad = mm(me_sum, value_rows, NT) + mm(
            se_all, key_query_rows, (((0,), (1,)), ((), ())), precision=HIGHEST
        )
        key_sum = (mm(s_all.astype(BF16), weight_rows) + mm(se_all.astype(BF16), var_embed)) * scaling
        head_rows = jnp.where(in_head.T, agg_q[None, :], 0.0)
        key_proj_grad = mm(own_cols(key_sum), head_rows, TN, precision=HIGHEST)
        crossed = mm(jnp.concatenate(split_high_low(key_sum), axis=0), key_proj)
        crossed = crossed[:HEADS] + crossed[HEADS:]
        aggq_grad = jnp.sum(jnp.where(in_head.T, crossed, 0.0), axis=0)
        query_proj_grad = own_query(agg_query) * aggq_grad[None, :]
        agg_query_grad = jnp.sum(own_rows(query_proj).astype(F32) * aggq_grad[None, :], axis=1)
        norm_one_grad = lax.dynamic_slice_in_dim(norm_sums[:, :head_dim].reshape(width), start, own_width, 0)
        norm_two_grad = lax.dynamic_slice_in_dim(norm_sums[:, head_dim:].reshape(width), start, own_width, 0)
    patch_grad = patch_grad.reshape(VARS, pixels, own_width)
    field_grad = field_grad.reshape(all_rows, var_local, pixels, seg).transpose(0, 3, 1, 2)
    return (
        block_out,
        field_grad,
        patch_grad,
        embed_grad,
        agg_query_grad,
        query_proj_grad,
        key_proj_grad,
        value_proj_grad,
        agg_out_grad,
        norm_one_grad,
        trunk_qkv_grad,
        trunk_out_grad,
        norm_two_grad,
        mlp_in_grad,
        mlp_out_grad,
    )


def solution(mesh):
    whole = P()
    placed = (P(None, "patch", "var", None),) + (whole,) * 15 + (P("var", "patch", None),)
    rows = P("patch", None)
    return jax.shard_map(
        local,
        mesh=mesh,
        in_specs=placed,
        out_specs=(
            P("var", "patch", None),
            P(None, "patch", "var", None),
            P(None, None, "patch"),
            P(None, "patch"),
            P("patch"),
            rows,
            rows,
            rows,
            rows,
            P("patch"),
            rows,
            rows,
            P("patch"),
            rows,
            rows,
        ),
        check_vma=False,
    )
```

```python
import functools
import math

import jax
import jax.numpy as jnp
from jax import lax
from jax.experimental import pallas as pl
from jax.experimental.pallas import tpu as pltpu
from jax.sharding import PartitionSpec as P

HEADS = 16
VARS = 48
EPSILON = 1e-05
MASKED = -1e30
HIGHEST = lax.Precision.HIGHEST
BF16 = jnp.bfloat16
F32 = jnp.float32
NN = (((1,), (0,)), ((), ()))
NT = (((1,), (1,)), ((), ()))
TN = (((0,), (0,)), ((), ()))


def cost(flops):
    return pl.CostEstimate(flops=flops, bytes_accessed=1 << 20, transcendentals=0)


def mm(a, b, dims=NN, precision=None):
    return lax.dot_general(a, b, dims, precision=precision, preferred_element_type=F32)


def layer_norm(values, gain_vec):
    average = jnp.mean(values, axis=-1, keepdims=True)
    center = values - average
    spread = jnp.mean(center * center, axis=-1, keepdims=True)
    return center * lax.rsqrt(spread + EPSILON) * gain_vec


def gelu_exact(values):
    return jax.nn.gelu(values, approximate=False)


def split_high_low(values):
    high = values.astype(BF16)
    return high, (values - high.astype(F32)).astype(BF16)


def front_forward_kernel(
    pixels, ids_ref, field_ref, weight_ref, bias_ref, vwt_ref, vet_ref, x_ref, p_ref, mixed_ref, spread_ref, mt_ref
):
    seg = field_ref.shape[1]
    head_dim = mixed_ref.shape[1] // HEADS
    for slot in range(VARS):
        start = pl.multiple_of(ids_ref[0, slot] * pixels, pixels)
        x_ref[pl.ds(start, pixels), :] = field_ref[slot * pixels : (slot + 1) * pixels, :]
    rows = VARS * pixels
    mine = lax.broadcasted_iota(jnp.int32, (VARS, rows), 1) // pixels
    mine = mine == lax.broadcasted_iota(jnp.int32, (VARS, rows), 0)
    bias = bias_ref[...].T
    parts = []
    for h in range(HEADS):
        spread = jnp.where(mine, weight_ref[h : h + 1, :], 0.0).astype(BF16)
        spread_ref[h * VARS : (h + 1) * VARS, :] = spread
        parts.append(mm(spread, x_ref[...]) + bias[:, h : h + 1])
    scores = jnp.stack(parts)
    top = jnp.max(scores, axis=1, keepdims=True)
    exponent = jnp.exp(scores - top)
    total = jnp.sum(exponent, axis=1, keepdims=True)
    p_ref[...] = (exponent * (1.0 / total)).reshape(HEADS * VARS, seg)

    def head(h, carry):
        shares = p_ref[pl.ds(pl.multiple_of(h * VARS, VARS), VARS), :]
        pix = x_ref[...].astype(F32).reshape(VARS, pixels, seg)
        scaled = (pix * shares[:, None, :]).astype(BF16).reshape(VARS * pixels, seg)
        rows = pl.ds(pl.multiple_of(h * head_dim, head_dim), head_dim)
        mt_ref[rows, :] = mm(vwt_ref[rows, :], scaled) + mm(vet_ref[rows, :], shares.astype(BF16))
        return carry

    lax.fori_loop(0, HEADS, head, 0, unroll=4)
    mixed_ref[...] = mt_ref[...].T.astype(BF16)


def front_forward(own_ids, own_field, score_weight, bias, vwt, vet):
    rows, seg = own_field.shape
    width = vwt.shape[0]
    vmem = pl.BlockSpec(memory_space=pltpu.VMEM)
    return pl.pallas_call(
        functools.partial(front_forward_kernel, rows // VARS),
        out_shape=(
            jax.ShapeDtypeStruct((rows, seg), BF16),
            jax.ShapeDtypeStruct((HEADS * VARS, seg), F32),
            jax.ShapeDtypeStruct((seg, width), BF16),
            jax.ShapeDtypeStruct((HEADS * VARS, rows), BF16),
        ),
        in_specs=[pl.BlockSpec(memory_space=pltpu.SMEM)] + [vmem] * 5,
        out_specs=(vmem,) * 4,
        scratch_shapes=[pltpu.VMEM((width, seg), F32)],
        cost_estimate=cost(60000000000),
        name="front_forward",
    )(own_ids, own_field, score_weight, bias, vwt, vet)


def front_backward_kernel(
    pixels,
    fast,
    place_ref,
    ids_ref,
    x_ref,
    p_ref,
    mg_ref,
    vw_ref,
    ve_ref,
    spread_ref,
    norm_one_ref,
    norm_two_ref,
    field_ref,
    *rest,
):
    rows, seg = x_ref.shape
    m_refs, (fs_ref, dx_ref, s_ref) = rest[:-3], rest[-3:]
    size = m_refs[0].shape[-1]

    def quarter_of(quarter, store):
        if not fast:
            store(m_refs[0].at[quarter])
            return
        mine = quarter // 2 == place_ref[CORE]
        pl.when(mine)(lambda: store(m_refs[0].at[quarter % 2]))
        pl.when(jnp.logical_not(mine))(lambda: store(m_refs[1].at[quarter % 2]))
    width = mg_ref.shape[1]
    head_dim = width // HEADS
    pair_dim = 2 * head_dim
    lane = lax.broadcasted_iota(jnp.int32, (seg, pair_dim), 1)
    dx_ref[...] = jnp.zeros_like(dx_ref)
    pairs = size // pair_dim

    def pair(q, carry):
        cols = pl.ds(pl.multiple_of(q * pair_dim, pair_dim), pair_dim)
        grad = mg_ref[:, cols]
        none = jnp.zeros_like(grad)
        both = jnp.concatenate(
            [jnp.where(lane < head_dim, grad, none), jnp.where(lane >= head_dim, grad, none)], axis=0
        )
        inner = mm(vw_ref[:, cols], both, NT)
        inner_e = mm(ve_ref[:, cols], both, NT)
        pix = x_ref[...].astype(F32).reshape(VARS, pixels, seg)
        scaled, weights = [], []
        for k in range(2):
            hrows = pl.ds(pl.multiple_of((2 * q + k) * VARS, VARS), VARS)
            shares = p_ref[hrows, :]
            part = inner[:, k * seg : (k + 1) * seg].reshape(VARS, pixels, seg)
            share_grad = jnp.sum(pix * part, axis=1) + inner_e[:, k * seg : (k + 1) * seg]
            delta = jnp.sum(shares * share_grad, axis=0, keepdims=True)
            fs_ref[hrows, :] = shares * (share_grad - delta)
            wide = shares[:, None, :]
            dx_ref[...] += (part * wide).reshape(rows, seg)
            scaled.append((pix * wide).astype(BF16).reshape(rows, seg))
            weights.append(shares.astype(BF16))
        quarter, within = q // pairs, pl.ds(pl.multiple_of(q % pairs * pair_dim, pair_dim), pair_dim)
        m_part = mm(jnp.concatenate(scaled, axis=1), both).astype(BF16)
        me_part = mm(jnp.concatenate(weights, axis=1), both).astype(BF16)

        def store(ref):
            ref[0:rows, within] = m_part
            ref[rows : rows + VARS, within] = me_part

        quarter_of(quarter, store)
        return carry

    lax.fori_loop(0, HEADS // 2, pair, 0)
    score_grad = fs_ref[...]
    low = score_grad.astype(BF16)
    dx = dx_ref[...] + mm(spread_ref[...], low, TN)
    dx_ref[...] = dx
    for slot in range(VARS):
        start = pl.multiple_of(ids_ref[0, slot] * pixels, pixels)
        field_ref[slot * pixels : (slot + 1) * pixels, :] = dx_ref[pl.ds(start, pixels), :].astype(BF16)
    ones = jnp.ones((8, seg), F32)
    s_ref[...] = jnp.zeros_like(s_ref)
    var_row = lax.broadcasted_iota(jnp.int32, (VARS, rows), 0)
    var_col = lax.broadcasted_iota(jnp.int32, (VARS, rows), 1) // pixels
    keep = var_row == var_col
    for h in range(HEADS):
        outer = mm(low[h * VARS : (h + 1) * VARS, :], x_ref[...], NT)
        s_ref[h : h + 1, 0:rows] = jnp.sum(jnp.where(keep, outer, 0.0), axis=0, keepdims=True)
        sums = mm(ones, score_grad[h * VARS : (h + 1) * VARS, :], NT, precision=HIGHEST)
        s_ref[h : h + 1, rows : rows + VARS] = sums[0:1, :]
    for h in range(HEADS):
        for ref, first in ((norm_one_ref, width - pair_dim), (norm_two_ref, width - head_dim)):
            s_ref[h : h + 1, first : first + head_dim] = ref[:, h * head_dim : (h + 1) * head_dim]
    for quarter in range(4):
        part = s_ref[:, quarter * size : (quarter + 1) * size].astype(BF16)

        def store_sums(ref, part=part):
            ref[rows + VARS :, :] = part

        quarter_of(quarter, store_sums)


def front_backward(fast, place, own_ids, x_own, shares, mixed_grad, vw, ve, spread, norm_one, norm_two):
    rows, seg = x_own.shape
    width = mixed_grad.shape[1]
    vmem = pl.BlockSpec(memory_space=pltpu.VMEM)
    smem = pl.BlockSpec(memory_space=pltpu.SMEM)
    tall = rows + VARS + HEADS
    if fast:
        sums = (jax.ShapeDtypeStruct((2, tall, width // 4), BF16),) * 2
    else:
        sums = (jax.ShapeDtypeStruct((4, tall, width // 4), BF16),)
    return pl.pallas_call(
        functools.partial(front_backward_kernel, rows // VARS, fast),
        out_shape=(jax.ShapeDtypeStruct((rows, seg), BF16), *sums),
        in_specs=[smem, smem] + [vmem] * 8,
        out_specs=(vmem,) * (1 + len(sums)),
        scratch_shapes=[
            pltpu.VMEM((HEADS * VARS, seg), F32),
            pltpu.VMEM((rows, seg), F32),
            pltpu.VMEM((HEADS, width), F32),
        ],
        cost_estimate=cost(100000000),
        name="front_backward",
    )(place, own_ids, x_own, shares, mixed_grad, vw, ve, spread, norm_one, norm_two)


def load_parts(ref, part, seg, out_ref):
    for source in range(ref.shape[0]):
        out_ref[source * seg : (source + 1) * seg, :] = ref[source, part * seg : (part + 1) * seg, :]


def attend_forward_kernel(head_dim, block, count_ref, qkv_ref, out_ref, lse_ref, q_ref, k_ref, vt_ref):
    full, width = q_ref.shape
    seg = full // qkv_ref.shape[0]
    scaling = jnp.asarray(1.0 / math.sqrt(head_dim), BF16)
    load_parts(qkv_ref, 2, seg, q_ref)
    vt_ref[...] = q_ref[...].T
    load_parts(qkv_ref, 0, seg, q_ref)
    load_parts(qkv_ref, 1, seg, k_ref)
    count = count_ref[0, 0]
    lane = lax.broadcasted_iota(jnp.int32, (block, width), 1) // head_dim
    row = lax.broadcasted_iota(jnp.int32, (width, block), 0) // head_dim
    valid = lax.broadcasted_iota(jnp.int32, (full, block), 0) < count

    def step(i, carry):
        part = pl.ds(pl.multiple_of(i * block, block), block)
        query = q_ref[part, :]
        total = jnp.zeros((width, block), F32)
        for h in range(width // head_dim):
            own = jnp.where(lane == h, query, jnp.zeros_like(query)) * scaling
            scores = jnp.where(valid, mm(k_ref[...], own, NT), MASKED)
            top = jnp.max(scores, axis=0, keepdims=True)
            exponent = jnp.exp(scores - top)
            denominator = jnp.sum(exponent, axis=0, keepdims=True)
            lse_ref[h : h + 1, part] = top + jnp.log(denominator)
            mixed = mm(vt_ref[...], exponent.astype(BF16)) * (1.0 / denominator)
            total = jnp.where(row == h, mixed, total)
        out_ref[part, :] = total.T.astype(BF16)
        return carry

    lax.fori_loop(0, full // block, step, 0)


def attend_forward(count, qkv, head_dim):
    parts, triple_rows, width = qkv.shape
    full = parts * triple_rows // 3
    vmem = pl.BlockSpec(memory_space=pltpu.VMEM)
    block = min(512, full)
    return pl.pallas_call(
        functools.partial(attend_forward_kernel, head_dim, block),
        out_shape=(
            jax.ShapeDtypeStruct((full, width), BF16),
            jax.ShapeDtypeStruct((width // head_dim, full), F32),
        ),
        in_specs=[pl.BlockSpec(memory_space=pltpu.SMEM), vmem],
        out_specs=(vmem, vmem),
        scratch_shapes=[
            pltpu.VMEM((full, width), BF16),
            pltpu.VMEM((full, width), BF16),
            pltpu.VMEM((width, full), BF16),
        ],
        cost_estimate=cost(60000000000),
        name="attend_forward",
    )(count, qkv)


def attend_backward_kernel(
    head_dim, block, count_ref, qkv_ref, grad_ref, lse_ref, out_ref, q_ref, k_ref, v_ref, kt_ref, dk_ref, dv_ref
):
    full, width = q_ref.shape
    seg = full // qkv_ref.shape[0]
    scaling = 1.0 / math.sqrt(head_dim)
    load_parts(qkv_ref, 0, seg, q_ref)
    load_parts(qkv_ref, 1, seg, k_ref)
    load_parts(qkv_ref, 2, seg, v_ref)
    kt_ref[...] = k_ref[...].T
    dk_ref[...] = jnp.zeros_like(dk_ref)
    dv_ref[...] = jnp.zeros_like(dv_ref)
    count = count_ref[0, 0]
    lane = lax.broadcasted_iota(jnp.int32, (block, width), 1) // head_dim
    row = lax.broadcasted_iota(jnp.int32, (width, block), 0) // head_dim
    valid = lax.broadcasted_iota(jnp.int32, (full, block), 0) < count

    def step(i, carry):
        part = pl.ds(pl.multiple_of(i * block, block), block)
        query = q_ref[part, :]
        grad = grad_ref[part, :]
        total = jnp.zeros((width, block), F32)
        for h in range(width // head_dim):
            own = jnp.where(lane == h, query, jnp.zeros_like(query)) * jnp.asarray(scaling, BF16)
            own_grad = jnp.where(lane == h, grad, jnp.zeros_like(grad))
            scores = jnp.where(valid, mm(k_ref[...], own, NT), MASKED)
            shares = jnp.exp(scores - lse_ref[h : h + 1, part])
            share_grad = mm(v_ref[...], own_grad, NT)
            dot = jnp.sum(shares * share_grad, axis=0, keepdims=True)
            score_grad = (shares * (share_grad - dot)).astype(BF16)
            dv_ref[...] += mm(shares.astype(BF16), own_grad)
            dk_ref[...] += mm(score_grad, own)
            total = jnp.where(row == h, mm(kt_ref[...], score_grad), total)
        turned = (total * scaling).T.astype(BF16)
        for piece in range(block // seg):
            out_ref[i * (block // seg) + piece, 0:seg, :] = turned[piece * seg : (piece + 1) * seg, :]
        return carry

    lax.fori_loop(0, full // block, step, 0)
    for source in range(full // seg):
        rows = slice(source * seg, (source + 1) * seg)
        out_ref[source, seg : 2 * seg, :] = dk_ref[rows, :].astype(BF16)
        out_ref[source, 2 * seg : 3 * seg, :] = dv_ref[rows, :].astype(BF16)


def attend_backward(count, qkv, grad, lse, head_dim):
    parts, triple_rows, width = qkv.shape
    full = parts * triple_rows // 3
    vmem = pl.BlockSpec(memory_space=pltpu.VMEM)
    block = min(256, full)
    return pl.pallas_call(
        functools.partial(attend_backward_kernel, head_dim, block),
        out_shape=jax.ShapeDtypeStruct(qkv.shape, BF16),
        in_specs=[pl.BlockSpec(memory_space=pltpu.SMEM), vmem, vmem, vmem],
        out_specs=vmem,
        scratch_shapes=[pltpu.VMEM((full, width), BF16)] * 3
        + [pltpu.VMEM((width, full), BF16)]
        + [pltpu.VMEM((full, width), F32)] * 2,
        cost_estimate=cost(100000000000),
        name="attend_backward",
    )(count, qkv, grad, lse)


def gathered_attention(triple, count, head_dim):
    seg, triple_width = triple.shape
    width = triple_width // 3
    scaling = 1.0 / math.sqrt(head_dim)
    full = seg * lax.axis_size("patch")
    query = triple[:, :width].reshape(seg, HEADS, head_dim)
    key = lax.all_gather(triple[:, width : 2 * width], "patch", axis=0, tiled=True)
    value = lax.all_gather(triple[:, 2 * width :], "patch", axis=0, tiled=True)
    key = key.reshape(full, HEADS, head_dim)
    value = value.reshape(full, HEADS, head_dim)
    valid = (jnp.arange(full, dtype=jnp.int32) < count)[None, None, :]

    def score():
        raw = jnp.einsum("qhd,khd->hqk", query, key, preferred_element_type=F32) * scaling
        return jnp.where(valid, raw, MASKED)

    masked = score()
    top = jnp.max(masked, axis=-1, keepdims=True)
    exponent = jnp.exp(masked - top)
    denominator = jnp.sum(exponent, axis=-1, keepdims=True)
    shares_low = (exponent / denominator).astype(BF16)
    lse = top + jnp.log(denominator)
    attended = jnp.einsum("hqk,khd->qhd", shares_low, value, preferred_element_type=F32)

    def backward(grad):
        grad = grad.reshape(seg, HEADS, head_dim)
        shares = jnp.exp(score() - lse)
        share_grad = jnp.einsum("qhd,khd->hqk", grad, value, preferred_element_type=F32)
        dot = jnp.sum(shares * share_grad, axis=-1, keepdims=True)
        score_grad = (shares * (share_grad - dot)).astype(BF16)
        q_grad = jnp.einsum("hqk,khd->qhd", score_grad, key, preferred_element_type=F32) * scaling
        v_all = jnp.einsum("hqk,qhd->khd", shares.astype(BF16), grad, preferred_element_type=F32)
        k_all = jnp.einsum("hqk,qhd->khd", score_grad, query, preferred_element_type=F32) * scaling
        k_grad, v_grad = (
            lax.psum_scatter(
                part.reshape(full, width).astype(BF16), "patch", scatter_dimension=0, tiled=True
            )
            for part in (k_all, v_all)
        )
        return jnp.concatenate([q_grad.reshape(seg, width).astype(BF16), k_grad, v_grad], axis=1)

    return attended.reshape(seg, width).astype(BF16), backward


def to_heads(values):
    return lax.all_to_all(values, "patch", split_axis=0, concat_axis=0, tiled=True)


def queries_to_heads(triple):
    seg, triple_width = triple.shape
    parts = lax.axis_size("patch")
    own = triple_width // (3 * parts)
    moved = triple.reshape(seg, 3, parts, own).transpose(2, 1, 0, 3).reshape(parts, 3 * seg, own)
    return to_heads(moved)


def weight_grad_kernel(jobs, index, near, away, place_ref, *refs):
    split = len(refs) - len(near) - len(away)
    arrays, outs = refs[:split], refs[split:]
    rows = outs[0].shape[1]

    def member(group, s):
        first, stacked = index[group]
        return arrays[first].at[place_ref[ME] ^ s] if stacked else arrays[first + s]

    sides = (1 - place_ref[Y],) * len(away) + (place_ref[Y],) * len(near)
    start = 0
    for left, left_start, right, right_start, cols in jobs:
        values = [member(right, s)[:, pl.ds(right_start, cols)] for s in range(4)]
        values = jnp.concatenate(values, axis=0)
        for out, side, blocks in zip(outs, sides, away + near):

            def step(slot, carry, out=out, side=side, blocks=blocks, start=start):
                k = blocks[0] + 2 * slot
                if len(blocks) == 4:
                    k = jnp.where(slot < 2, k, 2 * slot - 4)
                source = 2 * (place_ref[Z] ^ k) + side
                group = [member(left, s) for s in range(4)]
                if len(group[0].shape) == 3:
                    factor = [ref[source] for ref in group]
                else:
                    block = pl.ds(pl.multiple_of(left_start + source * rows, rows), rows)
                    factor = [ref[:, block] for ref in group]
                factor = jnp.concatenate(factor, axis=0)
                out[slot, :, start : start + cols] = mm(factor, values, TN).astype(BF16)
                return carry

            lax.fori_loop(0, len(blocks), step, 0)
        start += cols


def weight_grads(place, jobs, groups, rows, near, away):
    arrays, index = [], []
    for group in groups:
        stacked = not isinstance(group, (list, tuple))
        index.append((len(arrays), stacked))
        arrays += [group] if stacked else list(group)
    total = sum(job[-1] for job in jobs)
    shapes = [((len(blocks), rows, total), BF16) for blocks in away + near]
    kernel = functools.partial(weight_grad_kernel, jobs, index, near, away)
    outs = small_call(kernel, place, arrays, shapes, effort=2000, name="weight_grads")
    return outs[len(away) :], outs[: len(away)]


def swap(values, axis, bit):
    return lax.ppermute(values, axis, [(i, i ^ bit) for i in range(lax.axis_size(axis))])


def together(*values):
    return lax.optimization_barrier(values)


def after(value, *others):
    return lax.optimization_barrier((value, *others))[0]


def small_call(kernel, place, arrays, shapes, scratch=(), effort=200, name="small"):
    vmem = pl.BlockSpec(memory_space=pltpu.VMEM)
    return pl.pallas_call(
        kernel,
        out_shape=tuple(jax.ShapeDtypeStruct(dims, dtype) for dims, dtype in shapes),
        in_specs=[pl.BlockSpec(memory_space=pltpu.SMEM)] + [vmem] * len(arrays),
        out_specs=(vmem,) * len(shapes),
        scratch_shapes=list(scratch),
        cost_estimate=cost(int(effort * 10**9)),
        name=name,
    )(place, *arrays)


ME, CORE, X, Y, Z = range(5)


def tokens_of_group(values):
    across = swap(values, "var", 2)
    return values, swap(values, "var", 1), across, swap(across, "var", 1)


def copies_of_group(values):
    return (values,) + tuple(swap(values, "var", bit) for bit in (1, 2, 3))


def slices_of_group(pieces):
    return (pieces[0],) + tuple(swap(pieces[bit], "var", bit) for bit in (1, 2, 3))


def z_pieces(place, near, got):
    _, rows, cols = near.shape

    def kernel(place_ref, near_ref, got_ref, *outs):
        for bit in range(4):
            block = place_ref[Z] ^ bit
            outs[bit][...] = (near_ref[block].astype(F32) + got_ref[block].astype(F32)).astype(BF16)

    return small_call(kernel, place, (near, got), [((rows, cols), BF16)] * 4, name="z_pieces")


def z_exchange(pieces):
    return (pieces[0],) + tuple(swap(pieces[bit], "patch", 2 * bit) for bit in (1, 2, 3))


def z_sum(place, arrays):

    def kernel(place_ref, first, second, third, fourth, out):
        total = first[...].astype(F32) + second[...].astype(F32) + third[...].astype(F32) + fourth[...].astype(F32)
        out[...] = total.astype(BF16)

    return small_call(kernel, place, arrays, [(arrays[0].shape, BF16)], name="z_sum")[0]


def pair_sum(place, near, got):
    def kernel(place_ref, near_ref, got_ref, out):
        for k in range(2):
            out[k] = (near_ref[k].astype(F32) + got_ref[k].astype(F32)).astype(BF16)

    return small_call(kernel, place, (near, got), [(near.shape, BF16)], name="pair_sum")[0]


def z_first_sum(place, near, got, far):
    first = got.shape[0] - 2

    def kernel(place_ref, near_ref, got_ref, far_ref, stay, away):
        for out, k in ((away, 1), (stay, 0)):
            total = near_ref[k].astype(F32) + got_ref[first + k].astype(F32) + far_ref[k].astype(F32)
            out[...] = total.astype(BF16)

    return small_call(kernel, place, (near, got, far), [(near.shape[1:], BF16)] * 2, name="z_first_sum")


def z_last_sum(place, near, got):
    def kernel(place_ref, near_ref, got_ref, out):
        out[...] = (near_ref[...].astype(F32) + got_ref[...].astype(F32)).astype(BF16)

    return small_call(kernel, place, (near, got), [(near.shape, BF16)], name="z_last_sum")[0]


def gather_over_var(own):
    across = swap(own, "var", 2)
    return own, swap(own, "var", 1), across, swap(across, "var", 1)


def join(place, pieces, widths, stacked):
    rows = pieces[0].shape[0]

    def kernel(place_ref, *refs):
        start = 0
        for k, (out, size) in enumerate(zip(refs[4:], widths)):
            for s in range(4):
                v = place_ref[ME] ^ s
                values = refs[s][:, start : start + size].astype(F32)
                if k < stacked:
                    out[v] = values
                else:
                    out[:, pl.ds(pl.multiple_of(v * size, size), size)] = values
            start += size

    shapes = [((4, rows, size) if k < stacked else (rows, 4 * size), F32) for k, size in enumerate(widths)]
    return small_call(kernel, place, pieces, shapes, name="join")


def sum_over_all(place, stay, away, hooks, marks):
    _, rows, cols = stay.shape
    half = rows // 2
    size = half // 4
    hooks = iter(hooks)

    def core_kernel(place_ref, stay_ref, got_ref, stay_out, away_out):
        for out, which in ((away_out, 1 - place_ref[X]), (stay_out, place_ref[X])):
            out[...] = (stay_ref[which].astype(F32) + got_ref[which].astype(F32)).astype(BF16)

    got = next(hooks)(swap(away, "var", 1))
    stay, away = small_call(core_kernel, place, (stay, got), [((rows, cols), BF16)] * 2, name="core_sum")
    marks.append(stay)

    def x_kernel(place_ref, stay_ref, got_ref, stay_out, away_out):
        for out, which in ((away_out, 1 - place_ref[Y]), (stay_out, place_ref[Y])):
            out[...] = (stay_ref[which].astype(F32) + got_ref[which].astype(F32)).astype(BF16)

    got = next(hooks)(swap(away, "var", 2))
    halves = (2, half, cols)
    stay, away = small_call(
        x_kernel, place, (stay.reshape(halves), got.reshape(halves)), [((half, cols), BF16)] * 2, name="x_sum"
    )
    marks.append(stay)
    got = next(hooks)(swap(away, "patch", 1))
    pieces = z_exchange(z_pieces(place, stay.reshape(4, size, cols), got.reshape(4, size, cols)))
    kept = z_sum(place, next(hooks)(pieces))

    def z_kernel(place_ref, *refs):
        for s in range(4):
            refs[4][place_ref[Z] ^ s] = refs[s][...]

    arrays = (kept,) + tuple(swap(kept, "patch", 2 * bit) for bit in (1, 2, 3))
    own = small_call(z_kernel, place, next(hooks)(arrays), [((4, size, cols), BF16)], name="z_join")[0]

    def y_kernel(place_ref, own_ref, other_ref, out):
        out[place_ref[Y]] = own_ref[...]
        out[1 - place_ref[Y]] = other_ref[...]

    own = own.reshape(half, cols)
    arrays = (own, next(hooks)(swap(own, "patch", 1)))
    full = small_call(y_kernel, place, arrays, [(halves, BF16)], name="y_join")[0].reshape(rows, cols)

    across = next(hooks)(swap(full, "var", 2))
    return full, swap(full, "var", 1), across, swap(across, "var", 1)


def middle_kernel(
    sub,
    place_ref,
    att_ref,
    front_ref,
    valid_ref,
    og_ref,
    tout_ref,
    gain_ref,
    win_ref,
    wout_ref,
    block_ref,
    late_ref,
    *refs,
):
    actives, middles = refs[0:4], refs[4:8]
    grad_ref, after_ref, gain_grad_ref, residual_ref, unit_ref, rate_ref, acc_ref, back_ref, wide_ref, branch_ref = refs[8:]
    step = pl.program_id(0)
    seg, width = front_ref.shape
    parts = att_ref.shape[0]
    own = width // parts
    me = place_ref[0]
    block = win_ref.shape[1]
    slot = block // (4 * sub)
    quarter = width // 4
    hidden = slot * sub * pl.num_programs(0)

    @pl.when(step == 0)
    def _():
        for p in range(parts):
            branch_ref[:, p * own : (p + 1) * own] = att_ref[p]
        after = front_ref[...] + mm(branch_ref[...], tout_ref[...])
        residual_ref[...] = after
        center = after - jnp.mean(after, axis=1, keepdims=True)
        rate = lax.rsqrt(jnp.mean(center * center, axis=1, keepdims=True) + EPSILON)
        unit = center * rate
        unit_ref[...] = unit
        rate_ref[...] = rate
        late_ref[...] = (unit * gain_ref[...]).astype(BF16)
        acc_ref[...] = jnp.zeros_like(acc_ref)
        back_ref[...] = jnp.zeros_like(back_ref)

    inner = mm(late_ref[...], win_ref[...])
    cumulative = 0.5 * (1.0 + lax.erf(inner * math.sqrt(0.5)))
    active = (inner * cumulative).astype(BF16)
    acc_ref[...] += mm(active, wout_ref[...])
    slope = cumulative + inner * (jnp.exp(-0.5 * inner * inner) * (1.0 / math.sqrt(2.0 * math.pi)))
    inner_grad = (mm(og_ref[...], wout_ref[...], NT) * slope).astype(BF16)
    back_ref[...] += mm(inner_grad, win_ref[...], NT)
    wide_ref[...] = active
    for q in range(sub):
        cols = pl.ds(pl.multiple_of((step * sub + q) * slot, slot), slot)
        for s in range(4):
            actives[s][:, cols] = wide_ref[:, pl.ds(pl.multiple_of((4 * q + (me ^ s)) * slot, slot), slot)]
    owner = step * block // hidden
    place = pl.ds(pl.multiple_of(step * block - owner * hidden, block), block)
    for s in range(4):

        @pl.when((me ^ s) == owner)
        def _(s=s):
            middles[s][:, place] = inner_grad

    @pl.when(step == pl.num_programs(0) - 1)
    def _():
        valid = valid_ref[...]
        block_ref[...] = ((residual_ref[...] + acc_ref[...]) * valid).astype(BF16)
        unit = unit_ref[...]
        back = back_ref[...]
        gain_grad_ref[...] = jnp.sum(back * unit, axis=0, keepdims=True)
        scaled = back * gain_ref[...]
        inside = jnp.mean(scaled * unit, axis=1, keepdims=True)
        total = rate_ref[...] * (scaled - jnp.mean(scaled, axis=1, keepdims=True) - unit * inside)
        total = og_ref[...].astype(F32) + total
        after_ref[...] = total
        branch_ref[...] = total.astype(BF16)
        for s in range(4):
            start = pl.multiple_of((me ^ s) * quarter, quarter)
            middles[s][:, hidden:] = branch_ref[:, pl.ds(start, quarter)]
        turned = mm(branch_ref[...], tout_ref[...], NT).astype(BF16)
        for p in range(parts):
            grad_ref[p] = turned[:, p * own : (p + 1) * own]


def middle(place, attended, front_out, valid, out_grad, trunk_out, gain, mlp_in, mlp_out):
    seg, width = front_out.shape
    hidden = mlp_in.shape[1]
    parts = attended.shape[0]
    sub = 2
    block = hidden * sub // parts
    shape = jax.ShapeDtypeStruct

    def still(*dims):
        return pl.BlockSpec(dims, lambda i: (0,) * len(dims))

    piece, wider = shape((seg, hidden // 4), BF16), shape((seg, hidden // 4 + width // 4), BF16)
    return pl.pallas_call(
        functools.partial(middle_kernel, sub),
        grid=(parts // sub,),
        out_shape=(
            shape((seg, width), BF16),
            shape((seg, width), BF16),
            *((piece,) * 4),
            *((wider,) * 4),
            shape(attended.shape, BF16),
            shape((seg, width), F32),
            shape((1, width), F32),
        ),
        in_specs=[
            pl.BlockSpec(memory_space=pltpu.SMEM),
            still(*attended.shape),
            still(seg, width),
            still(seg, 1),
            still(seg, width),
            still(width, width),
            still(1, width),
            pl.BlockSpec((width, block), lambda i: (0, i)),
            pl.BlockSpec((block, width), lambda i: (i, 0)),
        ],
        out_specs=(
            still(seg, width),
            still(seg, width),
            *((still(*piece.shape),) * 4),
            *((still(*wider.shape),) * 4),
            still(*attended.shape),
            still(seg, width),
            still(1, width),
        ),
        scratch_shapes=[
            pltpu.VMEM((seg, width), F32),
            pltpu.VMEM((seg, width), F32),
            pltpu.VMEM((seg, 1), F32),
            pltpu.VMEM((seg, width), F32),
            pltpu.VMEM((seg, width), F32),
            pltpu.VMEM((seg, block), BF16),
            pltpu.VMEM((seg, width), BF16),
        ],
        compiler_params=pltpu.CompilerParams(dimension_semantics=("arbitrary",)),
        cost_estimate=cost(100000000000),
        name="trunk_middle",
    )(place, attended, front_out, valid, out_grad, trunk_out, gain, mlp_in, mlp_out)


def trunk_back_kernel(
    place_ref, grads_ref, front_ref, gain_ref, after_ref, valid_ref, aout_ref, wqkv_ref, mixed_ref, gain_grad_ref, *rest
):
    stack_ref, triple_ref, back_ref = rest
    step = pl.program_id(0)
    parts = grads_ref.shape[0]
    seg, width = front_ref.shape
    own = width // parts
    me = place_ref[ME]

    @pl.when(step == 0)
    def _():
        for c in range(3):
            for p in range(parts):
                triple_ref[c, :, p * own : (p + 1) * own] = grads_ref[p, c * seg : (c + 1) * seg, :]
        back_ref[...] = jnp.zeros_like(back_ref)

    back_ref[...] += mm(triple_ref[step], wqkv_ref[...], NT)

    @pl.when(step == pl.num_programs(0) - 1)
    def _():
        front = front_ref[...]
        center = front - jnp.mean(front, axis=1, keepdims=True)
        rate = lax.rsqrt(jnp.mean(center * center, axis=1, keepdims=True) + EPSILON)
        unit = center * rate
        back = back_ref[...]
        gain_grad_ref[...] = jnp.sum(back * unit, axis=0, keepdims=True)
        scaled = back * gain_ref[...]
        inside = jnp.mean(scaled * unit, axis=1, keepdims=True)
        total = rate * (scaled - jnp.mean(scaled, axis=1, keepdims=True) - unit * inside)
        total = ((after_ref[...] + total) * valid_ref[...]).astype(BF16)
        mixed_ref[...] = mm(total, aout_ref[...], NT).astype(BF16)
        part = width // 4
        for v in range(4):
            stack_ref[v, :, 3 * part :] = total[:, v * part : (v + 1) * part]
            for k in range(3):
                block = 3 * v + k
                source = triple_ref[block // 4, :, block % 4 * part : (block % 4 + 1) * part]
                stack_ref[v, :, k * part : (k + 1) * part] = source


def trunk_back(place, grads, front_out, gain, after_grad, valid, agg_out, trunk_qkv):
    seg, width = front_out.shape
    shape = jax.ShapeDtypeStruct

    def still(*dims):
        return pl.BlockSpec(dims, lambda i: (0,) * len(dims))

    piece = shape((seg, width), BF16)
    return pl.pallas_call(
        trunk_back_kernel,
        grid=(3,),
        out_shape=(piece, shape((1, width), F32), shape((4, seg, width), BF16)),
        in_specs=[
            pl.BlockSpec(memory_space=pltpu.SMEM),
            still(*grads.shape),
            still(seg, width),
            still(1, width),
            still(seg, width),
            still(seg, 1),
            still(width, width),
            pl.BlockSpec((width, width), lambda i: (0, i)),
        ],
        out_specs=(still(seg, width), still(1, width), still(4, seg, width)),
        scratch_shapes=[
            pltpu.VMEM((3, seg, width), BF16),
            pltpu.VMEM((seg, width), F32),
        ],
        compiler_params=pltpu.CompilerParams(dimension_semantics=("arbitrary",)),
        cost_estimate=cost(100000000000),
        name="trunk_back",
    )(place, grads, front_out, gain, after_grad, valid, agg_out, trunk_qkv)


def front_last_kernel(
    pixels,
    place_ref,
    m0,
    m1,
    m2,
    m3,
    weight_ref,
    embed_ref,
    weight_own_ref,
    embed_own_ref,
    value_rows_ref,
    key_query_ref,
    key_ref,
    aggq_ref,
    query_rows_ref,
    query_own_ref,
    value_out,
    patch_out,
    embed_out,
    key_out,
    query_out,
    agg_query_out,
    norm_one_out,
    norm_two_out,
    m_ref,
    sum_ref,
):
    rows, width = weight_ref.shape
    own = weight_own_ref.shape[1]
    size = m0.shape[1]
    head_dim = width // HEADS
    scaling = 1.0 / math.sqrt(head_dim)
    for s, ref in enumerate((m0, m1, m2, m3)):
        v = place_ref[ME] ^ s
        m_ref[:, pl.ds(pl.multiple_of((v % 2 * 2 + v // 2) * size, size), size)] = ref[...]
    m_sum, me_sum = m_ref[0:rows, :], m_ref[rows : rows + VARS, :]
    value_out[...] = mm(weight_own_ref[...], m_sum, TN) + mm(embed_own_ref[...], me_sum, TN)
    s_all = m_ref[rows + VARS : rows + VARS + HEADS, :]
    twice = jnp.concatenate([s_all, s_all], axis=0)
    patch_out[...] = mm(m_sum, value_rows_ref[...], NT) + mm(twice[:, 0:rows], key_query_ref[...], TN)
    embed_out[...] = mm(me_sum, value_rows_ref[...], NT) + mm(
        twice[:, rows : rows + VARS], key_query_ref[...], TN
    )
    key_sum = (mm(s_all[:, 0:rows], weight_ref[...]) + mm(s_all[:, rows : rows + VARS], embed_ref[...])) * scaling
    sum_ref[...] = key_sum
    lane = lax.broadcasted_iota(jnp.int32, (HEADS, width), 1) // head_dim
    mine = lane == lax.broadcasted_iota(jnp.int32, (HEADS, width), 0)
    start = pl.multiple_of((place_ref[Z] * 2 + place_ref[Y]) * own, own)
    head_rows = jnp.where(mine, aggq_ref[...], 0.0)
    key_out[...] = mm(sum_ref[:, pl.ds(start, own)], head_rows, TN, precision=HIGHEST)
    crossed = mm(jnp.concatenate(split_high_low(key_sum), axis=0), key_ref[...])
    crossed = crossed[0:HEADS, :] + crossed[HEADS:, :]
    aggq_grad = jnp.sum(jnp.where(mine, crossed, 0.0), axis=0, keepdims=True)
    query_out[...] = query_own_ref[...] * aggq_grad
    high, low = split_high_low(aggq_grad)
    agg_query_out[...] = mm(high, query_rows_ref[...], NT) + mm(low, query_rows_ref[...], NT)
    row = lax.broadcasted_iota(jnp.int32, (HEADS, own), 0)
    tail = s_all[:, width - own :].astype(F32)
    for k in range(own // head_dim):
        line = jnp.sum(jnp.where(row == start // head_dim + k, tail, 0.0), axis=0, keepdims=True)
        norm_one_out[:, k * head_dim : (k + 1) * head_dim] = line[:, 0:head_dim]
        norm_two_out[:, k * head_dim : (k + 1) * head_dim] = line[:, head_dim:own]


def front_last(place, pieces, arrays):
    weight_rows, own_weight, value_rows = arrays[0], arrays[2], arrays[4]
    rows, width = weight_rows.shape
    own = own_weight.shape[1]
    tall = pieces[0].shape[0]
    shapes = [((own, width), F32), ((rows, own), F32), ((VARS, own), F32)] + [((own, width), F32)] * 2
    shapes += [((1, own), F32)] * 3
    return small_call(
        functools.partial(front_last_kernel, rows // VARS),
        place,
        (*pieces, *arrays),
        shapes,
        scratch=[pltpu.VMEM((tall, width), BF16), pltpu.VMEM((HEADS, width), F32)],
        name="front_last",
    )


def local(
    input_field,
    counts,
    var_ids,
    patch_weight,
    var_embed,
    agg_query,
    query_proj,
    key_proj,
    value_proj,
    agg_out,
    norm_one,
    trunk_qkv,
    trunk_out,
    norm_two,
    mlp_in,
    mlp_out,
    cotangent,
):
    patches, group = lax.axis_size("patch"), lax.axis_size("var")
    fast = (patches, group) == (8, 4)
    me, spot = lax.axis_index("var"), lax.axis_index("patch")
    place = jnp.stack([me, me % 2, me // 2, spot % 2, spot // 2]).astype(jnp.int32)
    var_index = lax.axis_index("var")
    patch_index = lax.axis_index("patch")
    all_rows, seg, var_local, pixels = input_field.shape
    width = agg_out.shape[0]
    head_dim = width // HEADS
    hidden = mlp_in.shape[1]
    scaling = 1.0 / math.sqrt(head_dim)

    turned = input_field.transpose(0, 2, 3, 1).reshape(all_rows, var_local * pixels, seg)
    own_field = lax.all_to_all(turned, "var", split_axis=0, concat_axis=1, tiled=True)
    own_field = own_field.reshape(VARS * pixels, seg)
    own_ids = lax.dynamic_slice_in_dim(var_ids, var_index, 1, 0)
    own_count = lax.dynamic_slice_in_dim(counts, var_index, 1, 0)
    positions = patch_index * seg + jnp.arange(seg, dtype=jnp.int32)
    valid_rows = (positions < own_count).astype(F32)[:, None]
    out_grad = cotangent.reshape(seg, width).astype(F32) * valid_rows
    out_grad_low = out_grad.astype(BF16)

    weight_rows = patch_weight.reshape(VARS * pixels, width)
    agg_q = mm(agg_query[None], query_proj)[0]
    in_head = jnp.arange(width, dtype=jnp.int32)[:, None] // head_dim == jnp.arange(HEADS)[None, :]
    head_query = jnp.where(in_head, agg_q[:, None] * scaling, 0.0)
    key_query = mm(key_proj, jnp.concatenate(split_high_low(head_query), axis=1))
    key_query = key_query[:, :HEADS] + key_query[:, HEADS:]
    key_query_parts = jnp.concatenate(split_high_low(key_query), axis=1)
    score_weight = mm(key_query_parts, weight_rows, (((0,), (1,)), ((), ())))
    score_weight = score_weight[:HEADS] + score_weight[HEADS:]
    score_embed = mm(key_query_parts, var_embed, (((0,), (1,)), ((), ())))
    score_embed = score_embed[:HEADS] + score_embed[HEADS:]
    vwt = mm(value_proj, weight_rows, (((0,), (1,)), ((), ()))).astype(BF16)
    vet = mm(value_proj, var_embed, (((0,), (1,)), ((), ()))).astype(BF16)

    own_width = width // patches
    start = patch_index * own_width

    def own_cols(values):
        return lax.dynamic_slice_in_dim(values, start, own_width, 1)

    def own_rows(values):
        return lax.dynamic_slice_in_dim(values, start, own_width, 0)

    def own_query(values):
        return lax.dynamic_slice_in_dim(values, start, own_width, 0).astype(F32)[:, None]

    def last_operands(ready):
        weights, embeds, values, queries, line, key_queries, _ = together(
            weight_rows, var_embed, value_proj, query_proj, agg_query, key_query, ready
        )
        return (
            weights,
            embeds,
            own_cols(weights),
            own_cols(embeds),
            own_rows(values),
            jnp.concatenate(split_high_low(own_rows(key_queries)), axis=1).T,
            key_proj,
            agg_q[None],
            own_rows(queries),
            own_query(line),
        )

    x_own, shares, mixed_low, spread = front_forward(own_ids, own_field, score_weight, score_embed, vwt, vet)

    front_out = mm(mixed_low, agg_out) * valid_rows
    normed_one, norm_one_pull = jax.vjp(layer_norm, front_out, norm_one.astype(F32))
    normed_one_low = normed_one.astype(BF16)
    triple = mm(normed_one_low, trunk_qkv).astype(BF16)
    part = width // group
    quarter = hidden // group
    zs = patches // 2
    ready = after(value_proj, triple)
    vw = mm(weight_rows, ready).astype(BF16)
    ve = mm(var_embed, ready).astype(BF16)
    if fast:
        early = tokens_of_group(jnp.concatenate([out_grad_low, mixed_low, normed_one_low], axis=1))
        qkv, vw, ve, *arrays = together(queries_to_heads(triple), vw, ve, *last_operands(triple))
        count = own_count.reshape(1, 1)
        heads, lse = attend_forward(count, qkv, head_dim)
        attended = to_heads(heads.reshape(patches, seg, own_width))
        results = middle(
            place,
            attended,
            front_out,
            valid_rows,
            out_grad_low,
            trunk_out,
            norm_two.astype(F32)[None],
            mlp_in,
            mlp_out,
        )
        attended_group = copies_of_group(attended)
        results = together(*results, *attended_group, *early)
        attended_group, early = results[13:17], results[17:]
        block_out, normed_two_low, grads, after_grad, norm_two_grad = (results[k] for k in (0, 1, 10, 11, 12))
        block_out = block_out[None]
        grads = to_heads(grads)
        active_group = slices_of_group(results[2:6])
        across = swap(normed_two_low, "var", 2)
        result = attend_backward(count, qkv, grads.reshape(patches * seg, own_width), lse, head_dim)
        result, across, *rest = together(result, across, *active_group, *results[6:10])
        active_group, middle_group = rest[:4], slices_of_group(rest[4:])
        normed_group = (normed_two_low, swap(normed_two_low, "var", 1), across, swap(across, "var", 1))
        result = to_heads(result)
        pairs, whole_order = ((1, 3), (0, 2)), ((1, 3, 0, 2),)
        jobs = ((0, 0, 1, 0, width),)
        near_one, away_one = weight_grads(place, jobs, (active_group, early), own_width, pairs, whole_order)
        jobs = ((0, 0, 2, 0, quarter), (1, 0, 2, quarter, part))
        groups = (together(normed_group[0], *near_one)[:1] + normed_group[1:], attended_group, middle_group)
        near_two, away_two = weight_grads(place, jobs, groups, own_width, pairs, pairs)
        result = after(result, *near_two)
        one = {"near": near_one, "got": swap(away_one[0], "patch", 1)}
        two = {"near": near_two, "away": away_two}
        mixed_grad, norm_one_grad, stack = trunk_back(
            place, result, front_out, norm_one.astype(F32)[None], after_grad, valid_rows, agg_out, trunk_qkv
        )
        one["far"] = pair_sum(place, after(one["near"][0], mixed_grad), one["got"])
        mixed_grad = after(mixed_grad, one["far"])
        last_group = lax.all_to_all(stack, "var", split_axis=0, concat_axis=0, tiled=True)
    else:
        attended, attention_pull = gathered_attention(triple, own_count, head_dim)
        after_attn = front_out + mm(attended, trunk_out)
        normed_two, norm_two_pull = jax.vjp(layer_norm, after_attn, norm_two.astype(F32))
        normed_two_low = normed_two.astype(BF16)
        inner = mm(normed_two_low, mlp_in)
        active, gelu_pull = jax.vjp(gelu_exact, inner)
        active_low = active.astype(BF16)
        result = after_attn + mm(active_low, mlp_out)
        block_out = (result * valid_rows).astype(BF16)[None]
        inner_grad = gelu_pull(mm(out_grad_low, mlp_out, NT))[0].astype(BF16)
        normed_two_grad = mm(inner_grad, mlp_in, NT)
        after_ln_grad, norm_two_grad = norm_two_pull(normed_two_grad)
        after_grad = out_grad + after_ln_grad
        branch_low = after_grad.astype(BF16)
        triple_grad = attention_pull(mm(branch_low, trunk_out, NT).astype(BF16))
        normed_one_grad = mm(triple_grad, trunk_qkv, NT)
        front_ln_grad, norm_one_grad = norm_one_pull(normed_one_grad)
        agg_grad = ((after_grad + front_ln_grad) * valid_rows).astype(BF16)
        mixed_grad = mm(agg_grad, agg_out, NT).astype(BF16)
        norm_one_grad, norm_two_grad = norm_one_grad[None], norm_two_grad[None]

    field_low, *m_parts = front_backward(
        fast, place, own_ids, x_own, shares, mixed_grad, vw, ve, spread, norm_one_grad, norm_two_grad
    )

    field_low = field_low.reshape(group, var_local * pixels, seg)
    field_grad = None if fast else lax.all_to_all(field_low, "var", split_axis=0, concat_axis=0, tiled=True)

    if fast:
        m_stay, m_away, two["first"], last_group = together(*m_parts, swap(two["away"][0], "patch", 1), last_group)
        m_parts = (m_stay, m_away)
        two["far"] = pair_sum(place, two["near"][0], two["first"])
        last, marks = {}, []

        def core_done(values):
            return values

        def x_done(values):
            far = swap(one["far"], "patch", 2)
            far, near, _ = together(far, one["near"][1], *marks)
            one["pair"] = z_first_sum(place, near, one["got"], far)
            return after(values, one["pair"][0])

        def y_done(values):
            jobs = ((0, 2 * width, 1, 0, 3 * part), (0, width, 1, 3 * part, part))
            groups = (early, after(last_group, marks[-1]))
            last["near"], last["away"] = weight_grads(place, jobs, groups, own_width, pairs, whole_order)
            got = swap(after(two["away"][1], two["first"]), "patch", 1)
            values, got, far, *_ = together(values, got, swap(two["far"], "patch", 2), *last["near"])
            two["pair"] = z_first_sum(place, two["near"][1], got, far)
            return values

        def z_done(values):
            near, away = one["pair"]
            *values, got, _ = together(*values, swap(away, "patch", 4), two["pair"][0])
            one["own"] = z_last_sum(place, near, got)
            return values

        def b_done(values):
            near, away = two["pair"]
            *values, last["got"], got = together(*values, swap(last["away"][0], "patch", 1), swap(away, "patch", 4))
            late = after(field_low, last["got"])
            last["field"] = lax.all_to_all(late, "var", split_axis=0, concat_axis=0, tiled=True)
            last["far"] = pair_sum(place, last["near"][0], last["got"])
            two["own"] = z_last_sum(place, near, got)
            return [after(values[0], last["far"]), *values[1:]]

        def y_back(values):
            values, one["across"], last["field"] = together(values, swap(one["own"], "var", 2), last["field"])
            return values

        def var_done(values):
            far, across = swap(last["far"], "patch", 2), swap(two["own"], "var", 2)
            near, away = z_first_sum(place, last["near"][1], last["got"], far)
            two["parts"] = (two["own"], swap(two["own"], "var", 1), across, swap(across, "var", 1))
            last["own"] = z_last_sum(place, near, swap(away, "patch", 4))
            own, across = one["own"], one["across"]
            values, inner, corner, _ = together(values, swap(own, "var", 1), swap(across, "var", 1), near)
            one["parts"] = (own, inner, across, corner)
            return values

        m_pieces = sum_over_all(place, *m_parts, (core_done, x_done, y_done, z_done, b_done, y_back, var_done), marks)
        field_grad = last["field"]
        (mlp_out_grad,) = join(place, one["parts"], (width,), 1)
        mlp_in_grad, trunk_out_grad = join(place, two["parts"], (quarter, part), 0)
        mlp_out_grad = mlp_out_grad.reshape(hidden // patches, width)
        trunk_qkv_grad, agg_out_grad = join(place, gather_over_var(last["own"]), (3 * part, part), 0)
    else:

        def slices(values):
            values = values.reshape(seg, group, values.shape[1] // group).transpose(1, 0, 2)
            return lax.all_to_all(values, "var", split_axis=0, concat_axis=0, tiled=True)

        def everyone(values):
            return lax.all_gather(values, "var", axis=0, tiled=True)

        def total(left, right):
            value = mm(left.reshape(-1, left.shape[-1]), right.reshape(-1, right.shape[-1]), TN).astype(BF16)
            value = lax.psum_scatter(value, "patch", scatter_dimension=0, tiled=True)
            return lax.all_gather(value, "var", axis=0)

        def joined(value):
            return value.transpose(1, 0, 2).reshape(value.shape[1], -1).astype(F32)

        size = hidden // (patches * group)
        active_rows = active_low.reshape(seg, patches, group, size).transpose(0, 2, 1, 3).reshape(seg, hidden)
        mlp_out_grad = total(slices(active_rows), everyone(out_grad_low)).reshape(hidden // patches, width).astype(F32)
        mlp_in_grad = joined(total(everyone(normed_two_low), slices(inner_grad)))
        trunk_out_grad = joined(total(everyone(attended), slices(branch_low)))
        trunk_qkv_grad = joined(total(everyone(normed_one_low), slices(triple_grad)))
        agg_out_grad = joined(total(everyone(mixed_low), slices(agg_grad)))
        m_all = lax.psum(m_parts[0], ("patch", "var")).transpose(1, 0, 2).reshape(-1, width)
    if fast:
        value_proj_grad, patch_grad, embed_grad, key_proj_grad, query_proj_grad, *lines = front_last(
            place, m_pieces, arrays
        )
        agg_query_grad, norm_one_grad, norm_two_grad = (line[0] for line in lines)
    else:
        value_rows, key_query_rows = own_rows(value_proj), own_rows(key_query)
        m_sum, me_sum = m_all[: VARS * pixels], m_all[VARS * pixels : VARS * pixels + VARS]
        s_rows = m_all[VARS * pixels + VARS :].astype(F32)
        s_all = s_rows[:, : VARS * pixels]
        se_all = s_rows[:, VARS * pixels : VARS * pixels + VARS]
        norm_sums = s_rows[:, width - 2 * head_dim :]
        value_proj_grad = mm(own_cols(weight_rows), m_sum, TN) + mm(own_cols(var_embed), me_sum, TN)
        patch_grad = mm(m_sum, value_rows, NT) + mm(
            s_all, key_query_rows, (((0,), (1,)), ((), ())), precision=HIGHEST
        )
        embed_grad = mm(me_sum, value_rows, NT) + mm(
            se_all, key_query_rows, (((0,), (1,)), ((), ())), precision=HIGHEST
        )
        key_sum = (mm(s_all.astype(BF16), weight_rows) + mm(se_all.astype(BF16), var_embed)) * scaling
        head_rows = jnp.where(in_head.T, agg_q[None, :], 0.0)
        key_proj_grad = mm(own_cols(key_sum), head_rows, TN, precision=HIGHEST)
        crossed = mm(jnp.concatenate(split_high_low(key_sum), axis=0), key_proj)
        crossed = crossed[:HEADS] + crossed[HEADS:]
        aggq_grad = jnp.sum(jnp.where(in_head.T, crossed, 0.0), axis=0)
        query_proj_grad = own_query(agg_query) * aggq_grad[None, :]
        agg_query_grad = jnp.sum(own_rows(query_proj).astype(F32) * aggq_grad[None, :], axis=1)
        norm_one_grad = lax.dynamic_slice_in_dim(norm_sums[:, :head_dim].reshape(width), start, own_width, 0)
        norm_two_grad = lax.dynamic_slice_in_dim(norm_sums[:, head_dim:].reshape(width), start, own_width, 0)
    patch_grad = patch_grad.reshape(VARS, pixels, own_width)
    field_grad = field_grad.reshape(all_rows, var_local, pixels, seg).transpose(0, 3, 1, 2)
    return (
        block_out,
        field_grad,
        patch_grad,
        embed_grad,
        agg_query_grad,
        query_proj_grad,
        key_proj_grad,
        value_proj_grad,
        agg_out_grad,
        norm_one_grad,
        trunk_qkv_grad,
        trunk_out_grad,
        norm_two_grad,
        mlp_in_grad,
        mlp_out_grad,
    )


def solution(mesh):
    whole = P()
    placed = (P(None, "patch", "var", None),) + (whole,) * 15 + (P("var", "patch", None),)
    rows = P("patch", None)
    return jax.shard_map(
        local,
        mesh=mesh,
        in_specs=placed,
        out_specs=(
            P("var", "patch", None),
            P(None, "patch", "var", None),
            P(None, None, "patch"),
            P(None, "patch"),
            P("patch"),
            rows,
            rows,
            rows,
            rows,
            P("patch"),
            rows,
            rows,
            P("patch"),
            rows,
            rows,
        ),
        check_vma=False,
    )
```

```python
import functools
import math

import jax
import jax.numpy as jnp
from jax import lax
from jax.experimental import pallas as pl
from jax.experimental.pallas import tpu as pltpu
from jax.sharding import PartitionSpec as P

HEADS = 16
VARS = 48
EPSILON = 1e-05
MASKED = -1e30
HIGHEST = lax.Precision.HIGHEST
BF16 = jnp.bfloat16
F32 = jnp.float32
NN = (((1,), (0,)), ((), ()))
NT = (((1,), (1,)), ((), ()))
TN = (((0,), (0,)), ((), ()))


def cost(flops):
    return pl.CostEstimate(flops=flops, bytes_accessed=1 << 20, transcendentals=0)


def mm(a, b, dims=NN, precision=None):
    return lax.dot_general(a, b, dims, precision=precision, preferred_element_type=F32)


def layer_norm(values, gain_vec):
    average = jnp.mean(values, axis=-1, keepdims=True)
    center = values - average
    spread = jnp.mean(center * center, axis=-1, keepdims=True)
    return center * lax.rsqrt(spread + EPSILON) * gain_vec


def gelu_exact(values):
    return jax.nn.gelu(values, approximate=False)


def split_high_low(values):
    high = values.astype(BF16)
    return high, (values - high.astype(F32)).astype(BF16)


def front_forward_kernel(
    pixels, ids_ref, field_ref, weight_ref, bias_ref, vwt_ref, vet_ref, x_ref, p_ref, mixed_ref, spread_ref, mt_ref
):
    seg = field_ref.shape[1]
    head_dim = mixed_ref.shape[1] // HEADS
    for slot in range(VARS):
        start = pl.multiple_of(ids_ref[0, slot] * pixels, pixels)
        x_ref[pl.ds(start, pixels), :] = field_ref[slot * pixels : (slot + 1) * pixels, :]
    rows = VARS * pixels
    mine = lax.broadcasted_iota(jnp.int32, (VARS, rows), 1) // pixels
    mine = mine == lax.broadcasted_iota(jnp.int32, (VARS, rows), 0)
    bias = bias_ref[...].T
    parts = []
    for h in range(HEADS):
        spread = jnp.where(mine, weight_ref[h : h + 1, :], 0.0).astype(BF16)
        spread_ref[h * VARS : (h + 1) * VARS, :] = spread
        parts.append(mm(spread, x_ref[...]) + bias[:, h : h + 1])
    scores = jnp.stack(parts)
    top = jnp.max(scores, axis=1, keepdims=True)
    exponent = jnp.exp(scores - top)
    total = jnp.sum(exponent, axis=1, keepdims=True)
    p_ref[...] = (exponent * (1.0 / total)).reshape(HEADS * VARS, seg)

    def head(h, carry):
        shares = p_ref[pl.ds(pl.multiple_of(h * VARS, VARS), VARS), :]
        pix = x_ref[...].astype(F32).reshape(VARS, pixels, seg)
        scaled = (pix * shares[:, None, :]).astype(BF16).reshape(VARS * pixels, seg)
        rows = pl.ds(pl.multiple_of(h * head_dim, head_dim), head_dim)
        mt_ref[rows, :] = mm(vwt_ref[rows, :], scaled) + mm(vet_ref[rows, :], shares.astype(BF16))
        return carry

    lax.fori_loop(0, HEADS, head, 0, unroll=4)
    mixed_ref[...] = mt_ref[...].T.astype(BF16)


def front_forward(own_ids, own_field, score_weight, bias, vwt, vet):
    rows, seg = own_field.shape
    width = vwt.shape[0]
    vmem = pl.BlockSpec(memory_space=pltpu.VMEM)
    return pl.pallas_call(
        functools.partial(front_forward_kernel, rows // VARS),
        out_shape=(
            jax.ShapeDtypeStruct((rows, seg), BF16),
            jax.ShapeDtypeStruct((HEADS * VARS, seg), F32),
            jax.ShapeDtypeStruct((seg, width), BF16),
            jax.ShapeDtypeStruct((HEADS * VARS, rows), BF16),
        ),
        in_specs=[pl.BlockSpec(memory_space=pltpu.SMEM)] + [vmem] * 5,
        out_specs=(vmem,) * 4,
        scratch_shapes=[pltpu.VMEM((width, seg), F32)],
        cost_estimate=cost(60000000000),
        name="front_forward",
    )(own_ids, own_field, score_weight, bias, vwt, vet)


def front_backward_kernel(
    pixels,
    fast,
    place_ref,
    ids_ref,
    x_ref,
    p_ref,
    mg_ref,
    vw_ref,
    ve_ref,
    spread_ref,
    norm_one_ref,
    norm_two_ref,
    field_ref,
    *rest,
):
    rows, seg = x_ref.shape
    m_refs, (fs_ref, dx_ref, s_ref) = rest[:-3], rest[-3:]
    size = m_refs[0].shape[-1]

    def quarter_of(quarter, store):
        if not fast:
            store(m_refs[0].at[quarter])
            return
        mine = quarter // 2 == place_ref[CORE]
        pl.when(mine)(lambda: store(m_refs[0].at[quarter % 2]))
        pl.when(jnp.logical_not(mine))(lambda: store(m_refs[1].at[quarter % 2]))
    width = mg_ref.shape[1]
    head_dim = width // HEADS
    pair_dim = 2 * head_dim
    lane = lax.broadcasted_iota(jnp.int32, (seg, pair_dim), 1)
    dx_ref[...] = jnp.zeros_like(dx_ref)
    pairs = size // pair_dim

    def pair(q, carry):
        cols = pl.ds(pl.multiple_of(q * pair_dim, pair_dim), pair_dim)
        grad = mg_ref[:, cols]
        none = jnp.zeros_like(grad)
        both = jnp.concatenate(
            [jnp.where(lane < head_dim, grad, none), jnp.where(lane >= head_dim, grad, none)], axis=0
        )
        inner = mm(vw_ref[:, cols], both, NT)
        inner_e = mm(ve_ref[:, cols], both, NT)
        pix = x_ref[...].astype(F32).reshape(VARS, pixels, seg)
        scaled, weights = [], []
        for k in range(2):
            hrows = pl.ds(pl.multiple_of((2 * q + k) * VARS, VARS), VARS)
            shares = p_ref[hrows, :]
            part = inner[:, k * seg : (k + 1) * seg].reshape(VARS, pixels, seg)
            share_grad = jnp.sum(pix * part, axis=1) + inner_e[:, k * seg : (k + 1) * seg]
            delta = jnp.sum(shares * share_grad, axis=0, keepdims=True)
            fs_ref[hrows, :] = shares * (share_grad - delta)
            wide = shares[:, None, :]
            dx_ref[...] += (part * wide).reshape(rows, seg)
            scaled.append((pix * wide).astype(BF16).reshape(rows, seg))
            weights.append(shares.astype(BF16))
        quarter, within = q // pairs, pl.ds(pl.multiple_of(q % pairs * pair_dim, pair_dim), pair_dim)
        m_part = mm(jnp.concatenate(scaled, axis=1), both).astype(BF16)
        me_part = mm(jnp.concatenate(weights, axis=1), both).astype(BF16)

        def store(ref):
            ref[0:rows, within] = m_part
            ref[rows : rows + VARS, within] = me_part

        quarter_of(quarter, store)
        return carry

    lax.fori_loop(0, HEADS // 2, pair, 0)
    score_grad = fs_ref[...]
    low = score_grad.astype(BF16)
    dx = dx_ref[...] + mm(spread_ref[...], low, TN)
    dx_ref[...] = dx
    for slot in range(VARS):
        start = pl.multiple_of(ids_ref[0, slot] * pixels, pixels)
        field_ref[slot * pixels : (slot + 1) * pixels, :] = dx_ref[pl.ds(start, pixels), :].astype(BF16)
    ones = jnp.ones((8, seg), F32)
    s_ref[...] = jnp.zeros_like(s_ref)
    var_row = lax.broadcasted_iota(jnp.int32, (VARS, rows), 0)
    var_col = lax.broadcasted_iota(jnp.int32, (VARS, rows), 1) // pixels
    keep = var_row == var_col
    for h in range(HEADS):
        outer = mm(low[h * VARS : (h + 1) * VARS, :], x_ref[...], NT)
        s_ref[h : h + 1, 0:rows] = jnp.sum(jnp.where(keep, outer, 0.0), axis=0, keepdims=True)
        sums = mm(ones, score_grad[h * VARS : (h + 1) * VARS, :], NT, precision=HIGHEST)
        s_ref[h : h + 1, rows : rows + VARS] = sums[0:1, :]
    for h in range(HEADS):
        for ref, first in ((norm_one_ref, width - pair_dim), (norm_two_ref, width - head_dim)):
            s_ref[h : h + 1, first : first + head_dim] = ref[:, h * head_dim : (h + 1) * head_dim]
    for quarter in range(4):
        part = s_ref[:, quarter * size : (quarter + 1) * size].astype(BF16)

        def store_sums(ref, part=part):
            ref[rows + VARS :, :] = part

        quarter_of(quarter, store_sums)


def front_backward(fast, place, own_ids, x_own, shares, mixed_grad, vw, ve, spread, norm_one, norm_two):
    rows, seg = x_own.shape
    width = mixed_grad.shape[1]
    vmem = pl.BlockSpec(memory_space=pltpu.VMEM)
    smem = pl.BlockSpec(memory_space=pltpu.SMEM)
    tall = rows + VARS + HEADS
    if fast:
        sums = (jax.ShapeDtypeStruct((2, tall, width // 4), BF16),) * 2
    else:
        sums = (jax.ShapeDtypeStruct((4, tall, width // 4), BF16),)
    return pl.pallas_call(
        functools.partial(front_backward_kernel, rows // VARS, fast),
        out_shape=(jax.ShapeDtypeStruct((rows, seg), BF16), *sums),
        in_specs=[smem, smem] + [vmem] * 8,
        out_specs=(vmem,) * (1 + len(sums)),
        scratch_shapes=[
            pltpu.VMEM((HEADS * VARS, seg), F32),
            pltpu.VMEM((rows, seg), F32),
            pltpu.VMEM((HEADS, width), F32),
        ],
        cost_estimate=cost(100000000),
        name="front_backward",
    )(place, own_ids, x_own, shares, mixed_grad, vw, ve, spread, norm_one, norm_two)


def load_parts(ref, part, seg, out_ref):
    for source in range(ref.shape[0]):
        out_ref[source * seg : (source + 1) * seg, :] = ref[source, part * seg : (part + 1) * seg, :]


def attend_forward_kernel(head_dim, block, count_ref, qkv_ref, out_ref, lse_ref, q_ref, k_ref, vt_ref):
    full, width = q_ref.shape
    seg = full // qkv_ref.shape[0]
    scaling = jnp.asarray(1.0 / math.sqrt(head_dim), BF16)
    load_parts(qkv_ref, 2, seg, q_ref)
    vt_ref[...] = q_ref[...].T
    load_parts(qkv_ref, 0, seg, q_ref)
    load_parts(qkv_ref, 1, seg, k_ref)
    count = count_ref[0, 0]
    lane = lax.broadcasted_iota(jnp.int32, (block, width), 1) // head_dim
    row = lax.broadcasted_iota(jnp.int32, (width, block), 0) // head_dim
    valid = lax.broadcasted_iota(jnp.int32, (full, block), 0) < count

    def step(i, carry):
        part = pl.ds(pl.multiple_of(i * block, block), block)
        query = q_ref[part, :]
        total = jnp.zeros((width, block), F32)
        for h in range(width // head_dim):
            own = jnp.where(lane == h, query, jnp.zeros_like(query)) * scaling
            scores = jnp.where(valid, mm(k_ref[...], own, NT), MASKED)
            top = jnp.max(scores, axis=0, keepdims=True)
            exponent = jnp.exp(scores - top)
            denominator = jnp.sum(exponent, axis=0, keepdims=True)
            lse_ref[h : h + 1, part] = top + jnp.log(denominator)
            mixed = mm(vt_ref[...], exponent.astype(BF16)) * (1.0 / denominator)
            total = jnp.where(row == h, mixed, total)
        out_ref[part, :] = total.T.astype(BF16)
        return carry

    lax.fori_loop(0, full // block, step, 0)


def attend_forward(count, qkv, head_dim):
    parts, triple_rows, width = qkv.shape
    full = parts * triple_rows // 3
    vmem = pl.BlockSpec(memory_space=pltpu.VMEM)
    block = min(512, full)
    return pl.pallas_call(
        functools.partial(attend_forward_kernel, head_dim, block),
        out_shape=(
            jax.ShapeDtypeStruct((full, width), BF16),
            jax.ShapeDtypeStruct((width // head_dim, full), F32),
        ),
        in_specs=[pl.BlockSpec(memory_space=pltpu.SMEM), vmem],
        out_specs=(vmem, vmem),
        scratch_shapes=[
            pltpu.VMEM((full, width), BF16),
            pltpu.VMEM((full, width), BF16),
            pltpu.VMEM((width, full), BF16),
        ],
        cost_estimate=cost(60000000000),
        name="attend_forward",
    )(count, qkv)


def attend_backward_kernel(
    head_dim, block, count_ref, qkv_ref, grad_ref, lse_ref, out_ref, q_ref, k_ref, v_ref, kt_ref, dk_ref, dv_ref
):
    full, width = q_ref.shape
    seg = full // qkv_ref.shape[0]
    scaling = 1.0 / math.sqrt(head_dim)
    load_parts(qkv_ref, 0, seg, q_ref)
    load_parts(qkv_ref, 1, seg, k_ref)
    load_parts(qkv_ref, 2, seg, v_ref)
    kt_ref[...] = k_ref[...].T
    dk_ref[...] = jnp.zeros_like(dk_ref)
    dv_ref[...] = jnp.zeros_like(dv_ref)
    count = count_ref[0, 0]
    lane = lax.broadcasted_iota(jnp.int32, (block, width), 1) // head_dim
    row = lax.broadcasted_iota(jnp.int32, (width, block), 0) // head_dim
    valid = lax.broadcasted_iota(jnp.int32, (full, block), 0) < count

    def step(i, carry):
        part = pl.ds(pl.multiple_of(i * block, block), block)
        query = q_ref[part, :]
        grad = grad_ref[part, :]
        total = jnp.zeros((width, block), F32)
        for h in range(width // head_dim):
            own = jnp.where(lane == h, query, jnp.zeros_like(query)) * jnp.asarray(scaling, BF16)
            own_grad = jnp.where(lane == h, grad, jnp.zeros_like(grad))
            scores = jnp.where(valid, mm(k_ref[...], own, NT), MASKED)
            shares = jnp.exp(scores - lse_ref[h : h + 1, part])
            share_grad = mm(v_ref[...], own_grad, NT)
            dot = jnp.sum(shares * share_grad, axis=0, keepdims=True)
            score_grad = (shares * (share_grad - dot)).astype(BF16)
            dv_ref[...] += mm(shares.astype(BF16), own_grad)
            dk_ref[...] += mm(score_grad, own)
            total = jnp.where(row == h, mm(kt_ref[...], score_grad), total)
        turned = (total * scaling).T.astype(BF16)
        for piece in range(block // seg):
            out_ref[i * (block // seg) + piece, 0:seg, :] = turned[piece * seg : (piece + 1) * seg, :]
        return carry

    lax.fori_loop(0, full // block, step, 0)
    for source in range(full // seg):
        rows = slice(source * seg, (source + 1) * seg)
        out_ref[source, seg : 2 * seg, :] = dk_ref[rows, :].astype(BF16)
        out_ref[source, 2 * seg : 3 * seg, :] = dv_ref[rows, :].astype(BF16)


def attend_backward(count, qkv, grad, lse, head_dim):
    parts, triple_rows, width = qkv.shape
    full = parts * triple_rows // 3
    vmem = pl.BlockSpec(memory_space=pltpu.VMEM)
    block = min(256, full)
    return pl.pallas_call(
        functools.partial(attend_backward_kernel, head_dim, block),
        out_shape=jax.ShapeDtypeStruct(qkv.shape, BF16),
        in_specs=[pl.BlockSpec(memory_space=pltpu.SMEM), vmem, vmem, vmem],
        out_specs=vmem,
        scratch_shapes=[pltpu.VMEM((full, width), BF16)] * 3
        + [pltpu.VMEM((width, full), BF16)]
        + [pltpu.VMEM((full, width), F32)] * 2,
        cost_estimate=cost(100000000000),
        name="attend_backward",
    )(count, qkv, grad, lse)


def gathered_attention(triple, count, head_dim):
    seg, triple_width = triple.shape
    width = triple_width // 3
    scaling = 1.0 / math.sqrt(head_dim)
    full = seg * lax.axis_size("patch")
    query = triple[:, :width].reshape(seg, HEADS, head_dim)
    key = lax.all_gather(triple[:, width : 2 * width], "patch", axis=0, tiled=True)
    value = lax.all_gather(triple[:, 2 * width :], "patch", axis=0, tiled=True)
    key = key.reshape(full, HEADS, head_dim)
    value = value.reshape(full, HEADS, head_dim)
    valid = (jnp.arange(full, dtype=jnp.int32) < count)[None, None, :]

    def score():
        raw = jnp.einsum("qhd,khd->hqk", query, key, preferred_element_type=F32) * scaling
        return jnp.where(valid, raw, MASKED)

    masked = score()
    top = jnp.max(masked, axis=-1, keepdims=True)
    exponent = jnp.exp(masked - top)
    denominator = jnp.sum(exponent, axis=-1, keepdims=True)
    shares_low = (exponent / denominator).astype(BF16)
    lse = top + jnp.log(denominator)
    attended = jnp.einsum("hqk,khd->qhd", shares_low, value, preferred_element_type=F32)

    def backward(grad):
        grad = grad.reshape(seg, HEADS, head_dim)
        shares = jnp.exp(score() - lse)
        share_grad = jnp.einsum("qhd,khd->hqk", grad, value, preferred_element_type=F32)
        dot = jnp.sum(shares * share_grad, axis=-1, keepdims=True)
        score_grad = (shares * (share_grad - dot)).astype(BF16)
        q_grad = jnp.einsum("hqk,khd->qhd", score_grad, key, preferred_element_type=F32) * scaling
        v_all = jnp.einsum("hqk,qhd->khd", shares.astype(BF16), grad, preferred_element_type=F32)
        k_all = jnp.einsum("hqk,qhd->khd", score_grad, query, preferred_element_type=F32) * scaling
        k_grad, v_grad = (
            lax.psum_scatter(
                part.reshape(full, width).astype(BF16), "patch", scatter_dimension=0, tiled=True
            )
            for part in (k_all, v_all)
        )
        return jnp.concatenate([q_grad.reshape(seg, width).astype(BF16), k_grad, v_grad], axis=1)

    return attended.reshape(seg, width).astype(BF16), backward


def to_heads(values):
    return lax.all_to_all(values, "patch", split_axis=0, concat_axis=0, tiled=True)


def queries_to_heads(triple):
    seg, triple_width = triple.shape
    parts = lax.axis_size("patch")
    own = triple_width // (3 * parts)
    moved = triple.reshape(seg, 3, parts, own).transpose(2, 1, 0, 3).reshape(parts, 3 * seg, own)
    return to_heads(moved)


def weight_grad_kernel(jobs, index, near, away, place_ref, *refs):
    split = len(refs) - len(near) - len(away)
    arrays, outs = refs[:split], refs[split:]
    rows = outs[0].shape[1]

    def member(group, s):
        first, stacked = index[group]
        return arrays[first].at[place_ref[ME] ^ s] if stacked else arrays[first + s]

    sides = (1 - place_ref[Y],) * len(away) + (place_ref[Y],) * len(near)
    start = 0
    for left, left_start, right, right_start, cols in jobs:
        values = [member(right, s)[:, pl.ds(right_start, cols)] for s in range(4)]
        values = jnp.concatenate(values, axis=0)
        for out, side, blocks in zip(outs, sides, away + near):
            for slot, k in enumerate(blocks):
                source = 2 * (place_ref[Z] ^ k) + side
                group = [member(left, s) for s in range(4)]
                if len(group[0].shape) == 3:
                    factor = [ref[source] for ref in group]
                else:
                    block = pl.ds(pl.multiple_of(left_start + source * rows, rows), rows)
                    factor = [ref[:, block] for ref in group]
                factor = jnp.concatenate(factor, axis=0)
                out[slot, :, start : start + cols] = mm(factor, values, TN).astype(BF16)
        start += cols


def weight_grads(place, jobs, groups, rows, near, away):
    arrays, index = [], []
    for group in groups:
        stacked = not isinstance(group, (list, tuple))
        index.append((len(arrays), stacked))
        arrays += [group] if stacked else list(group)
    total = sum(job[-1] for job in jobs)
    shapes = [((len(blocks), rows, total), BF16) for blocks in away + near]
    kernel = functools.partial(weight_grad_kernel, jobs, index, near, away)
    outs = small_call(kernel, place, arrays, shapes, effort=2000, name="weight_grads")
    return outs[len(away) :], outs[: len(away)]


def swap(values, axis, bit):
    return lax.ppermute(values, axis, [(i, i ^ bit) for i in range(lax.axis_size(axis))])


def together(*values):
    return lax.optimization_barrier(values)


def after(value, *others):
    return lax.optimization_barrier((value, *others))[0]


def small_call(kernel, place, arrays, shapes, scratch=(), effort=200, name="small"):
    vmem = pl.BlockSpec(memory_space=pltpu.VMEM)
    return pl.pallas_call(
        kernel,
        out_shape=tuple(jax.ShapeDtypeStruct(dims, dtype) for dims, dtype in shapes),
        in_specs=[pl.BlockSpec(memory_space=pltpu.SMEM)] + [vmem] * len(arrays),
        out_specs=(vmem,) * len(shapes),
        scratch_shapes=list(scratch),
        cost_estimate=cost(int(effort * 10**9)),
        name=name,
    )(place, *arrays)


ME, CORE, X, Y, Z = range(5)


def tokens_of_group(values):
    across = swap(values, "var", 2)
    return values, swap(values, "var", 1), across, swap(across, "var", 1)


def copies_of_group(values):
    return (values,) + tuple(swap(values, "var", bit) for bit in (1, 2, 3))


def slices_of_group(pieces):
    return (pieces[0],) + tuple(swap(pieces[bit], "var", bit) for bit in (1, 2, 3))


def z_pieces(place, near, got):
    _, rows, cols = near.shape

    def kernel(place_ref, near_ref, got_ref, *outs):
        for bit in range(4):
            block = place_ref[Z] ^ bit
            outs[bit][...] = (near_ref[block].astype(F32) + got_ref[block].astype(F32)).astype(BF16)

    return small_call(kernel, place, (near, got), [((rows, cols), BF16)] * 4, name="z_pieces")


def z_exchange(pieces):
    return (pieces[0],) + tuple(swap(pieces[bit], "patch", 2 * bit) for bit in (1, 2, 3))


def z_sum(place, arrays):

    def kernel(place_ref, first, second, third, fourth, out):
        total = first[...].astype(F32) + second[...].astype(F32) + third[...].astype(F32) + fourth[...].astype(F32)
        out[...] = total.astype(BF16)

    return small_call(kernel, place, arrays, [(arrays[0].shape, BF16)], name="z_sum")[0]


def pair_sum(place, near, got):
    def kernel(place_ref, near_ref, got_ref, out):
        for k in range(2):
            out[k] = (near_ref[k].astype(F32) + got_ref[k].astype(F32)).astype(BF16)

    return small_call(kernel, place, (near, got), [(near.shape, BF16)], name="pair_sum")[0]


def z_first_sum(place, near, got, far):
    first = got.shape[0] - 2

    def kernel(place_ref, near_ref, got_ref, far_ref, stay, away):
        for out, k in ((away, 1), (stay, 0)):
            total = near_ref[k].astype(F32) + got_ref[first + k].astype(F32) + far_ref[k].astype(F32)
            out[...] = total.astype(BF16)

    return small_call(kernel, place, (near, got, far), [(near.shape[1:], BF16)] * 2, name="z_first_sum")


def z_last_sum(place, near, got):
    def kernel(place_ref, near_ref, got_ref, out):
        out[...] = (near_ref[...].astype(F32) + got_ref[...].astype(F32)).astype(BF16)

    return small_call(kernel, place, (near, got), [(near.shape, BF16)], name="z_last_sum")[0]


def gather_over_var(own):
    across = swap(own, "var", 2)
    return own, swap(own, "var", 1), across, swap(across, "var", 1)


def join(place, pieces, widths, stacked):
    rows = pieces[0].shape[0]

    def kernel(place_ref, *refs):
        start = 0
        for k, (out, size) in enumerate(zip(refs[4:], widths)):
            for s in range(4):
                v = place_ref[ME] ^ s
                values = refs[s][:, start : start + size].astype(F32)
                if k < stacked:
                    out[v] = values
                else:
                    out[:, pl.ds(pl.multiple_of(v * size, size), size)] = values
            start += size

    shapes = [((4, rows, size) if k < stacked else (rows, 4 * size), F32) for k, size in enumerate(widths)]
    return small_call(kernel, place, pieces, shapes, name="join")


def sum_over_all(place, stay, away, hooks, marks):
    _, rows, cols = stay.shape
    half = rows // 2
    size = half // 4
    hooks = iter(hooks)

    def core_kernel(place_ref, stay_ref, got_ref, stay_out, away_out):
        for out, which in ((away_out, 1 - place_ref[X]), (stay_out, place_ref[X])):
            out[...] = (stay_ref[which].astype(F32) + got_ref[which].astype(F32)).astype(BF16)

    got = next(hooks)(swap(away, "var", 1))
    stay, away = small_call(core_kernel, place, (stay, got), [((rows, cols), BF16)] * 2, name="core_sum")
    marks.append(stay)

    def x_kernel(place_ref, stay_ref, got_ref, stay_out, away_out):
        for out, which in ((away_out, 1 - place_ref[Y]), (stay_out, place_ref[Y])):
            out[...] = (stay_ref[which].astype(F32) + got_ref[which].astype(F32)).astype(BF16)

    got = next(hooks)(swap(away, "var", 2))
    halves = (2, half, cols)
    stay, away = small_call(
        x_kernel, place, (stay.reshape(halves), got.reshape(halves)), [((half, cols), BF16)] * 2, name="x_sum"
    )
    marks.append(stay)
    got = next(hooks)(swap(away, "patch", 1))
    pieces = z_exchange(z_pieces(place, stay.reshape(4, size, cols), got.reshape(4, size, cols)))
    kept = z_sum(place, next(hooks)(pieces))

    def z_kernel(place_ref, *refs):
        for s in range(4):
            refs[4][place_ref[Z] ^ s] = refs[s][...]

    arrays = (kept,) + tuple(swap(kept, "patch", 2 * bit) for bit in (1, 2, 3))
    own = small_call(z_kernel, place, next(hooks)(arrays), [((4, size, cols), BF16)], name="z_join")[0]

    def y_kernel(place_ref, own_ref, other_ref, out):
        out[place_ref[Y]] = own_ref[...]
        out[1 - place_ref[Y]] = other_ref[...]

    own = own.reshape(half, cols)
    arrays = (own, next(hooks)(swap(own, "patch", 1)))
    full = small_call(y_kernel, place, arrays, [(halves, BF16)], name="y_join")[0].reshape(rows, cols)

    across = next(hooks)(swap(full, "var", 2))
    return full, swap(full, "var", 1), across, swap(across, "var", 1)


def middle_kernel(
    sub,
    place_ref,
    att_ref,
    front_ref,
    valid_ref,
    og_ref,
    tout_ref,
    gain_ref,
    win_ref,
    wout_ref,
    block_ref,
    late_ref,
    *refs,
):
    actives, middles = refs[0:4], refs[4:8]
    grad_ref, after_ref, gain_grad_ref, residual_ref, unit_ref, rate_ref, acc_ref, back_ref, wide_ref, branch_ref = refs[8:]
    step = pl.program_id(0)
    seg, width = front_ref.shape
    parts = att_ref.shape[0]
    own = width // parts
    me = place_ref[0]
    block = win_ref.shape[1]
    slot = block // (4 * sub)
    quarter = width // 4
    hidden = slot * sub * pl.num_programs(0)

    @pl.when(step == 0)
    def _():
        for p in range(parts):
            branch_ref[:, p * own : (p + 1) * own] = att_ref[p]
        after = front_ref[...] + mm(branch_ref[...], tout_ref[...])
        residual_ref[...] = after
        center = after - jnp.mean(after, axis=1, keepdims=True)
        rate = lax.rsqrt(jnp.mean(center * center, axis=1, keepdims=True) + EPSILON)
        unit = center * rate
        unit_ref[...] = unit
        rate_ref[...] = rate
        late_ref[...] = (unit * gain_ref[...]).astype(BF16)
        acc_ref[...] = jnp.zeros_like(acc_ref)
        back_ref[...] = jnp.zeros_like(back_ref)

    inner = mm(late_ref[...], win_ref[...])
    cumulative = 0.5 * (1.0 + lax.erf(inner * math.sqrt(0.5)))
    active = (inner * cumulative).astype(BF16)
    acc_ref[...] += mm(active, wout_ref[...])
    slope = cumulative + inner * (jnp.exp(-0.5 * inner * inner) * (1.0 / math.sqrt(2.0 * math.pi)))
    inner_grad = (mm(og_ref[...], wout_ref[...], NT) * slope).astype(BF16)
    back_ref[...] += mm(inner_grad, win_ref[...], NT)
    wide_ref[...] = active
    for q in range(sub):
        cols = pl.ds(pl.multiple_of((step * sub + q) * slot, slot), slot)
        for s in range(4):
            actives[s][:, cols] = wide_ref[:, pl.ds(pl.multiple_of((4 * q + (me ^ s)) * slot, slot), slot)]
    owner = step * block // hidden
    place = pl.ds(pl.multiple_of(step * block - owner * hidden, block), block)
    for s in range(4):

        @pl.when((me ^ s) == owner)
        def _(s=s):
            middles[s][:, place] = inner_grad

    @pl.when(step == pl.num_programs(0) - 1)
    def _():
        valid = valid_ref[...]
        block_ref[...] = ((residual_ref[...] + acc_ref[...]) * valid).astype(BF16)
        unit = unit_ref[...]
        back = back_ref[...]
        gain_grad_ref[...] = jnp.sum(back * unit, axis=0, keepdims=True)
        scaled = back * gain_ref[...]
        inside = jnp.mean(scaled * unit, axis=1, keepdims=True)
        total = rate_ref[...] * (scaled - jnp.mean(scaled, axis=1, keepdims=True) - unit * inside)
        total = og_ref[...].astype(F32) + total
        after_ref[...] = total
        branch_ref[...] = total.astype(BF16)
        for s in range(4):
            start = pl.multiple_of((me ^ s) * quarter, quarter)
            middles[s][:, hidden:] = branch_ref[:, pl.ds(start, quarter)]
        turned = mm(branch_ref[...], tout_ref[...], NT).astype(BF16)
        for p in range(parts):
            grad_ref[p] = turned[:, p * own : (p + 1) * own]


def middle(place, attended, front_out, valid, out_grad, trunk_out, gain, mlp_in, mlp_out):
    seg, width = front_out.shape
    hidden = mlp_in.shape[1]
    parts = attended.shape[0]
    sub = 1
    block = hidden * sub // parts
    shape = jax.ShapeDtypeStruct

    def still(*dims):
        return pl.BlockSpec(dims, lambda i: (0,) * len(dims))

    piece, wider = shape((seg, hidden // 4), BF16), shape((seg, hidden // 4 + width // 4), BF16)
    return pl.pallas_call(
        functools.partial(middle_kernel, sub),
        grid=(parts // sub,),
        out_shape=(
            shape((seg, width), BF16),
            shape((seg, width), BF16),
            *((piece,) * 4),
            *((wider,) * 4),
            shape(attended.shape, BF16),
            shape((seg, width), F32),
            shape((1, width), F32),
        ),
        in_specs=[
            pl.BlockSpec(memory_space=pltpu.SMEM),
            still(*attended.shape),
            still(seg, width),
            still(seg, 1),
            still(seg, width),
            still(width, width),
            still(1, width),
            pl.BlockSpec((width, block), lambda i: (0, i)),
            pl.BlockSpec((block, width), lambda i: (i, 0)),
        ],
        out_specs=(
            still(seg, width),
            still(seg, width),
            *((still(*piece.shape),) * 4),
            *((still(*wider.shape),) * 4),
            still(*attended.shape),
            still(seg, width),
            still(1, width),
        ),
        scratch_shapes=[
            pltpu.VMEM((seg, width), F32),
            pltpu.VMEM((seg, width), F32),
            pltpu.VMEM((seg, 1), F32),
            pltpu.VMEM((seg, width), F32),
            pltpu.VMEM((seg, width), F32),
            pltpu.VMEM((seg, block), BF16),
            pltpu.VMEM((seg, width), BF16),
        ],
        compiler_params=pltpu.CompilerParams(dimension_semantics=("arbitrary",)),
        cost_estimate=cost(100000000000),
        name="trunk_middle",
    )(place, attended, front_out, valid, out_grad, trunk_out, gain, mlp_in, mlp_out)


def trunk_back_kernel(
    place_ref, grads_ref, front_ref, gain_ref, after_ref, valid_ref, aout_ref, wqkv_ref, mixed_ref, gain_grad_ref, *rest
):
    stack_ref, triple_ref, back_ref = rest
    step = pl.program_id(0)
    parts = grads_ref.shape[0]
    seg, width = front_ref.shape
    own = width // parts
    me = place_ref[ME]

    @pl.when(step == 0)
    def _():
        for c in range(3):
            for p in range(parts):
                triple_ref[c, :, p * own : (p + 1) * own] = grads_ref[p, c * seg : (c + 1) * seg, :]
        back_ref[...] = jnp.zeros_like(back_ref)

    back_ref[...] += mm(triple_ref[step], wqkv_ref[...], NT)

    @pl.when(step == pl.num_programs(0) - 1)
    def _():
        front = front_ref[...]
        center = front - jnp.mean(front, axis=1, keepdims=True)
        rate = lax.rsqrt(jnp.mean(center * center, axis=1, keepdims=True) + EPSILON)
        unit = center * rate
        back = back_ref[...]
        gain_grad_ref[...] = jnp.sum(back * unit, axis=0, keepdims=True)
        scaled = back * gain_ref[...]
        inside = jnp.mean(scaled * unit, axis=1, keepdims=True)
        total = rate * (scaled - jnp.mean(scaled, axis=1, keepdims=True) - unit * inside)
        total = ((after_ref[...] + total) * valid_ref[...]).astype(BF16)
        mixed_ref[...] = mm(total, aout_ref[...], NT).astype(BF16)
        part = width // 4
        for v in range(4):
            stack_ref[v, :, 3 * part :] = total[:, v * part : (v + 1) * part]
            for k in range(3):
                block = 3 * v + k
                source = triple_ref[block // 4, :, block % 4 * part : (block % 4 + 1) * part]
                stack_ref[v, :, k * part : (k + 1) * part] = source


def trunk_back(place, grads, front_out, gain, after_grad, valid, agg_out, trunk_qkv):
    seg, width = front_out.shape
    shape = jax.ShapeDtypeStruct

    def still(*dims):
        return pl.BlockSpec(dims, lambda i: (0,) * len(dims))

    piece = shape((seg, width), BF16)
    return pl.pallas_call(
        trunk_back_kernel,
        grid=(3,),
        out_shape=(piece, shape((1, width), F32), shape((4, seg, width), BF16)),
        in_specs=[
            pl.BlockSpec(memory_space=pltpu.SMEM),
            still(*grads.shape),
            still(seg, width),
            still(1, width),
            still(seg, width),
            still(seg, 1),
            still(width, width),
            pl.BlockSpec((width, width), lambda i: (0, i)),
        ],
        out_specs=(still(seg, width), still(1, width), still(4, seg, width)),
        scratch_shapes=[
            pltpu.VMEM((3, seg, width), BF16),
            pltpu.VMEM((seg, width), F32),
        ],
        compiler_params=pltpu.CompilerParams(dimension_semantics=("arbitrary",)),
        cost_estimate=cost(100000000000),
        name="trunk_back",
    )(place, grads, front_out, gain, after_grad, valid, agg_out, trunk_qkv)


def front_last_kernel(
    pixels,
    place_ref,
    m0,
    m1,
    m2,
    m3,
    weight_ref,
    embed_ref,
    weight_own_ref,
    embed_own_ref,
    value_rows_ref,
    key_query_ref,
    key_ref,
    aggq_ref,
    query_rows_ref,
    query_own_ref,
    value_out,
    patch_out,
    embed_out,
    key_out,
    query_out,
    agg_query_out,
    norm_one_out,
    norm_two_out,
    m_ref,
    sum_ref,
):
    rows, width = weight_ref.shape
    own = weight_own_ref.shape[1]
    size = m0.shape[1]
    head_dim = width // HEADS
    scaling = 1.0 / math.sqrt(head_dim)
    for s, ref in enumerate((m0, m1, m2, m3)):
        v = place_ref[ME] ^ s
        m_ref[:, pl.ds(pl.multiple_of((v % 2 * 2 + v // 2) * size, size), size)] = ref[...]
    m_sum, me_sum = m_ref[0:rows, :], m_ref[rows : rows + VARS, :]
    value_out[...] = mm(weight_own_ref[...], m_sum, TN) + mm(embed_own_ref[...], me_sum, TN)
    s_all = m_ref[rows + VARS : rows + VARS + HEADS, :]
    twice = jnp.concatenate([s_all, s_all], axis=0)
    patch_out[...] = mm(m_sum, value_rows_ref[...], NT) + mm(twice[:, 0:rows], key_query_ref[...], TN)
    embed_out[...] = mm(me_sum, value_rows_ref[...], NT) + mm(
        twice[:, rows : rows + VARS], key_query_ref[...], TN
    )
    key_sum = (mm(s_all[:, 0:rows], weight_ref[...]) + mm(s_all[:, rows : rows + VARS], embed_ref[...])) * scaling
    sum_ref[...] = key_sum
    lane = lax.broadcasted_iota(jnp.int32, (HEADS, width), 1) // head_dim
    mine = lane == lax.broadcasted_iota(jnp.int32, (HEADS, width), 0)
    start = pl.multiple_of((place_ref[Z] * 2 + place_ref[Y]) * own, own)
    head_rows = jnp.where(mine, aggq_ref[...], 0.0)
    key_out[...] = mm(sum_ref[:, pl.ds(start, own)], head_rows, TN, precision=HIGHEST)
    crossed = mm(jnp.concatenate(split_high_low(key_sum), axis=0), key_ref[...])
    crossed = crossed[0:HEADS, :] + crossed[HEADS:, :]
    aggq_grad = jnp.sum(jnp.where(mine, crossed, 0.0), axis=0, keepdims=True)
    query_out[...] = query_own_ref[...] * aggq_grad
    high, low = split_high_low(aggq_grad)
    agg_query_out[...] = mm(high, query_rows_ref[...], NT) + mm(low, query_rows_ref[...], NT)
    row = lax.broadcasted_iota(jnp.int32, (HEADS, own), 0)
    tail = s_all[:, width - own :].astype(F32)
    for k in range(own // head_dim):
        line = jnp.sum(jnp.where(row == start // head_dim + k, tail, 0.0), axis=0, keepdims=True)
        norm_one_out[:, k * head_dim : (k + 1) * head_dim] = line[:, 0:head_dim]
        norm_two_out[:, k * head_dim : (k + 1) * head_dim] = line[:, head_dim:own]


def front_last(place, pieces, arrays):
    weight_rows, own_weight, value_rows = arrays[0], arrays[2], arrays[4]
    rows, width = weight_rows.shape
    own = own_weight.shape[1]
    tall = pieces[0].shape[0]
    shapes = [((own, width), F32), ((rows, own), F32), ((VARS, own), F32)] + [((own, width), F32)] * 2
    shapes += [((1, own), F32)] * 3
    return small_call(
        functools.partial(front_last_kernel, rows // VARS),
        place,
        (*pieces, *arrays),
        shapes,
        scratch=[pltpu.VMEM((tall, width), BF16), pltpu.VMEM((HEADS, width), F32)],
        name="front_last",
    )


def local(
    input_field,
    counts,
    var_ids,
    patch_weight,
    var_embed,
    agg_query,
    query_proj,
    key_proj,
    value_proj,
    agg_out,
    norm_one,
    trunk_qkv,
    trunk_out,
    norm_two,
    mlp_in,
    mlp_out,
    cotangent,
):
    patches, group = lax.axis_size("patch"), lax.axis_size("var")
    fast = (patches, group) == (8, 4)
    me, spot = lax.axis_index("var"), lax.axis_index("patch")
    place = jnp.stack([me, me % 2, me // 2, spot % 2, spot // 2]).astype(jnp.int32)
    var_index = lax.axis_index("var")
    patch_index = lax.axis_index("patch")
    all_rows, seg, var_local, pixels = input_field.shape
    width = agg_out.shape[0]
    head_dim = width // HEADS
    hidden = mlp_in.shape[1]
    scaling = 1.0 / math.sqrt(head_dim)

    turned = input_field.transpose(0, 2, 3, 1).reshape(all_rows, var_local * pixels, seg)
    own_field = lax.all_to_all(turned, "var", split_axis=0, concat_axis=1, tiled=True)
    own_field = own_field.reshape(VARS * pixels, seg)
    own_ids = lax.dynamic_slice_in_dim(var_ids, var_index, 1, 0)
    own_count = lax.dynamic_slice_in_dim(counts, var_index, 1, 0)
    positions = patch_index * seg + jnp.arange(seg, dtype=jnp.int32)
    valid_rows = (positions < own_count).astype(F32)[:, None]
    out_grad = cotangent.reshape(seg, width).astype(F32) * valid_rows
    out_grad_low = out_grad.astype(BF16)

    weight_rows = patch_weight.reshape(VARS * pixels, width)
    agg_q = mm(agg_query[None], query_proj)[0]
    in_head = jnp.arange(width, dtype=jnp.int32)[:, None] // head_dim == jnp.arange(HEADS)[None, :]
    head_query = jnp.where(in_head, agg_q[:, None] * scaling, 0.0)
    key_query = mm(key_proj, jnp.concatenate(split_high_low(head_query), axis=1))
    key_query = key_query[:, :HEADS] + key_query[:, HEADS:]
    key_query_parts = jnp.concatenate(split_high_low(key_query), axis=1)
    score_weight = mm(key_query_parts, weight_rows, (((0,), (1,)), ((), ())))
    score_weight = score_weight[:HEADS] + score_weight[HEADS:]
    score_embed = mm(key_query_parts, var_embed, (((0,), (1,)), ((), ())))
    score_embed = score_embed[:HEADS] + score_embed[HEADS:]
    vwt = mm(value_proj, weight_rows, (((0,), (1,)), ((), ()))).astype(BF16)
    vet = mm(value_proj, var_embed, (((0,), (1,)), ((), ()))).astype(BF16)

    own_width = width // patches
    start = patch_index * own_width

    def own_cols(values):
        return lax.dynamic_slice_in_dim(values, start, own_width, 1)

    def own_rows(values):
        return lax.dynamic_slice_in_dim(values, start, own_width, 0)

    def own_query(values):
        return lax.dynamic_slice_in_dim(values, start, own_width, 0).astype(F32)[:, None]

    def last_operands(ready):
        weights, embeds, values, queries, line, key_queries, _ = together(
            weight_rows, var_embed, value_proj, query_proj, agg_query, key_query, ready
        )
        return (
            weights,
            embeds,
            own_cols(weights),
            own_cols(embeds),
            own_rows(values),
            jnp.concatenate(split_high_low(own_rows(key_queries)), axis=1).T,
            key_proj,
            agg_q[None],
            own_rows(queries),
            own_query(line),
        )

    x_own, shares, mixed_low, spread = front_forward(own_ids, own_field, score_weight, score_embed, vwt, vet)

    front_out = mm(mixed_low, agg_out) * valid_rows
    normed_one, norm_one_pull = jax.vjp(layer_norm, front_out, norm_one.astype(F32))
    normed_one_low = normed_one.astype(BF16)
    triple = mm(normed_one_low, trunk_qkv).astype(BF16)
    part = width // group
    quarter = hidden // group
    zs = patches // 2
    ready = after(value_proj, triple)
    vw = mm(weight_rows, ready).astype(BF16)
    ve = mm(var_embed, ready).astype(BF16)
    if fast:
        early = tokens_of_group(jnp.concatenate([out_grad_low, mixed_low, normed_one_low], axis=1))
        qkv, vw, ve, *arrays = together(queries_to_heads(triple), vw, ve, *last_operands(triple))
        count = own_count.reshape(1, 1)
        heads, lse = attend_forward(count, qkv, head_dim)
        attended = to_heads(heads.reshape(patches, seg, own_width))
        results = middle(
            place,
            attended,
            front_out,
            valid_rows,
            out_grad_low,
            trunk_out,
            norm_two.astype(F32)[None],
            mlp_in,
            mlp_out,
        )
        attended_group = copies_of_group(attended)
        results = together(*results, *attended_group, *early)
        attended_group, early = results[13:17], results[17:]
        block_out, normed_two_low, grads, after_grad, norm_two_grad = (results[k] for k in (0, 1, 10, 11, 12))
        block_out = block_out[None]
        grads = to_heads(grads)
        active_group = slices_of_group(results[2:6])
        across = swap(normed_two_low, "var", 2)
        result = attend_backward(count, qkv, grads.reshape(patches * seg, own_width), lse, head_dim)
        result, across, *rest = together(result, across, *active_group, *results[6:10])
        active_group, middle_group = rest[:4], slices_of_group(rest[4:])
        normed_group = (normed_two_low, swap(normed_two_low, "var", 1), across, swap(across, "var", 1))
        result = to_heads(result)
        pairs, whole_order = ((1, 3), (0, 2)), ((1, 3, 0, 2),)
        jobs = ((0, 0, 1, 0, width),)
        near_one, away_one = weight_grads(place, jobs, (active_group, early), own_width, pairs, whole_order)
        jobs = ((0, 0, 2, 0, quarter), (1, 0, 2, quarter, part))
        groups = (together(normed_group[0], *near_one)[:1] + normed_group[1:], attended_group, middle_group)
        near_two, away_two = weight_grads(place, jobs, groups, own_width, pairs, pairs)
        result = after(result, *near_two)
        one = {"near": near_one, "got": swap(away_one[0], "patch", 1)}
        two = {"near": near_two, "away": away_two}
        mixed_grad, norm_one_grad, stack = trunk_back(
            place, result, front_out, norm_one.astype(F32)[None], after_grad, valid_rows, agg_out, trunk_qkv
        )
        one["far"] = pair_sum(place, after(one["near"][0], mixed_grad), one["got"])
        mixed_grad = after(mixed_grad, one["far"])
        last_group = lax.all_to_all(stack, "var", split_axis=0, concat_axis=0, tiled=True)
    else:
        attended, attention_pull = gathered_attention(triple, own_count, head_dim)
        after_attn = front_out + mm(attended, trunk_out)
        normed_two, norm_two_pull = jax.vjp(layer_norm, after_attn, norm_two.astype(F32))
        normed_two_low = normed_two.astype(BF16)
        inner = mm(normed_two_low, mlp_in)
        active, gelu_pull = jax.vjp(gelu_exact, inner)
        active_low = active.astype(BF16)
        result = after_attn + mm(active_low, mlp_out)
        block_out = (result * valid_rows).astype(BF16)[None]
        inner_grad = gelu_pull(mm(out_grad_low, mlp_out, NT))[0].astype(BF16)
        normed_two_grad = mm(inner_grad, mlp_in, NT)
        after_ln_grad, norm_two_grad = norm_two_pull(normed_two_grad)
        after_grad = out_grad + after_ln_grad
        branch_low = after_grad.astype(BF16)
        triple_grad = attention_pull(mm(branch_low, trunk_out, NT).astype(BF16))
        normed_one_grad = mm(triple_grad, trunk_qkv, NT)
        front_ln_grad, norm_one_grad = norm_one_pull(normed_one_grad)
        agg_grad = ((after_grad + front_ln_grad) * valid_rows).astype(BF16)
        mixed_grad = mm(agg_grad, agg_out, NT).astype(BF16)
        norm_one_grad, norm_two_grad = norm_one_grad[None], norm_two_grad[None]

    field_low, *m_parts = front_backward(
        fast, place, own_ids, x_own, shares, mixed_grad, vw, ve, spread, norm_one_grad, norm_two_grad
    )

    field_low = field_low.reshape(group, var_local * pixels, seg)
    field_grad = None if fast else lax.all_to_all(field_low, "var", split_axis=0, concat_axis=0, tiled=True)

    if fast:
        m_stay, m_away, two["first"], last_group = together(*m_parts, swap(two["away"][0], "patch", 1), last_group)
        m_parts = (m_stay, m_away)
        two["far"] = pair_sum(place, two["near"][0], two["first"])
        last, marks = {}, []

        def core_done(values):
            return values

        def x_done(values):
            far = swap(one["far"], "patch", 2)
            far, near, _ = together(far, one["near"][1], *marks)
            one["pair"] = z_first_sum(place, near, one["got"], far)
            return after(values, one["pair"][0])

        def y_done(values):
            jobs = ((0, 2 * width, 1, 0, 3 * part), (0, width, 1, 3 * part, part))
            groups = (early, after(last_group, marks[-1]))
            last["near"], last["away"] = weight_grads(place, jobs, groups, own_width, pairs, whole_order)
            got = swap(after(two["away"][1], two["first"]), "patch", 1)
            values, got, far, *_ = together(values, got, swap(two["far"], "patch", 2), *last["near"])
            two["pair"] = z_first_sum(place, two["near"][1], got, far)
            return values

        def z_done(values):
            near, away = one["pair"]
            *values, got, _ = together(*values, swap(away, "patch", 4), two["pair"][0])
            one["own"] = z_last_sum(place, near, got)
            return values

        def b_done(values):
            near, away = two["pair"]
            *values, last["got"], got = together(*values, swap(last["away"][0], "patch", 1), swap(away, "patch", 4))
            late = after(field_low, last["got"])
            last["field"] = lax.all_to_all(late, "var", split_axis=0, concat_axis=0, tiled=True)
            last["far"] = pair_sum(place, last["near"][0], last["got"])
            two["own"] = z_last_sum(place, near, got)
            return [after(values[0], last["far"]), *values[1:]]

        def y_back(values):
            values, one["across"], last["field"] = together(values, swap(one["own"], "var", 2), last["field"])
            return values

        def var_done(values):
            far, across = swap(last["far"], "patch", 2), swap(two["own"], "var", 2)
            near, away = z_first_sum(place, last["near"][1], last["got"], far)
            two["parts"] = (two["own"], swap(two["own"], "var", 1), across, swap(across, "var", 1))
            last["own"] = z_last_sum(place, near, swap(away, "patch", 4))
            own, across = one["own"], one["across"]
            values, inner, corner, _ = together(values, swap(own, "var", 1), swap(across, "var", 1), near)
            one["parts"] = (own, inner, across, corner)
            return values

        m_pieces = sum_over_all(place, *m_parts, (core_done, x_done, y_done, z_done, b_done, y_back, var_done), marks)
        field_grad = last["field"]
        (mlp_out_grad,) = join(place, one["parts"], (width,), 1)
        mlp_in_grad, trunk_out_grad = join(place, two["parts"], (quarter, part), 0)
        mlp_out_grad = mlp_out_grad.reshape(hidden // patches, width)
        trunk_qkv_grad, agg_out_grad = join(place, gather_over_var(last["own"]), (3 * part, part), 0)
    else:

        def slices(values):
            values = values.reshape(seg, group, values.shape[1] // group).transpose(1, 0, 2)
            return lax.all_to_all(values, "var", split_axis=0, concat_axis=0, tiled=True)

        def everyone(values):
            return lax.all_gather(values, "var", axis=0, tiled=True)

        def total(left, right):
            value = mm(left.reshape(-1, left.shape[-1]), right.reshape(-1, right.shape[-1]), TN).astype(BF16)
            value = lax.psum_scatter(value, "patch", scatter_dimension=0, tiled=True)
            return lax.all_gather(value, "var", axis=0)

        def joined(value):
            return value.transpose(1, 0, 2).reshape(value.shape[1], -1).astype(F32)

        size = hidden // (patches * group)
        active_rows = active_low.reshape(seg, patches, group, size).transpose(0, 2, 1, 3).reshape(seg, hidden)
        mlp_out_grad = total(slices(active_rows), everyone(out_grad_low)).reshape(hidden // patches, width).astype(F32)
        mlp_in_grad = joined(total(everyone(normed_two_low), slices(inner_grad)))
        trunk_out_grad = joined(total(everyone(attended), slices(branch_low)))
        trunk_qkv_grad = joined(total(everyone(normed_one_low), slices(triple_grad)))
        agg_out_grad = joined(total(everyone(mixed_low), slices(agg_grad)))
        m_all = lax.psum(m_parts[0], ("patch", "var")).transpose(1, 0, 2).reshape(-1, width)
    if fast:
        value_proj_grad, patch_grad, embed_grad, key_proj_grad, query_proj_grad, *lines = front_last(
            place, m_pieces, arrays
        )
        agg_query_grad, norm_one_grad, norm_two_grad = (line[0] for line in lines)
    else:
        value_rows, key_query_rows = own_rows(value_proj), own_rows(key_query)
        m_sum, me_sum = m_all[: VARS * pixels], m_all[VARS * pixels : VARS * pixels + VARS]
        s_rows = m_all[VARS * pixels + VARS :].astype(F32)
        s_all = s_rows[:, : VARS * pixels]
        se_all = s_rows[:, VARS * pixels : VARS * pixels + VARS]
        norm_sums = s_rows[:, width - 2 * head_dim :]
        value_proj_grad = mm(own_cols(weight_rows), m_sum, TN) + mm(own_cols(var_embed), me_sum, TN)
        patch_grad = mm(m_sum, value_rows, NT) + mm(
            s_all, key_query_rows, (((0,), (1,)), ((), ())), precision=HIGHEST
        )
        embed_grad = mm(me_sum, value_rows, NT) + mm(
            se_all, key_query_rows, (((0,), (1,)), ((), ())), precision=HIGHEST
        )
        key_sum = (mm(s_all.astype(BF16), weight_rows) + mm(se_all.astype(BF16), var_embed)) * scaling
        head_rows = jnp.where(in_head.T, agg_q[None, :], 0.0)
        key_proj_grad = mm(own_cols(key_sum), head_rows, TN, precision=HIGHEST)
        crossed = mm(jnp.concatenate(split_high_low(key_sum), axis=0), key_proj)
        crossed = crossed[:HEADS] + crossed[HEADS:]
        aggq_grad = jnp.sum(jnp.where(in_head.T, crossed, 0.0), axis=0)
        query_proj_grad = own_query(agg_query) * aggq_grad[None, :]
        agg_query_grad = jnp.sum(own_rows(query_proj).astype(F32) * aggq_grad[None, :], axis=1)
        norm_one_grad = lax.dynamic_slice_in_dim(norm_sums[:, :head_dim].reshape(width), start, own_width, 0)
        norm_two_grad = lax.dynamic_slice_in_dim(norm_sums[:, head_dim:].reshape(width), start, own_width, 0)
    patch_grad = patch_grad.reshape(VARS, pixels, own_width)
    field_grad = field_grad.reshape(all_rows, var_local, pixels, seg).transpose(0, 3, 1, 2)
    return (
        block_out,
        field_grad,
        patch_grad,
        embed_grad,
        agg_query_grad,
        query_proj_grad,
        key_proj_grad,
        value_proj_grad,
        agg_out_grad,
        norm_one_grad,
        trunk_qkv_grad,
        trunk_out_grad,
        norm_two_grad,
        mlp_in_grad,
        mlp_out_grad,
    )


def solution(mesh):
    whole = P()
    placed = (P(None, "patch", "var", None),) + (whole,) * 15 + (P("var", "patch", None),)
    rows = P("patch", None)
    return jax.shard_map(
        local,
        mesh=mesh,
        in_specs=placed,
        out_specs=(
            P("var", "patch", None),
            P(None, "patch", "var", None),
            P(None, None, "patch"),
            P(None, "patch"),
            P("patch"),
            rows,
            rows,
            rows,
            rows,
            P("patch"),
            rows,
            rows,
            P("patch"),
            rows,
            rows,
        ),
        check_vma=False,
    )
```

```python
import functools
import math

import jax
import jax.numpy as jnp
from jax import lax
from jax.experimental import pallas as pl
from jax.experimental.pallas import tpu as pltpu
from jax.sharding import PartitionSpec as P

HEADS = 16
VARS = 48
EPSILON = 1e-05
MASKED = -1e30
HIGHEST = lax.Precision.HIGHEST
BF16 = jnp.bfloat16
F32 = jnp.float32
NN = (((1,), (0,)), ((), ()))
NT = (((1,), (1,)), ((), ()))
TN = (((0,), (0,)), ((), ()))


def cost(flops):
    return pl.CostEstimate(flops=flops, bytes_accessed=1 << 20, transcendentals=0)


def mm(a, b, dims=NN, precision=None):
    return lax.dot_general(a, b, dims, precision=precision, preferred_element_type=F32)


def layer_norm(values, gain_vec):
    average = jnp.mean(values, axis=-1, keepdims=True)
    center = values - average
    spread = jnp.mean(center * center, axis=-1, keepdims=True)
    return center * lax.rsqrt(spread + EPSILON) * gain_vec


def gelu_exact(values):
    return jax.nn.gelu(values, approximate=False)


def split_high_low(values):
    high = values.astype(BF16)
    return high, (values - high.astype(F32)).astype(BF16)


def front_forward_kernel(
    pixels, ids_ref, field_ref, weight_ref, bias_ref, vwt_ref, vet_ref, x_ref, p_ref, mixed_ref, spread_ref, mt_ref
):
    seg = field_ref.shape[1]
    head_dim = mixed_ref.shape[1] // HEADS
    for slot in range(VARS):
        start = pl.multiple_of(ids_ref[0, slot] * pixels, pixels)
        x_ref[pl.ds(start, pixels), :] = field_ref[slot * pixels : (slot + 1) * pixels, :]
    rows = VARS * pixels
    mine = lax.broadcasted_iota(jnp.int32, (VARS, rows), 1) // pixels
    mine = mine == lax.broadcasted_iota(jnp.int32, (VARS, rows), 0)
    bias = bias_ref[...].T
    parts = []
    for h in range(HEADS):
        spread = jnp.where(mine, weight_ref[h : h + 1, :], 0.0).astype(BF16)
        spread_ref[h * VARS : (h + 1) * VARS, :] = spread
        parts.append(mm(spread, x_ref[...]) + bias[:, h : h + 1])
    scores = jnp.stack(parts)
    top = jnp.max(scores, axis=1, keepdims=True)
    exponent = jnp.exp(scores - top)
    total = jnp.sum(exponent, axis=1, keepdims=True)
    p_ref[...] = (exponent * (1.0 / total)).reshape(HEADS * VARS, seg)

    def head(h, carry):
        shares = p_ref[pl.ds(pl.multiple_of(h * VARS, VARS), VARS), :]
        pix = x_ref[...].astype(F32).reshape(VARS, pixels, seg)
        scaled = (pix * shares[:, None, :]).astype(BF16).reshape(VARS * pixels, seg)
        rows = pl.ds(pl.multiple_of(h * head_dim, head_dim), head_dim)
        mt_ref[rows, :] = mm(vwt_ref[rows, :], scaled) + mm(vet_ref[rows, :], shares.astype(BF16))
        return carry

    lax.fori_loop(0, HEADS, head, 0, unroll=2)
    mixed_ref[...] = mt_ref[...].T.astype(BF16)


def front_forward(own_ids, own_field, score_weight, bias, vwt, vet):
    rows, seg = own_field.shape
    width = vwt.shape[0]
    vmem = pl.BlockSpec(memory_space=pltpu.VMEM)
    return pl.pallas_call(
        functools.partial(front_forward_kernel, rows // VARS),
        out_shape=(
            jax.ShapeDtypeStruct((rows, seg), BF16),
            jax.ShapeDtypeStruct((HEADS * VARS, seg), F32),
            jax.ShapeDtypeStruct((seg, width), BF16),
            jax.ShapeDtypeStruct((HEADS * VARS, rows), BF16),
        ),
        in_specs=[pl.BlockSpec(memory_space=pltpu.SMEM)] + [vmem] * 5,
        out_specs=(vmem,) * 4,
        scratch_shapes=[pltpu.VMEM((width, seg), F32)],
        cost_estimate=cost(60000000000),
        name="front_forward",
    )(own_ids, own_field, score_weight, bias, vwt, vet)


def front_backward_kernel(
    pixels,
    fast,
    place_ref,
    ids_ref,
    x_ref,
    p_ref,
    mg_ref,
    vw_ref,
    ve_ref,
    spread_ref,
    norm_one_ref,
    norm_two_ref,
    field_ref,
    *rest,
):
    rows, seg = x_ref.shape
    m_refs, (fs_ref, dx_ref, s_ref) = rest[:-3], rest[-3:]
    size = m_refs[0].shape[-1]

    def quarter_of(quarter, store):
        if not fast:
            store(m_refs[0].at[quarter])
            return
        mine = quarter // 2 == place_ref[CORE]
        pl.when(mine)(lambda: store(m_refs[0].at[quarter % 2]))
        pl.when(jnp.logical_not(mine))(lambda: store(m_refs[1].at[quarter % 2]))
    width = mg_ref.shape[1]
    head_dim = width // HEADS
    pair_dim = 2 * head_dim
    lane = lax.broadcasted_iota(jnp.int32, (seg, pair_dim), 1)
    dx_ref[...] = jnp.zeros_like(dx_ref)
    pairs = size // pair_dim

    def pair(q, carry):
        cols = pl.ds(pl.multiple_of(q * pair_dim, pair_dim), pair_dim)
        grad = mg_ref[:, cols]
        none = jnp.zeros_like(grad)
        both = jnp.concatenate(
            [jnp.where(lane < head_dim, grad, none), jnp.where(lane >= head_dim, grad, none)], axis=0
        )
        inner = mm(vw_ref[:, cols], both, NT)
        inner_e = mm(ve_ref[:, cols], both, NT)
        pix = x_ref[...].astype(F32).reshape(VARS, pixels, seg)
        scaled, weights = [], []
        for k in range(2):
            hrows = pl.ds(pl.multiple_of((2 * q + k) * VARS, VARS), VARS)
            shares = p_ref[hrows, :]
            part = inner[:, k * seg : (k + 1) * seg].reshape(VARS, pixels, seg)
            share_grad = jnp.sum(pix * part, axis=1) + inner_e[:, k * seg : (k + 1) * seg]
            delta = jnp.sum(shares * share_grad, axis=0, keepdims=True)
            fs_ref[hrows, :] = shares * (share_grad - delta)
            wide = shares[:, None, :]
            dx_ref[...] += (part * wide).reshape(rows, seg)
            scaled.append((pix * wide).astype(BF16).reshape(rows, seg))
            weights.append(shares.astype(BF16))
        quarter, within = q // pairs, pl.ds(pl.multiple_of(q % pairs * pair_dim, pair_dim), pair_dim)
        m_part = mm(jnp.concatenate(scaled, axis=1), both).astype(BF16)
        me_part = mm(jnp.concatenate(weights, axis=1), both).astype(BF16)

        def store(ref):
            ref[0:rows, within] = m_part
            ref[rows : rows + VARS, within] = me_part

        quarter_of(quarter, store)
        return carry

    lax.fori_loop(0, HEADS // 2, pair, 0)
    score_grad = fs_ref[...]
    low = score_grad.astype(BF16)
    dx = dx_ref[...] + mm(spread_ref[...], low, TN)
    dx_ref[...] = dx
    for slot in range(VARS):
        start = pl.multiple_of(ids_ref[0, slot] * pixels, pixels)
        field_ref[slot * pixels : (slot + 1) * pixels, :] = dx_ref[pl.ds(start, pixels), :].astype(BF16)
    ones = jnp.ones((8, seg), F32)
    s_ref[...] = jnp.zeros_like(s_ref)
    var_row = lax.broadcasted_iota(jnp.int32, (VARS, rows), 0)
    var_col = lax.broadcasted_iota(jnp.int32, (VARS, rows), 1) // pixels
    keep = var_row == var_col
    for h in range(HEADS):
        outer = mm(low[h * VARS : (h + 1) * VARS, :], x_ref[...], NT)
        s_ref[h : h + 1, 0:rows] = jnp.sum(jnp.where(keep, outer, 0.0), axis=0, keepdims=True)
        sums = mm(ones, score_grad[h * VARS : (h + 1) * VARS, :], NT, precision=HIGHEST)
        s_ref[h : h + 1, rows : rows + VARS] = sums[0:1, :]
    for h in range(HEADS):
        for ref, first in ((norm_one_ref, width - pair_dim), (norm_two_ref, width - head_dim)):
            s_ref[h : h + 1, first : first + head_dim] = ref[:, h * head_dim : (h + 1) * head_dim]
    for quarter in range(4):
        part = s_ref[:, quarter * size : (quarter + 1) * size].astype(BF16)

        def store_sums(ref, part=part):
            ref[rows + VARS :, :] = part

        quarter_of(quarter, store_sums)


def front_backward(fast, place, own_ids, x_own, shares, mixed_grad, vw, ve, spread, norm_one, norm_two):
    rows, seg = x_own.shape
    width = mixed_grad.shape[1]
    vmem = pl.BlockSpec(memory_space=pltpu.VMEM)
    smem = pl.BlockSpec(memory_space=pltpu.SMEM)
    tall = rows + VARS + HEADS
    if fast:
        sums = (jax.ShapeDtypeStruct((2, tall, width // 4), BF16),) * 2
    else:
        sums = (jax.ShapeDtypeStruct((4, tall, width // 4), BF16),)
    return pl.pallas_call(
        functools.partial(front_backward_kernel, rows // VARS, fast),
        out_shape=(jax.ShapeDtypeStruct((rows, seg), BF16), *sums),
        in_specs=[smem, smem] + [vmem] * 8,
        out_specs=(vmem,) * (1 + len(sums)),
        scratch_shapes=[
            pltpu.VMEM((HEADS * VARS, seg), F32),
            pltpu.VMEM((rows, seg), F32),
            pltpu.VMEM((HEADS, width), F32),
        ],
        cost_estimate=cost(100000000),
        name="front_backward",
    )(place, own_ids, x_own, shares, mixed_grad, vw, ve, spread, norm_one, norm_two)


def load_parts(ref, part, seg, out_ref):
    for source in range(ref.shape[0]):
        out_ref[source * seg : (source + 1) * seg, :] = ref[source, part * seg : (part + 1) * seg, :]


def attend_forward_kernel(head_dim, block, count_ref, qkv_ref, out_ref, lse_ref, q_ref, k_ref, vt_ref):
    full, width = q_ref.shape
    seg = full // qkv_ref.shape[0]
    scaling = jnp.asarray(1.0 / math.sqrt(head_dim), BF16)
    load_parts(qkv_ref, 2, seg, q_ref)
    vt_ref[...] = q_ref[...].T
    load_parts(qkv_ref, 0, seg, q_ref)
    load_parts(qkv_ref, 1, seg, k_ref)
    count = count_ref[0, 0]
    lane = lax.broadcasted_iota(jnp.int32, (block, width), 1) // head_dim
    row = lax.broadcasted_iota(jnp.int32, (width, block), 0) // head_dim
    valid = lax.broadcasted_iota(jnp.int32, (full, block), 0) < count

    def step(i, carry):
        part = pl.ds(pl.multiple_of(i * block, block), block)
        query = q_ref[part, :]
        total = jnp.zeros((width, block), F32)
        for h in range(width // head_dim):
            own = jnp.where(lane == h, query, jnp.zeros_like(query)) * scaling
            scores = jnp.where(valid, mm(k_ref[...], own, NT), MASKED)
            top = jnp.max(scores, axis=0, keepdims=True)
            exponent = jnp.exp(scores - top)
            denominator = jnp.sum(exponent, axis=0, keepdims=True)
            lse_ref[h : h + 1, part] = top + jnp.log(denominator)
            mixed = mm(vt_ref[...], exponent.astype(BF16)) * (1.0 / denominator)
            total = jnp.where(row == h, mixed, total)
        out_ref[part, :] = total.T.astype(BF16)
        return carry

    lax.fori_loop(0, full // block, step, 0)


def attend_forward(count, qkv, head_dim):
    parts, triple_rows, width = qkv.shape
    full = parts * triple_rows // 3
    vmem = pl.BlockSpec(memory_space=pltpu.VMEM)
    block = min(512, full)
    return pl.pallas_call(
        functools.partial(attend_forward_kernel, head_dim, block),
        out_shape=(
            jax.ShapeDtypeStruct((full, width), BF16),
            jax.ShapeDtypeStruct((width // head_dim, full), F32),
        ),
        in_specs=[pl.BlockSpec(memory_space=pltpu.SMEM), vmem],
        out_specs=(vmem, vmem),
        scratch_shapes=[
            pltpu.VMEM((full, width), BF16),
            pltpu.VMEM((full, width), BF16),
            pltpu.VMEM((width, full), BF16),
        ],
        cost_estimate=cost(60000000000),
        name="attend_forward",
    )(count, qkv)


def attend_backward_kernel(
    head_dim, block, count_ref, qkv_ref, grad_ref, lse_ref, out_ref, q_ref, k_ref, v_ref, kt_ref, dk_ref, dv_ref
):
    full, width = q_ref.shape
    seg = full // qkv_ref.shape[0]
    scaling = 1.0 / math.sqrt(head_dim)
    load_parts(qkv_ref, 0, seg, q_ref)
    load_parts(qkv_ref, 1, seg, k_ref)
    load_parts(qkv_ref, 2, seg, v_ref)
    kt_ref[...] = k_ref[...].T
    dk_ref[...] = jnp.zeros_like(dk_ref)
    dv_ref[...] = jnp.zeros_like(dv_ref)
    count = count_ref[0, 0]
    lane = lax.broadcasted_iota(jnp.int32, (block, width), 1) // head_dim
    row = lax.broadcasted_iota(jnp.int32, (width, block), 0) // head_dim
    valid = lax.broadcasted_iota(jnp.int32, (full, block), 0) < count

    def step(i, carry):
        part = pl.ds(pl.multiple_of(i * block, block), block)
        query = q_ref[part, :]
        grad = grad_ref[part, :]
        total = jnp.zeros((width, block), F32)
        for h in range(width // head_dim):
            own = jnp.where(lane == h, query, jnp.zeros_like(query)) * jnp.asarray(scaling, BF16)
            own_grad = jnp.where(lane == h, grad, jnp.zeros_like(grad))
            scores = jnp.where(valid, mm(k_ref[...], own, NT), MASKED)
            shares = jnp.exp(scores - lse_ref[h : h + 1, part])
            share_grad = mm(v_ref[...], own_grad, NT)
            dot = jnp.sum(shares * share_grad, axis=0, keepdims=True)
            score_grad = (shares * (share_grad - dot)).astype(BF16)
            dv_ref[...] += mm(shares.astype(BF16), own_grad)
            dk_ref[...] += mm(score_grad, own)
            total = jnp.where(row == h, mm(kt_ref[...], score_grad), total)
        turned = (total * scaling).T.astype(BF16)
        for piece in range(block // seg):
            out_ref[i * (block // seg) + piece, 0:seg, :] = turned[piece * seg : (piece + 1) * seg, :]
        return carry

    lax.fori_loop(0, full // block, step, 0)
    for source in range(full // seg):
        rows = slice(source * seg, (source + 1) * seg)
        out_ref[source, seg : 2 * seg, :] = dk_ref[rows, :].astype(BF16)
        out_ref[source, 2 * seg : 3 * seg, :] = dv_ref[rows, :].astype(BF16)


def attend_backward(count, qkv, grad, lse, head_dim):
    parts, triple_rows, width = qkv.shape
    full = parts * triple_rows // 3
    vmem = pl.BlockSpec(memory_space=pltpu.VMEM)
    block = min(256, full)
    return pl.pallas_call(
        functools.partial(attend_backward_kernel, head_dim, block),
        out_shape=jax.ShapeDtypeStruct(qkv.shape, BF16),
        in_specs=[pl.BlockSpec(memory_space=pltpu.SMEM), vmem, vmem, vmem],
        out_specs=vmem,
        scratch_shapes=[pltpu.VMEM((full, width), BF16)] * 3
        + [pltpu.VMEM((width, full), BF16)]
        + [pltpu.VMEM((full, width), F32)] * 2,
        cost_estimate=cost(100000000000),
        name="attend_backward",
    )(count, qkv, grad, lse)


def gathered_attention(triple, count, head_dim):
    seg, triple_width = triple.shape
    width = triple_width // 3
    scaling = 1.0 / math.sqrt(head_dim)
    full = seg * lax.axis_size("patch")
    query = triple[:, :width].reshape(seg, HEADS, head_dim)
    key = lax.all_gather(triple[:, width : 2 * width], "patch", axis=0, tiled=True)
    value = lax.all_gather(triple[:, 2 * width :], "patch", axis=0, tiled=True)
    key = key.reshape(full, HEADS, head_dim)
    value = value.reshape(full, HEADS, head_dim)
    valid = (jnp.arange(full, dtype=jnp.int32) < count)[None, None, :]

    def score():
        raw = jnp.einsum("qhd,khd->hqk", query, key, preferred_element_type=F32) * scaling
        return jnp.where(valid, raw, MASKED)

    masked = score()
    top = jnp.max(masked, axis=-1, keepdims=True)
    exponent = jnp.exp(masked - top)
    denominator = jnp.sum(exponent, axis=-1, keepdims=True)
    shares_low = (exponent / denominator).astype(BF16)
    lse = top + jnp.log(denominator)
    attended = jnp.einsum("hqk,khd->qhd", shares_low, value, preferred_element_type=F32)

    def backward(grad):
        grad = grad.reshape(seg, HEADS, head_dim)
        shares = jnp.exp(score() - lse)
        share_grad = jnp.einsum("qhd,khd->hqk", grad, value, preferred_element_type=F32)
        dot = jnp.sum(shares * share_grad, axis=-1, keepdims=True)
        score_grad = (shares * (share_grad - dot)).astype(BF16)
        q_grad = jnp.einsum("hqk,khd->qhd", score_grad, key, preferred_element_type=F32) * scaling
        v_all = jnp.einsum("hqk,qhd->khd", shares.astype(BF16), grad, preferred_element_type=F32)
        k_all = jnp.einsum("hqk,qhd->khd", score_grad, query, preferred_element_type=F32) * scaling
        k_grad, v_grad = (
            lax.psum_scatter(
                part.reshape(full, width).astype(BF16), "patch", scatter_dimension=0, tiled=True
            )
            for part in (k_all, v_all)
        )
        return jnp.concatenate([q_grad.reshape(seg, width).astype(BF16), k_grad, v_grad], axis=1)

    return attended.reshape(seg, width).astype(BF16), backward


def to_heads(values):
    return lax.all_to_all(values, "patch", split_axis=0, concat_axis=0, tiled=True)


def queries_to_heads(triple):
    seg, triple_width = triple.shape
    parts = lax.axis_size("patch")
    own = triple_width // (3 * parts)
    moved = triple.reshape(seg, 3, parts, own).transpose(2, 1, 0, 3).reshape(parts, 3 * seg, own)
    return to_heads(moved)


def weight_grad_kernel(jobs, index, near, away, place_ref, *refs):
    split = len(refs) - len(near) - len(away)
    arrays, outs = refs[:split], refs[split:]
    rows = outs[0].shape[1]

    def member(group, s):
        first, stacked = index[group]
        return arrays[first].at[place_ref[ME] ^ s] if stacked else arrays[first + s]

    sides = (1 - place_ref[Y],) * len(away) + (place_ref[Y],) * len(near)
    start = 0
    for left, left_start, right, right_start, cols in jobs:
        values = [member(right, s)[:, pl.ds(right_start, cols)] for s in range(4)]
        values = jnp.concatenate(values, axis=0)
        for out, side, blocks in zip(outs, sides, away + near):
            for slot, k in enumerate(blocks):
                source = 2 * (place_ref[Z] ^ k) + side
                group = [member(left, s) for s in range(4)]
                if len(group[0].shape) == 3:
                    factor = [ref[source] for ref in group]
                else:
                    block = pl.ds(pl.multiple_of(left_start + source * rows, rows), rows)
                    factor = [ref[:, block] for ref in group]
                factor = jnp.concatenate(factor, axis=0)
                out[slot, :, start : start + cols] = mm(factor, values, TN).astype(BF16)
        start += cols


def weight_grads(place, jobs, groups, rows, near, away):
    arrays, index = [], []
    for group in groups:
        stacked = not isinstance(group, (list, tuple))
        index.append((len(arrays), stacked))
        arrays += [group] if stacked else list(group)
    total = sum(job[-1] for job in jobs)
    shapes = [((len(blocks), rows, total), BF16) for blocks in away + near]
    kernel = functools.partial(weight_grad_kernel, jobs, index, near, away)
    outs = small_call(kernel, place, arrays, shapes, effort=2000, name="weight_grads")
    return outs[len(away) :], outs[: len(away)]


def swap(values, axis, bit):
    return lax.ppermute(values, axis, [(i, i ^ bit) for i in range(lax.axis_size(axis))])


def together(*values):
    return lax.optimization_barrier(values)


def after(value, *others):
    return lax.optimization_barrier((value, *others))[0]


def small_call(kernel, place, arrays, shapes, scratch=(), effort=200, name="small"):
    vmem = pl.BlockSpec(memory_space=pltpu.VMEM)
    return pl.pallas_call(
        kernel,
        out_shape=tuple(jax.ShapeDtypeStruct(dims, dtype) for dims, dtype in shapes),
        in_specs=[pl.BlockSpec(memory_space=pltpu.SMEM)] + [vmem] * len(arrays),
        out_specs=(vmem,) * len(shapes),
        scratch_shapes=list(scratch),
        cost_estimate=cost(int(effort * 10**9)),
        name=name,
    )(place, *arrays)


ME, CORE, X, Y, Z = range(5)


def tokens_of_group(values):
    across = swap(values, "var", 2)
    return values, swap(values, "var", 1), across, swap(across, "var", 1)


def copies_of_group(values):
    return (values,) + tuple(swap(values, "var", bit) for bit in (1, 2, 3))


def slices_of_group(pieces):
    return (pieces[0],) + tuple(swap(pieces[bit], "var", bit) for bit in (1, 2, 3))


def z_pieces(place, near, got):
    _, rows, cols = near.shape

    def kernel(place_ref, near_ref, got_ref, *outs):
        for bit in range(4):
            block = place_ref[Z] ^ bit
            outs[bit][...] = (near_ref[block].astype(F32) + got_ref[block].astype(F32)).astype(BF16)

    return small_call(kernel, place, (near, got), [((rows, cols), BF16)] * 4, name="z_pieces")


def z_exchange(pieces):
    return (pieces[0],) + tuple(swap(pieces[bit], "patch", 2 * bit) for bit in (1, 2, 3))


def z_sum(place, arrays):

    def kernel(place_ref, first, second, third, fourth, out):
        total = first[...].astype(F32) + second[...].astype(F32) + third[...].astype(F32) + fourth[...].astype(F32)
        out[...] = total.astype(BF16)

    return small_call(kernel, place, arrays, [(arrays[0].shape, BF16)], name="z_sum")[0]


def pair_sum(place, near, got):
    def kernel(place_ref, near_ref, got_ref, out):
        for k in range(2):
            out[k] = (near_ref[k].astype(F32) + got_ref[k].astype(F32)).astype(BF16)

    return small_call(kernel, place, (near, got), [(near.shape, BF16)], name="pair_sum")[0]


def z_first_sum(place, near, got, far):
    first = got.shape[0] - 2

    def kernel(place_ref, near_ref, got_ref, far_ref, stay, away):
        for out, k in ((away, 1), (stay, 0)):
            total = near_ref[k].astype(F32) + got_ref[first + k].astype(F32) + far_ref[k].astype(F32)
            out[...] = total.astype(BF16)

    return small_call(kernel, place, (near, got, far), [(near.shape[1:], BF16)] * 2, name="z_first_sum")


def z_last_sum(place, near, got):
    def kernel(place_ref, near_ref, got_ref, out):
        out[...] = (near_ref[...].astype(F32) + got_ref[...].astype(F32)).astype(BF16)

    return small_call(kernel, place, (near, got), [(near.shape, BF16)], name="z_last_sum")[0]


def gather_over_var(own):
    across = swap(own, "var", 2)
    return own, swap(own, "var", 1), across, swap(across, "var", 1)


def join(place, pieces, widths, stacked):
    rows = pieces[0].shape[0]

    def kernel(place_ref, *refs):
        start = 0
        for k, (out, size) in enumerate(zip(refs[4:], widths)):
            for s in range(4):
                v = place_ref[ME] ^ s
                values = refs[s][:, start : start + size].astype(F32)
                if k < stacked:
                    out[v] = values
                else:
                    out[:, pl.ds(pl.multiple_of(v * size, size), size)] = values
            start += size

    shapes = [((4, rows, size) if k < stacked else (rows, 4 * size), F32) for k, size in enumerate(widths)]
    return small_call(kernel, place, pieces, shapes, name="join")


def sum_over_all(place, stay, away, hooks, marks):
    _, rows, cols = stay.shape
    half = rows // 2
    size = half // 4
    hooks = iter(hooks)

    def core_kernel(place_ref, stay_ref, got_ref, stay_out, away_out):
        for out, which in ((away_out, 1 - place_ref[X]), (stay_out, place_ref[X])):
            out[...] = (stay_ref[which].astype(F32) + got_ref[which].astype(F32)).astype(BF16)

    got = next(hooks)(swap(away, "var", 1))
    stay, away = small_call(core_kernel, place, (stay, got), [((rows, cols), BF16)] * 2, name="core_sum")
    marks.append(stay)

    def x_kernel(place_ref, stay_ref, got_ref, stay_out, away_out):
        for out, which in ((away_out, 1 - place_ref[Y]), (stay_out, place_ref[Y])):
            out[...] = (stay_ref[which].astype(F32) + got_ref[which].astype(F32)).astype(BF16)

    got = next(hooks)(swap(away, "var", 2))
    halves = (2, half, cols)
    stay, away = small_call(
        x_kernel, place, (stay.reshape(halves), got.reshape(halves)), [((half, cols), BF16)] * 2, name="x_sum"
    )
    marks.append(stay)
    got = next(hooks)(swap(away, "patch", 1))
    pieces = z_exchange(z_pieces(place, stay.reshape(4, size, cols), got.reshape(4, size, cols)))
    kept = z_sum(place, next(hooks)(pieces))

    def z_kernel(place_ref, *refs):
        for s in range(4):
            refs[4][place_ref[Z] ^ s] = refs[s][...]

    arrays = (kept,) + tuple(swap(kept, "patch", 2 * bit) for bit in (1, 2, 3))
    own = small_call(z_kernel, place, next(hooks)(arrays), [((4, size, cols), BF16)], name="z_join")[0]

    def y_kernel(place_ref, own_ref, other_ref, out):
        out[place_ref[Y]] = own_ref[...]
        out[1 - place_ref[Y]] = other_ref[...]

    own = own.reshape(half, cols)
    arrays = (own, next(hooks)(swap(own, "patch", 1)))
    full = small_call(y_kernel, place, arrays, [(halves, BF16)], name="y_join")[0].reshape(rows, cols)

    across = next(hooks)(swap(full, "var", 2))
    return full, swap(full, "var", 1), across, swap(across, "var", 1)


def middle_kernel(
    sub,
    place_ref,
    att_ref,
    front_ref,
    valid_ref,
    og_ref,
    tout_ref,
    gain_ref,
    win_ref,
    wout_ref,
    block_ref,
    late_ref,
    *refs,
):
    actives, middles = refs[0:4], refs[4:8]
    grad_ref, after_ref, gain_grad_ref, residual_ref, unit_ref, rate_ref, acc_ref, back_ref, wide_ref, branch_ref = refs[8:]
    step = pl.program_id(0)
    seg, width = front_ref.shape
    parts = att_ref.shape[0]
    own = width // parts
    me = place_ref[0]
    block = win_ref.shape[1]
    slot = block // (4 * sub)
    quarter = width // 4
    hidden = slot * sub * pl.num_programs(0)

    @pl.when(step == 0)
    def _():
        for p in range(parts):
            branch_ref[:, p * own : (p + 1) * own] = att_ref[p]
        after = front_ref[...] + mm(branch_ref[...], tout_ref[...])
        residual_ref[...] = after
        center = after - jnp.mean(after, axis=1, keepdims=True)
        rate = lax.rsqrt(jnp.mean(center * center, axis=1, keepdims=True) + EPSILON)
        unit = center * rate
        unit_ref[...] = unit
        rate_ref[...] = rate
        late_ref[...] = (unit * gain_ref[...]).astype(BF16)
        acc_ref[...] = jnp.zeros_like(acc_ref)
        back_ref[...] = jnp.zeros_like(back_ref)

    inner = mm(late_ref[...], win_ref[...])
    cumulative = 0.5 * (1.0 + lax.erf(inner * math.sqrt(0.5)))
    active = (inner * cumulative).astype(BF16)
    acc_ref[...] += mm(active, wout_ref[...])
    slope = cumulative + inner * (jnp.exp(-0.5 * inner * inner) * (1.0 / math.sqrt(2.0 * math.pi)))
    inner_grad = (mm(og_ref[...], wout_ref[...], NT) * slope).astype(BF16)
    back_ref[...] += mm(inner_grad, win_ref[...], NT)
    wide_ref[...] = active
    for q in range(sub):
        cols = pl.ds(pl.multiple_of((step * sub + q) * slot, slot), slot)
        for s in range(4):
            actives[s][:, cols] = wide_ref[:, pl.ds(pl.multiple_of((4 * q + (me ^ s)) * slot, slot), slot)]
    owner = step * block // hidden
    place = pl.ds(pl.multiple_of(step * block - owner * hidden, block), block)
    for s in range(4):

        @pl.when((me ^ s) == owner)
        def _(s=s):
            middles[s][:, place] = inner_grad

    @pl.when(step == pl.num_programs(0) - 1)
    def _():
        valid = valid_ref[...]
        block_ref[...] = ((residual_ref[...] + acc_ref[...]) * valid).astype(BF16)
        unit = unit_ref[...]
        back = back_ref[...]
        gain_grad_ref[...] = jnp.sum(back * unit, axis=0, keepdims=True)
        scaled = back * gain_ref[...]
        inside = jnp.mean(scaled * unit, axis=1, keepdims=True)
        total = rate_ref[...] * (scaled - jnp.mean(scaled, axis=1, keepdims=True) - unit * inside)
        total = og_ref[...].astype(F32) + total
        after_ref[...] = total
        branch_ref[...] = total.astype(BF16)
        for s in range(4):
            start = pl.multiple_of((me ^ s) * quarter, quarter)
            middles[s][:, hidden:] = branch_ref[:, pl.ds(start, quarter)]
        turned = mm(branch_ref[...], tout_ref[...], NT).astype(BF16)
        for p in range(parts):
            grad_ref[p] = turned[:, p * own : (p + 1) * own]


def middle(place, attended, front_out, valid, out_grad, trunk_out, gain, mlp_in, mlp_out):
    seg, width = front_out.shape
    hidden = mlp_in.shape[1]
    parts = attended.shape[0]
    sub = 2
    block = hidden * sub // parts
    shape = jax.ShapeDtypeStruct

    def still(*dims):
        return pl.BlockSpec(dims, lambda i: (0,) * len(dims))

    piece, wider = shape((seg, hidden // 4), BF16), shape((seg, hidden // 4 + width // 4), BF16)
    return pl.pallas_call(
        functools.partial(middle_kernel, sub),
        grid=(parts // sub,),
        out_shape=(
            shape((seg, width), BF16),
            shape((seg, width), BF16),
            *((piece,) * 4),
            *((wider,) * 4),
            shape(attended.shape, BF16),
            shape((seg, width), F32),
            shape((1, width), F32),
        ),
        in_specs=[
            pl.BlockSpec(memory_space=pltpu.SMEM),
            still(*attended.shape),
            still(seg, width),
            still(seg, 1),
            still(seg, width),
            still(width, width),
            still(1, width),
            pl.BlockSpec((width, block), lambda i: (0, i)),
            pl.BlockSpec((block, width), lambda i: (i, 0)),
        ],
        out_specs=(
            still(seg, width),
            still(seg, width),
            *((still(*piece.shape),) * 4),
            *((still(*wider.shape),) * 4),
            still(*attended.shape),
            still(seg, width),
            still(1, width),
        ),
        scratch_shapes=[
            pltpu.VMEM((seg, width), F32),
            pltpu.VMEM((seg, width), F32),
            pltpu.VMEM((seg, 1), F32),
            pltpu.VMEM((seg, width), F32),
            pltpu.VMEM((seg, width), F32),
            pltpu.VMEM((seg, block), BF16),
            pltpu.VMEM((seg, width), BF16),
        ],
        compiler_params=pltpu.CompilerParams(dimension_semantics=("arbitrary",)),
        cost_estimate=cost(100000000000),
        name="trunk_middle",
    )(place, attended, front_out, valid, out_grad, trunk_out, gain, mlp_in, mlp_out)


def trunk_back_kernel(
    place_ref, grads_ref, front_ref, gain_ref, after_ref, valid_ref, aout_ref, wqkv_ref, mixed_ref, gain_grad_ref, *rest
):
    stack_ref, triple_ref, back_ref = rest
    step = pl.program_id(0)
    parts = grads_ref.shape[0]
    seg, width = front_ref.shape
    own = width // parts
    me = place_ref[ME]

    @pl.when(step == 0)
    def _():
        for c in range(3):
            for p in range(parts):
                triple_ref[c, :, p * own : (p + 1) * own] = grads_ref[p, c * seg : (c + 1) * seg, :]
        back_ref[...] = jnp.zeros_like(back_ref)

    back_ref[...] += mm(triple_ref[step], wqkv_ref[...], NT)

    @pl.when(step == pl.num_programs(0) - 1)
    def _():
        front = front_ref[...]
        center = front - jnp.mean(front, axis=1, keepdims=True)
        rate = lax.rsqrt(jnp.mean(center * center, axis=1, keepdims=True) + EPSILON)
        unit = center * rate
        back = back_ref[...]
        gain_grad_ref[...] = jnp.sum(back * unit, axis=0, keepdims=True)
        scaled = back * gain_ref[...]
        inside = jnp.mean(scaled * unit, axis=1, keepdims=True)
        total = rate * (scaled - jnp.mean(scaled, axis=1, keepdims=True) - unit * inside)
        total = ((after_ref[...] + total) * valid_ref[...]).astype(BF16)
        mixed_ref[...] = mm(total, aout_ref[...], NT).astype(BF16)
        part = width // 4
        for v in range(4):
            stack_ref[v, :, 3 * part :] = total[:, v * part : (v + 1) * part]
            for k in range(3):
                block = 3 * v + k
                source = triple_ref[block // 4, :, block % 4 * part : (block % 4 + 1) * part]
                stack_ref[v, :, k * part : (k + 1) * part] = source


def trunk_back(place, grads, front_out, gain, after_grad, valid, agg_out, trunk_qkv):
    seg, width = front_out.shape
    shape = jax.ShapeDtypeStruct

    def still(*dims):
        return pl.BlockSpec(dims, lambda i: (0,) * len(dims))

    piece = shape((seg, width), BF16)
    return pl.pallas_call(
        trunk_back_kernel,
        grid=(3,),
        out_shape=(piece, shape((1, width), F32), shape((4, seg, width), BF16)),
        in_specs=[
            pl.BlockSpec(memory_space=pltpu.SMEM),
            still(*grads.shape),
            still(seg, width),
            still(1, width),
            still(seg, width),
            still(seg, 1),
            still(width, width),
            pl.BlockSpec((width, width), lambda i: (0, i)),
        ],
        out_specs=(still(seg, width), still(1, width), still(4, seg, width)),
        scratch_shapes=[
            pltpu.VMEM((3, seg, width), BF16),
            pltpu.VMEM((seg, width), F32),
        ],
        compiler_params=pltpu.CompilerParams(dimension_semantics=("arbitrary",)),
        cost_estimate=cost(100000000000),
        name="trunk_back",
    )(place, grads, front_out, gain, after_grad, valid, agg_out, trunk_qkv)


def front_last_kernel(
    pixels,
    place_ref,
    m0,
    m1,
    m2,
    m3,
    weight_ref,
    embed_ref,
    weight_own_ref,
    embed_own_ref,
    value_rows_ref,
    key_query_ref,
    key_ref,
    aggq_ref,
    query_rows_ref,
    query_own_ref,
    value_out,
    patch_out,
    embed_out,
    key_out,
    query_out,
    agg_query_out,
    norm_one_out,
    norm_two_out,
    m_ref,
    sum_ref,
):
    rows, width = weight_ref.shape
    own = weight_own_ref.shape[1]
    size = m0.shape[1]
    head_dim = width // HEADS
    scaling = 1.0 / math.sqrt(head_dim)
    for s, ref in enumerate((m0, m1, m2, m3)):
        v = place_ref[ME] ^ s
        m_ref[:, pl.ds(pl.multiple_of((v % 2 * 2 + v // 2) * size, size), size)] = ref[...]
    m_sum, me_sum = m_ref[0:rows, :], m_ref[rows : rows + VARS, :]
    value_out[...] = mm(weight_own_ref[...], m_sum, TN) + mm(embed_own_ref[...], me_sum, TN)
    s_all = m_ref[rows + VARS : rows + VARS + HEADS, :]
    twice = jnp.concatenate([s_all, s_all], axis=0)
    patch_out[...] = mm(m_sum, value_rows_ref[...], NT) + mm(twice[:, 0:rows], key_query_ref[...], TN)
    embed_out[...] = mm(me_sum, value_rows_ref[...], NT) + mm(
        twice[:, rows : rows + VARS], key_query_ref[...], TN
    )
    key_sum = (mm(s_all[:, 0:rows], weight_ref[...]) + mm(s_all[:, rows : rows + VARS], embed_ref[...])) * scaling
    sum_ref[...] = key_sum
    lane = lax.broadcasted_iota(jnp.int32, (HEADS, width), 1) // head_dim
    mine = lane == lax.broadcasted_iota(jnp.int32, (HEADS, width), 0)
    start = pl.multiple_of((place_ref[Z] * 2 + place_ref[Y]) * own, own)
    head_rows = jnp.where(mine, aggq_ref[...], 0.0)
    key_out[...] = mm(sum_ref[:, pl.ds(start, own)], head_rows, TN, precision=HIGHEST)
    crossed = mm(jnp.concatenate(split_high_low(key_sum), axis=0), key_ref[...])
    crossed = crossed[0:HEADS, :] + crossed[HEADS:, :]
    aggq_grad = jnp.sum(jnp.where(mine, crossed, 0.0), axis=0, keepdims=True)
    query_out[...] = query_own_ref[...] * aggq_grad
    high, low = split_high_low(aggq_grad)
    agg_query_out[...] = mm(high, query_rows_ref[...], NT) + mm(low, query_rows_ref[...], NT)
    row = lax.broadcasted_iota(jnp.int32, (HEADS, own), 0)
    tail = s_all[:, width - own :].astype(F32)
    for k in range(own // head_dim):
        line = jnp.sum(jnp.where(row == start // head_dim + k, tail, 0.0), axis=0, keepdims=True)
        norm_one_out[:, k * head_dim : (k + 1) * head_dim] = line[:, 0:head_dim]
        norm_two_out[:, k * head_dim : (k + 1) * head_dim] = line[:, head_dim:own]


def front_last(place, pieces, arrays):
    weight_rows, own_weight, value_rows = arrays[0], arrays[2], arrays[4]
    rows, width = weight_rows.shape
    own = own_weight.shape[1]
    tall = pieces[0].shape[0]
    shapes = [((own, width), F32), ((rows, own), F32), ((VARS, own), F32)] + [((own, width), F32)] * 2
    shapes += [((1, own), F32)] * 3
    return small_call(
        functools.partial(front_last_kernel, rows // VARS),
        place,
        (*pieces, *arrays),
        shapes,
        scratch=[pltpu.VMEM((tall, width), BF16), pltpu.VMEM((HEADS, width), F32)],
        name="front_last",
    )


def local(
    input_field,
    counts,
    var_ids,
    patch_weight,
    var_embed,
    agg_query,
    query_proj,
    key_proj,
    value_proj,
    agg_out,
    norm_one,
    trunk_qkv,
    trunk_out,
    norm_two,
    mlp_in,
    mlp_out,
    cotangent,
):
    patches, group = lax.axis_size("patch"), lax.axis_size("var")
    fast = (patches, group) == (8, 4)
    me, spot = lax.axis_index("var"), lax.axis_index("patch")
    place = jnp.stack([me, me % 2, me // 2, spot % 2, spot // 2]).astype(jnp.int32)
    var_index = lax.axis_index("var")
    patch_index = lax.axis_index("patch")
    all_rows, seg, var_local, pixels = input_field.shape
    width = agg_out.shape[0]
    head_dim = width // HEADS
    hidden = mlp_in.shape[1]
    scaling = 1.0 / math.sqrt(head_dim)

    turned = input_field.transpose(0, 2, 3, 1).reshape(all_rows, var_local * pixels, seg)
    own_field = lax.all_to_all(turned, "var", split_axis=0, concat_axis=1, tiled=True)
    own_field = own_field.reshape(VARS * pixels, seg)
    own_ids = lax.dynamic_slice_in_dim(var_ids, var_index, 1, 0)
    own_count = lax.dynamic_slice_in_dim(counts, var_index, 1, 0)
    positions = patch_index * seg + jnp.arange(seg, dtype=jnp.int32)
    valid_rows = (positions < own_count).astype(F32)[:, None]
    out_grad = cotangent.reshape(seg, width).astype(F32) * valid_rows
    out_grad_low = out_grad.astype(BF16)

    weight_rows = patch_weight.reshape(VARS * pixels, width)
    agg_q = mm(agg_query[None], query_proj)[0]
    in_head = jnp.arange(width, dtype=jnp.int32)[:, None] // head_dim == jnp.arange(HEADS)[None, :]
    head_query = jnp.where(in_head, agg_q[:, None] * scaling, 0.0)
    key_query = mm(key_proj, jnp.concatenate(split_high_low(head_query), axis=1))
    key_query = key_query[:, :HEADS] + key_query[:, HEADS:]
    key_query_parts = jnp.concatenate(split_high_low(key_query), axis=1)
    score_weight = mm(key_query_parts, weight_rows, (((0,), (1,)), ((), ())))
    score_weight = score_weight[:HEADS] + score_weight[HEADS:]
    score_embed = mm(key_query_parts, var_embed, (((0,), (1,)), ((), ())))
    score_embed = score_embed[:HEADS] + score_embed[HEADS:]
    vwt = mm(value_proj, weight_rows, (((0,), (1,)), ((), ()))).astype(BF16)
    vet = mm(value_proj, var_embed, (((0,), (1,)), ((), ()))).astype(BF16)

    own_width = width // patches
    start = patch_index * own_width

    def own_cols(values):
        return lax.dynamic_slice_in_dim(values, start, own_width, 1)

    def own_rows(values):
        return lax.dynamic_slice_in_dim(values, start, own_width, 0)

    def own_query(values):
        return lax.dynamic_slice_in_dim(values, start, own_width, 0).astype(F32)[:, None]

    def last_operands(ready):
        weights, embeds, values, queries, line, key_queries, _ = together(
            weight_rows, var_embed, value_proj, query_proj, agg_query, key_query, ready
        )
        return (
            weights,
            embeds,
            own_cols(weights),
            own_cols(embeds),
            own_rows(values),
            jnp.concatenate(split_high_low(own_rows(key_queries)), axis=1).T,
            key_proj,
            agg_q[None],
            own_rows(queries),
            own_query(line),
        )

    x_own, shares, mixed_low, spread = front_forward(own_ids, own_field, score_weight, score_embed, vwt, vet)

    front_out = mm(mixed_low, agg_out) * valid_rows
    normed_one, norm_one_pull = jax.vjp(layer_norm, front_out, norm_one.astype(F32))
    normed_one_low = normed_one.astype(BF16)
    triple = mm(normed_one_low, trunk_qkv).astype(BF16)
    part = width // group
    quarter = hidden // group
    zs = patches // 2
    ready = after(value_proj, triple)
    vw = mm(weight_rows, ready).astype(BF16)
    ve = mm(var_embed, ready).astype(BF16)
    if fast:
        early = tokens_of_group(jnp.concatenate([out_grad_low, mixed_low, normed_one_low], axis=1))
        qkv, vw, ve, *arrays = together(queries_to_heads(triple), vw, ve, *last_operands(triple))
        count = own_count.reshape(1, 1)
        heads, lse = attend_forward(count, qkv, head_dim)
        attended = to_heads(heads.reshape(patches, seg, own_width))
        results = middle(
            place,
            attended,
            front_out,
            valid_rows,
            out_grad_low,
            trunk_out,
            norm_two.astype(F32)[None],
            mlp_in,
            mlp_out,
        )
        attended_group = copies_of_group(attended)
        results = together(*results, *attended_group, *early)
        attended_group, early = results[13:17], results[17:]
        block_out, normed_two_low, grads, after_grad, norm_two_grad = (results[k] for k in (0, 1, 10, 11, 12))
        block_out = block_out[None]
        grads = to_heads(grads)
        active_group = slices_of_group(results[2:6])
        across = swap(normed_two_low, "var", 2)
        result = attend_backward(count, qkv, grads.reshape(patches * seg, own_width), lse, head_dim)
        result, across, *rest = together(result, across, *active_group, *results[6:10])
        active_group, middle_group = rest[:4], slices_of_group(rest[4:])
        normed_group = (normed_two_low, swap(normed_two_low, "var", 1), across, swap(across, "var", 1))
        result = to_heads(result)
        pairs, whole_order = ((1, 3), (0, 2)), ((1, 3, 0, 2),)
        jobs = ((0, 0, 1, 0, width),)
        near_one, away_one = weight_grads(place, jobs, (active_group, early), own_width, pairs, whole_order)
        jobs = ((0, 0, 2, 0, quarter), (1, 0, 2, quarter, part))
        groups = (together(normed_group[0], *near_one)[:1] + normed_group[1:], attended_group, middle_group)
        near_two, away_two = weight_grads(place, jobs, groups, own_width, pairs, pairs)
        result = after(result, *near_two)
        one = {"near": near_one, "got": swap(away_one[0], "patch", 1)}
        two = {"near": near_two, "away": away_two}
        mixed_grad, norm_one_grad, stack = trunk_back(
            place, result, front_out, norm_one.astype(F32)[None], after_grad, valid_rows, agg_out, trunk_qkv
        )
        one["far"] = pair_sum(place, after(one["near"][0], mixed_grad), one["got"])
        mixed_grad = after(mixed_grad, one["far"])
        last_group = lax.all_to_all(stack, "var", split_axis=0, concat_axis=0, tiled=True)
    else:
        attended, attention_pull = gathered_attention(triple, own_count, head_dim)
        after_attn = front_out + mm(attended, trunk_out)
        normed_two, norm_two_pull = jax.vjp(layer_norm, after_attn, norm_two.astype(F32))
        normed_two_low = normed_two.astype(BF16)
        inner = mm(normed_two_low, mlp_in)
        active, gelu_pull = jax.vjp(gelu_exact, inner)
        active_low = active.astype(BF16)
        result = after_attn + mm(active_low, mlp_out)
        block_out = (result * valid_rows).astype(BF16)[None]
        inner_grad = gelu_pull(mm(out_grad_low, mlp_out, NT))[0].astype(BF16)
        normed_two_grad = mm(inner_grad, mlp_in, NT)
        after_ln_grad, norm_two_grad = norm_two_pull(normed_two_grad)
        after_grad = out_grad + after_ln_grad
        branch_low = after_grad.astype(BF16)
        triple_grad = attention_pull(mm(branch_low, trunk_out, NT).astype(BF16))
        normed_one_grad = mm(triple_grad, trunk_qkv, NT)
        front_ln_grad, norm_one_grad = norm_one_pull(normed_one_grad)
        agg_grad = ((after_grad + front_ln_grad) * valid_rows).astype(BF16)
        mixed_grad = mm(agg_grad, agg_out, NT).astype(BF16)
        norm_one_grad, norm_two_grad = norm_one_grad[None], norm_two_grad[None]

    field_low, *m_parts = front_backward(
        fast, place, own_ids, x_own, shares, mixed_grad, vw, ve, spread, norm_one_grad, norm_two_grad
    )

    field_low = field_low.reshape(group, var_local * pixels, seg)
    field_grad = None if fast else lax.all_to_all(field_low, "var", split_axis=0, concat_axis=0, tiled=True)

    if fast:
        m_stay, m_away, two["first"], last_group = together(*m_parts, swap(two["away"][0], "patch", 1), last_group)
        m_parts = (m_stay, m_away)
        two["far"] = pair_sum(place, two["near"][0], two["first"])
        last, marks = {}, []

        def core_done(values):
            return values

        def x_done(values):
            far = swap(one["far"], "patch", 2)
            far, near, _ = together(far, one["near"][1], *marks)
            one["pair"] = z_first_sum(place, near, one["got"], far)
            return after(values, one["pair"][0])

        def y_done(values):
            jobs = ((0, 2 * width, 1, 0, 3 * part), (0, width, 1, 3 * part, part))
            groups = (early, after(last_group, marks[-1]))
            last["near"], last["away"] = weight_grads(place, jobs, groups, own_width, pairs, whole_order)
            got = swap(after(two["away"][1], two["first"]), "patch", 1)
            values, got, far, *_ = together(values, got, swap(two["far"], "patch", 2), *last["near"])
            two["pair"] = z_first_sum(place, two["near"][1], got, far)
            return values

        def z_done(values):
            near, away = one["pair"]
            *values, got, _ = together(*values, swap(away, "patch", 4), two["pair"][0])
            one["own"] = z_last_sum(place, near, got)
            return values

        def b_done(values):
            near, away = two["pair"]
            *values, last["got"], got = together(*values, swap(last["away"][0], "patch", 1), swap(away, "patch", 4))
            late = after(field_low, last["got"])
            last["field"] = lax.all_to_all(late, "var", split_axis=0, concat_axis=0, tiled=True)
            last["far"] = pair_sum(place, last["near"][0], last["got"])
            two["own"] = z_last_sum(place, near, got)
            return [after(values[0], last["far"]), *values[1:]]

        def y_back(values):
            values, one["across"], last["field"] = together(values, swap(one["own"], "var", 2), last["field"])
            return values

        def var_done(values):
            far, across = swap(last["far"], "patch", 2), swap(two["own"], "var", 2)
            near, away = z_first_sum(place, last["near"][1], last["got"], far)
            two["parts"] = (two["own"], swap(two["own"], "var", 1), across, swap(across, "var", 1))
            last["own"] = z_last_sum(place, near, swap(away, "patch", 4))
            own, across = one["own"], one["across"]
            values, inner, corner, _ = together(values, swap(own, "var", 1), swap(across, "var", 1), near)
            one["parts"] = (own, inner, across, corner)
            return values

        m_pieces = sum_over_all(place, *m_parts, (core_done, x_done, y_done, z_done, b_done, y_back, var_done), marks)
        field_grad = last["field"]
        (mlp_out_grad,) = join(place, one["parts"], (width,), 1)
        mlp_in_grad, trunk_out_grad = join(place, two["parts"], (quarter, part), 0)
        mlp_out_grad = mlp_out_grad.reshape(hidden // patches, width)
        trunk_qkv_grad, agg_out_grad = join(place, gather_over_var(last["own"]), (3 * part, part), 0)
    else:

        def slices(values):
            values = values.reshape(seg, group, values.shape[1] // group).transpose(1, 0, 2)
            return lax.all_to_all(values, "var", split_axis=0, concat_axis=0, tiled=True)

        def everyone(values):
            return lax.all_gather(values, "var", axis=0, tiled=True)

        def total(left, right):
            value = mm(left.reshape(-1, left.shape[-1]), right.reshape(-1, right.shape[-1]), TN).astype(BF16)
            value = lax.psum_scatter(value, "patch", scatter_dimension=0, tiled=True)
            return lax.all_gather(value, "var", axis=0)

        def joined(value):
            return value.transpose(1, 0, 2).reshape(value.shape[1], -1).astype(F32)

        size = hidden // (patches * group)
        active_rows = active_low.reshape(seg, patches, group, size).transpose(0, 2, 1, 3).reshape(seg, hidden)
        mlp_out_grad = total(slices(active_rows), everyone(out_grad_low)).reshape(hidden // patches, width).astype(F32)
        mlp_in_grad = joined(total(everyone(normed_two_low), slices(inner_grad)))
        trunk_out_grad = joined(total(everyone(attended), slices(branch_low)))
        trunk_qkv_grad = joined(total(everyone(normed_one_low), slices(triple_grad)))
        agg_out_grad = joined(total(everyone(mixed_low), slices(agg_grad)))
        m_all = lax.psum(m_parts[0], ("patch", "var")).transpose(1, 0, 2).reshape(-1, width)
    if fast:
        value_proj_grad, patch_grad, embed_grad, key_proj_grad, query_proj_grad, *lines = front_last(
            place, m_pieces, arrays
        )
        agg_query_grad, norm_one_grad, norm_two_grad = (line[0] for line in lines)
    else:
        value_rows, key_query_rows = own_rows(value_proj), own_rows(key_query)
        m_sum, me_sum = m_all[: VARS * pixels], m_all[VARS * pixels : VARS * pixels + VARS]
        s_rows = m_all[VARS * pixels + VARS :].astype(F32)
        s_all = s_rows[:, : VARS * pixels]
        se_all = s_rows[:, VARS * pixels : VARS * pixels + VARS]
        norm_sums = s_rows[:, width - 2 * head_dim :]
        value_proj_grad = mm(own_cols(weight_rows), m_sum, TN) + mm(own_cols(var_embed), me_sum, TN)
        patch_grad = mm(m_sum, value_rows, NT) + mm(
            s_all, key_query_rows, (((0,), (1,)), ((), ())), precision=HIGHEST
        )
        embed_grad = mm(me_sum, value_rows, NT) + mm(
            se_all, key_query_rows, (((0,), (1,)), ((), ())), precision=HIGHEST
        )
        key_sum = (mm(s_all.astype(BF16), weight_rows) + mm(se_all.astype(BF16), var_embed)) * scaling
        head_rows = jnp.where(in_head.T, agg_q[None, :], 0.0)
        key_proj_grad = mm(own_cols(key_sum), head_rows, TN, precision=HIGHEST)
        crossed = mm(jnp.concatenate(split_high_low(key_sum), axis=0), key_proj)
        crossed = crossed[:HEADS] + crossed[HEADS:]
        aggq_grad = jnp.sum(jnp.where(in_head.T, crossed, 0.0), axis=0)
        query_proj_grad = own_query(agg_query) * aggq_grad[None, :]
        agg_query_grad = jnp.sum(own_rows(query_proj).astype(F32) * aggq_grad[None, :], axis=1)
        norm_one_grad = lax.dynamic_slice_in_dim(norm_sums[:, :head_dim].reshape(width), start, own_width, 0)
        norm_two_grad = lax.dynamic_slice_in_dim(norm_sums[:, head_dim:].reshape(width), start, own_width, 0)
    patch_grad = patch_grad.reshape(VARS, pixels, own_width)
    field_grad = field_grad.reshape(all_rows, var_local, pixels, seg).transpose(0, 3, 1, 2)
    return (
        block_out,
        field_grad,
        patch_grad,
        embed_grad,
        agg_query_grad,
        query_proj_grad,
        key_proj_grad,
        value_proj_grad,
        agg_out_grad,
        norm_one_grad,
        trunk_qkv_grad,
        trunk_out_grad,
        norm_two_grad,
        mlp_in_grad,
        mlp_out_grad,
    )


def solution(mesh):
    whole = P()
    placed = (P(None, "patch", "var", None),) + (whole,) * 15 + (P("var", "patch", None),)
    rows = P("patch", None)
    return jax.shard_map(
        local,
        mesh=mesh,
        in_specs=placed,
        out_specs=(
            P("var", "patch", None),
            P(None, "patch", "var", None),
            P(None, None, "patch"),
            P(None, "patch"),
            P("patch"),
            rows,
            rows,
            rows,
            rows,
            P("patch"),
            rows,
            rows,
            P("patch"),
            rows,
            rows,
        ),
        check_vma=False,
    )
```

```python
import functools
import math

import jax
import jax.numpy as jnp
from jax import lax
from jax.experimental import pallas as pl
from jax.experimental.pallas import tpu as pltpu
from jax.sharding import PartitionSpec as P

HEADS = 16
VARS = 48
EPSILON = 1e-05
MASKED = -1e30
HIGHEST = lax.Precision.HIGHEST
BF16 = jnp.bfloat16
F32 = jnp.float32
NN = (((1,), (0,)), ((), ()))
NT = (((1,), (1,)), ((), ()))
TN = (((0,), (0,)), ((), ()))


def cost(flops):
    return pl.CostEstimate(flops=flops, bytes_accessed=1 << 20, transcendentals=0)


def mm(a, b, dims=NN, precision=None):
    return lax.dot_general(a, b, dims, precision=precision, preferred_element_type=F32)


def layer_norm(values, gain_vec):
    average = jnp.mean(values, axis=-1, keepdims=True)
    center = values - average
    spread = jnp.mean(center * center, axis=-1, keepdims=True)
    return center * lax.rsqrt(spread + EPSILON) * gain_vec


def gelu_exact(values):
    return jax.nn.gelu(values, approximate=False)


def split_high_low(values):
    high = values.astype(BF16)
    return high, (values - high.astype(F32)).astype(BF16)


def front_forward_kernel(
    pixels, ids_ref, field_ref, weight_ref, bias_ref, vwt_ref, vet_ref, x_ref, p_ref, mixed_ref, spread_ref, mt_ref
):
    seg = field_ref.shape[1]
    head_dim = mixed_ref.shape[1] // HEADS
    for slot in range(VARS):
        start = pl.multiple_of(ids_ref[0, slot] * pixels, pixels)
        x_ref[pl.ds(start, pixels), :] = field_ref[slot * pixels : (slot + 1) * pixels, :]
    rows = VARS * pixels
    mine = lax.broadcasted_iota(jnp.int32, (VARS, rows), 1) // pixels
    mine = mine == lax.broadcasted_iota(jnp.int32, (VARS, rows), 0)
    bias = bias_ref[...].T
    parts = []
    for h in range(HEADS):
        spread = jnp.where(mine, weight_ref[h : h + 1, :], 0.0).astype(BF16)
        spread_ref[h * VARS : (h + 1) * VARS, :] = spread
        parts.append(mm(spread, x_ref[...]) + bias[:, h : h + 1])
    scores = jnp.stack(parts)
    top = jnp.max(scores, axis=1, keepdims=True)
    exponent = jnp.exp(scores - top)
    total = jnp.sum(exponent, axis=1, keepdims=True)
    p_ref[...] = (exponent * (1.0 / total)).reshape(HEADS * VARS, seg)

    def head(h, carry):
        shares = p_ref[pl.ds(pl.multiple_of(h * VARS, VARS), VARS), :]
        pix = x_ref[...].astype(F32).reshape(VARS, pixels, seg)
        scaled = (pix * shares[:, None, :]).astype(BF16).reshape(VARS * pixels, seg)
        rows = pl.ds(pl.multiple_of(h * head_dim, head_dim), head_dim)
        mt_ref[rows, :] = mm(vwt_ref[rows, :], scaled) + mm(vet_ref[rows, :], shares.astype(BF16))
        return carry

    lax.fori_loop(0, HEADS, head, 0, unroll=2)
    mixed_ref[...] = mt_ref[...].T.astype(BF16)


def front_forward(own_ids, own_field, score_weight, bias, vwt, vet):
    rows, seg = own_field.shape
    width = vwt.shape[0]
    vmem = pl.BlockSpec(memory_space=pltpu.VMEM)
    return pl.pallas_call(
        functools.partial(front_forward_kernel, rows // VARS),
        out_shape=(
            jax.ShapeDtypeStruct((rows, seg), BF16),
            jax.ShapeDtypeStruct((HEADS * VARS, seg), F32),
            jax.ShapeDtypeStruct((seg, width), BF16),
            jax.ShapeDtypeStruct((HEADS * VARS, rows), BF16),
        ),
        in_specs=[pl.BlockSpec(memory_space=pltpu.SMEM)] + [vmem] * 5,
        out_specs=(vmem,) * 4,
        scratch_shapes=[pltpu.VMEM((width, seg), F32)],
        cost_estimate=cost(60000000000),
        name="front_forward",
    )(own_ids, own_field, score_weight, bias, vwt, vet)


def front_backward_kernel(
    pixels,
    fast,
    place_ref,
    ids_ref,
    x_ref,
    p_ref,
    mg_ref,
    vw_ref,
    ve_ref,
    spread_ref,
    norm_one_ref,
    norm_two_ref,
    field_ref,
    *rest,
):
    rows, seg = x_ref.shape
    m_refs, (fs_ref, dx_ref, s_ref) = rest[:-3], rest[-3:]
    size = m_refs[0].shape[-1]

    def quarter_of(quarter, store):
        if not fast:
            store(m_refs[0].at[quarter])
            return
        mine = quarter // 2 == place_ref[CORE]
        pl.when(mine)(lambda: store(m_refs[0].at[quarter % 2]))
        pl.when(jnp.logical_not(mine))(lambda: store(m_refs[1].at[quarter % 2]))
    width = mg_ref.shape[1]
    head_dim = width // HEADS
    pair_dim = 2 * head_dim
    lane = lax.broadcasted_iota(jnp.int32, (seg, pair_dim), 1)
    dx_ref[...] = jnp.zeros_like(dx_ref)
    pairs = size // pair_dim

    def pair(q, carry):
        cols = pl.ds(pl.multiple_of(q * pair_dim, pair_dim), pair_dim)
        grad = mg_ref[:, cols]
        none = jnp.zeros_like(grad)
        both = jnp.concatenate(
            [jnp.where(lane < head_dim, grad, none), jnp.where(lane >= head_dim, grad, none)], axis=0
        )
        inner = mm(vw_ref[:, cols], both, NT)
        inner_e = mm(ve_ref[:, cols], both, NT)
        pix = x_ref[...].astype(F32).reshape(VARS, pixels, seg)
        scaled, weights = [], []
        for k in range(2):
            hrows = pl.ds(pl.multiple_of((2 * q + k) * VARS, VARS), VARS)
            shares = p_ref[hrows, :]
            part = inner[:, k * seg : (k + 1) * seg].reshape(VARS, pixels, seg)
            share_grad = jnp.sum(pix * part, axis=1) + inner_e[:, k * seg : (k + 1) * seg]
            delta = jnp.sum(shares * share_grad, axis=0, keepdims=True)
            fs_ref[hrows, :] = shares * (share_grad - delta)
            wide = shares[:, None, :]
            dx_ref[...] += (part * wide).reshape(rows, seg)
            scaled.append((pix * wide).astype(BF16).reshape(rows, seg))
            weights.append(shares.astype(BF16))
        quarter, within = q // pairs, pl.ds(pl.multiple_of(q % pairs * pair_dim, pair_dim), pair_dim)
        m_part = mm(jnp.concatenate(scaled, axis=1), both).astype(BF16)
        me_part = mm(jnp.concatenate(weights, axis=1), both).astype(BF16)

        def store(ref):
            ref[0:rows, within] = m_part
            ref[rows : rows + VARS, within] = me_part

        quarter_of(quarter, store)
        return carry

    lax.fori_loop(0, HEADS // 2, pair, 0)
    score_grad = fs_ref[...]
    low = score_grad.astype(BF16)
    dx = dx_ref[...] + mm(spread_ref[...], low, TN)
    dx_ref[...] = dx
    for slot in range(VARS):
        start = pl.multiple_of(ids_ref[0, slot] * pixels, pixels)
        field_ref[slot * pixels : (slot + 1) * pixels, :] = dx_ref[pl.ds(start, pixels), :].astype(BF16)
    ones = jnp.ones((8, seg), F32)
    s_ref[...] = jnp.zeros_like(s_ref)
    var_row = lax.broadcasted_iota(jnp.int32, (VARS, rows), 0)
    var_col = lax.broadcasted_iota(jnp.int32, (VARS, rows), 1) // pixels
    keep = var_row == var_col
    for h in range(HEADS):
        outer = mm(low[h * VARS : (h + 1) * VARS, :], x_ref[...], NT)
        s_ref[h : h + 1, 0:rows] = jnp.sum(jnp.where(keep, outer, 0.0), axis=0, keepdims=True)
        sums = mm(ones, score_grad[h * VARS : (h + 1) * VARS, :], NT, precision=HIGHEST)
        s_ref[h : h + 1, rows : rows + VARS] = sums[0:1, :]
    for h in range(HEADS):
        for ref, first in ((norm_one_ref, width - pair_dim), (norm_two_ref, width - head_dim)):
            s_ref[h : h + 1, first : first + head_dim] = ref[:, h * head_dim : (h + 1) * head_dim]
    for quarter in range(4):
        part = s_ref[:, quarter * size : (quarter + 1) * size].astype(BF16)

        def store_sums(ref, part=part):
            ref[rows + VARS :, :] = part

        quarter_of(quarter, store_sums)


def front_backward(fast, place, own_ids, x_own, shares, mixed_grad, vw, ve, spread, norm_one, norm_two):
    rows, seg = x_own.shape
    width = mixed_grad.shape[1]
    vmem = pl.BlockSpec(memory_space=pltpu.VMEM)
    smem = pl.BlockSpec(memory_space=pltpu.SMEM)
    tall = rows + VARS + HEADS
    if fast:
        sums = (jax.ShapeDtypeStruct((2, tall, width // 4), BF16),) * 2
    else:
        sums = (jax.ShapeDtypeStruct((4, tall, width // 4), BF16),)
    return pl.pallas_call(
        functools.partial(front_backward_kernel, rows // VARS, fast),
        out_shape=(jax.ShapeDtypeStruct((rows, seg), BF16), *sums),
        in_specs=[smem, smem] + [vmem] * 8,
        out_specs=(vmem,) * (1 + len(sums)),
        scratch_shapes=[
            pltpu.VMEM((HEADS * VARS, seg), F32),
            pltpu.VMEM((rows, seg), F32),
            pltpu.VMEM((HEADS, width), F32),
        ],
        cost_estimate=cost(100000000),
        name="front_backward",
    )(place, own_ids, x_own, shares, mixed_grad, vw, ve, spread, norm_one, norm_two)


def load_parts(ref, part, seg, out_ref):
    for source in range(ref.shape[0]):
        out_ref[source * seg : (source + 1) * seg, :] = ref[source, part * seg : (part + 1) * seg, :]


def attend_forward_kernel(head_dim, block, count_ref, qkv_ref, out_ref, lse_ref, q_ref, k_ref, vt_ref):
    full, width = q_ref.shape
    seg = full // qkv_ref.shape[0]
    scaling = jnp.asarray(1.0 / math.sqrt(head_dim), BF16)
    load_parts(qkv_ref, 2, seg, q_ref)
    vt_ref[...] = q_ref[...].T
    load_parts(qkv_ref, 0, seg, q_ref)
    load_parts(qkv_ref, 1, seg, k_ref)
    count = count_ref[0, 0]
    lane = lax.broadcasted_iota(jnp.int32, (block, width), 1) // head_dim
    row = lax.broadcasted_iota(jnp.int32, (width, block), 0) // head_dim
    valid = lax.broadcasted_iota(jnp.int32, (full, block), 0) < count

    def step(i, carry):
        part = pl.ds(pl.multiple_of(i * block, block), block)
        query = q_ref[part, :]
        total = jnp.zeros((width, block), F32)
        for h in range(width // head_dim):
            own = jnp.where(lane == h, query, jnp.zeros_like(query)) * scaling
            scores = jnp.where(valid, mm(k_ref[...], own, NT), MASKED)
            top = jnp.max(scores, axis=0, keepdims=True)
            exponent = jnp.exp(scores - top)
            denominator = jnp.sum(exponent, axis=0, keepdims=True)
            lse_ref[h : h + 1, part] = top + jnp.log(denominator)
            mixed = mm(vt_ref[...], exponent.astype(BF16)) * (1.0 / denominator)
            total = jnp.where(row == h, mixed, total)
        out_ref[part, :] = total.T.astype(BF16)
        return carry

    lax.fori_loop(0, full // block, step, 0)


def attend_forward(count, qkv, head_dim):
    parts, triple_rows, width = qkv.shape
    full = parts * triple_rows // 3
    vmem = pl.BlockSpec(memory_space=pltpu.VMEM)
    block = min(512, full)
    return pl.pallas_call(
        functools.partial(attend_forward_kernel, head_dim, block),
        out_shape=(
            jax.ShapeDtypeStruct((full, width), BF16),
            jax.ShapeDtypeStruct((width // head_dim, full), F32),
        ),
        in_specs=[pl.BlockSpec(memory_space=pltpu.SMEM), vmem],
        out_specs=(vmem, vmem),
        scratch_shapes=[
            pltpu.VMEM((full, width), BF16),
            pltpu.VMEM((full, width), BF16),
            pltpu.VMEM((width, full), BF16),
        ],
        cost_estimate=cost(60000000000),
        name="attend_forward",
    )(count, qkv)


def attend_backward_kernel(
    head_dim, block, count_ref, qkv_ref, grad_ref, lse_ref, out_ref, q_ref, k_ref, v_ref, kt_ref, dk_ref, dv_ref
):
    full, width = q_ref.shape
    seg = full // qkv_ref.shape[0]
    scaling = 1.0 / math.sqrt(head_dim)
    load_parts(qkv_ref, 0, seg, q_ref)
    load_parts(qkv_ref, 1, seg, k_ref)
    load_parts(qkv_ref, 2, seg, v_ref)
    kt_ref[...] = k_ref[...].T
    dk_ref[...] = jnp.zeros_like(dk_ref)
    dv_ref[...] = jnp.zeros_like(dv_ref)
    count = count_ref[0, 0]
    lane = lax.broadcasted_iota(jnp.int32, (block, width), 1) // head_dim
    row = lax.broadcasted_iota(jnp.int32, (width, block), 0) // head_dim
    valid = lax.broadcasted_iota(jnp.int32, (full, block), 0) < count

    def step(i, carry):
        part = pl.ds(pl.multiple_of(i * block, block), block)
        query = q_ref[part, :]
        grad = grad_ref[part, :]
        total = jnp.zeros((width, block), F32)
        for h in range(width // head_dim):
            own = jnp.where(lane == h, query, jnp.zeros_like(query)) * jnp.asarray(scaling, BF16)
            own_grad = jnp.where(lane == h, grad, jnp.zeros_like(grad))
            scores = jnp.where(valid, mm(k_ref[...], own, NT), MASKED)
            shares = jnp.exp(scores - lse_ref[h : h + 1, part])
            share_grad = mm(v_ref[...], own_grad, NT)
            dot = jnp.sum(shares * share_grad, axis=0, keepdims=True)
            score_grad = (shares * (share_grad - dot)).astype(BF16)
            dv_ref[...] += mm(shares.astype(BF16), own_grad)
            dk_ref[...] += mm(score_grad, own)
            total = jnp.where(row == h, mm(kt_ref[...], score_grad), total)
        turned = (total * scaling).T.astype(BF16)
        for piece in range(block // seg):
            out_ref[i * (block // seg) + piece, 0:seg, :] = turned[piece * seg : (piece + 1) * seg, :]
        return carry

    lax.fori_loop(0, full // block, step, 0)
    for source in range(full // seg):
        rows = slice(source * seg, (source + 1) * seg)
        out_ref[source, seg : 2 * seg, :] = dk_ref[rows, :].astype(BF16)
        out_ref[source, 2 * seg : 3 * seg, :] = dv_ref[rows, :].astype(BF16)


def attend_backward(count, qkv, grad, lse, head_dim):
    parts, triple_rows, width = qkv.shape
    full = parts * triple_rows // 3
    vmem = pl.BlockSpec(memory_space=pltpu.VMEM)
    block = min(256, full)
    return pl.pallas_call(
        functools.partial(attend_backward_kernel, head_dim, block),
        out_shape=jax.ShapeDtypeStruct(qkv.shape, BF16),
        in_specs=[pl.BlockSpec(memory_space=pltpu.SMEM), vmem, vmem, vmem],
        out_specs=vmem,
        scratch_shapes=[pltpu.VMEM((full, width), BF16)] * 3
        + [pltpu.VMEM((width, full), BF16)]
        + [pltpu.VMEM((full, width), F32)] * 2,
        cost_estimate=cost(100000000000),
        name="attend_backward",
    )(count, qkv, grad, lse)


def gathered_attention(triple, count, head_dim):
    seg, triple_width = triple.shape
    width = triple_width // 3
    scaling = 1.0 / math.sqrt(head_dim)
    full = seg * lax.axis_size("patch")
    query = triple[:, :width].reshape(seg, HEADS, head_dim)
    key = lax.all_gather(triple[:, width : 2 * width], "patch", axis=0, tiled=True)
    value = lax.all_gather(triple[:, 2 * width :], "patch", axis=0, tiled=True)
    key = key.reshape(full, HEADS, head_dim)
    value = value.reshape(full, HEADS, head_dim)
    valid = (jnp.arange(full, dtype=jnp.int32) < count)[None, None, :]

    def score():
        raw = jnp.einsum("qhd,khd->hqk", query, key, preferred_element_type=F32) * scaling
        return jnp.where(valid, raw, MASKED)

    masked = score()
    top = jnp.max(masked, axis=-1, keepdims=True)
    exponent = jnp.exp(masked - top)
    denominator = jnp.sum(exponent, axis=-1, keepdims=True)
    shares_low = (exponent / denominator).astype(BF16)
    lse = top + jnp.log(denominator)
    attended = jnp.einsum("hqk,khd->qhd", shares_low, value, preferred_element_type=F32)

    def backward(grad):
        grad = grad.reshape(seg, HEADS, head_dim)
        shares = jnp.exp(score() - lse)
        share_grad = jnp.einsum("qhd,khd->hqk", grad, value, preferred_element_type=F32)
        dot = jnp.sum(shares * share_grad, axis=-1, keepdims=True)
        score_grad = (shares * (share_grad - dot)).astype(BF16)
        q_grad = jnp.einsum("hqk,khd->qhd", score_grad, key, preferred_element_type=F32) * scaling
        v_all = jnp.einsum("hqk,qhd->khd", shares.astype(BF16), grad, preferred_element_type=F32)
        k_all = jnp.einsum("hqk,qhd->khd", score_grad, query, preferred_element_type=F32) * scaling
        k_grad, v_grad = (
            lax.psum_scatter(
                part.reshape(full, width).astype(BF16), "patch", scatter_dimension=0, tiled=True
            )
            for part in (k_all, v_all)
        )
        return jnp.concatenate([q_grad.reshape(seg, width).astype(BF16), k_grad, v_grad], axis=1)

    return attended.reshape(seg, width).astype(BF16), backward


def to_heads(values):
    return lax.all_to_all(values, "patch", split_axis=0, concat_axis=0, tiled=True)


def queries_to_heads(triple):
    seg, triple_width = triple.shape
    parts = lax.axis_size("patch")
    own = triple_width // (3 * parts)
    moved = triple.reshape(seg, 3, parts, own).transpose(2, 1, 0, 3).reshape(parts, 3 * seg, own)
    return to_heads(moved)


def weight_grad_kernel(jobs, index, near, away, place_ref, *refs):
    split = len(refs) - len(near) - len(away)
    arrays, outs = refs[:split], refs[split:]
    rows = outs[0].shape[1]

    def member(group, s):
        first, stacked = index[group]
        return arrays[first].at[place_ref[ME] ^ s] if stacked else arrays[first + s]

    sides = (1 - place_ref[Y],) * len(away) + (place_ref[Y],) * len(near)
    start = 0
    for left, left_start, right, right_start, cols in jobs:
        values = [member(right, s)[:, pl.ds(right_start, cols)] for s in range(4)]
        values = jnp.concatenate(values, axis=0)
        for out, side, blocks in zip(outs, sides, away + near):
            for slot, k in enumerate(blocks):
                source = 2 * (place_ref[Z] ^ k) + side
                group = [member(left, s) for s in range(4)]
                if len(group[0].shape) == 3:
                    factor = [ref[source] for ref in group]
                else:
                    block = pl.ds(pl.multiple_of(left_start + source * rows, rows), rows)
                    factor = [ref[:, block] for ref in group]
                factor = jnp.concatenate(factor, axis=0)
                out[slot, :, start : start + cols] = mm(factor, values, TN).astype(BF16)
        start += cols


def weight_grads(place, jobs, groups, rows, near, away):
    arrays, index = [], []
    for group in groups:
        stacked = not isinstance(group, (list, tuple))
        index.append((len(arrays), stacked))
        arrays += [group] if stacked else list(group)
    total = sum(job[-1] for job in jobs)
    shapes = [((len(blocks), rows, total), BF16) for blocks in away + near]
    kernel = functools.partial(weight_grad_kernel, jobs, index, near, away)
    outs = small_call(kernel, place, arrays, shapes, effort=2000, name="weight_grads")
    return outs[len(away) :], outs[: len(away)]


def swap(values, axis, bit):
    return lax.ppermute(values, axis, [(i, i ^ bit) for i in range(lax.axis_size(axis))])


def together(*values):
    return lax.optimization_barrier(values)


def after(value, *others):
    return lax.optimization_barrier((value, *others))[0]


def small_call(kernel, place, arrays, shapes, scratch=(), effort=200, name="small"):
    vmem = pl.BlockSpec(memory_space=pltpu.VMEM)
    return pl.pallas_call(
        kernel,
        out_shape=tuple(jax.ShapeDtypeStruct(dims, dtype) for dims, dtype in shapes),
        in_specs=[pl.BlockSpec(memory_space=pltpu.SMEM)] + [vmem] * len(arrays),
        out_specs=(vmem,) * len(shapes),
        scratch_shapes=list(scratch),
        cost_estimate=cost(int(effort * 10**9)),
        name=name,
    )(place, *arrays)


ME, CORE, X, Y, Z = range(5)


def tokens_of_group(values):
    across = swap(values, "var", 2)
    return values, swap(values, "var", 1), across, swap(across, "var", 1)


def copies_of_group(values):
    return (values,) + tuple(swap(values, "var", bit) for bit in (1, 2, 3))


def slices_of_group(pieces):
    return (pieces[0],) + tuple(swap(pieces[bit], "var", bit) for bit in (1, 2, 3))


def z_pieces(place, near, got):
    _, rows, cols = near.shape

    def kernel(place_ref, near_ref, got_ref, *outs):
        for bit in range(4):
            block = place_ref[Z] ^ bit
            outs[bit][...] = (near_ref[block].astype(F32) + got_ref[block].astype(F32)).astype(BF16)

    return small_call(kernel, place, (near, got), [((rows, cols), BF16)] * 4, name="z_pieces")


def z_exchange(pieces):
    return (pieces[0],) + tuple(swap(pieces[bit], "patch", 2 * bit) for bit in (1, 2, 3))


def z_sum(place, arrays):

    def kernel(place_ref, first, second, third, fourth, out):
        total = first[...].astype(F32) + second[...].astype(F32) + third[...].astype(F32) + fourth[...].astype(F32)
        out[...] = total.astype(BF16)

    return small_call(kernel, place, arrays, [(arrays[0].shape, BF16)], name="z_sum")[0]


def pair_sum(place, near, got):
    def kernel(place_ref, near_ref, got_ref, out):
        for k in range(2):
            out[k] = (near_ref[k].astype(F32) + got_ref[k].astype(F32)).astype(BF16)

    return small_call(kernel, place, (near, got), [(near.shape, BF16)], name="pair_sum")[0]


def z_first_sum(place, near, got, far):
    first = got.shape[0] - 2

    def kernel(place_ref, near_ref, got_ref, far_ref, stay, away):
        for out, k in ((away, 1), (stay, 0)):
            total = near_ref[k].astype(F32) + got_ref[first + k].astype(F32) + far_ref[k].astype(F32)
            out[...] = total.astype(BF16)

    return small_call(kernel, place, (near, got, far), [(near.shape[1:], BF16)] * 2, name="z_first_sum")


def z_last_sum(place, near, got):
    def kernel(place_ref, near_ref, got_ref, out):
        out[...] = (near_ref[...].astype(F32) + got_ref[...].astype(F32)).astype(BF16)

    return small_call(kernel, place, (near, got), [(near.shape, BF16)], name="z_last_sum")[0]


def gather_over_var(own):
    across = swap(own, "var", 2)
    return own, swap(own, "var", 1), across, swap(across, "var", 1)


def join(place, pieces, widths, stacked):
    rows = pieces[0].shape[0]

    def kernel(place_ref, *refs):
        start = 0
        for k, (out, size) in enumerate(zip(refs[4:], widths)):
            for s in range(4):
                v = place_ref[ME] ^ s
                values = refs[s][:, start : start + size].astype(F32)
                if k < stacked:
                    out[v] = values
                else:
                    out[:, pl.ds(pl.multiple_of(v * size, size), size)] = values
            start += size

    shapes = [((4, rows, size) if k < stacked else (rows, 4 * size), F32) for k, size in enumerate(widths)]
    return small_call(kernel, place, pieces, shapes, name="join")


def sum_over_all(place, stay, away, hooks, marks):
    _, rows, cols = stay.shape
    half = rows // 2
    size = half // 4
    hooks = iter(hooks)

    def core_kernel(place_ref, stay_ref, got_ref, stay_out, away_out):
        for out, which in ((away_out, 1 - place_ref[X]), (stay_out, place_ref[X])):
            out[...] = (stay_ref[which].astype(F32) + got_ref[which].astype(F32)).astype(BF16)

    got = next(hooks)(swap(away, "var", 1))
    stay, away = small_call(core_kernel, place, (stay, got), [((rows, cols), BF16)] * 2, name="core_sum")
    marks.append(stay)

    def x_kernel(place_ref, stay_ref, got_ref, stay_out, away_out):
        for out, which in ((away_out, 1 - place_ref[Y]), (stay_out, place_ref[Y])):
            out[...] = (stay_ref[which].astype(F32) + got_ref[which].astype(F32)).astype(BF16)

    got = next(hooks)(swap(away, "var", 2))
    halves = (2, half, cols)
    stay, away = small_call(
        x_kernel, place, (stay.reshape(halves), got.reshape(halves)), [((half, cols), BF16)] * 2, name="x_sum"
    )
    marks.append(stay)
    got = next(hooks)(swap(away, "patch", 1))
    pieces = z_exchange(z_pieces(place, stay.reshape(4, size, cols), got.reshape(4, size, cols)))
    kept = z_sum(place, next(hooks)(pieces))

    def z_kernel(place_ref, *refs):
        for s in range(4):
            refs[4][place_ref[Z] ^ s] = refs[s][...]

    arrays = (kept,) + tuple(swap(kept, "patch", 2 * bit) for bit in (1, 2, 3))
    own = small_call(z_kernel, place, next(hooks)(arrays), [((4, size, cols), BF16)], name="z_join")[0]

    def y_kernel(place_ref, own_ref, other_ref, out):
        out[place_ref[Y]] = own_ref[...]
        out[1 - place_ref[Y]] = other_ref[...]

    own = own.reshape(half, cols)
    arrays = (own, next(hooks)(swap(own, "patch", 1)))
    full = small_call(y_kernel, place, arrays, [(halves, BF16)], name="y_join")[0].reshape(rows, cols)

    across = next(hooks)(swap(full, "var", 2))
    return full, swap(full, "var", 1), across, swap(across, "var", 1)


def middle_kernel(
    sub,
    place_ref,
    att_ref,
    front_ref,
    valid_ref,
    og_ref,
    tout_ref,
    gain_ref,
    win_ref,
    wout_ref,
    block_ref,
    late_ref,
    *refs,
):
    actives, middles = refs[0:4], refs[4:8]
    grad_ref, after_ref, gain_grad_ref, residual_ref, unit_ref, rate_ref, acc_ref, back_ref, wide_ref, branch_ref = refs[8:]
    step = pl.program_id(0)
    seg, width = front_ref.shape
    parts = att_ref.shape[0]
    own = width // parts
    me = place_ref[0]
    block = win_ref.shape[1]
    slot = block // (4 * sub)
    quarter = width // 4
    hidden = slot * sub * pl.num_programs(0)

    @pl.when(step == 0)
    def _():
        for p in range(parts):
            branch_ref[:, p * own : (p + 1) * own] = att_ref[p]
        after = front_ref[...] + mm(branch_ref[...], tout_ref[...])
        residual_ref[...] = after
        center = after - jnp.mean(after, axis=1, keepdims=True)
        rate = lax.rsqrt(jnp.mean(center * center, axis=1, keepdims=True) + EPSILON)
        unit = center * rate
        unit_ref[...] = unit
        rate_ref[...] = rate
        late_ref[...] = (unit * gain_ref[...]).astype(BF16)
        acc_ref[...] = jnp.zeros_like(acc_ref)
        back_ref[...] = jnp.zeros_like(back_ref)

    inner = mm(late_ref[...], win_ref[...])
    cumulative = 0.5 * (1.0 + lax.erf(inner * math.sqrt(0.5)))
    active = (inner * cumulative).astype(BF16)
    acc_ref[...] += mm(active, wout_ref[...])
    slope = cumulative + inner * (jnp.exp(-0.5 * inner * inner) * (1.0 / math.sqrt(2.0 * math.pi)))
    inner_grad = (mm(og_ref[...], wout_ref[...], NT) * slope).astype(BF16)
    back_ref[...] += mm(inner_grad, win_ref[...], NT)
    wide_ref[...] = active
    for q in range(sub):
        cols = pl.ds(pl.multiple_of((step * sub + q) * slot, slot), slot)
        for s in range(4):
            actives[s][:, cols] = wide_ref[:, pl.ds(pl.multiple_of((4 * q + (me ^ s)) * slot, slot), slot)]
    owner = step * block // hidden
    place = pl.ds(pl.multiple_of(step * block - owner * hidden, block), block)
    for s in range(4):

        @pl.when((me ^ s) == owner)
        def _(s=s):
            middles[s][:, place] = inner_grad

    @pl.when(step == pl.num_programs(0) - 1)
    def _():
        valid = valid_ref[...]
        block_ref[...] = ((residual_ref[...] + acc_ref[...]) * valid).astype(BF16)
        unit = unit_ref[...]
        back = back_ref[...]
        gain_grad_ref[...] = jnp.sum(back * unit, axis=0, keepdims=True)
        scaled = back * gain_ref[...]
        inside = jnp.mean(scaled * unit, axis=1, keepdims=True)
        total = rate_ref[...] * (scaled - jnp.mean(scaled, axis=1, keepdims=True) - unit * inside)
        total = og_ref[...].astype(F32) + total
        after_ref[...] = total
        branch_ref[...] = total.astype(BF16)
        for s in range(4):
            start = pl.multiple_of((me ^ s) * quarter, quarter)
            middles[s][:, hidden:] = branch_ref[:, pl.ds(start, quarter)]
        turned = mm(branch_ref[...], tout_ref[...], NT).astype(BF16)
        for p in range(parts):
            grad_ref[p] = turned[:, p * own : (p + 1) * own]


def middle(place, attended, front_out, valid, out_grad, trunk_out, gain, mlp_in, mlp_out):
    seg, width = front_out.shape
    hidden = mlp_in.shape[1]
    parts = attended.shape[0]
    sub = 2
    block = hidden * sub // parts
    shape = jax.ShapeDtypeStruct

    def still(*dims):
        return pl.BlockSpec(dims, lambda i: (0,) * len(dims))

    piece, wider = shape((seg, hidden // 4), BF16), shape((seg, hidden // 4 + width // 4), BF16)
    return pl.pallas_call(
        functools.partial(middle_kernel, sub),
        grid=(parts // sub,),
        out_shape=(
            shape((seg, width), BF16),
            shape((seg, width), BF16),
            *((piece,) * 4),
            *((wider,) * 4),
            shape(attended.shape, BF16),
            shape((seg, width), F32),
            shape((1, width), F32),
        ),
        in_specs=[
            pl.BlockSpec(memory_space=pltpu.SMEM),
            still(*attended.shape),
            still(seg, width),
            still(seg, 1),
            still(seg, width),
            still(width, width),
            still(1, width),
            pl.BlockSpec((width, block), lambda i: (0, i)),
            pl.BlockSpec((block, width), lambda i: (i, 0)),
        ],
        out_specs=(
            still(seg, width),
            still(seg, width),
            *((still(*piece.shape),) * 4),
            *((still(*wider.shape),) * 4),
            still(*attended.shape),
            still(seg, width),
            still(1, width),
        ),
        scratch_shapes=[
            pltpu.VMEM((seg, width), F32),
            pltpu.VMEM((seg, width), F32),
            pltpu.VMEM((seg, 1), F32),
            pltpu.VMEM((seg, width), F32),
            pltpu.VMEM((seg, width), F32),
            pltpu.VMEM((seg, block), BF16),
            pltpu.VMEM((seg, width), BF16),
        ],
        compiler_params=pltpu.CompilerParams(dimension_semantics=("arbitrary",)),
        cost_estimate=cost(100000000000),
        name="trunk_middle",
    )(place, attended, front_out, valid, out_grad, trunk_out, gain, mlp_in, mlp_out)


def trunk_back_kernel(
    place_ref, grads_ref, front_ref, gain_ref, after_ref, valid_ref, aout_ref, wqkv_ref, mixed_ref, gain_grad_ref, *rest
):
    stack_ref, triple_ref, back_ref = rest
    step = pl.program_id(0)
    parts = grads_ref.shape[0]
    seg, width = front_ref.shape
    own = width // parts
    me = place_ref[ME]

    @pl.when(step == 0)
    def _():
        for c in range(3):
            for p in range(parts):
                triple_ref[c, :, p * own : (p + 1) * own] = grads_ref[p, c * seg : (c + 1) * seg, :]
        back_ref[...] = jnp.zeros_like(back_ref)

    back_ref[...] += mm(triple_ref[step], wqkv_ref[...], NT)

    @pl.when(step == pl.num_programs(0) - 1)
    def _():
        front = front_ref[...]
        center = front - jnp.mean(front, axis=1, keepdims=True)
        rate = lax.rsqrt(jnp.mean(center * center, axis=1, keepdims=True) + EPSILON)
        unit = center * rate
        back = back_ref[...]
        gain_grad_ref[...] = jnp.sum(back * unit, axis=0, keepdims=True)
        scaled = back * gain_ref[...]
        inside = jnp.mean(scaled * unit, axis=1, keepdims=True)
        total = rate * (scaled - jnp.mean(scaled, axis=1, keepdims=True) - unit * inside)
        total = ((after_ref[...] + total) * valid_ref[...]).astype(BF16)
        mixed_ref[...] = mm(total, aout_ref[...], NT).astype(BF16)
        part = width // 4
        for v in range(4):
            stack_ref[v, :, 3 * part :] = total[:, v * part : (v + 1) * part]
            for k in range(3):
                block = 3 * v + k
                source = triple_ref[block // 4, :, block % 4 * part : (block % 4 + 1) * part]
                stack_ref[v, :, k * part : (k + 1) * part] = source


def trunk_back(place, grads, front_out, gain, after_grad, valid, agg_out, trunk_qkv):
    seg, width = front_out.shape
    shape = jax.ShapeDtypeStruct

    def still(*dims):
        return pl.BlockSpec(dims, lambda i: (0,) * len(dims))

    piece = shape((seg, width), BF16)
    return pl.pallas_call(
        trunk_back_kernel,
        grid=(3,),
        out_shape=(piece, shape((1, width), F32), shape((4, seg, width), BF16)),
        in_specs=[
            pl.BlockSpec(memory_space=pltpu.SMEM),
            still(*grads.shape),
            still(seg, width),
            still(1, width),
            still(seg, width),
            still(seg, 1),
            still(width, width),
            pl.BlockSpec((width, width), lambda i: (0, i)),
        ],
        out_specs=(still(seg, width), still(1, width), still(4, seg, width)),
        scratch_shapes=[
            pltpu.VMEM((3, seg, width), BF16),
            pltpu.VMEM((seg, width), F32),
        ],
        compiler_params=pltpu.CompilerParams(dimension_semantics=("arbitrary",)),
        cost_estimate=cost(100000000000),
        name="trunk_back",
    )(place, grads, front_out, gain, after_grad, valid, agg_out, trunk_qkv)


def front_last_kernel(
    pixels,
    place_ref,
    m0,
    m1,
    m2,
    m3,
    weight_ref,
    embed_ref,
    weight_own_ref,
    embed_own_ref,
    value_rows_ref,
    key_query_ref,
    key_ref,
    aggq_ref,
    query_rows_ref,
    query_own_ref,
    value_out,
    patch_out,
    embed_out,
    key_out,
    query_out,
    agg_query_out,
    norm_one_out,
    norm_two_out,
    m_ref,
    sum_ref,
):
    rows, width = weight_ref.shape
    own = weight_own_ref.shape[1]
    size = m0.shape[1]
    head_dim = width // HEADS
    scaling = 1.0 / math.sqrt(head_dim)
    for s, ref in enumerate((m0, m1, m2, m3)):
        v = place_ref[ME] ^ s
        m_ref[:, pl.ds(pl.multiple_of((v % 2 * 2 + v // 2) * size, size), size)] = ref[...]
    m_sum, me_sum = m_ref[0:rows, :], m_ref[rows : rows + VARS, :]
    value_out[...] = mm(weight_own_ref[...], m_sum, TN) + mm(embed_own_ref[...], me_sum, TN)
    s_all = m_ref[rows + VARS : rows + VARS + HEADS, :]
    twice = jnp.concatenate([s_all, s_all], axis=0)
    patch_out[...] = mm(m_sum, value_rows_ref[...], NT) + mm(twice[:, 0:rows], key_query_ref[...], TN)
    embed_out[...] = mm(me_sum, value_rows_ref[...], NT) + mm(
        twice[:, rows : rows + VARS], key_query_ref[...], TN
    )
    key_sum = (mm(s_all[:, 0:rows], weight_ref[...]) + mm(s_all[:, rows : rows + VARS], embed_ref[...])) * scaling
    sum_ref[...] = key_sum
    lane = lax.broadcasted_iota(jnp.int32, (HEADS, width), 1) // head_dim
    mine = lane == lax.broadcasted_iota(jnp.int32, (HEADS, width), 0)
    start = pl.multiple_of((place_ref[Z] * 2 + place_ref[Y]) * own, own)
    head_rows = jnp.where(mine, aggq_ref[...], 0.0)
    key_out[...] = mm(sum_ref[:, pl.ds(start, own)], head_rows, TN, precision=HIGHEST)
    crossed = mm(jnp.concatenate(split_high_low(key_sum), axis=0), key_ref[...])
    crossed = crossed[0:HEADS, :] + crossed[HEADS:, :]
    aggq_grad = jnp.sum(jnp.where(mine, crossed, 0.0), axis=0, keepdims=True)
    query_out[...] = query_own_ref[...] * aggq_grad
    high, low = split_high_low(aggq_grad)
    agg_query_out[...] = mm(high, query_rows_ref[...], NT) + mm(low, query_rows_ref[...], NT)
    row = lax.broadcasted_iota(jnp.int32, (HEADS, own), 0)
    tail = s_all[:, width - own :].astype(F32)
    for k in range(own // head_dim):
        line = jnp.sum(jnp.where(row == start // head_dim + k, tail, 0.0), axis=0, keepdims=True)
        norm_one_out[:, k * head_dim : (k + 1) * head_dim] = line[:, 0:head_dim]
        norm_two_out[:, k * head_dim : (k + 1) * head_dim] = line[:, head_dim:own]


def front_last(place, pieces, arrays):
    weight_rows, own_weight, value_rows = arrays[0], arrays[2], arrays[4]
    rows, width = weight_rows.shape
    own = own_weight.shape[1]
    tall = pieces[0].shape[0]
    shapes = [((own, width), F32), ((rows, own), F32), ((VARS, own), F32)] + [((own, width), F32)] * 2
    shapes += [((1, own), F32)] * 3
    return small_call(
        functools.partial(front_last_kernel, rows // VARS),
        place,
        (*pieces, *arrays),
        shapes,
        scratch=[pltpu.VMEM((tall, width), BF16), pltpu.VMEM((HEADS, width), F32)],
        name="front_last",
    )


def local(
    input_field,
    counts,
    var_ids,
    patch_weight,
    var_embed,
    agg_query,
    query_proj,
    key_proj,
    value_proj,
    agg_out,
    norm_one,
    trunk_qkv,
    trunk_out,
    norm_two,
    mlp_in,
    mlp_out,
    cotangent,
):
    patches, group = lax.axis_size("patch"), lax.axis_size("var")
    fast = (patches, group) == (8, 4)
    me, spot = lax.axis_index("var"), lax.axis_index("patch")
    place = jnp.stack([me, me % 2, me // 2, spot % 2, spot // 2]).astype(jnp.int32)
    var_index = lax.axis_index("var")
    patch_index = lax.axis_index("patch")
    all_rows, seg, var_local, pixels = input_field.shape
    width = agg_out.shape[0]
    head_dim = width // HEADS
    hidden = mlp_in.shape[1]
    scaling = 1.0 / math.sqrt(head_dim)

    turned = input_field.transpose(0, 2, 3, 1).reshape(all_rows, var_local * pixels, seg)
    own_field = lax.all_to_all(turned, "var", split_axis=0, concat_axis=1, tiled=True)
    own_field = own_field.reshape(VARS * pixels, seg)
    own_ids = lax.dynamic_slice_in_dim(var_ids, var_index, 1, 0)
    own_count = lax.dynamic_slice_in_dim(counts, var_index, 1, 0)
    positions = patch_index * seg + jnp.arange(seg, dtype=jnp.int32)
    valid_rows = (positions < own_count).astype(F32)[:, None]
    out_grad = cotangent.reshape(seg, width).astype(F32) * valid_rows
    out_grad_low = out_grad.astype(BF16)

    weight_rows = patch_weight.reshape(VARS * pixels, width)
    agg_q = mm(agg_query[None], query_proj)[0]
    in_head = jnp.arange(width, dtype=jnp.int32)[:, None] // head_dim == jnp.arange(HEADS)[None, :]
    head_query = jnp.where(in_head, agg_q[:, None] * scaling, 0.0)
    key_query = mm(key_proj, jnp.concatenate(split_high_low(head_query), axis=1))
    key_query = key_query[:, :HEADS] + key_query[:, HEADS:]
    key_query_parts = jnp.concatenate(split_high_low(key_query), axis=1)
    score_weight = mm(key_query_parts, weight_rows, (((0,), (1,)), ((), ())))
    score_weight = score_weight[:HEADS] + score_weight[HEADS:]
    score_embed = mm(key_query_parts, var_embed, (((0,), (1,)), ((), ())))
    score_embed = score_embed[:HEADS] + score_embed[HEADS:]
    vwt = mm(value_proj, weight_rows, (((0,), (1,)), ((), ()))).astype(BF16)
    vet = mm(value_proj, var_embed, (((0,), (1,)), ((), ()))).astype(BF16)

    own_width = width // patches
    start = patch_index * own_width

    def own_cols(values):
        return lax.dynamic_slice_in_dim(values, start, own_width, 1)

    def own_rows(values):
        return lax.dynamic_slice_in_dim(values, start, own_width, 0)

    def own_query(values):
        return lax.dynamic_slice_in_dim(values, start, own_width, 0).astype(F32)[:, None]

    def last_operands(ready):
        weights, embeds, values, queries, line, key_queries, _ = together(
            weight_rows, var_embed, value_proj, query_proj, agg_query, key_query, ready
        )
        return (
            weights,
            embeds,
            own_cols(weights),
            own_cols(embeds),
            own_rows(values),
            jnp.concatenate(split_high_low(own_rows(key_queries)), axis=1).T,
            key_proj,
            agg_q[None],
            own_rows(queries),
            own_query(line),
        )

    x_own, shares, mixed_low, spread = front_forward(own_ids, own_field, score_weight, score_embed, vwt, vet)

    front_out = mm(mixed_low, agg_out) * valid_rows
    normed_one, norm_one_pull = jax.vjp(layer_norm, front_out, norm_one.astype(F32))
    normed_one_low = normed_one.astype(BF16)
    triple = mm(normed_one_low, trunk_qkv).astype(BF16)
    part = width // group
    quarter = hidden // group
    zs = patches // 2
    ready = after(value_proj, triple)
    vw = mm(weight_rows, ready).astype(BF16)
    ve = mm(var_embed, ready).astype(BF16)
    if fast:
        early = tokens_of_group(jnp.concatenate([out_grad_low, mixed_low, normed_one_low], axis=1))
        qkv, vw, ve, *arrays = together(queries_to_heads(triple), vw, ve, *last_operands(triple))
        count = own_count.reshape(1, 1)
        heads, lse = attend_forward(count, qkv, head_dim)
        attended = to_heads(heads.reshape(patches, seg, own_width))
        results = middle(
            place,
            attended,
            front_out,
            valid_rows,
            out_grad_low,
            trunk_out,
            norm_two.astype(F32)[None],
            mlp_in,
            mlp_out,
        )
        attended_group = copies_of_group(attended)
        results = together(*results, *attended_group, *early)
        attended_group, early = results[13:17], results[17:]
        block_out, normed_two_low, grads, after_grad, norm_two_grad = (results[k] for k in (0, 1, 10, 11, 12))
        block_out = block_out[None]
        grads = to_heads(grads)
        active_group = slices_of_group(results[2:6])
        across = swap(normed_two_low, "var", 2)
        result = attend_backward(count, qkv, grads.reshape(patches * seg, own_width), lse, head_dim)
        result, across, *rest = together(result, across, *active_group, *results[6:10])
        active_group, middle_group = rest[:4], slices_of_group(rest[4:])
        normed_group = (normed_two_low, swap(normed_two_low, "var", 1), across, swap(across, "var", 1))
        result = to_heads(result)
        pairs, whole_order = ((1, 3), (0, 2)), ((1, 3, 0, 2),)
        jobs = ((0, 0, 1, 0, width),)
        near_one, away_one = weight_grads(place, jobs, (active_group, early), own_width, pairs, whole_order)
        jobs = ((0, 0, 2, 0, quarter), (1, 0, 2, quarter, part))
        groups = (together(normed_group[0], *near_one)[:1] + normed_group[1:], attended_group, middle_group)
        near_two, away_two = weight_grads(place, jobs, groups, own_width, pairs, pairs)
        result = after(result, *near_two)
        one = {"near": near_one, "got": swap(away_one[0], "patch", 1)}
        two = {"near": near_two, "away": away_two}
        mixed_grad, norm_one_grad, stack = trunk_back(
            place, result, front_out, norm_one.astype(F32)[None], after_grad, valid_rows, agg_out, trunk_qkv
        )
        one["far"] = pair_sum(place, after(one["near"][0], mixed_grad), one["got"])
        mixed_grad = after(mixed_grad, one["far"])
        last_group = lax.all_to_all(stack, "var", split_axis=0, concat_axis=0, tiled=True)
    else:
        attended, attention_pull = gathered_attention(triple, own_count, head_dim)
        after_attn = front_out + mm(attended, trunk_out)
        normed_two, norm_two_pull = jax.vjp(layer_norm, after_attn, norm_two.astype(F32))
        normed_two_low = normed_two.astype(BF16)
        inner = mm(normed_two_low, mlp_in)
        active, gelu_pull = jax.vjp(gelu_exact, inner)
        active_low = active.astype(BF16)
        result = after_attn + mm(active_low, mlp_out)
        block_out = (result * valid_rows).astype(BF16)[None]
        inner_grad = gelu_pull(mm(out_grad_low, mlp_out, NT))[0].astype(BF16)
        normed_two_grad = mm(inner_grad, mlp_in, NT)
        after_ln_grad, norm_two_grad = norm_two_pull(normed_two_grad)
        after_grad = out_grad + after_ln_grad
        branch_low = after_grad.astype(BF16)
        triple_grad = attention_pull(mm(branch_low, trunk_out, NT).astype(BF16))
        normed_one_grad = mm(triple_grad, trunk_qkv, NT)
        front_ln_grad, norm_one_grad = norm_one_pull(normed_one_grad)
        agg_grad = ((after_grad + front_ln_grad) * valid_rows).astype(BF16)
        mixed_grad = mm(agg_grad, agg_out, NT).astype(BF16)
        norm_one_grad, norm_two_grad = norm_one_grad[None], norm_two_grad[None]

    field_low, *m_parts = front_backward(
        fast, place, own_ids, x_own, shares, mixed_grad, vw, ve, spread, norm_one_grad, norm_two_grad
    )

    field_low = field_low.reshape(group, var_local * pixels, seg)
    field_grad = None if fast else lax.all_to_all(field_low, "var", split_axis=0, concat_axis=0, tiled=True)

    if fast:
        m_stay, m_away, two["first"], last_group = together(*m_parts, swap(two["away"][0], "patch", 1), last_group)
        m_parts = (m_stay, m_away)
        two["far"] = pair_sum(place, two["near"][0], two["first"])
        last, marks = {}, []

        def core_done(values):
            return values

        def x_done(values):
            far = swap(one["far"], "patch", 2)
            far, near, _ = together(far, one["near"][1], *marks)
            one["pair"] = z_first_sum(place, near, one["got"], far)
            return after(values, one["pair"][0])

        def y_done(values):
            jobs = ((0, 2 * width, 1, 0, 3 * part), (0, width, 1, 3 * part, part))
            groups = (early, after(last_group, marks[-1]))
            last["near"], last["away"] = weight_grads(place, jobs, groups, own_width, pairs, whole_order)
            got = swap(after(two["away"][1], two["first"]), "patch", 1)
            values, got, far, *_ = together(values, got, swap(two["far"], "patch", 2), *last["near"])
            two["pair"] = z_first_sum(place, two["near"][1], got, far)
            return values

        def z_done(values):
            near, away = one["pair"]
            *values, got, _ = together(*values, swap(away, "patch", 4), two["pair"][0])
            one["own"] = z_last_sum(place, near, got)
            return values

        def b_done(values):
            near, away = two["pair"]
            *values, last["got"], got = together(*values, swap(last["away"][0], "patch", 1), swap(away, "patch", 4))
            late = after(field_low, last["got"])
            last["field"] = lax.all_to_all(late, "var", split_axis=0, concat_axis=0, tiled=True)
            last["far"] = pair_sum(place, last["near"][0], last["got"])
            two["own"] = z_last_sum(place, near, got)
            return [after(values[0], last["far"]), *values[1:]]

        def y_back(values):
            values, one["across"], last["field"] = together(values, swap(one["own"], "var", 2), last["field"])

            def field_kernel(place_ref, field_ref, out):
                out[...] = field_ref[...]

            field = last["field"]
            last["field"] = small_call(field_kernel, place, (field,), [(field.shape, BF16)], name="field_out")[0]
            return values

        def var_done(values):
            far, across = swap(last["far"], "patch", 2), swap(two["own"], "var", 2)
            near, away = z_first_sum(place, last["near"][1], last["got"], far)
            two["parts"] = (two["own"], swap(two["own"], "var", 1), across, swap(across, "var", 1))
            last["own"] = z_last_sum(place, near, swap(away, "patch", 4))
            own, across = one["own"], one["across"]
            moved = (swap(own, "var", 1), swap(across, "var", 1), near)
            values, inner, corner, *_ = together(values, *moved, last["field"])
            one["parts"] = (own, inner, across, corner)
            return values

        m_pieces = sum_over_all(place, *m_parts, (core_done, x_done, y_done, z_done, b_done, y_back, var_done), marks)
        field_grad = last["field"]
        (mlp_out_grad,) = join(place, one["parts"], (width,), 1)
        mlp_in_grad, trunk_out_grad = join(place, two["parts"], (quarter, part), 0)
        mlp_out_grad = mlp_out_grad.reshape(hidden // patches, width)
        trunk_qkv_grad, agg_out_grad = join(place, gather_over_var(last["own"]), (3 * part, part), 0)
    else:

        def slices(values):
            values = values.reshape(seg, group, values.shape[1] // group).transpose(1, 0, 2)
            return lax.all_to_all(values, "var", split_axis=0, concat_axis=0, tiled=True)

        def everyone(values):
            return lax.all_gather(values, "var", axis=0, tiled=True)

        def total(left, right):
            value = mm(left.reshape(-1, left.shape[-1]), right.reshape(-1, right.shape[-1]), TN).astype(BF16)
            value = lax.psum_scatter(value, "patch", scatter_dimension=0, tiled=True)
            return lax.all_gather(value, "var", axis=0)

        def joined(value):
            return value.transpose(1, 0, 2).reshape(value.shape[1], -1).astype(F32)

        size = hidden // (patches * group)
        active_rows = active_low.reshape(seg, patches, group, size).transpose(0, 2, 1, 3).reshape(seg, hidden)
        mlp_out_grad = total(slices(active_rows), everyone(out_grad_low)).reshape(hidden // patches, width).astype(F32)
        mlp_in_grad = joined(total(everyone(normed_two_low), slices(inner_grad)))
        trunk_out_grad = joined(total(everyone(attended), slices(branch_low)))
        trunk_qkv_grad = joined(total(everyone(normed_one_low), slices(triple_grad)))
        agg_out_grad = joined(total(everyone(mixed_low), slices(agg_grad)))
        m_all = lax.psum(m_parts[0], ("patch", "var")).transpose(1, 0, 2).reshape(-1, width)
    if fast:
        value_proj_grad, patch_grad, embed_grad, key_proj_grad, query_proj_grad, *lines = front_last(
            place, m_pieces, arrays
        )
        agg_query_grad, norm_one_grad, norm_two_grad = (line[0] for line in lines)
    else:
        value_rows, key_query_rows = own_rows(value_proj), own_rows(key_query)
        m_sum, me_sum = m_all[: VARS * pixels], m_all[VARS * pixels : VARS * pixels + VARS]
        s_rows = m_all[VARS * pixels + VARS :].astype(F32)
        s_all = s_rows[:, : VARS * pixels]
        se_all = s_rows[:, VARS * pixels : VARS * pixels + VARS]
        norm_sums = s_rows[:, width - 2 * head_dim :]
        value_proj_grad = mm(own_cols(weight_rows), m_sum, TN) + mm(own_cols(var_embed), me_sum, TN)
        patch_grad = mm(m_sum, value_rows, NT) + mm(
            s_all, key_query_rows, (((0,), (1,)), ((), ())), precision=HIGHEST
        )
        embed_grad = mm(me_sum, value_rows, NT) + mm(
            se_all, key_query_rows, (((0,), (1,)), ((), ())), precision=HIGHEST
        )
        key_sum = (mm(s_all.astype(BF16), weight_rows) + mm(se_all.astype(BF16), var_embed)) * scaling
        head_rows = jnp.where(in_head.T, agg_q[None, :], 0.0)
        key_proj_grad = mm(own_cols(key_sum), head_rows, TN, precision=HIGHEST)
        crossed = mm(jnp.concatenate(split_high_low(key_sum), axis=0), key_proj)
        crossed = crossed[:HEADS] + crossed[HEADS:]
        aggq_grad = jnp.sum(jnp.where(in_head.T, crossed, 0.0), axis=0)
        query_proj_grad = own_query(agg_query) * aggq_grad[None, :]
        agg_query_grad = jnp.sum(own_rows(query_proj).astype(F32) * aggq_grad[None, :], axis=1)
        norm_one_grad = lax.dynamic_slice_in_dim(norm_sums[:, :head_dim].reshape(width), start, own_width, 0)
        norm_two_grad = lax.dynamic_slice_in_dim(norm_sums[:, head_dim:].reshape(width), start, own_width, 0)
    patch_grad = patch_grad.reshape(VARS, pixels, own_width)
    field_grad = field_grad.reshape(all_rows, var_local, pixels, seg).transpose(0, 3, 1, 2)
    return (
        block_out,
        field_grad,
        patch_grad,
        embed_grad,
        agg_query_grad,
        query_proj_grad,
        key_proj_grad,
        value_proj_grad,
        agg_out_grad,
        norm_one_grad,
        trunk_qkv_grad,
        trunk_out_grad,
        norm_two_grad,
        mlp_in_grad,
        mlp_out_grad,
    )


def solution(mesh):
    whole = P()
    placed = (P(None, "patch", "var", None),) + (whole,) * 15 + (P("var", "patch", None),)
    rows = P("patch", None)
    return jax.shard_map(
        local,
        mesh=mesh,
        in_specs=placed,
        out_specs=(
            P("var", "patch", None),
            P(None, "patch", "var", None),
            P(None, None, "patch"),
            P(None, "patch"),
            P("patch"),
            rows,
            rows,
            rows,
            rows,
            P("patch"),
            rows,
            rows,
            P("patch"),
            rows,
            rows,
        ),
        check_vma=False,
    )
```
